32 devices in a mesh: seq: 2 (over core), fsdp: 16 (over z, y, x).
Axes of the slice: x: 2, y: 2, z: 4, core: 2. Of those that a mesh axis runs over, the one named last changes fastest.
Arguments:
- byte_inputs: bfloat16 [16, 2048, 768], P('fsdp', 'seq'), may hold values from -6 to 6
- segment_ids: int32 [16, 256], P('fsdp'), may hold values from 0 to 31, never falling along the last dimension, each value on 1 to 128 neighbouring positions
- cotangent: bfloat16 [16, 2048, 768], P('fsdp', 'seq'), may hold values from -6 to 6
- patch_weight: bfloat16 [6144, 768], P('fsdp'), may hold values from -0.078125 to 0.078125
- coarse_first_gain: bfloat16 [768], P('fsdp'), may hold values from 0.25 to 1.75
- coarse_first_bias: bfloat16 [768], P('fsdp'), may hold values from -3 to 3
- coarse_project: bfloat16 [768, 2304], P('fsdp'), may hold values from -0.21875 to 0.21875
- coarse_output: bfloat16 [768, 768], P(None, 'fsdp'), may hold values from -0.875 to 0.875
- coarse_second_gain: bfloat16 [768], P('fsdp'), may hold values from 0.25 to 1.75
- coarse_second_bias: bfloat16 [768], P('fsdp'), may hold values from -3 to 3
- coarse_expand: bfloat16 [768, 3072], P('fsdp'), may hold values from -0.21875 to 0.21875
- coarse_narrow: bfloat16 [3072, 768], P(None, 'fsdp'), may hold values from -0.15625 to 0.15625
- fine_first_gain: bfloat16 [768], P('fsdp'), may hold values from 0.25 to 1.75
- fine_first_bias: bfloat16 [768], P('fsdp'), may hold values from -3 to 3
- fine_project: bfloat16 [768, 2304], P('fsdp'), may hold values from -0.21875 to 0.21875
- fine_output: bfloat16 [768, 768], P(None, 'fsdp'), may hold values from -0.4375 to 0.4375
- fine_second_gain: bfloat16 [768], P('fsdp'), may hold values from 0.25 to 1.75
- fine_second_bias: bfloat16 [768], P('fsdp'), may hold values from -3 to 3
- fine_expand: bfloat16 [768, 3072], P('fsdp'), may hold values from -0.21875 to 0.21875
- fine_narrow: bfloat16 [3072, 768], P(None, 'fsdp'), may hold values from -0.15625 to 0.15625
Outputs:
- layer_output: bfloat16 [16, 2048, 768], P('fsdp', 'seq')
- input_gradient: bfloat16 [16, 2048, 768], P('fsdp', 'seq')
- gradient_patch_weight: float32 [6144, 768], P('fsdp')
- gradient_coarse_first_gain: float32 [768], P('fsdp')
- gradient_coarse_first_bias: float32 [768], P('fsdp')
- gradient_coarse_project: float32 [768, 2304], P('fsdp')
- gradient_coarse_output: float32 [768, 768], P(None, 'fsdp')
- gradient_coarse_second_gain: float32 [768], P('fsdp')
- gradient_coarse_second_bias: float32 [768], P('fsdp')
- gradient_coarse_expand: float32 [768, 3072], P('fsdp')
- gradient_coarse_narrow: float32 [3072, 768], P(None, 'fsdp')
- gradient_fine_first_gain: float32 [768], P('fsdp')
- gradient_fine_first_bias: float32 [768], P('fsdp')
- gradient_fine_project: float32 [768, 2304], P('fsdp')
- gradient_fine_output: float32 [768, 768], P(None, 'fsdp')
- gradient_fine_second_gain: float32 [768], P('fsdp')
- gradient_fine_second_bias: float32 [768], P('fsdp')
- gradient_fine_expand: float32 [768, 3072], P('fsdp')
- gradient_fine_narrow: float32 [3072, 768], P(None, 'fsdp')
The draws below stay inside these ranges and needn't reach their ends.
Inputs may be any that keep to these rules, and one draw needn't show every extreme that they name: `segment_ids`: along each sequence the document number never falls from one patch to the next, starting at 0; a document covers at most 128 patches.
All inputs are finite; a program needn't handle non-finite values.
Results may differ from the reference program's by a relative error of at most 0.018.
Values may be sent and summed in bfloat16 or wider, within the bound.
A program may use at most 256 MiB of HBM per device.

```python
import math
from functools import partial
import jax
import jax.numpy as jnp
import numpy as np
from jax import lax

D = 768
HEADS = 12
HEAD_DIM = 64
FF = 3072
PATCH = 8
NPATCH = 256
LEN = 2048
SEQS = 16


def strengthened(values, rng, source, target, blocks, factor):
    owner, partner = [(jnp.arange(values.shape[position]) // (values.shape[position] // blocks)).reshape([-1 if axis == position else 1 for axis in range(values.ndim)]) for position in (source, target)]
    chosen = jax.random.permutation(rng, blocks)[partner]
    strong = (owner == chosen) | (owner == (partner + blocks // 2) % blocks)
    return jnp.where(strong, factor * values, values)


def shard_levels(own_key, dims, pieces, low, largest):
    level = 1.0
    for axis_at, parts in pieces:
        draws = jax.random.uniform(jax.random.fold_in(jax.random.fold_in(own_key, 6), axis_at), (parts,), jnp.float32, low / len(pieces), largest / len(pieces))
        level = level * jnp.repeat(jnp.exp(draws), dims[axis_at] // parts).reshape((-1,) + (1,) * (len(dims) - 1 - axis_at))
    return level


def profile(count, total, reach, slope):
    loads = [(1 << 20) // math.isqrt(standing ** slope) + 1 for standing in range(2, count + 1)]
    surplus, counts = total - reach - (count - 1), [1] * (count - 1)
    while surplus > 0:
        candidates = [i for i in range(count - 1) if counts[i] < reach]
        whole, remaining = sum([loads[i] for i in candidates]), surplus
        for i in candidates:
            more = min(reach - counts[i], max(1, remaining * loads[i] // whole), surplus)
            counts[i] = counts[i] + more
            surplus = surplus - more
    return np.array([reach] + counts)


def uneven_parts(own_key, count, total, reach, slope):
    if count == 2:
        one = jax.random.randint(own_key, (), max(1, total - reach), min(reach, total - 1) + 1)
        return jnp.stack([one, total - one])
    sizes = jnp.asarray(profile(count, total, reach, slope), jnp.int32)
    couples = (count - 1) // 2
    giver, receiver = sizes[1:1 + 2 * couples:2], sizes[2:2 + 2 * couples:2]
    slack = jnp.minimum(giver - 1, reach - receiver)
    passed = jax.random.randint(jax.random.fold_in(own_key, 1), (couples,), 0, 1 << 20) % (slack + 1)
    sizes = sizes.at[1:1 + 2 * couples:2].set(giver - passed).at[2:2 + 2 * couples:2].set(receiver + passed)
    return sizes[jax.random.permutation(jax.random.fold_in(own_key, 2), count)]


def scatter_about(own_key, dims, scale, most, cuts=(), dtype=jnp.bfloat16):
    values = scale * jax.random.normal(own_key, dims, jnp.float32)
    if cuts:
        values = values * shard_levels(own_key, dims, cuts, -0.22, 0.18)
    return jnp.clip(values, -most, most).astype(dtype)


def noise_with(key, shape, deviation, bound, cuts, heavy, dtype=jnp.bfloat16):
    entries = deviation * jax.random.normal(key, shape, jnp.float32)
    if cuts:
        entries = entries * shard_levels(key, shape, cuts, -0.22, 0.18)
    return jnp.clip(strengthened(entries, jax.random.fold_in(key, 3), *heavy), -bound, bound).astype(dtype)


def setup_inputs(seed: int = 0) -> dict:
    key_of = jax.random.split(jax.random.key(seed), 21)
    byte_inputs = scatter_about(key_of[0], (SEQS, LEN, D), 1.0, 6.0, ((0, 16), (1, 2)))
    segment_ids = jax.vmap(lambda own: jnp.searchsorted(jnp.cumsum(uneven_parts(own, max(4, NPATCH // 8), NPATCH, NPATCH // 2, 2)), jnp.arange(NPATCH), side="right"))(jax.random.split(key_of[1], SEQS)).reshape((SEQS, NPATCH)).astype(jnp.int32)
    cotangent = noise_with(key_of[2], (SEQS, LEN, D), 1.0, 6.0, ((0, 16), (1, 2)), (0, 2, 16, 2.0))
    patch_weight = scatter_about(key_of[3], (PATCH * D, D), (PATCH * D) ** -0.5, 0.078125, ((0, 16),))
    coarse_first_gain = jnp.clip(1.0 + 0.15 * jax.random.normal(key_of[4], (D,), jnp.float32), 0.25, 1.75).astype(jnp.bfloat16)
    coarse_first_bias = scatter_about(key_of[5], (D,), 0.3, 3.0, ((0, 16),))
    coarse_project = scatter_about(key_of[6], (D, 3 * D), D ** -0.5, 0.21875, ((0, 16),))
    coarse_output = scatter_about(key_of[7], (D, D), (D // 16) ** -0.5, 0.875, ((1, 16),))
    coarse_second_gain = jnp.clip(1.0 + 0.15 * jax.random.normal(key_of[8], (D,), jnp.float32), 0.25, 1.75).astype(jnp.bfloat16)
    coarse_second_bias = scatter_about(key_of[9], (D,), 0.3, 3.0, ((0, 16),))
    coarse_expand = scatter_about(key_of[10], (D, FF), D ** -0.5, 0.21875, ((0, 16),))
    coarse_narrow = scatter_about(key_of[11], (FF, D), (FF // 2) ** -0.5, 0.15625, ((1, 16),))
    fine_first_gain = jnp.clip(1.0 + 0.15 * jax.random.normal(key_of[12], (D,), jnp.float32), 0.25, 1.75).astype(jnp.bfloat16)
    fine_first_bias = scatter_about(key_of[13], (D,), 0.3, 3.0, ((0, 16),))
    fine_project = scatter_about(key_of[14], (D, 3 * D), D ** -0.5, 0.21875, ((0, 16),))
    fine_output = scatter_about(key_of[15], (D, D), (D // 4) ** -0.5, 0.4375, ((1, 16),))
    fine_second_gain = jnp.clip(1.0 + 0.15 * jax.random.normal(key_of[16], (D,), jnp.float32), 0.25, 1.75).astype(jnp.bfloat16)
    fine_second_bias = scatter_about(key_of[17], (D,), 0.3, 3.0, ((0, 16),))
    fine_expand = scatter_about(key_of[18], (D, FF), D ** -0.5, 0.21875, ((0, 16),))
    fine_narrow = scatter_about(key_of[19], (FF, D), (FF // 2) ** -0.5, 0.15625, ((1, 16),))
    return dict(byte_inputs=byte_inputs, segment_ids=segment_ids, cotangent=cotangent, patch_weight=patch_weight, coarse_first_gain=coarse_first_gain, coarse_first_bias=coarse_first_bias, coarse_project=coarse_project, coarse_output=coarse_output, coarse_second_gain=coarse_second_gain, coarse_second_bias=coarse_second_bias, coarse_expand=coarse_expand, coarse_narrow=coarse_narrow, fine_first_gain=fine_first_gain, fine_first_bias=fine_first_bias, fine_project=fine_project, fine_output=fine_output, fine_second_gain=fine_second_gain, fine_second_bias=fine_second_bias, fine_expand=fine_expand, fine_narrow=fine_narrow)


epsilon = 1e-05

@jax.custom_vjp
def low(v):
    return lax.optimization_barrier(v.astype(jnp.bfloat16)).astype(jnp.float32)

@jax.custom_vjp
def low_back(v):
    return v

def low_keep(v):
    return (low(v), None)

def low_pass(kept, grad):
    return (grad,)

def back_keep(v):
    return (v, None)

def back_low(kept, grad):
    return (low(grad),)
low.defvjp(low_keep, low_pass)
low_back.defvjp(back_keep, back_low)

def layer_norm(values, norm_gain, norm_bias):
    center = lax.optimization_barrier(jnp.mean(values, -1, keepdims=True))
    centred = values - center
    spread = lax.optimization_barrier(jnp.mean(centred * centred, -1, keepdims=True))
    return centred * lax.rsqrt(spread + epsilon) * norm_gain + norm_bias

def product(left_side, right_side):
    return jnp.dot(left_side, right_side, precision=lax.Precision.HIGHEST)

def attention(queries, key_part, value_part, allowed):
    factor = 1.0 / math.sqrt(HEAD_DIM)
    scores = low_back(jnp.einsum('bqhd,bkhd->bhqk', queries, key_part, precision=lax.Precision.HIGHEST) * factor)
    scores = jnp.where(allowed[:, None], scores, -1e+30)
    chances = low(jax.nn.softmax(scores, axis=-1))
    return jnp.einsum('bhqk,bkhd->bqhd', chances, value_part, precision=lax.Precision.HIGHEST)

def coarse_mix(triple, segment_row):
    grouped = triple.reshape(1, NPATCH, 3, HEADS, HEAD_DIM)
    places = jnp.arange(NPATCH)
    allowed = ((places[:, None] >= places[None, :]) & (segment_row[:, None] == segment_row[None, :]))[None]
    mixture = attention(grouped[:, :, 0], grouped[:, :, 1], grouped[:, :, 2], allowed)
    return mixture.reshape(NPATCH, D)

def fine_mix(triple):
    grouped = triple.reshape(NPATCH, PATCH, 3, HEADS, HEAD_DIM)
    places = jnp.arange(PATCH)
    allowed = (places[:, None] >= places[None, :])[None]
    mixture = attention(grouped[:, :, 0], grouped[:, :, 1], grouped[:, :, 2], allowed)
    return mixture.reshape(LEN, D)

def residual_block(inputs, weights, mixer):
    first_gain, first_bias, project, output, second_gain, second_bias, expand, narrow = weights
    normed = low(layer_norm(inputs, first_gain, first_bias))
    triple = low(low_back(product(normed, project)))
    mixture = low(low_back(mixer(triple)))
    middle = inputs + low_back(product(mixture, output))
    second = low(layer_norm(middle, second_gain, second_bias))
    lifted = low_back(product(second, expand))
    hidden = low(jax.nn.gelu(lifted, approximate=True))
    return middle + low_back(product(hidden, narrow))

def sequence_forward(byte_rows, segment_row, params):
    grouped = byte_rows.reshape(NPATCH, PATCH * D)
    embedded = low_back(product(grouped, params[0]))
    coarse_out = residual_block(embedded, params[1:9], partial(coarse_mix, segment_row=segment_row))
    coarse_low = low(coarse_out)
    padded = jnp.concatenate([segment_row[:1] - 1, segment_row])
    joined = (padded[:-1] == segment_row).astype(jnp.float32)
    previous = jnp.concatenate([jnp.zeros((1, D), jnp.float32), coarse_low[:-1]]) * joined[:, None]
    fine_in = (byte_rows.reshape(NPATCH, PATCH, D) + previous[:, None, :]).reshape(LEN, D)
    return residual_block(fine_in, params[9:17], fine_mix)

def reference(byte_inputs, segment_ids, cotangent, patch_weight, coarse_first_gain, coarse_first_bias, coarse_project, coarse_output, coarse_second_gain, coarse_second_bias, coarse_expand, coarse_narrow, fine_first_gain, fine_first_bias, fine_project, fine_output, fine_second_gain, fine_second_bias, fine_expand, fine_narrow):
    params = tuple((weight_item.astype(jnp.float32) for weight_item in (patch_weight, coarse_first_gain, coarse_first_bias, coarse_project, coarse_output, coarse_second_gain, coarse_second_bias, coarse_expand, coarse_narrow, fine_first_gain, fine_first_bias, fine_project, fine_output, fine_second_gain, fine_second_bias, fine_expand, fine_narrow)))

    def per_sequence(running, sequence_inputs):
        byte_rows, segment_row, grad_rows = sequence_inputs
        layer_rows, pullback = jax.vjp(lambda row_values, weight_set: sequence_forward(row_values, segment_row, weight_set), byte_rows.astype(jnp.float32), params)
        grad_bytes, grad_params = pullback(grad_rows.astype(jnp.float32))
        running = jax.tree.map(lambda total, term: total + term, running, grad_params)
        return (running, (layer_rows.astype(jnp.bfloat16), grad_bytes.astype(jnp.bfloat16)))
    empty = jax.tree.map(jnp.zeros_like, params)
    totals, (layer_output, input_gradient) = lax.scan(per_sequence, empty, (byte_inputs, segment_ids, cotangent))
    return (layer_output, input_gradient, totals[0], totals[1], totals[2], totals[3], totals[4], totals[5], totals[6], totals[7], totals[8], totals[9], totals[10], totals[11], totals[12], totals[13], totals[14], totals[15], totals[16])
```

```python
import functools
import math

import jax
import jax.numpy as jnp
from jax import lax
from jax.experimental import pallas as pl
from jax.experimental.pallas import tpu as pltpu
from jax.sharding import PartitionSpec as P


D = 768
HEAD_DIM = 64
PATCH = 8


epsilon = 1e-05


def shifted(block, axis, distance):
    devices = range(lax.axis_size(axis))
    route = [(i - distance, i) for i in devices if i - distance in devices]
    return lax.ppermute(block, axis, route)


def layer_norm(values, norm_gain, norm_bias):
    center = jnp.mean(values, -1, keepdims=True)
    centred = values - center
    spread = jnp.mean(centred * centred, -1, keepdims=True)
    return centred * lax.rsqrt(spread + epsilon) * norm_gain + norm_bias


def smooth_gate(values):
    return jax.nn.gelu(values, approximate=True)


def product(left_side, right_side):
    return jnp.dot(left_side, right_side, preferred_element_type=jnp.float32)


def left_product(left_side, right_side):
    return lax.dot_general(
        left_side, right_side, (((0,), (0,)), ((), ())), preferred_element_type=jnp.float32
    )


def right_product(left_side, right_side):
    return lax.dot_general(
        left_side, right_side, (((1,), (1,)), ((), ())), preferred_element_type=jnp.float32
    )


def attend_forward(queries, key_part, value_part, allowed):
    factor = 1.0 / math.sqrt(HEAD_DIM)
    scores = (
        jnp.einsum("bqhd,bkhd->bhqk", queries, key_part, preferred_element_type=jnp.float32)
        * factor
    )
    scores = jnp.where(allowed[:, None], scores, -1e30)
    highest = jnp.max(scores, -1, keepdims=True)
    log_total = highest + jnp.log(jnp.sum(jnp.exp(scores - highest), -1, keepdims=True))
    rounded = jnp.exp(scores - log_total).astype(jnp.bfloat16)
    mixture = jnp.einsum("bhqk,bkhd->bqhd", rounded, value_part, preferred_element_type=jnp.float32)
    return (mixture, log_total)


def attend_backward(queries, key_part, value_part, allowed, log_total, grad_mixture):
    factor = 1.0 / math.sqrt(HEAD_DIM)
    scores = (
        jnp.einsum("bqhd,bkhd->bhqk", queries, key_part, preferred_element_type=jnp.float32)
        * factor
    )
    scores = jnp.where(allowed[:, None], scores, -1e30)
    chances = jnp.exp(scores - log_total)
    rounded = chances.astype(jnp.bfloat16)
    grad_values = jnp.einsum(
        "bhqk,bqhd->bkhd", rounded, grad_mixture, preferred_element_type=jnp.float32
    )
    grad_chances = jnp.einsum(
        "bqhd,bkhd->bhqk", grad_mixture, value_part, preferred_element_type=jnp.float32
    )
    grad_scores = (
        chances * (grad_chances - jnp.sum(grad_chances * chances, -1, keepdims=True))
    ).astype(jnp.bfloat16)
    grad_queries = (
        jnp.einsum("bhqk,bkhd->bqhd", grad_scores, key_part, preferred_element_type=jnp.float32)
        * factor
    )
    grad_keys = (
        jnp.einsum("bhqk,bqhd->bkhd", grad_scores, queries, preferred_element_type=jnp.float32)
        * factor
    )
    return (grad_queries, grad_keys, grad_values)


def block_forward(inputs, weights, attend):
    first_gain, first_bias, project, output, second_gain, second_bias, expand, narrow = weights
    normed = layer_norm(
        inputs, first_gain.astype(jnp.float32), first_bias.astype(jnp.float32)
    ).astype(jnp.bfloat16)
    triple = product(normed, project).astype(jnp.bfloat16)
    mixture, attend_stored = attend(triple)
    middle = inputs + product(mixture, output)
    second = layer_norm(
        middle, second_gain.astype(jnp.float32), second_bias.astype(jnp.float32)
    ).astype(jnp.bfloat16)
    lifted = product(second, expand)
    hidden = smooth_gate(lifted).astype(jnp.bfloat16)
    result = middle + product(hidden, narrow)
    stored = (inputs, normed, attend_stored, mixture, middle, second, lifted, hidden)
    return (result, stored)


def block_backward(grad_result, weights, stored, attend_back):
    first_gain, first_bias, project, output, second_gain, second_bias, expand, narrow = weights
    inputs, normed, attend_stored, mixture, middle, second, lifted, hidden = stored
    grad_branch = grad_result.astype(jnp.bfloat16)
    grad_narrow = left_product(hidden, grad_branch)
    grad_hidden = right_product(grad_branch, narrow)
    grad_lifted = jax.vjp(smooth_gate, lifted)[1](grad_hidden)[0].astype(jnp.bfloat16)
    grad_expand = left_product(second, grad_lifted)
    grad_second = right_product(grad_lifted, expand)
    pullback = jax.vjp(
        layer_norm, middle, second_gain.astype(jnp.float32), second_bias.astype(jnp.float32)
    )[1]
    grad_middle, grad_gain_two, grad_bias_two = pullback(grad_second)
    grad_middle = grad_middle + grad_result
    grad_attended = grad_middle.astype(jnp.bfloat16)
    grad_output = left_product(mixture, grad_attended)
    grad_mixture = right_product(grad_attended, output).astype(jnp.bfloat16)
    grad_triple = attend_back(grad_mixture, attend_stored)
    grad_project = left_product(normed, grad_triple)
    grad_normed = right_product(grad_triple, project)
    pullback = jax.vjp(
        layer_norm, inputs, first_gain.astype(jnp.float32), first_bias.astype(jnp.float32)
    )[1]
    grad_inputs, grad_gain_one, grad_bias_one = pullback(grad_normed)
    grad_inputs = grad_inputs + grad_middle
    return (
        grad_inputs,
        (
            grad_gain_one,
            grad_bias_one,
            grad_project,
            grad_output,
            grad_gain_two,
            grad_bias_two,
            grad_expand,
            grad_narrow,
        ),
    )


def body(
    byte_inputs,
    segment_ids,
    cotangent,
    patch_weight,
    coarse_first_gain,
    coarse_first_bias,
    coarse_project,
    coarse_output,
    coarse_second_gain,
    coarse_second_bias,
    coarse_expand,
    coarse_narrow,
    fine_first_gain,
    fine_first_bias,
    fine_project,
    fine_output,
    fine_second_gain,
    fine_second_bias,
    fine_expand,
    fine_narrow,
):
    coarse_full = (
        lax.all_gather(patch_weight, "fsdp", axis=0, tiled=True),
        lax.all_gather(coarse_first_gain, "fsdp", axis=0, tiled=True),
        lax.all_gather(coarse_first_bias, "fsdp", axis=0, tiled=True),
        lax.all_gather(coarse_project, "fsdp", axis=0, tiled=True),
        lax.all_gather(coarse_output, "fsdp", axis=1, tiled=True),
        lax.all_gather(coarse_second_gain, "fsdp", axis=0, tiled=True),
        lax.all_gather(coarse_second_bias, "fsdp", axis=0, tiled=True),
        lax.all_gather(coarse_expand, "fsdp", axis=0, tiled=True),
        lax.all_gather(coarse_narrow, "fsdp", axis=1, tiled=True),
    )
    fine_full = (
        lax.all_gather(fine_first_gain, "fsdp", axis=0, tiled=True),
        lax.all_gather(fine_first_bias, "fsdp", axis=0, tiled=True),
        lax.all_gather(fine_project, "fsdp", axis=0, tiled=True),
        lax.all_gather(fine_output, "fsdp", axis=1, tiled=True),
        lax.all_gather(fine_second_gain, "fsdp", axis=0, tiled=True),
        lax.all_gather(fine_second_bias, "fsdp", axis=0, tiled=True),
        lax.all_gather(fine_expand, "fsdp", axis=0, tiled=True),
        lax.all_gather(fine_narrow, "fsdp", axis=1, tiled=True),
    )
    byte_rows = byte_inputs[0]
    bytes_here = byte_rows.shape[0]
    patches = bytes_here // PATCH
    segment_row = segment_ids[0]
    all_patches = segment_row.shape[0]
    places = jnp.arange(all_patches)
    coarse_allowed = (
        (places[:, None] >= places[None, :]) & (segment_row[:, None] == segment_row[None, :])
    )[None]
    inner = jnp.arange(PATCH)
    fine_allowed = (inner[:, None] >= inner[None, :])[None]

    def coarse_attend(triple):
        head_block = lax.all_to_all(
            triple.reshape(patches, 3, D), "seq", split_axis=2, concat_axis=0, tiled=True
        )
        all_rows = head_block.shape[0]
        columns = head_block.shape[2]
        local_heads = columns // HEAD_DIM
        queries = head_block[:, 0].reshape(1, all_rows, local_heads, HEAD_DIM)
        key_part = head_block[:, 1].reshape(1, all_rows, local_heads, HEAD_DIM)
        value_part = head_block[:, 2].reshape(1, all_rows, local_heads, HEAD_DIM)
        mixture, log_total = attend_forward(queries, key_part, value_part, coarse_allowed)
        merged = mixture.reshape(all_rows, columns).astype(jnp.bfloat16)
        back_rows = lax.all_to_all(merged, "seq", split_axis=0, concat_axis=1, tiled=True)
        return (back_rows, (queries, key_part, value_part, log_total))

    def coarse_back(grad_mixture, stored):
        queries, key_part, value_part, log_total = stored
        head_grad = lax.all_to_all(grad_mixture, "seq", split_axis=1, concat_axis=0, tiled=True)
        all_rows = head_grad.shape[0]
        columns = head_grad.shape[1]
        grad_queries, grad_keys, grad_values = attend_backward(
            queries,
            key_part,
            value_part,
            coarse_allowed,
            log_total,
            head_grad.reshape(1, all_rows, columns // HEAD_DIM, HEAD_DIM),
        )
        stacked = jnp.stack(
            [
                grad_queries.reshape(all_rows, columns),
                grad_keys.reshape(all_rows, columns),
                grad_values.reshape(all_rows, columns),
            ],
            1,
        ).astype(jnp.bfloat16)
        back_rows = lax.all_to_all(stacked, "seq", split_axis=0, concat_axis=2, tiled=True)
        return back_rows.reshape(back_rows.shape[0], 3 * D)

    def fine_attend(triple):
        grouped = triple.reshape(patches, PATCH, 3, D // HEAD_DIM, HEAD_DIM)
        queries = grouped[:, :, 0]
        key_part = grouped[:, :, 1]
        value_part = grouped[:, :, 2]
        mixture, log_total = attend_forward(queries, key_part, value_part, fine_allowed)
        return (
            mixture.reshape(bytes_here, D).astype(jnp.bfloat16),
            (queries, key_part, value_part, log_total),
        )

    def fine_back(grad_mixture, stored):
        queries, key_part, value_part, log_total = stored
        grad_queries, grad_keys, grad_values = attend_backward(
            queries,
            key_part,
            value_part,
            fine_allowed,
            log_total,
            grad_mixture.reshape(patches, PATCH, D // HEAD_DIM, HEAD_DIM),
        )
        stacked = jnp.stack([grad_queries, grad_keys, grad_values], 2).astype(jnp.bfloat16)
        return stacked.reshape(bytes_here, 3 * D)

    grouped_bytes = byte_rows.reshape(patches, PATCH * D)
    embedded = product(grouped_bytes, coarse_full[0])
    coarse_out, coarse_stored = block_forward(embedded, coarse_full[1:], coarse_attend)
    coarse_low = coarse_out.astype(jnp.bfloat16)
    arrived = shifted(coarse_low[-1:], "seq", 1)
    offset = lax.axis_index("seq") * patches
    padded = jnp.concatenate([segment_row[:1] - 1, segment_row])
    before = lax.dynamic_slice_in_dim(padded, offset, patches)
    current = lax.dynamic_slice_in_dim(segment_row, offset, patches)
    joined = (before == current).astype(jnp.float32)[:, None]
    previous = jnp.concatenate([arrived, coarse_low[:-1]]).astype(jnp.float32) * joined
    fine_in = (
        byte_rows.astype(jnp.float32).reshape(patches, PATCH, D) + previous[:, None, :]
    ).reshape(bytes_here, D)
    layer_rows, fine_stored = block_forward(fine_in, fine_full, fine_attend)
    fine_weights_back = (
        lax.all_gather(fine_first_gain, "fsdp", axis=0, tiled=True),
        lax.all_gather(fine_first_bias, "fsdp", axis=0, tiled=True),
        lax.all_gather(fine_project, "fsdp", axis=0, tiled=True),
        lax.all_gather(fine_output, "fsdp", axis=1, tiled=True),
        lax.all_gather(fine_second_gain, "fsdp", axis=0, tiled=True),
        lax.all_gather(fine_second_bias, "fsdp", axis=0, tiled=True),
        lax.all_gather(fine_expand, "fsdp", axis=0, tiled=True),
        lax.all_gather(fine_narrow, "fsdp", axis=1, tiled=True),
    )
    grad_fine_in, fine_grads = block_backward(
        cotangent[0].astype(jnp.float32), fine_weights_back, fine_stored, fine_back
    )
    grad_previous = jnp.sum(grad_fine_in.reshape(patches, PATCH, D), 1) * joined
    arrived_back = shifted(grad_previous[:1], "seq", -1)
    grad_coarse_out = jnp.concatenate([grad_previous[1:], arrived_back])
    coarse_weights_back = (
        lax.all_gather(patch_weight, "fsdp", axis=0, tiled=True),
        lax.all_gather(coarse_first_gain, "fsdp", axis=0, tiled=True),
        lax.all_gather(coarse_first_bias, "fsdp", axis=0, tiled=True),
        lax.all_gather(coarse_project, "fsdp", axis=0, tiled=True),
        lax.all_gather(coarse_output, "fsdp", axis=1, tiled=True),
        lax.all_gather(coarse_second_gain, "fsdp", axis=0, tiled=True),
        lax.all_gather(coarse_second_bias, "fsdp", axis=0, tiled=True),
        lax.all_gather(coarse_expand, "fsdp", axis=0, tiled=True),
        lax.all_gather(coarse_narrow, "fsdp", axis=1, tiled=True),
    )
    grad_embedded, coarse_grads = block_backward(
        grad_coarse_out, coarse_weights_back[1:], coarse_stored, coarse_back
    )
    grad_embed_low = grad_embedded.astype(jnp.bfloat16)
    grad_patch = left_product(grouped_bytes, grad_embed_low)
    grad_grouped = right_product(grad_embed_low, coarse_weights_back[0])
    input_gradient = (grad_fine_in + grad_grouped.reshape(bytes_here, D)).astype(jnp.bfloat16)
    shards = (
        lax.psum_scatter(grad_patch, "fsdp", scatter_dimension=0, tiled=True),
        lax.psum_scatter(coarse_grads[0], "fsdp", scatter_dimension=0, tiled=True),
        lax.psum_scatter(coarse_grads[1], "fsdp", scatter_dimension=0, tiled=True),
        lax.psum_scatter(coarse_grads[2], "fsdp", scatter_dimension=0, tiled=True),
        lax.psum_scatter(coarse_grads[3], "fsdp", scatter_dimension=1, tiled=True),
        lax.psum_scatter(coarse_grads[4], "fsdp", scatter_dimension=0, tiled=True),
        lax.psum_scatter(coarse_grads[5], "fsdp", scatter_dimension=0, tiled=True),
        lax.psum_scatter(coarse_grads[6], "fsdp", scatter_dimension=0, tiled=True),
        lax.psum_scatter(coarse_grads[7], "fsdp", scatter_dimension=1, tiled=True),
        lax.psum_scatter(fine_grads[0], "fsdp", scatter_dimension=0, tiled=True),
        lax.psum_scatter(fine_grads[1], "fsdp", scatter_dimension=0, tiled=True),
        lax.psum_scatter(fine_grads[2], "fsdp", scatter_dimension=0, tiled=True),
        lax.psum_scatter(fine_grads[3], "fsdp", scatter_dimension=1, tiled=True),
        lax.psum_scatter(fine_grads[4], "fsdp", scatter_dimension=0, tiled=True),
        lax.psum_scatter(fine_grads[5], "fsdp", scatter_dimension=0, tiled=True),
        lax.psum_scatter(fine_grads[6], "fsdp", scatter_dimension=0, tiled=True),
        lax.psum_scatter(fine_grads[7], "fsdp", scatter_dimension=1, tiled=True),
    )
    totals = (
        lax.psum(shards[0].astype(jnp.bfloat16), "seq").astype(jnp.float32),
        lax.psum(shards[1].astype(jnp.bfloat16), "seq").astype(jnp.float32),
        lax.psum(shards[2].astype(jnp.bfloat16), "seq").astype(jnp.float32),
        lax.psum(shards[3].astype(jnp.bfloat16), "seq").astype(jnp.float32),
        lax.psum(shards[4].astype(jnp.bfloat16), "seq").astype(jnp.float32),
        lax.psum(shards[5].astype(jnp.bfloat16), "seq").astype(jnp.float32),
        lax.psum(shards[6].astype(jnp.bfloat16), "seq").astype(jnp.float32),
        lax.psum(shards[7].astype(jnp.bfloat16), "seq").astype(jnp.float32),
        lax.psum(shards[8].astype(jnp.bfloat16), "seq").astype(jnp.float32),
        lax.psum(shards[9].astype(jnp.bfloat16), "seq").astype(jnp.float32),
        lax.psum(shards[10].astype(jnp.bfloat16), "seq").astype(jnp.float32),
        lax.psum(shards[11].astype(jnp.bfloat16), "seq").astype(jnp.float32),
        lax.psum(shards[12].astype(jnp.bfloat16), "seq").astype(jnp.float32),
        lax.psum(shards[13].astype(jnp.bfloat16), "seq").astype(jnp.float32),
        lax.psum(shards[14].astype(jnp.bfloat16), "seq").astype(jnp.float32),
        lax.psum(shards[15].astype(jnp.bfloat16), "seq").astype(jnp.float32),
        lax.psum(shards[16].astype(jnp.bfloat16), "seq").astype(jnp.float32),
    )
    layer_output = layer_rows.astype(jnp.bfloat16)[None]
    return (
        layer_output,
        input_gradient[None],
        totals[0],
        totals[1],
        totals[2],
        totals[3],
        totals[4],
        totals[5],
        totals[6],
        totals[7],
        totals[8],
        totals[9],
        totals[10],
        totals[11],
        totals[12],
        totals[13],
        totals[14],
        totals[15],
        totals[16],
    )


MESH = pl.DeviceIdType.MESH
HBM = pltpu.MemorySpace.HBM
VMEM = pltpu.MemorySpace.VMEM


class Place:
    def __init__(self):
        self.core = lax.axis_index("seq")
        self.at = lax.axis_index("fsdp")
        self.z = self.at // 4
        self.plane = self.at % 4
        self.near = 1 + self.core
        self.far = 2 - self.core

    def flip(self, mask):
        return self.at ^ mask

    def across(self, mask):
        return (self.core, self.at ^ mask)

    def partner(self):
        return (1 - self.core, self.at)


def enter(place, masks, partner=True):
    barrier = pltpu.get_barrier_semaphore()
    for mask in masks:
        pl.semaphore_signal(barrier, inc=1, device_id=place.across(mask), device_id_type=MESH)
    if partner:
        pl.semaphore_signal(barrier, inc=1, device_id=place.partner(), device_id_type=MESH)
    pl.semaphore_wait(barrier, len(masks) + (1 if partner else 0))


MASKS = (1, 2, 4, 8, 12)


class Gather:
    EVENTS = 12

    def __init__(self, place, source, buffer, rows, column, width, z_first, sends, receives, local):
        self.p, self.source, self.buffer, self.rows = place, source, buffer, rows
        self.z_first, self.sends, self.receives, self.local = z_first, sends, receives, local
        self.half = width // 2
        self.column, self.width = column, width
        self.mine = pl.ds(pl.multiple_of(column + place.core * self.half, 128), self.half)
        self.theirs = pl.ds(pl.multiple_of(column + (1 - place.core) * self.half, 128), self.half)
        self.started = []

    def group(self, plane, columns=None):
        return self.buffer.at[:, plane, self.rows, self.mine if columns is None else columns]

    def block(self, z, plane):
        return self.buffer.at[z, plane, self.rows, self.mine]

    def send(self, event, view, device, source=None):
        copy = pltpu.make_async_remote_copy(
            src_ref=view if source is None else source,
            dst_ref=view,
            send_sem=self.sends.at[event],
            recv_sem=self.receives.at[event],
            device_id=device,
            device_id_type=MESH,
        )
        copy.start()
        self.started.append(copy)

    def arrived(self, event, view):
        pltpu.make_async_remote_copy(
            src_ref=view,
            dst_ref=view,
            send_sem=self.sends.at[event],
            recv_sem=self.receives.at[event],
            device_id=self.p.partner(),
            device_id_type=MESH,
        ).wait_recv()

    def start(self):
        p = self.p
        own = self.source.at[self.rows, pl.ds(pl.multiple_of(p.core * self.half, 128), self.half)]
        self.copy = pltpu.make_async_copy(own, self.block(p.z, p.plane), self.local)
        self.copy.start()
        if not self.z_first:
            self.send(6, self.block(p.z, p.plane), p.across(p.near), own)
        for j in (1, 2, 3):
            self.send(j - 1, self.block(p.z, p.plane), p.across(4 * j), own)

    def one(self):
        p = self.p
        self.copy.wait()
        if self.z_first:
            for j in (1, 2, 3):
                self.arrived(j - 1, self.block(p.z ^ j, p.plane))
            self.send(6, self.group(p.plane), p.across(p.near))
            self.send(7, self.group(p.plane), p.across(p.far))
            self.send(9, self.group(p.plane), p.partner())
        else:
            self.arrived(6, self.block(p.z, p.plane ^ p.near))
            for j in (1, 2, 3):
                self.send(2 + j, self.block(p.z, p.plane ^ p.near), p.across(4 * j))

    def two(self):
        p = self.p
        if self.z_first:
            self.arrived(6, self.group(p.plane ^ p.near))
        else:
            for j in (1, 2, 3):
                self.arrived(j - 1, self.block(p.z ^ j, p.plane))
            self.send(7, self.group(p.plane), p.across(p.far))
            self.send(9, self.group(p.plane), p.partner())
            for j in (1, 2, 3):
                self.arrived(2 + j, self.block(p.z ^ j, p.plane ^ p.near))
        self.send(8, self.group(p.plane ^ p.near), p.across(p.far))
        self.send(10, self.group(p.plane ^ p.near), p.partner())

    def three(self):
        p = self.p
        self.arrived(7, self.group(p.plane ^ p.far))
        self.send(11, self.group(p.plane ^ p.far), p.partner())
        self.arrived(8, self.group(p.plane ^ 3))
        self.send(12, self.group(p.plane ^ 3), p.partner())

    def four(self):
        p = self.p
        self.arrived(9, self.group(p.plane, self.theirs))
        self.arrived(10, self.group(p.plane ^ p.far, self.theirs))
        self.arrived(11, self.group(p.plane ^ p.near, self.theirs))
        self.arrived(12, self.group(p.plane ^ 3, self.theirs))

    def drain(self):
        for copy in self.started:
            copy.wait_send()


def run_gathers(gathers, ahead, tick):
    n = len(gathers)
    for k in range(min(ahead, n)):
        gathers[k].start()
    for t in range(n + 3):
        if t < n:
            gathers[t].one()
            if t + ahead < n:
                gathers[t + ahead].start()
        if 0 <= t - 1 < n:
            gathers[t - 1].two()
        if 0 <= t - 2 < n:
            gathers[t - 2].three()
        if 0 <= t - 3 < n:
            gathers[t - 3].four()
        tick()
    for g in gathers:
        g.drain()


def gather_kernel(plan, ahead, *refs):
    sources, small, rows, rest = refs[:9], refs[9], refs[10], refs[11:]
    buffers, small_out, all_rows = rest[:3], rest[3], rest[4]
    sends, receives, local, value, arriving, small_sends, small_receives, row_sems = rest[5:]
    place = Place()
    enter(place, MASKS)
    value[0] = small[...]
    total = Total(place, (1, 2, 4, 8), value, arriving, small_sends, small_receives, small_out)
    stay = pltpu.make_async_copy(rows, all_rows.at[place.core], row_sems.at[0])
    stay.start()
    cross = pltpu.make_async_remote_copy(
        src_ref=rows, dst_ref=all_rows.at[place.core], send_sem=row_sems.at[1], recv_sem=row_sems.at[2],
        device_id=place.partner(), device_id_type=MESH,
    )
    cross.start()
    gathers = []
    for k, (source, buffer, first, rows, column, width, z_first) in enumerate(plan):
        gathers.append(
            Gather(place, sources[source], buffers[buffer], pl.ds(first, rows), column, width, z_first,
                   sends.at[k], receives.at[k], local.at[k])
        )
    run_gathers(gathers, ahead, total.advance)
    stay.wait()
    cross.wait()


PLAN = (
    (0, 0, 0, 192, 0, 768, True),
    (0, 0, 192, 192, 0, 768, False),
    (1, 1, 0, 48, 0, 2304, True),
    (2, 1, 0, 48, 2304, 768, True),
    (3, 1, 0, 48, 3072, 3072, True),
    (4, 1, 0, 48, 6144, 3072, False),
    (5, 2, 0, 48, 0, 2304, True),
    (6, 2, 0, 48, 2304, 768, True),
    (7, 2, 0, 48, 3072, 3072, False),
    (8, 2, 0, 48, 6144, 3072, True),
)


def gather_all(sources, small, rows, ahead=2, plan=PLAN):
    n = len(plan)
    bf = jnp.bfloat16
    return pl.pallas_call(
        functools.partial(gather_kernel, plan, ahead),
        out_shape=(
            jax.ShapeDtypeStruct((4, 4, 384, 768), bf),
            jax.ShapeDtypeStruct((4, 4, 48, 9216), bf),
            jax.ShapeDtypeStruct((4, 4, 48, 9216), bf),
            jax.ShapeDtypeStruct((8, 768), jnp.float32),
            jax.ShapeDtypeStruct((2,) + rows.shape, bf),
        ),
        in_specs=[pl.BlockSpec(memory_space=VMEM)] * 10 + [pl.BlockSpec(memory_space=HBM)],
        out_specs=[pl.BlockSpec(memory_space=HBM)] * 3 + [pl.BlockSpec(memory_space=VMEM), pl.BlockSpec(memory_space=HBM)],
        scratch_shapes=[
            pltpu.SemaphoreType.DMA((n, 13)),
            pltpu.SemaphoreType.DMA((n, 13)),
            pltpu.SemaphoreType.DMA((n,)),
            pltpu.VMEM((5, 8, 768), jnp.float32),
            pltpu.VMEM((4, 8, 768), jnp.float32),
            pltpu.SemaphoreType.DMA((4,)),
            pltpu.SemaphoreType.DMA((4,)),
            pltpu.SemaphoreType.DMA((3,)),
        ],
        compiler_params=pltpu.CompilerParams(collective_id=0, has_side_effects=True),
        name="gather_all",
    )(*sources, small, rows)


class Total:
    def __init__(self, place, masks, value, arriving, sends, receives, result):
        self.p, self.masks, self.value, self.arriving = place, masks, value, arriving
        self.sends, self.receives, self.result = sends, receives, result
        self.step, self.copy = 0, None

    def advance(self):
        if self.step > len(self.masks):
            return
        if self.copy is not None:
            self.copy.wait()
            i = self.step - 1
            self.value[i + 1] = self.value[i] + self.arriving[i]
        if self.step < len(self.masks):
            i = self.step
            mask = self.masks[i]
            self.copy = pltpu.make_async_remote_copy(
                src_ref=self.value.at[i],
                dst_ref=self.arriving.at[i],
                send_sem=self.sends.at[i],
                recv_sem=self.receives.at[i],
                device_id=self.p.across(mask) if mask else self.p.partner(),
                device_id_type=MESH,
            )
            self.copy.start()
        else:
            self.result[...] = self.value[len(self.masks)]
        self.step += 1


def add(left, right):
    return left.astype(jnp.float32) + right.astype(jnp.float32)


class Reduce:
    def __init__(self, place, held, paired, far, near, line, out, rows, column, width, z_last, sends, receives):
        self.p, self.held, self.from_partner, self.from_far = place, held, paired, far
        self.from_near, self.from_line, self.out, self.rows = near, line, out, rows
        self.z_last, self.sends, self.receives = z_last, sends, receives
        self.half = width // 2
        self.mine = pl.ds(pl.multiple_of(column + place.core * self.half, 128), self.half)
        self.theirs = pl.ds(pl.multiple_of(column + (1 - place.core) * self.half, 128), self.half)
        self.started = []

    def send(self, event, source, target, device):
        copy = pltpu.make_async_remote_copy(
            src_ref=source, dst_ref=target, send_sem=self.sends.at[event], recv_sem=self.receives.at[event],
            device_id=device, device_id_type=MESH,
        )
        copy.start()
        self.started.append(copy)

    def arrived(self, event, target):
        pltpu.make_async_remote_copy(
            src_ref=target, dst_ref=target, send_sem=self.sends.at[event], recv_sem=self.receives.at[event],
            device_id=self.p.partner(), device_id_type=MESH,
        ).wait_recv()

    def pair(self, theirs):
        self.send(0, theirs, self.from_partner, self.p.partner())

    def fold(self, plane, others):
        def step(z, _):
            self.held[z, plane] = add(self.held[z, plane], others[z]).astype(jnp.bfloat16)
            return 0

        lax.fori_loop(0, 4, step, 0)

    def one(self):
        p = self.p
        if self.from_partner is not None:
            self.arrived(0, self.from_partner)
            self.fold(p.plane ^ p.far, self.from_partner.at[:, p.plane ^ p.far])
        self.send(1, self.held.at[:, p.plane ^ p.far], self.from_far.at[0], p.across(p.far))
        if self.from_partner is not None:
            self.fold(p.plane ^ 3, self.from_partner.at[:, p.plane ^ 3])
        self.send(2, self.held.at[:, p.plane ^ 3], self.from_far.at[1], p.across(p.far))
        if self.from_partner is not None:
            self.fold(p.plane, self.from_partner.at[:, p.plane])
            self.fold(p.plane ^ p.near, self.from_partner.at[:, p.plane ^ p.near])

    def two(self):
        p = self.p
        self.arrived(2, self.from_far.at[1])
        self.fold(p.plane ^ p.near, self.from_far.at[1])
        if self.z_last:
            self.send(3, self.held.at[:, p.plane ^ p.near], self.from_near, p.across(p.near))
        else:
            for j in (1, 2, 3):
                self.send(6 + j, self.held.at[p.z ^ j, p.plane ^ p.near], self.from_line.at[2 + j], p.across(4 * j))
        self.arrived(1, self.from_far.at[0])
        self.fold(p.plane, self.from_far.at[0])
        if not self.z_last:
            for j in (1, 2, 3):
                self.send(3 + j, self.held.at[p.z ^ j, p.plane], self.from_line.at[j - 1], p.across(4 * j))

    def three(self):
        p = self.p
        if self.z_last:
            self.arrived(3, self.from_near)
            self.fold(p.plane, self.from_near)
            for j in (1, 2, 3):
                self.send(3 + j, self.held.at[p.z ^ j, p.plane], self.from_line.at[j - 1], p.across(4 * j))
        else:
            for j in (1, 2, 3):
                self.arrived(6 + j, self.from_line.at[2 + j])
            near = (add(self.held[p.z, p.plane ^ p.near], self.from_line[3]) + add(self.from_line[4], self.from_line[5]))
            self.held[p.z, p.plane ^ p.near] = near.astype(jnp.bfloat16)
            self.send(3, self.held.at[p.z, p.plane ^ p.near], self.from_near.at[0], p.across(p.near))

    def four(self):
        p = self.p
        for j in (1, 2, 3):
            self.arrived(3 + j, self.from_line.at[j - 1])
        total = add(self.held[p.z, p.plane], self.from_line[0]) + add(self.from_line[1], self.from_line[2])
        if not self.z_last:
            self.arrived(3, self.from_near.at[0])
            total = total + self.from_near[0].astype(jnp.float32)
        self.out[self.rows, self.mine] = total
        view = self.out.at[self.rows, self.mine]
        self.send(10, view, view, p.partner())

    def drain(self):
        for copy in self.started:
            copy.wait_send()
        self.started = []

    def five(self):
        self.arrived(10, self.out.at[self.rows, self.theirs])


BACK_PLAN = (
    (2, 0, 48, 6144, 3072, True),
    (2, 0, 48, 3072, 3072, False),
    (2, 0, 48, 2304, 768, True),
    (2, 0, 48, 0, 2304, True),
    (1, 0, 48, 6144, 3072, True),
    (1, 0, 48, 3072, 3072, False),
    (1, 0, 48, 2304, 768, True),
    (1, 0, 48, 0, 2304, True),
    (0, 0, 192, 0, 768, False),
    (0, 192, 192, 0, 768, True),
)
SLOTS = 3


def reduce_kernel(plan, grads, small, outs, small_out, slots, pairs, fars, nears, lines, sends, receives, loads,
                  value, arriving, small_sends, small_receives):
    place = Place()
    enter(place, MASKS)
    n = len(plan)
    value[0] = small[...]
    total = Total(place, (0, 1, 2, 4, 8), value, arriving, small_sends, small_receives, small_out)
    used = [0, 0]
    reduces, copies = [], []
    for k, (array, first, rows, column, width, z_last) in enumerate(plan):
        kind = 0 if array == 0 else 1
        slot = used[kind] % SLOTS if kind else used[kind]
        used[kind] += 1
        half = width // 2
        cut = (lambda ref, kind=kind, half=half: ref if not kind or half == 1536 else ref.at[..., pl.ds(0, half)])
        reduces.append(
            Reduce(place, cut(slots[kind].at[slot]), cut(pairs.at[used[kind] - 1]) if array == 2 else None, cut(fars[kind].at[used[kind] - 1]),
                   cut(nears[kind].at[used[kind] - 1]), cut(lines[kind].at[used[kind] - 1]), outs[array],
                   pl.ds(first, rows), column, width, z_last, sends.at[k], receives.at[k])
        )

    def load(k):
        array, first, rows, column, width, z_last = plan[k]
        r = reduces[k]
        if k - SLOTS >= 0:
            reduces[k - SLOTS].drain()
        copy = pltpu.make_async_copy(grads[array].at[:, :, r.rows, r.mine], r.held, loads.at[k])
        copy.start()
        copies.append(copy)
        if array == 2:
            r.pair(grads[array].at[:, :, r.rows, r.theirs])

    for t in range(n + 4):
        if t - 4 >= 0:
            reduces[t - 4].five()
        if 0 <= t - 3 < n:
            reduces[t - 3].four()
        if t < n:
            load(t)
        if 0 <= t - 2 < n:
            reduces[t - 2].three()
        if 0 <= t - 1 < n:
            reduces[t - 1].two()
        if t < n:
            copies[t].wait()
            reduces[t].one()
        total.advance()
    for r in reduces:
        r.drain()


def reduce_all(grads, small, plan=BACK_PLAN):
    n = len(plan)
    bf = jnp.bfloat16
    shapes = ((2, 192, 384), (8, 48, 1536))

    def kernel(*refs):
        grads, small, outs, small_out = refs[:3], refs[3], refs[4:7], refs[7]
        pairs = refs[8]
        slots, fars, nears, lines = (refs[9 + 2 * i : 11 + 2 * i] for i in range(4))
        reduce_kernel(plan, grads, small, outs, small_out, slots, pairs, fars, nears, lines, *refs[17:])

    scratch = [pltpu.VMEM((4, 4, 4, 48, 1536), bf)]
    for lead in (((2, 4, 4), (SLOTS, 4, 4)), ((2, 2, 4), (8, 2, 4)), ((2, 4), (8, 4)), ((2, 6), (8, 6))):
        scratch += [pltpu.VMEM(lead[i] + shapes[i][1:], bf) for i in (0, 1)]
    scratch += [
        pltpu.SemaphoreType.DMA((n, 11)),
        pltpu.SemaphoreType.DMA((n, 11)),
        pltpu.SemaphoreType.DMA((n,)),
        pltpu.VMEM((6, 8, 768), jnp.float32),
        pltpu.VMEM((5, 8, 768), jnp.float32),
        pltpu.SemaphoreType.DMA((5,)),
        pltpu.SemaphoreType.DMA((5,)),
    ]
    return pl.pallas_call(
        kernel,
        out_shape=(
            jax.ShapeDtypeStruct((384, 768), jnp.float32),
            jax.ShapeDtypeStruct((48, 9216), jnp.float32),
            jax.ShapeDtypeStruct((48, 9216), jnp.float32),
            jax.ShapeDtypeStruct((8, 768), jnp.float32),
        ),
        in_specs=[pl.BlockSpec(memory_space=HBM)] * 3 + [pl.BlockSpec(memory_space=VMEM)],
        out_specs=[pl.BlockSpec(memory_space=VMEM)] * 4,
        scratch_shapes=scratch,
        compiler_params=pltpu.CompilerParams(collective_id=1, has_side_effects=True, vmem_limit_bytes=66_000_000),
        name="reduce_all",
    )(*grads, small)


def fast_body(byte_inputs, segment_ids, cotangent, patch_weight, *weights):
    coarse, fine = weights[:8], weights[8:]
    core, at = lax.axis_index("seq"), lax.axis_index("fsdp")
    vectors = jnp.stack([w[i] for w in (coarse, fine) for i in (0, 1, 4, 5)]).astype(jnp.float32)
    small = lax.dynamic_update_slice(jnp.zeros((8, D), jnp.float32), vectors, (0, at * vectors.shape[1]))
    sources = [patch_weight]
    for w in (coarse, fine):
        sources += [w[2], w[3].T, w[6], w[7].T]
    byte_rows = byte_inputs[0]
    bytes_here = byte_rows.shape[0]
    patches = bytes_here // PATCH
    patch_full, coarse_full, fine_full, small, all_rows = gather_all(sources, small, byte_rows)
    patch_full = patch_full.reshape(-1, D)

    def unpack(full, first):
        full = full.reshape(D, -1)
        return (small[first], small[first + 1], full[:, : 3 * D], full[:, 3 * D : 4 * D], small[first + 2], small[first + 3],
                full[:, 4 * D : 8 * D], full[:, 8 * D :])

    coarse_w, fine_w = unpack(coarse_full, 0), unpack(fine_full, 4)
    segment_row = segment_ids[0]
    all_patches = segment_row.shape[0]
    places = jnp.arange(all_patches)
    coarse_allowed = (
        (places[:, None] >= places[None, :]) & (segment_row[:, None] == segment_row[None, :])
    )[None]
    inner = jnp.arange(PATCH)
    fine_allowed = (inner[:, None] >= inner[None, :])[None]

    def attend(shape, allowed):
        rows = shape[0] * shape[1]

        def forward(triple):
            grouped = triple.reshape(shape + (3, D // HEAD_DIM, HEAD_DIM))
            parts = grouped[:, :, 0], grouped[:, :, 1], grouped[:, :, 2]
            mixture, log_total = attend_forward(*parts, allowed)
            return (mixture.reshape(rows, D).astype(jnp.bfloat16), parts + (log_total,))

        def backward(grad_mixture, stored):
            queries, key_part, value_part, log_total = stored
            grads = attend_backward(
                queries, key_part, value_part, allowed, log_total,
                grad_mixture.reshape(shape + (D // HEAD_DIM, HEAD_DIM)),
            )
            return jnp.stack(grads, 2).astype(jnp.bfloat16).reshape(rows, 3 * D)

        return forward, backward

    coarse_attend, coarse_back = attend((1, all_patches), coarse_allowed)
    fine_attend, fine_back = attend((patches, PATCH), fine_allowed)
    grouped_bytes = all_rows.reshape(all_patches, PATCH * D)
    embedded = product(grouped_bytes, patch_full)
    coarse_out, coarse_stored = block_forward_t(embedded, coarse_w, coarse_attend)
    coarse_low = coarse_out.astype(jnp.bfloat16)
    joined = jnp.concatenate([jnp.zeros((1,), bool), segment_row[1:] == segment_row[:-1]]).astype(jnp.float32)[:, None]
    previous = jnp.concatenate([jnp.zeros((1, D), jnp.bfloat16), coarse_low[:-1]]).astype(jnp.float32) * joined
    previous = lax.dynamic_slice_in_dim(previous, core * patches, patches)
    fine_in = (
        byte_rows.astype(jnp.float32).reshape(patches, PATCH, D) + previous[:, None, :]
    ).reshape(bytes_here, D)
    layer_rows, fine_stored = block_forward_t(fine_in, fine_w, fine_attend)
    grad_fine_in, fine_grads = block_backward_t(cotangent[0].astype(jnp.float32), fine_w, fine_stored, fine_back)
    grad_previous = jnp.sum(grad_fine_in.reshape(patches, PATCH, D), 1)
    grad_previous = lax.all_gather(grad_previous, "seq", axis=0, tiled=True) * joined
    grad_coarse_out = jnp.concatenate([grad_previous[1:], jnp.zeros((1, D), jnp.float32)])
    grad_embedded, coarse_grads = block_backward_t(grad_coarse_out, coarse_w, coarse_stored, coarse_back)
    grad_embed_low = grad_embedded.astype(jnp.bfloat16)
    grad_patch = left_product(grouped_bytes, grad_embed_low)
    grad_here = lax.dynamic_slice_in_dim(grad_embed_low, core * patches, patches)
    grad_grouped = right_product(grad_here, patch_full)
    input_gradient = (grad_fine_in + grad_grouped.reshape(bytes_here, D)).astype(jnp.bfloat16)

    def pack(grads):
        return jnp.concatenate([grads[2], grads[3], grads[6], grads[7]], 1).astype(jnp.bfloat16).reshape(4, 4, 48, 12 * D)

    once = (core == 0).astype(jnp.float32)
    small = jnp.stack([coarse_grads[i] * once for i in (0, 1, 4, 5)] + [fine_grads[i] for i in (0, 1, 4, 5)])
    patch_shard, coarse_shard, fine_shard, small = reduce_all(
        (grad_patch.astype(jnp.bfloat16).reshape(4, 4, 384, D), pack(coarse_grads), pack(fine_grads)), small
    )
    small = lax.dynamic_slice_in_dim(small, at * vectors.shape[1], vectors.shape[1], 1)

    def shards(full, first):
        return (small[first], small[first + 1], full[:, : 3 * D], full[:, 3 * D : 4 * D].T, small[first + 2],
                small[first + 3], full[:, 4 * D : 8 * D], full[:, 8 * D :].T)

    return (layer_rows.astype(jnp.bfloat16)[None], input_gradient[None], patch_shard) + shards(coarse_shard, 0) + shards(fine_shard, 4)


def block_forward_t(inputs, weights, attend):
    first_gain, first_bias, project, output_t, second_gain, second_bias, expand, narrow_t = weights
    normed = layer_norm(inputs, first_gain, first_bias).astype(jnp.bfloat16)
    triple = product(normed, project).astype(jnp.bfloat16)
    mixture, attend_stored = attend(triple)
    middle = inputs + right_product(mixture, output_t)
    second = layer_norm(middle, second_gain, second_bias).astype(jnp.bfloat16)
    lifted = product(second, expand)
    hidden = smooth_gate(lifted).astype(jnp.bfloat16)
    result = middle + right_product(hidden, narrow_t)
    stored = (inputs, normed, attend_stored, mixture, middle, second, lifted, hidden)
    return (result, stored)


def block_backward_t(grad_result, weights, stored, attend_back):
    first_gain, first_bias, project, output_t, second_gain, second_bias, expand, narrow_t = weights
    inputs, normed, attend_stored, mixture, middle, second, lifted, hidden = stored
    grad_branch = grad_result.astype(jnp.bfloat16)
    grad_narrow_t = left_product(grad_branch, hidden)
    grad_hidden = product(grad_branch, narrow_t)
    grad_lifted = jax.vjp(smooth_gate, lifted)[1](grad_hidden)[0].astype(jnp.bfloat16)
    grad_expand = left_product(second, grad_lifted)
    grad_second = right_product(grad_lifted, expand)
    pullback = jax.vjp(layer_norm, middle, second_gain, second_bias)[1]
    grad_middle, grad_gain_two, grad_bias_two = pullback(grad_second)
    grad_middle = grad_middle + grad_result
    grad_attended = grad_middle.astype(jnp.bfloat16)
    grad_output_t = left_product(grad_attended, mixture)
    grad_mixture = product(grad_attended, output_t).astype(jnp.bfloat16)
    grad_triple = attend_back(grad_mixture, attend_stored)
    grad_project = left_product(normed, grad_triple)
    grad_normed = right_product(grad_triple, project)
    pullback = jax.vjp(layer_norm, inputs, first_gain, first_bias)[1]
    grad_inputs, grad_gain_one, grad_bias_one = pullback(grad_normed)
    grad_inputs = grad_inputs + grad_middle
    return (
        grad_inputs,
        (grad_gain_one, grad_bias_one, grad_project, grad_output_t, grad_gain_two, grad_bias_two, grad_expand, grad_narrow_t),
    )


def solution(mesh):
    return jax.shard_map(
        fast_body if (mesh.shape["seq"], mesh.shape["fsdp"]) == (2, 16) else body,
        mesh=mesh,
        in_specs=(
            P("fsdp", "seq", None),
            P("fsdp", None),
            P("fsdp", "seq", None),
            P("fsdp", None),
            P("fsdp"),
            P("fsdp"),
            P("fsdp", None),
            P(None, "fsdp"),
            P("fsdp"),
            P("fsdp"),
            P("fsdp", None),
            P(None, "fsdp"),
            P("fsdp"),
            P("fsdp"),
            P("fsdp", None),
            P(None, "fsdp"),
            P("fsdp"),
            P("fsdp"),
            P("fsdp", None),
            P(None, "fsdp"),
        ),
        out_specs=(
            P("fsdp", "seq", None),
            P("fsdp", "seq", None),
            P("fsdp", None),
            P("fsdp"),
            P("fsdp"),
            P("fsdp", None),
            P(None, "fsdp"),
            P("fsdp"),
            P("fsdp"),
            P("fsdp", None),
            P(None, "fsdp"),
            P("fsdp"),
            P("fsdp"),
            P("fsdp", None),
            P(None, "fsdp"),
            P("fsdp"),
            P("fsdp"),
            P("fsdp", None),
            P(None, "fsdp"),
        ),
        check_vma=False,
    )
```

```python
import functools
import math

import jax
import jax.numpy as jnp
from jax import lax
from jax.experimental import pallas as pl
from jax.experimental.pallas import tpu as pltpu
from jax.sharding import PartitionSpec as P


D = 768
HEAD_DIM = 64
PATCH = 8


epsilon = 1e-05


def shifted(block, axis, distance):
    devices = range(lax.axis_size(axis))
    route = [(i - distance, i) for i in devices if i - distance in devices]
    return lax.ppermute(block, axis, route)


def layer_norm(values, norm_gain, norm_bias):
    center = jnp.mean(values, -1, keepdims=True)
    centred = values - center
    spread = jnp.mean(centred * centred, -1, keepdims=True)
    return centred * lax.rsqrt(spread + epsilon) * norm_gain + norm_bias


def smooth_gate(values):
    return jax.nn.gelu(values, approximate=True)


def product(left_side, right_side):
    return jnp.dot(left_side, right_side, preferred_element_type=jnp.float32)


def left_product(left_side, right_side):
    return lax.dot_general(
        left_side, right_side, (((0,), (0,)), ((), ())), preferred_element_type=jnp.float32
    )


def right_product(left_side, right_side):
    return lax.dot_general(
        left_side, right_side, (((1,), (1,)), ((), ())), preferred_element_type=jnp.float32
    )


def attend_forward(queries, key_part, value_part, allowed):
    factor = 1.0 / math.sqrt(HEAD_DIM)
    scores = (
        jnp.einsum("bqhd,bkhd->bhqk", queries, key_part, preferred_element_type=jnp.float32)
        * factor
    )
    scores = jnp.where(allowed[:, None], scores, -1e30)
    highest = jnp.max(scores, -1, keepdims=True)
    log_total = highest + jnp.log(jnp.sum(jnp.exp(scores - highest), -1, keepdims=True))
    rounded = jnp.exp(scores - log_total).astype(jnp.bfloat16)
    mixture = jnp.einsum("bhqk,bkhd->bqhd", rounded, value_part, preferred_element_type=jnp.float32)
    return (mixture, log_total)


def attend_backward(queries, key_part, value_part, allowed, log_total, grad_mixture):
    factor = 1.0 / math.sqrt(HEAD_DIM)
    scores = (
        jnp.einsum("bqhd,bkhd->bhqk", queries, key_part, preferred_element_type=jnp.float32)
        * factor
    )
    scores = jnp.where(allowed[:, None], scores, -1e30)
    chances = jnp.exp(scores - log_total)
    rounded = chances.astype(jnp.bfloat16)
    grad_values = jnp.einsum(
        "bhqk,bqhd->bkhd", rounded, grad_mixture, preferred_element_type=jnp.float32
    )
    grad_chances = jnp.einsum(
        "bqhd,bkhd->bhqk", grad_mixture, value_part, preferred_element_type=jnp.float32
    )
    grad_scores = (
        chances * (grad_chances - jnp.sum(grad_chances * chances, -1, keepdims=True))
    ).astype(jnp.bfloat16)
    grad_queries = (
        jnp.einsum("bhqk,bkhd->bqhd", grad_scores, key_part, preferred_element_type=jnp.float32)
        * factor
    )
    grad_keys = (
        jnp.einsum("bhqk,bqhd->bkhd", grad_scores, queries, preferred_element_type=jnp.float32)
        * factor
    )
    return (grad_queries, grad_keys, grad_values)


def block_forward(inputs, weights, attend):
    first_gain, first_bias, project, output, second_gain, second_bias, expand, narrow = weights
    normed = layer_norm(
        inputs, first_gain.astype(jnp.float32), first_bias.astype(jnp.float32)
    ).astype(jnp.bfloat16)
    triple = product(normed, project).astype(jnp.bfloat16)
    mixture, attend_stored = attend(triple)
    middle = inputs + product(mixture, output)
    second = layer_norm(
        middle, second_gain.astype(jnp.float32), second_bias.astype(jnp.float32)
    ).astype(jnp.bfloat16)
    lifted = product(second, expand)
    hidden = smooth_gate(lifted).astype(jnp.bfloat16)
    result = middle + product(hidden, narrow)
    stored = (inputs, normed, attend_stored, mixture, middle, second, lifted, hidden)
    return (result, stored)


def block_backward(grad_result, weights, stored, attend_back):
    first_gain, first_bias, project, output, second_gain, second_bias, expand, narrow = weights
    inputs, normed, attend_stored, mixture, middle, second, lifted, hidden = stored
    grad_branch = grad_result.astype(jnp.bfloat16)
    grad_narrow = left_product(hidden, grad_branch)
    grad_hidden = right_product(grad_branch, narrow)
    grad_lifted = jax.vjp(smooth_gate, lifted)[1](grad_hidden)[0].astype(jnp.bfloat16)
    grad_expand = left_product(second, grad_lifted)
    grad_second = right_product(grad_lifted, expand)
    pullback = jax.vjp(
        layer_norm, middle, second_gain.astype(jnp.float32), second_bias.astype(jnp.float32)
    )[1]
    grad_middle, grad_gain_two, grad_bias_two = pullback(grad_second)
    grad_middle = grad_middle + grad_result
    grad_attended = grad_middle.astype(jnp.bfloat16)
    grad_output = left_product(mixture, grad_attended)
    grad_mixture = right_product(grad_attended, output).astype(jnp.bfloat16)
    grad_triple = attend_back(grad_mixture, attend_stored)
    grad_project = left_product(normed, grad_triple)
    grad_normed = right_product(grad_triple, project)
    pullback = jax.vjp(
        layer_norm, inputs, first_gain.astype(jnp.float32), first_bias.astype(jnp.float32)
    )[1]
    grad_inputs, grad_gain_one, grad_bias_one = pullback(grad_normed)
    grad_inputs = grad_inputs + grad_middle
    return (
        grad_inputs,
        (
            grad_gain_one,
            grad_bias_one,
            grad_project,
            grad_output,
            grad_gain_two,
            grad_bias_two,
            grad_expand,
            grad_narrow,
        ),
    )


def body(
    byte_inputs,
    segment_ids,
    cotangent,
    patch_weight,
    coarse_first_gain,
    coarse_first_bias,
    coarse_project,
    coarse_output,
    coarse_second_gain,
    coarse_second_bias,
    coarse_expand,
    coarse_narrow,
    fine_first_gain,
    fine_first_bias,
    fine_project,
    fine_output,
    fine_second_gain,
    fine_second_bias,
    fine_expand,
    fine_narrow,
):
    coarse_full = (
        lax.all_gather(patch_weight, "fsdp", axis=0, tiled=True),
        lax.all_gather(coarse_first_gain, "fsdp", axis=0, tiled=True),
        lax.all_gather(coarse_first_bias, "fsdp", axis=0, tiled=True),
        lax.all_gather(coarse_project, "fsdp", axis=0, tiled=True),
        lax.all_gather(coarse_output, "fsdp", axis=1, tiled=True),
        lax.all_gather(coarse_second_gain, "fsdp", axis=0, tiled=True),
        lax.all_gather(coarse_second_bias, "fsdp", axis=0, tiled=True),
        lax.all_gather(coarse_expand, "fsdp", axis=0, tiled=True),
        lax.all_gather(coarse_narrow, "fsdp", axis=1, tiled=True),
    )
    fine_full = (
        lax.all_gather(fine_first_gain, "fsdp", axis=0, tiled=True),
        lax.all_gather(fine_first_bias, "fsdp", axis=0, tiled=True),
        lax.all_gather(fine_project, "fsdp", axis=0, tiled=True),
        lax.all_gather(fine_output, "fsdp", axis=1, tiled=True),
        lax.all_gather(fine_second_gain, "fsdp", axis=0, tiled=True),
        lax.all_gather(fine_second_bias, "fsdp", axis=0, tiled=True),
        lax.all_gather(fine_expand, "fsdp", axis=0, tiled=True),
        lax.all_gather(fine_narrow, "fsdp", axis=1, tiled=True),
    )
    byte_rows = byte_inputs[0]
    bytes_here = byte_rows.shape[0]
    patches = bytes_here // PATCH
    segment_row = segment_ids[0]
    all_patches = segment_row.shape[0]
    places = jnp.arange(all_patches)
    coarse_allowed = (
        (places[:, None] >= places[None, :]) & (segment_row[:, None] == segment_row[None, :])
    )[None]
    inner = jnp.arange(PATCH)
    fine_allowed = (inner[:, None] >= inner[None, :])[None]

    def coarse_attend(triple):
        head_block = lax.all_to_all(
            triple.reshape(patches, 3, D), "seq", split_axis=2, concat_axis=0, tiled=True
        )
        all_rows = head_block.shape[0]
        columns = head_block.shape[2]
        local_heads = columns // HEAD_DIM
        queries = head_block[:, 0].reshape(1, all_rows, local_heads, HEAD_DIM)
        key_part = head_block[:, 1].reshape(1, all_rows, local_heads, HEAD_DIM)
        value_part = head_block[:, 2].reshape(1, all_rows, local_heads, HEAD_DIM)
        mixture, log_total = attend_forward(queries, key_part, value_part, coarse_allowed)
        merged = mixture.reshape(all_rows, columns).astype(jnp.bfloat16)
        back_rows = lax.all_to_all(merged, "seq", split_axis=0, concat_axis=1, tiled=True)
        return (back_rows, (queries, key_part, value_part, log_total))

    def coarse_back(grad_mixture, stored):
        queries, key_part, value_part, log_total = stored
        head_grad = lax.all_to_all(grad_mixture, "seq", split_axis=1, concat_axis=0, tiled=True)
        all_rows = head_grad.shape[0]
        columns = head_grad.shape[1]
        grad_queries, grad_keys, grad_values = attend_backward(
            queries,
            key_part,
            value_part,
            coarse_allowed,
            log_total,
            head_grad.reshape(1, all_rows, columns // HEAD_DIM, HEAD_DIM),
        )
        stacked = jnp.stack(
            [
                grad_queries.reshape(all_rows, columns),
                grad_keys.reshape(all_rows, columns),
                grad_values.reshape(all_rows, columns),
            ],
            1,
        ).astype(jnp.bfloat16)
        back_rows = lax.all_to_all(stacked, "seq", split_axis=0, concat_axis=2, tiled=True)
        return back_rows.reshape(back_rows.shape[0], 3 * D)

    def fine_attend(triple):
        grouped = triple.reshape(patches, PATCH, 3, D // HEAD_DIM, HEAD_DIM)
        queries = grouped[:, :, 0]
        key_part = grouped[:, :, 1]
        value_part = grouped[:, :, 2]
        mixture, log_total = attend_forward(queries, key_part, value_part, fine_allowed)
        return (
            mixture.reshape(bytes_here, D).astype(jnp.bfloat16),
            (queries, key_part, value_part, log_total),
        )

    def fine_back(grad_mixture, stored):
        queries, key_part, value_part, log_total = stored
        grad_queries, grad_keys, grad_values = attend_backward(
            queries,
            key_part,
            value_part,
            fine_allowed,
            log_total,
            grad_mixture.reshape(patches, PATCH, D // HEAD_DIM, HEAD_DIM),
        )
        stacked = jnp.stack([grad_queries, grad_keys, grad_values], 2).astype(jnp.bfloat16)
        return stacked.reshape(bytes_here, 3 * D)

    grouped_bytes = byte_rows.reshape(patches, PATCH * D)
    embedded = product(grouped_bytes, coarse_full[0])
    coarse_out, coarse_stored = block_forward(embedded, coarse_full[1:], coarse_attend)
    coarse_low = coarse_out.astype(jnp.bfloat16)
    arrived = shifted(coarse_low[-1:], "seq", 1)
    offset = lax.axis_index("seq") * patches
    padded = jnp.concatenate([segment_row[:1] - 1, segment_row])
    before = lax.dynamic_slice_in_dim(padded, offset, patches)
    current = lax.dynamic_slice_in_dim(segment_row, offset, patches)
    joined = (before == current).astype(jnp.float32)[:, None]
    previous = jnp.concatenate([arrived, coarse_low[:-1]]).astype(jnp.float32) * joined
    fine_in = (
        byte_rows.astype(jnp.float32).reshape(patches, PATCH, D) + previous[:, None, :]
    ).reshape(bytes_here, D)
    layer_rows, fine_stored = block_forward(fine_in, fine_full, fine_attend)
    fine_weights_back = (
        lax.all_gather(fine_first_gain, "fsdp", axis=0, tiled=True),
        lax.all_gather(fine_first_bias, "fsdp", axis=0, tiled=True),
        lax.all_gather(fine_project, "fsdp", axis=0, tiled=True),
        lax.all_gather(fine_output, "fsdp", axis=1, tiled=True),
        lax.all_gather(fine_second_gain, "fsdp", axis=0, tiled=True),
        lax.all_gather(fine_second_bias, "fsdp", axis=0, tiled=True),
        lax.all_gather(fine_expand, "fsdp", axis=0, tiled=True),
        lax.all_gather(fine_narrow, "fsdp", axis=1, tiled=True),
    )
    grad_fine_in, fine_grads = block_backward(
        cotangent[0].astype(jnp.float32), fine_weights_back, fine_stored, fine_back
    )
    grad_previous = jnp.sum(grad_fine_in.reshape(patches, PATCH, D), 1) * joined
    arrived_back = shifted(grad_previous[:1], "seq", -1)
    grad_coarse_out = jnp.concatenate([grad_previous[1:], arrived_back])
    coarse_weights_back = (
        lax.all_gather(patch_weight, "fsdp", axis=0, tiled=True),
        lax.all_gather(coarse_first_gain, "fsdp", axis=0, tiled=True),
        lax.all_gather(coarse_first_bias, "fsdp", axis=0, tiled=True),
        lax.all_gather(coarse_project, "fsdp", axis=0, tiled=True),
        lax.all_gather(coarse_output, "fsdp", axis=1, tiled=True),
        lax.all_gather(coarse_second_gain, "fsdp", axis=0, tiled=True),
        lax.all_gather(coarse_second_bias, "fsdp", axis=0, tiled=True),
        lax.all_gather(coarse_expand, "fsdp", axis=0, tiled=True),
        lax.all_gather(coarse_narrow, "fsdp", axis=1, tiled=True),
    )
    grad_embedded, coarse_grads = block_backward(
        grad_coarse_out, coarse_weights_back[1:], coarse_stored, coarse_back
    )
    grad_embed_low = grad_embedded.astype(jnp.bfloat16)
    grad_patch = left_product(grouped_bytes, grad_embed_low)
    grad_grouped = right_product(grad_embed_low, coarse_weights_back[0])
    input_gradient = (grad_fine_in + grad_grouped.reshape(bytes_here, D)).astype(jnp.bfloat16)
    shards = (
        lax.psum_scatter(grad_patch, "fsdp", scatter_dimension=0, tiled=True),
        lax.psum_scatter(coarse_grads[0], "fsdp", scatter_dimension=0, tiled=True),
        lax.psum_scatter(coarse_grads[1], "fsdp", scatter_dimension=0, tiled=True),
        lax.psum_scatter(coarse_grads[2], "fsdp", scatter_dimension=0, tiled=True),
        lax.psum_scatter(coarse_grads[3], "fsdp", scatter_dimension=1, tiled=True),
        lax.psum_scatter(coarse_grads[4], "fsdp", scatter_dimension=0, tiled=True),
        lax.psum_scatter(coarse_grads[5], "fsdp", scatter_dimension=0, tiled=True),
        lax.psum_scatter(coarse_grads[6], "fsdp", scatter_dimension=0, tiled=True),
        lax.psum_scatter(coarse_grads[7], "fsdp", scatter_dimension=1, tiled=True),
        lax.psum_scatter(fine_grads[0], "fsdp", scatter_dimension=0, tiled=True),
        lax.psum_scatter(fine_grads[1], "fsdp", scatter_dimension=0, tiled=True),
        lax.psum_scatter(fine_grads[2], "fsdp", scatter_dimension=0, tiled=True),
        lax.psum_scatter(fine_grads[3], "fsdp", scatter_dimension=1, tiled=True),
        lax.psum_scatter(fine_grads[4], "fsdp", scatter_dimension=0, tiled=True),
        lax.psum_scatter(fine_grads[5], "fsdp", scatter_dimension=0, tiled=True),
        lax.psum_scatter(fine_grads[6], "fsdp", scatter_dimension=0, tiled=True),
        lax.psum_scatter(fine_grads[7], "fsdp", scatter_dimension=1, tiled=True),
    )
    totals = (
        lax.psum(shards[0].astype(jnp.bfloat16), "seq").astype(jnp.float32),
        lax.psum(shards[1].astype(jnp.bfloat16), "seq").astype(jnp.float32),
        lax.psum(shards[2].astype(jnp.bfloat16), "seq").astype(jnp.float32),
        lax.psum(shards[3].astype(jnp.bfloat16), "seq").astype(jnp.float32),
        lax.psum(shards[4].astype(jnp.bfloat16), "seq").astype(jnp.float32),
        lax.psum(shards[5].astype(jnp.bfloat16), "seq").astype(jnp.float32),
        lax.psum(shards[6].astype(jnp.bfloat16), "seq").astype(jnp.float32),
        lax.psum(shards[7].astype(jnp.bfloat16), "seq").astype(jnp.float32),
        lax.psum(shards[8].astype(jnp.bfloat16), "seq").astype(jnp.float32),
        lax.psum(shards[9].astype(jnp.bfloat16), "seq").astype(jnp.float32),
        lax.psum(shards[10].astype(jnp.bfloat16), "seq").astype(jnp.float32),
        lax.psum(shards[11].astype(jnp.bfloat16), "seq").astype(jnp.float32),
        lax.psum(shards[12].astype(jnp.bfloat16), "seq").astype(jnp.float32),
        lax.psum(shards[13].astype(jnp.bfloat16), "seq").astype(jnp.float32),
        lax.psum(shards[14].astype(jnp.bfloat16), "seq").astype(jnp.float32),
        lax.psum(shards[15].astype(jnp.bfloat16), "seq").astype(jnp.float32),
        lax.psum(shards[16].astype(jnp.bfloat16), "seq").astype(jnp.float32),
    )
    layer_output = layer_rows.astype(jnp.bfloat16)[None]
    return (
        layer_output,
        input_gradient[None],
        totals[0],
        totals[1],
        totals[2],
        totals[3],
        totals[4],
        totals[5],
        totals[6],
        totals[7],
        totals[8],
        totals[9],
        totals[10],
        totals[11],
        totals[12],
        totals[13],
        totals[14],
        totals[15],
        totals[16],
    )


MESH = pl.DeviceIdType.MESH
HBM = pltpu.MemorySpace.HBM
VMEM = pltpu.MemorySpace.VMEM


class Place:
    def __init__(self):
        self.core = lax.axis_index("seq")
        self.at = lax.axis_index("fsdp")
        self.z = self.at // 4
        self.plane = self.at % 4
        self.near = 1 + self.core
        self.far = 2 - self.core

    def flip(self, mask):
        return self.at ^ mask

    def across(self, mask):
        return (self.core, self.at ^ mask)

    def partner(self):
        return (1 - self.core, self.at)


def enter(place, masks, partner=True):
    barrier = pltpu.get_barrier_semaphore()
    for mask in masks:
        pl.semaphore_signal(barrier, inc=1, device_id=place.across(mask), device_id_type=MESH)
    if partner:
        pl.semaphore_signal(barrier, inc=1, device_id=place.partner(), device_id_type=MESH)
    pl.semaphore_wait(barrier, len(masks) + (1 if partner else 0))


MASKS = (1, 2, 4, 8, 12)


class Gather:
    EVENTS = 12

    def __init__(self, place, source, buffer, rows, column, width, z_first, sends, receives, local):
        self.p, self.source, self.buffer, self.rows = place, source, buffer, rows
        self.z_first, self.sends, self.receives, self.local = z_first, sends, receives, local
        self.half = width // 2
        self.column, self.width = column, width
        self.mine = pl.ds(pl.multiple_of(column + place.core * self.half, 128), self.half)
        self.theirs = pl.ds(pl.multiple_of(column + (1 - place.core) * self.half, 128), self.half)
        self.started = []

    def group(self, plane, columns=None):
        return self.buffer.at[:, plane, self.rows, self.mine if columns is None else columns]

    def block(self, z, plane):
        return self.buffer.at[z, plane, self.rows, self.mine]

    def send(self, event, view, device, source=None):
        copy = pltpu.make_async_remote_copy(
            src_ref=view if source is None else source,
            dst_ref=view,
            send_sem=self.sends.at[event],
            recv_sem=self.receives.at[event],
            device_id=device,
            device_id_type=MESH,
        )
        copy.start()
        self.started.append(copy)

    def arrived(self, event, view):
        pltpu.make_async_remote_copy(
            src_ref=view,
            dst_ref=view,
            send_sem=self.sends.at[event],
            recv_sem=self.receives.at[event],
            device_id=self.p.partner(),
            device_id_type=MESH,
        ).wait_recv()

    def start(self):
        p = self.p
        own = self.source.at[self.rows, pl.ds(pl.multiple_of(p.core * self.half, 128), self.half)]
        self.copy = pltpu.make_async_copy(own, self.block(p.z, p.plane), self.local)
        self.copy.start()
        if not self.z_first:
            self.send(6, self.block(p.z, p.plane), p.across(p.near), own)
        for j in (1, 2, 3):
            self.send(j - 1, self.block(p.z, p.plane), p.across(4 * j), own)

    def one(self):
        p = self.p
        self.copy.wait()
        if self.z_first:
            for j in (1, 2, 3):
                self.arrived(j - 1, self.block(p.z ^ j, p.plane))
            self.send(6, self.group(p.plane), p.across(p.near))
            self.send(7, self.group(p.plane), p.across(p.far))
            self.send(9, self.group(p.plane), p.partner())
        else:
            self.arrived(6, self.block(p.z, p.plane ^ p.near))
            for j in (1, 2, 3):
                self.send(2 + j, self.block(p.z, p.plane ^ p.near), p.across(4 * j))

    def two(self):
        p = self.p
        if self.z_first:
            self.arrived(6, self.group(p.plane ^ p.near))
        else:
            for j in (1, 2, 3):
                self.arrived(j - 1, self.block(p.z ^ j, p.plane))
            self.send(7, self.group(p.plane), p.across(p.far))
            self.send(9, self.group(p.plane), p.partner())
            for j in (1, 2, 3):
                self.arrived(2 + j, self.block(p.z ^ j, p.plane ^ p.near))
        self.send(8, self.group(p.plane ^ p.near), p.across(p.far))
        self.send(10, self.group(p.plane ^ p.near), p.partner())

    def three(self):
        p = self.p
        self.arrived(7, self.group(p.plane ^ p.far))
        self.send(11, self.group(p.plane ^ p.far), p.partner())
        self.arrived(8, self.group(p.plane ^ 3))
        self.send(12, self.group(p.plane ^ 3), p.partner())

    def four(self):
        p = self.p
        self.arrived(9, self.group(p.plane, self.theirs))
        self.arrived(10, self.group(p.plane ^ p.far, self.theirs))
        self.arrived(11, self.group(p.plane ^ p.near, self.theirs))
        self.arrived(12, self.group(p.plane ^ 3, self.theirs))

    def drain(self):
        for copy in self.started:
            copy.wait_send()


def run_gathers(gathers, ahead, tick):
    n = len(gathers)
    for k in range(min(ahead, n)):
        gathers[k].start()
    for t in range(n + 3):
        if t < n:
            gathers[t].one()
            if t + ahead < n:
                gathers[t + ahead].start()
        if 0 <= t - 1 < n:
            gathers[t - 1].two()
        if 0 <= t - 2 < n:
            gathers[t - 2].three()
        if 0 <= t - 3 < n:
            gathers[t - 3].four()
        tick()
    for g in gathers:
        g.drain()


def gather_kernel(plan, ahead, *refs):
    sources, small, rows, rest = refs[:9], refs[9], refs[10], refs[11:]
    buffers, small_out, all_rows = rest[:3], rest[3], rest[4]
    sends, receives, local, value, arriving, small_sends, small_receives, row_sems = rest[5:]
    place = Place()
    enter(place, MASKS)
    value[0] = small[...]
    total = Total(place, (1, 2, 4, 8), value, arriving, small_sends, small_receives, small_out)
    stay = pltpu.make_async_copy(rows, all_rows.at[place.core], row_sems.at[0])
    stay.start()
    cross = pltpu.make_async_remote_copy(
        src_ref=rows, dst_ref=all_rows.at[place.core], send_sem=row_sems.at[1], recv_sem=row_sems.at[2],
        device_id=place.partner(), device_id_type=MESH,
    )
    cross.start()
    gathers = []
    for k, (source, buffer, first, rows, column, width, z_first) in enumerate(plan):
        gathers.append(
            Gather(place, sources[source], buffers[buffer], pl.ds(first, rows), column, width, z_first,
                   sends.at[k], receives.at[k], local.at[k])
        )
    run_gathers(gathers, ahead, total.advance)
    stay.wait()
    cross.wait()


PLAN = (
    (0, 0, 0, 192, 0, 768, True),
    (0, 0, 192, 192, 0, 768, False),
    (1, 1, 0, 48, 0, 2304, True),
    (2, 1, 0, 48, 2304, 768, True),
    (3, 1, 0, 48, 3072, 3072, True),
    (4, 1, 0, 48, 6144, 3072, False),
    (5, 2, 0, 48, 0, 2304, True),
    (6, 2, 0, 48, 2304, 768, True),
    (7, 2, 0, 48, 3072, 3072, False),
    (8, 2, 0, 48, 6144, 3072, True),
)


def gather_all(sources, small, rows, ahead=2, plan=PLAN):
    n = len(plan)
    bf = jnp.bfloat16
    return pl.pallas_call(
        functools.partial(gather_kernel, plan, ahead),
        out_shape=(
            jax.ShapeDtypeStruct((4, 4, 384, 768), bf),
            jax.ShapeDtypeStruct((4, 4, 48, 9216), bf),
            jax.ShapeDtypeStruct((4, 4, 48, 9216), bf),
            jax.ShapeDtypeStruct((8, 768), jnp.float32),
            jax.ShapeDtypeStruct((2,) + rows.shape, bf),
        ),
        in_specs=[pl.BlockSpec(memory_space=VMEM)] * 10 + [pl.BlockSpec(memory_space=HBM)],
        out_specs=[pl.BlockSpec(memory_space=HBM)] * 3 + [pl.BlockSpec(memory_space=VMEM), pl.BlockSpec(memory_space=HBM)],
        scratch_shapes=[
            pltpu.SemaphoreType.DMA((n, 13)),
            pltpu.SemaphoreType.DMA((n, 13)),
            pltpu.SemaphoreType.DMA((n,)),
            pltpu.VMEM((5, 8, 768), jnp.float32),
            pltpu.VMEM((4, 8, 768), jnp.float32),
            pltpu.SemaphoreType.DMA((4,)),
            pltpu.SemaphoreType.DMA((4,)),
            pltpu.SemaphoreType.DMA((3,)),
        ],
        compiler_params=pltpu.CompilerParams(collective_id=0, has_side_effects=True),
        name="gather_all",
    )(*sources, small, rows)


class Total:
    def __init__(self, place, masks, value, arriving, sends, receives, result):
        self.p, self.masks, self.value, self.arriving = place, masks, value, arriving
        self.sends, self.receives, self.result = sends, receives, result
        self.step, self.copy = 0, None

    def advance(self):
        if self.step > len(self.masks):
            return
        if self.copy is not None:
            self.copy.wait()
            i = self.step - 1
            self.value[i + 1] = self.value[i] + self.arriving[i]
        if self.step < len(self.masks):
            i = self.step
            mask = self.masks[i]
            self.copy = pltpu.make_async_remote_copy(
                src_ref=self.value.at[i],
                dst_ref=self.arriving.at[i],
                send_sem=self.sends.at[i],
                recv_sem=self.receives.at[i],
                device_id=self.p.across(mask) if mask else self.p.partner(),
                device_id_type=MESH,
            )
            self.copy.start()
        else:
            self.result[...] = self.value[len(self.masks)]
        self.step += 1


def add(left, right):
    return left.astype(jnp.float32) + right.astype(jnp.float32)


class Reduce:
    def __init__(self, place, held, paired, far, near, line, out, rows, column, width, z_last, sends, receives):
        self.p, self.held, self.from_partner, self.from_far = place, held, paired, far
        self.from_near, self.from_line, self.out, self.rows = near, line, out, rows
        self.z_last, self.sends, self.receives = z_last, sends, receives
        self.half = width // 2
        self.mine = pl.ds(pl.multiple_of(column + place.core * self.half, 128), self.half)
        self.theirs = pl.ds(pl.multiple_of(column + (1 - place.core) * self.half, 128), self.half)
        self.started = []

    def send(self, event, source, target, device):
        copy = pltpu.make_async_remote_copy(
            src_ref=source, dst_ref=target, send_sem=self.sends.at[event], recv_sem=self.receives.at[event],
            device_id=device, device_id_type=MESH,
        )
        copy.start()
        self.started.append(copy)

    def arrived(self, event, target):
        pltpu.make_async_remote_copy(
            src_ref=target, dst_ref=target, send_sem=self.sends.at[event], recv_sem=self.receives.at[event],
            device_id=self.p.partner(), device_id_type=MESH,
        ).wait_recv()

    def pair(self, theirs):
        self.send(0, theirs, self.from_partner, self.p.partner())

    def fold(self, plane, others):
        def step(z, _):
            self.held[z, plane] = add(self.held[z, plane], others[z]).astype(jnp.bfloat16)
            return 0

        lax.fori_loop(0, 4, step, 0)

    def one(self):
        p = self.p
        if self.from_partner is not None:
            self.arrived(0, self.from_partner)
            self.fold(p.plane ^ p.far, self.from_partner.at[:, p.plane ^ p.far])
        self.send(1, self.held.at[:, p.plane ^ p.far], self.from_far.at[0], p.across(p.far))
        if self.from_partner is not None:
            self.fold(p.plane ^ 3, self.from_partner.at[:, p.plane ^ 3])
        self.send(2, self.held.at[:, p.plane ^ 3], self.from_far.at[1], p.across(p.far))
        if self.from_partner is not None:
            self.fold(p.plane, self.from_partner.at[:, p.plane])
            self.fold(p.plane ^ p.near, self.from_partner.at[:, p.plane ^ p.near])

    def two(self):
        p = self.p
        self.arrived(2, self.from_far.at[1])
        self.fold(p.plane ^ p.near, self.from_far.at[1])
        if self.z_last:
            self.send(3, self.held.at[:, p.plane ^ p.near], self.from_near, p.across(p.near))
        else:
            for j in (1, 2, 3):
                self.send(6 + j, self.held.at[p.z ^ j, p.plane ^ p.near], self.from_line.at[2 + j], p.across(4 * j))
        self.arrived(1, self.from_far.at[0])
        self.fold(p.plane, self.from_far.at[0])
        if not self.z_last:
            for j in (1, 2, 3):
                self.send(3 + j, self.held.at[p.z ^ j, p.plane], self.from_line.at[j - 1], p.across(4 * j))

    def three(self):
        p = self.p
        if self.z_last:
            self.arrived(3, self.from_near)
            self.fold(p.plane, self.from_near)
            for j in (1, 2, 3):
                self.send(3 + j, self.held.at[p.z ^ j, p.plane], self.from_line.at[j - 1], p.across(4 * j))
        else:
            for j in (1, 2, 3):
                self.arrived(6 + j, self.from_line.at[2 + j])
            near = (add(self.held[p.z, p.plane ^ p.near], self.from_line[3]) + add(self.from_line[4], self.from_line[5]))
            self.held[p.z, p.plane ^ p.near] = near.astype(jnp.bfloat16)
            self.send(3, self.held.at[p.z, p.plane ^ p.near], self.from_near.at[0], p.across(p.near))

    def four(self):
        p = self.p
        for j in (1, 2, 3):
            self.arrived(3 + j, self.from_line.at[j - 1])
        total = add(self.held[p.z, p.plane], self.from_line[0]) + add(self.from_line[1], self.from_line[2])
        if not self.z_last:
            self.arrived(3, self.from_near.at[0])
            total = total + self.from_near[0].astype(jnp.float32)
        self.out[self.rows, self.mine] = total
        view = self.out.at[self.rows, self.mine]
        self.send(10, view, view, p.partner())

    def drain(self):
        for copy in self.started:
            copy.wait_send()
        self.started = []

    def five(self):
        self.arrived(10, self.out.at[self.rows, self.theirs])


BACK_PLAN = (
    (8, 0, 48, 3072, True),
    (7, 0, 48, 3072, False),
    (6, 0, 48, 768, True),
    (5, 0, 48, 2304, True),
    (4, 0, 48, 3072, True),
    (3, 0, 48, 3072, False),
    (2, 0, 48, 768, True),
    (1, 0, 48, 2304, True),
    (0, 0, 192, 768, False),
    (0, 192, 192, 768, True),
)
SLOTS = 3
ARRAYS = 9


def reduce_kernel(plan, grads, small, outs, small_out, slots, pairs, fars, nears, lines, sends, receives, loads,
                  value, arriving, small_sends, small_receives):
    place = Place()
    enter(place, MASKS)
    n = len(plan)
    value[0] = small[...]
    total = Total(place, (0, 1, 2, 4, 8), value, arriving, small_sends, small_receives, small_out)
    used = [0, 0]
    reduces, copies = [], []
    for k, (array, first, rows, width, z_last) in enumerate(plan):
        kind = 0 if array == 0 else 1
        slot = used[kind] % SLOTS if kind else used[kind]
        used[kind] += 1
        half = width // 2
        cut = (lambda ref, kind=kind, half=half: ref if not kind or half == 1536 else ref.at[..., pl.ds(0, half)])
        reduces.append(
            Reduce(place, cut(slots[kind].at[slot]), cut(pairs.at[used[kind] - 1]) if array > 4 else None, cut(fars[kind].at[used[kind] - 1]),
                   cut(nears[kind].at[used[kind] - 1]), cut(lines[kind].at[used[kind] - 1]), outs[array],
                   pl.ds(first, rows), 0, width, z_last, sends.at[k], receives.at[k])
        )

    def load(k):
        array = plan[k][0]
        r = reduces[k]
        if k - SLOTS >= 0:
            reduces[k - SLOTS].drain()
        copy = pltpu.make_async_copy(grads[array].at[:, :, r.rows, r.mine], r.held, loads.at[k])
        copy.start()
        copies.append(copy)
        if array > 4:
            r.pair(grads[array].at[:, :, r.rows, r.theirs])

    for t in range(n + 4):
        if t - 4 >= 0:
            reduces[t - 4].five()
        if 0 <= t - 3 < n:
            reduces[t - 3].four()
        if t < n:
            load(t)
        if 0 <= t - 2 < n:
            reduces[t - 2].three()
        if 0 <= t - 1 < n:
            reduces[t - 1].two()
        if t < n:
            copies[t].wait()
            reduces[t].one()
        total.advance()
    for r in reduces:
        r.drain()


def reduce_all(grads, small, plan=BACK_PLAN):
    n = len(plan)
    bf = jnp.bfloat16
    shapes = ((2, 192, 384), (8, 48, 1536))

    def kernel(*refs):
        grads, small, outs, small_out = refs[:ARRAYS], refs[ARRAYS], refs[ARRAYS + 1 : 2 * ARRAYS + 1], refs[2 * ARRAYS + 1]
        pairs, rest = refs[2 * ARRAYS + 2], refs[2 * ARRAYS + 3 :]
        slots, fars, nears, lines = (rest[2 * i : 2 * i + 2] for i in range(4))
        reduce_kernel(plan, grads, small, outs, small_out, slots, pairs, fars, nears, lines, *rest[8:])

    scratch = [pltpu.VMEM((4, 4, 4, 48, 1536), bf)]
    for lead in (((2, 4, 4), (SLOTS, 4, 4)), ((2, 2, 4), (8, 2, 4)), ((2, 4), (8, 4)), ((2, 6), (8, 6))):
        scratch += [pltpu.VMEM(lead[i] + shapes[i][1:], bf) for i in (0, 1)]
    scratch += [
        pltpu.SemaphoreType.DMA((n, 11)),
        pltpu.SemaphoreType.DMA((n, 11)),
        pltpu.SemaphoreType.DMA((n,)),
        pltpu.VMEM((6, 8, 768), jnp.float32),
        pltpu.VMEM((5, 8, 768), jnp.float32),
        pltpu.SemaphoreType.DMA((5,)),
        pltpu.SemaphoreType.DMA((5,)),
    ]
    grads = [g.reshape(4, 4, g.shape[0] // 16, g.shape[1]) for g in grads]
    return pl.pallas_call(
        kernel,
        out_shape=[jax.ShapeDtypeStruct(g.shape[2:], jnp.float32) for g in grads] + [jax.ShapeDtypeStruct((8, 768), jnp.float32)],
        in_specs=[pl.BlockSpec(memory_space=HBM)] * ARRAYS + [pl.BlockSpec(memory_space=VMEM)],
        out_specs=[pl.BlockSpec(memory_space=VMEM)] * (ARRAYS + 1),
        scratch_shapes=scratch,
        compiler_params=pltpu.CompilerParams(collective_id=1, has_side_effects=True, vmem_limit_bytes=66_000_000),
        name="reduce_all",
    )(*grads, small)


def fast_body(byte_inputs, segment_ids, cotangent, patch_weight, *weights):
    coarse, fine = weights[:8], weights[8:]
    core, at = lax.axis_index("seq"), lax.axis_index("fsdp")
    vectors = jnp.stack([w[i] for w in (coarse, fine) for i in (0, 1, 4, 5)]).astype(jnp.float32)
    small = lax.dynamic_update_slice(jnp.zeros((8, D), jnp.float32), vectors, (0, at * vectors.shape[1]))
    sources = [patch_weight]
    for w in (coarse, fine):
        sources += [w[2], w[3].T, w[6], w[7].T]
    byte_rows = byte_inputs[0]
    bytes_here = byte_rows.shape[0]
    patches = bytes_here // PATCH
    patch_full, coarse_full, fine_full, small, all_rows = gather_all(sources, small, byte_rows)
    patch_full = patch_full.reshape(-1, D)

    def unpack(full, first):
        full = full.reshape(D, -1)
        return (small[first], small[first + 1], full[:, : 3 * D], full[:, 3 * D : 4 * D], small[first + 2], small[first + 3],
                full[:, 4 * D : 8 * D], full[:, 8 * D :])

    coarse_w = unpack(coarse_full, 0)
    segment_row = segment_ids[0]
    all_patches = segment_row.shape[0]
    places = jnp.arange(all_patches)
    coarse_allowed = (
        (places[:, None] >= places[None, :]) & (segment_row[:, None] == segment_row[None, :])
    )[None]

    def attend(shape, allowed):
        rows = shape[0] * shape[1]

        def forward(triple):
            grouped = triple.reshape(shape + (3, D // HEAD_DIM, HEAD_DIM))
            parts = grouped[:, :, 0], grouped[:, :, 1], grouped[:, :, 2]
            mixture, log_total = attend_forward(*parts, allowed)
            return (mixture.reshape(rows, D).astype(jnp.bfloat16), parts + (log_total,))

        def backward(grad_mixture, stored):
            queries, key_part, value_part, log_total = stored
            grads = attend_backward(
                queries, key_part, value_part, allowed, log_total,
                grad_mixture.reshape(shape + (D // HEAD_DIM, HEAD_DIM)),
            )
            return jnp.stack(grads, 2).astype(jnp.bfloat16).reshape(rows, 3 * D)

        return forward, backward

    coarse_attend, coarse_back = attend((1, all_patches), coarse_allowed)
    grouped_bytes = all_rows.reshape(all_patches, PATCH * D)
    embedded = product(grouped_bytes, patch_full)
    coarse_out, coarse_stored = block_forward_t(embedded, coarse_w, coarse_attend)
    coarse_low = coarse_out.astype(jnp.bfloat16)
    joined = jnp.concatenate([jnp.zeros((1,), bool), segment_row[1:] == segment_row[:-1]]).astype(jnp.float32)[:, None]
    previous = jnp.concatenate([jnp.zeros((1, D), jnp.bfloat16), coarse_low[:-1]]).astype(jnp.float32) * joined
    previous = lax.dynamic_slice_in_dim(previous, core * patches, patches)
    (layer_rows, grad_fine_in, grad_previous, fine_vectors, normed, mixture, second, hidden, grad_middle, grad_lifted,
     grad_triple) = fine_block(byte_rows, previous, cotangent[0], small, fine_full.reshape(D, -1))
    fine_grads = [
        left_product(*pair).astype(jnp.bfloat16)
        for pair in ((normed, grad_triple), (grad_middle, mixture), (second, grad_lifted), (cotangent[0], hidden))
    ]
    grad_previous = lax.all_gather(grad_previous, "seq", axis=0, tiled=True) * joined
    grad_coarse_out = jnp.concatenate([grad_previous[1:], jnp.zeros((1, D), jnp.float32)])
    grad_embedded, coarse_grads = block_backward_t(grad_coarse_out, coarse_w, coarse_stored, coarse_back)
    grad_embed_low = grad_embedded.astype(jnp.bfloat16)
    grad_patch = left_product(grouped_bytes, grad_embed_low).astype(jnp.bfloat16)
    grad_here = lax.dynamic_slice_in_dim(grad_embed_low, core * patches, patches)
    grad_grouped = right_product(grad_here, patch_full)
    input_gradient = (grad_fine_in + grad_grouped.reshape(bytes_here, D)).astype(jnp.bfloat16)
    once = (core == 0).astype(jnp.float32)
    small = jnp.concatenate([jnp.stack([coarse_grads[i] * once for i in (0, 1, 4, 5)]), fine_vectors[4:]])
    *shards, small = reduce_all(
        [grad_patch] + [coarse_grads[i].astype(jnp.bfloat16) for i in (2, 3, 6, 7)] + fine_grads, small
    )
    small = lax.dynamic_slice_in_dim(small, at * vectors.shape[1], vectors.shape[1], 1)

    def gradients(parts, first):
        return (small[first], small[first + 1], parts[0], parts[1].T, small[first + 2], small[first + 3], parts[2], parts[3].T)

    return (layer_rows[None], input_gradient[None], shards[0]) + gradients(shards[1:5], 0) + gradients(shards[5:], 4)


def block_forward_t(inputs, weights, attend):
    first_gain, first_bias, project, output_t, second_gain, second_bias, expand, narrow_t = weights
    normed = layer_norm(inputs, first_gain, first_bias).astype(jnp.bfloat16)
    triple = product(normed, project).astype(jnp.bfloat16)
    mixture, attend_stored = attend(triple)
    middle = inputs + right_product(mixture, output_t)
    second = layer_norm(middle, second_gain, second_bias).astype(jnp.bfloat16)
    lifted = product(second, expand)
    hidden = smooth_gate(lifted).astype(jnp.bfloat16)
    result = middle + right_product(hidden, narrow_t)
    stored = (inputs, normed, attend_stored, mixture, middle, second, lifted, hidden)
    return (result, stored)


def block_backward_t(grad_result, weights, stored, attend_back):
    first_gain, first_bias, project, output_t, second_gain, second_bias, expand, narrow_t = weights
    inputs, normed, attend_stored, mixture, middle, second, lifted, hidden = stored
    grad_branch = grad_result.astype(jnp.bfloat16)
    grad_narrow_t = left_product(grad_branch, hidden)
    grad_hidden = product(grad_branch, narrow_t)
    grad_lifted = jax.vjp(smooth_gate, lifted)[1](grad_hidden)[0].astype(jnp.bfloat16)
    grad_expand = left_product(second, grad_lifted)
    grad_second = right_product(grad_lifted, expand)
    pullback = jax.vjp(layer_norm, middle, second_gain, second_bias)[1]
    grad_middle, grad_gain_two, grad_bias_two = pullback(grad_second)
    grad_middle = grad_middle + grad_result
    grad_attended = grad_middle.astype(jnp.bfloat16)
    grad_output_t = left_product(grad_attended, mixture)
    grad_mixture = product(grad_attended, output_t).astype(jnp.bfloat16)
    grad_triple = attend_back(grad_mixture, attend_stored)
    grad_project = left_product(normed, grad_triple)
    grad_normed = right_product(grad_triple, project)
    pullback = jax.vjp(layer_norm, inputs, first_gain, first_bias)[1]
    grad_inputs, grad_gain_one, grad_bias_one = pullback(grad_normed)
    grad_inputs = grad_inputs + grad_middle
    return (
        grad_inputs,
        (grad_gain_one, grad_bias_one, grad_project, grad_output_t, grad_gain_two, grad_bias_two, grad_expand, grad_narrow_t),
    )


def normalize(values):
    centred = values - jnp.mean(values, -1, keepdims=True)
    scale = lax.rsqrt(jnp.mean(centred * centred, -1, keepdims=True) + epsilon)
    return centred * scale, scale


def normalize_back(grad, unit, scale, norm_gain):
    scaled = grad * norm_gain
    return scale * (
        scaled - jnp.mean(scaled, -1, keepdims=True) - unit * jnp.mean(scaled * unit, -1, keepdims=True)
    )


def gate_both(values):
    root = math.sqrt(2.0 / math.pi)
    square = values * values
    bend = jnp.tanh(root * values * (1.0 + 0.044715 * square))
    half = 0.5 + 0.5 * bend
    slope = half + 0.5 * values * (1.0 - bend * bend) * (root * (1.0 + 3.0 * 0.044715 * square))
    return values * half, slope


def head_lanes(pair):
    lane = lax.broadcasted_iota(jnp.int32, pair.shape, 1)
    zero = jnp.zeros_like(pair)
    return jnp.where(lane < HEAD_DIM, pair, zero), jnp.where(lane < HEAD_DIM, zero, pair)


def chances_of(queries, keys, allowed):
    scores = right_product(queries, keys) * (1.0 / math.sqrt(HEAD_DIM))
    scores = jnp.where(allowed, scores, -1e30)
    powers = jnp.exp(scores - jnp.max(scores, -1, keepdims=True))
    return powers * (1.0 / jnp.sum(powers, -1, keepdims=True))


TILE = 128
PAIRS = 6


def fine_kernel(byte_ref, previous_ref, cotangent_ref, small_ref, w_ref,
                out_ref, grad_in_ref, patch_grad_ref, vectors_ref,
                normed_ref, mixture_ref, second_ref, hidden_ref, low_ref, lifted_grad_ref, triple_grad_ref,
                triple, chances, result, grad_second):
    rows = byte_ref.shape[0]
    bf = jnp.bfloat16
    first_gain, first_bias, second_gain, second_bias = (small_ref[i : i + 1] for i in (4, 5, 6, 7))
    previous = previous_ref[...]
    inputs = (
        byte_ref[...].astype(jnp.float32).reshape(rows // PATCH, PATCH, D) + previous[:, None, :]
    ).reshape(rows, D)
    unit_one, scale_one = normalize(inputs)
    normed = (unit_one * first_gain + first_bias).astype(bf)
    normed_ref[...] = normed
    triple[...] = product(normed, w_ref[:, : 3 * D]).astype(bf)
    row = lax.broadcasted_iota(jnp.int32, (TILE, TILE), 0)
    column = lax.broadcasted_iota(jnp.int32, (TILE, TILE), 1)
    allowed = (row // PATCH == column // PATCH) & (column <= row)
    tiles = rows // TILE

    def attend(pair, _):
        lanes = [pl.ds(pl.multiple_of(i * D + pair * 128, 128), 128) for i in range(3)]
        for tile in range(tiles):
            here = slice(tile * TILE, tile * TILE + TILE)
            queries = head_lanes(triple[here, lanes[0]])
            keys = triple[here, lanes[1]]
            values = head_lanes(triple[here, lanes[2]])
            mixed = None
            for head in range(2):
                found = chances_of(queries[head], keys, allowed)
                chances[pair * 2 + head, here] = found
                term = product(found.astype(bf), values[head])
                mixed = term if mixed is None else mixed + term
            mixture_ref[here, lanes[0]] = mixed.astype(bf)
        return 0

    lax.fori_loop(0, PAIRS, attend, 0)
    middle = inputs + right_product(mixture_ref[...], w_ref[:, 3 * D : 4 * D])
    unit_two, scale_two = normalize(middle)
    second = (unit_two * second_gain + second_bias).astype(bf)
    second_ref[...] = second
    grad_low = cotangent_ref[...]
    result[...] = middle
    for j in range(4):
        here = slice(j * D, j * D + D)
        expand = w_ref[:, 4 * D + j * D : 5 * D + j * D]
        narrow_t = w_ref[:, 8 * D + j * D : 9 * D + j * D]
        hidden, slope = gate_both(product(second, expand))
        hidden = hidden.astype(bf)
        hidden_ref[:, here] = hidden
        lifted_grad = (product(grad_low, narrow_t) * slope).astype(bf)
        lifted_grad_ref[:, here] = lifted_grad
        result[...] += right_product(hidden, narrow_t)
        term = right_product(lifted_grad, expand)
        if j:
            grad_second[...] += term
        else:
            grad_second[...] = term
    out_ref[...] = result[...].astype(bf)
    grad_two = grad_second[...]
    grad_middle = grad_low.astype(jnp.float32) + normalize_back(grad_two, unit_two, scale_two, second_gain)
    low = grad_middle.astype(bf)
    low_ref[...] = low
    grad_second[...] = grad_middle
    grad_mixture = product(low, w_ref[:, 3 * D : 4 * D]).astype(bf)
    result[...] = grad_mixture.astype(jnp.float32)

    def attend_back(pair, _):
        lanes = [pl.ds(pl.multiple_of(i * D + pair * 128, 128), 128) for i in range(3)]
        factor = 1.0 / math.sqrt(HEAD_DIM)
        for tile in range(tiles):
            here = slice(tile * TILE, tile * TILE + TILE)
            queries = head_lanes(triple[here, lanes[0]])
            keys = head_lanes(triple[here, lanes[1]])
            values = triple[here, lanes[2]]
            mixed = head_lanes(result[here, lanes[0]].astype(bf))
            sums = [None, None, None]
            for head in range(2):
                found = chances[pair * 2 + head, here]
                grad = right_product(mixed[head], values)
                scores = (found * (grad - jnp.sum(grad * found, -1, keepdims=True))).astype(bf)
                terms = (
                    product(scores, keys[head]),
                    left_product(scores, queries[head]),
                    left_product(found.astype(bf), mixed[head]),
                )
                sums = [t if s is None else s + t for s, t in zip(sums, terms)]
            triple_grad_ref[here, lanes[0]] = (sums[0] * factor).astype(bf)
            triple_grad_ref[here, lanes[1]] = (sums[1] * factor).astype(bf)
            triple_grad_ref[here, lanes[2]] = sums[2].astype(bf)
        return 0

    lax.fori_loop(0, PAIRS, attend_back, 0)
    grad_one = right_product(triple_grad_ref[...], w_ref[:, : 3 * D])
    grad_in = grad_second[...] + normalize_back(grad_one, unit_one, scale_one, first_gain)
    grad_in_ref[...] = grad_in
    patch_grad_ref[...] = jnp.sum(grad_in.reshape(rows // PATCH, PATCH, D), 1)
    terms = [jnp.sum(t, 0, keepdims=True) for t in (grad_one * unit_one, grad_one, grad_two * unit_two, grad_two)]

    @pl.when(pl.program_id(0) == 0)
    def _():
        vectors_ref[...] = jnp.zeros_like(vectors_ref)

    for i, term in enumerate(terms):
        vectors_ref[4 + i : 5 + i] += term


def fine_block(byte_rows, previous, cotangent, small, full, rows=256):
    count = byte_rows.shape[0]
    bf, f32 = jnp.bfloat16, jnp.float32

    def spec(height, width):
        return pl.BlockSpec((height, width), lambda i: (i, 0))

    def whole(shape):
        return pl.BlockSpec(shape, lambda i: (0, 0), pipeline_mode=pl.Buffered(1))

    outs = [(rows, D, bf), (rows, D, f32), (rows // PATCH, D, f32), None]
    outs += [(rows, D, bf)] * 3 + [(rows, 4 * D, bf), (rows, D, bf), (rows, 4 * D, bf), (rows, 3 * D, bf)]
    steps = count // rows
    return pl.pallas_call(
        fine_kernel,
        grid=(steps,),
        out_shape=[
            jax.ShapeDtypeStruct((o[0] * steps, o[1]), o[2]) if o else jax.ShapeDtypeStruct((8, D), f32) for o in outs
        ],
        in_specs=[spec(rows, D), spec(rows // PATCH, D), spec(rows, D), whole((8, D)), whole(full.shape)],
        out_specs=[spec(o[0], o[1]) if o else pl.BlockSpec((8, D), lambda i: (0, 0)) for o in outs],
        scratch_shapes=[
            pltpu.VMEM((rows, 3 * D), bf),
            pltpu.VMEM((2 * PAIRS, rows, TILE), f32),
            pltpu.VMEM((rows, D), f32),
            pltpu.VMEM((rows, D), f32),
        ],
        compiler_params=pltpu.CompilerParams(dimension_semantics=("arbitrary",), vmem_limit_bytes=64_000_000),
        name="fine_block",
    )(byte_rows, previous, cotangent, small, full)


def solution(mesh):
    return jax.shard_map(
        fast_body if (mesh.shape["seq"], mesh.shape["fsdp"]) == (2, 16) else body,
        mesh=mesh,
        in_specs=(
            P("fsdp", "seq", None),
            P("fsdp", None),
            P("fsdp", "seq", None),
            P("fsdp", None),
            P("fsdp"),
            P("fsdp"),
            P("fsdp", None),
            P(None, "fsdp"),
            P("fsdp"),
            P("fsdp"),
            P("fsdp", None),
            P(None, "fsdp"),
            P("fsdp"),
            P("fsdp"),
            P("fsdp", None),
            P(None, "fsdp"),
            P("fsdp"),
            P("fsdp"),
            P("fsdp", None),
            P(None, "fsdp"),
        ),
        out_specs=(
            P("fsdp", "seq", None),
            P("fsdp", "seq", None),
            P("fsdp", None),
            P("fsdp"),
            P("fsdp"),
            P("fsdp", None),
            P(None, "fsdp"),
            P("fsdp"),
            P("fsdp"),
            P("fsdp", None),
            P(None, "fsdp"),
            P("fsdp"),
            P("fsdp"),
            P("fsdp", None),
            P(None, "fsdp"),
            P("fsdp"),
            P("fsdp"),
            P("fsdp", None),
            P(None, "fsdp"),
        ),
        check_vma=False,
    )
```

```python
import functools
import math

import jax
import jax.numpy as jnp
from jax import lax
from jax.experimental import pallas as pl
from jax.experimental.pallas import tpu as pltpu
from jax.sharding import PartitionSpec as P


D = 768
HEAD_DIM = 64
PATCH = 8


epsilon = 1e-05


def shifted(block, axis, distance):
    devices = range(lax.axis_size(axis))
    route = [(i - distance, i) for i in devices if i - distance in devices]
    return lax.ppermute(block, axis, route)


def layer_norm(values, norm_gain, norm_bias):
    center = jnp.mean(values, -1, keepdims=True)
    centred = values - center
    spread = jnp.mean(centred * centred, -1, keepdims=True)
    return centred * lax.rsqrt(spread + epsilon) * norm_gain + norm_bias


def smooth_gate(values):
    return jax.nn.gelu(values, approximate=True)


def product(left_side, right_side):
    return jnp.dot(left_side, right_side, preferred_element_type=jnp.float32)


def left_product(left_side, right_side):
    return lax.dot_general(
        left_side, right_side, (((0,), (0,)), ((), ())), preferred_element_type=jnp.float32
    )


def right_product(left_side, right_side):
    return lax.dot_general(
        left_side, right_side, (((1,), (1,)), ((), ())), preferred_element_type=jnp.float32
    )


def attend_forward(queries, key_part, value_part, allowed):
    factor = 1.0 / math.sqrt(HEAD_DIM)
    scores = (
        jnp.einsum("bqhd,bkhd->bhqk", queries, key_part, preferred_element_type=jnp.float32)
        * factor
    )
    scores = jnp.where(allowed[:, None], scores, -1e30)
    highest = jnp.max(scores, -1, keepdims=True)
    log_total = highest + jnp.log(jnp.sum(jnp.exp(scores - highest), -1, keepdims=True))
    rounded = jnp.exp(scores - log_total).astype(jnp.bfloat16)
    mixture = jnp.einsum("bhqk,bkhd->bqhd", rounded, value_part, preferred_element_type=jnp.float32)
    return (mixture, log_total)


def attend_backward(queries, key_part, value_part, allowed, log_total, grad_mixture):
    factor = 1.0 / math.sqrt(HEAD_DIM)
    scores = (
        jnp.einsum("bqhd,bkhd->bhqk", queries, key_part, preferred_element_type=jnp.float32)
        * factor
    )
    scores = jnp.where(allowed[:, None], scores, -1e30)
    chances = jnp.exp(scores - log_total)
    rounded = chances.astype(jnp.bfloat16)
    grad_values = jnp.einsum(
        "bhqk,bqhd->bkhd", rounded, grad_mixture, preferred_element_type=jnp.float32
    )
    grad_chances = jnp.einsum(
        "bqhd,bkhd->bhqk", grad_mixture, value_part, preferred_element_type=jnp.float32
    )
    grad_scores = (
        chances * (grad_chances - jnp.sum(grad_chances * chances, -1, keepdims=True))
    ).astype(jnp.bfloat16)
    grad_queries = (
        jnp.einsum("bhqk,bkhd->bqhd", grad_scores, key_part, preferred_element_type=jnp.float32)
        * factor
    )
    grad_keys = (
        jnp.einsum("bhqk,bqhd->bkhd", grad_scores, queries, preferred_element_type=jnp.float32)
        * factor
    )
    return (grad_queries, grad_keys, grad_values)


def block_forward(inputs, weights, attend):
    first_gain, first_bias, project, output, second_gain, second_bias, expand, narrow = weights
    normed = layer_norm(
        inputs, first_gain.astype(jnp.float32), first_bias.astype(jnp.float32)
    ).astype(jnp.bfloat16)
    triple = product(normed, project).astype(jnp.bfloat16)
    mixture, attend_stored = attend(triple)
    middle = inputs + product(mixture, output)
    second = layer_norm(
        middle, second_gain.astype(jnp.float32), second_bias.astype(jnp.float32)
    ).astype(jnp.bfloat16)
    lifted = product(second, expand)
    hidden = smooth_gate(lifted).astype(jnp.bfloat16)
    result = middle + product(hidden, narrow)
    stored = (inputs, normed, attend_stored, mixture, middle, second, lifted, hidden)
    return (result, stored)


def block_backward(grad_result, weights, stored, attend_back):
    first_gain, first_bias, project, output, second_gain, second_bias, expand, narrow = weights
    inputs, normed, attend_stored, mixture, middle, second, lifted, hidden = stored
    grad_branch = grad_result.astype(jnp.bfloat16)
    grad_narrow = left_product(hidden, grad_branch)
    grad_hidden = right_product(grad_branch, narrow)
    grad_lifted = jax.vjp(smooth_gate, lifted)[1](grad_hidden)[0].astype(jnp.bfloat16)
    grad_expand = left_product(second, grad_lifted)
    grad_second = right_product(grad_lifted, expand)
    pullback = jax.vjp(
        layer_norm, middle, second_gain.astype(jnp.float32), second_bias.astype(jnp.float32)
    )[1]
    grad_middle, grad_gain_two, grad_bias_two = pullback(grad_second)
    grad_middle = grad_middle + grad_result
    grad_attended = grad_middle.astype(jnp.bfloat16)
    grad_output = left_product(mixture, grad_attended)
    grad_mixture = right_product(grad_attended, output).astype(jnp.bfloat16)
    grad_triple = attend_back(grad_mixture, attend_stored)
    grad_project = left_product(normed, grad_triple)
    grad_normed = right_product(grad_triple, project)
    pullback = jax.vjp(
        layer_norm, inputs, first_gain.astype(jnp.float32), first_bias.astype(jnp.float32)
    )[1]
    grad_inputs, grad_gain_one, grad_bias_one = pullback(grad_normed)
    grad_inputs = grad_inputs + grad_middle
    return (
        grad_inputs,
        (
            grad_gain_one,
            grad_bias_one,
            grad_project,
            grad_output,
            grad_gain_two,
            grad_bias_two,
            grad_expand,
            grad_narrow,
        ),
    )


def body(
    byte_inputs,
    segment_ids,
    cotangent,
    patch_weight,
    coarse_first_gain,
    coarse_first_bias,
    coarse_project,
    coarse_output,
    coarse_second_gain,
    coarse_second_bias,
    coarse_expand,
    coarse_narrow,
    fine_first_gain,
    fine_first_bias,
    fine_project,
    fine_output,
    fine_second_gain,
    fine_second_bias,
    fine_expand,
    fine_narrow,
):
    coarse_full = (
        lax.all_gather(patch_weight, "fsdp", axis=0, tiled=True),
        lax.all_gather(coarse_first_gain, "fsdp", axis=0, tiled=True),
        lax.all_gather(coarse_first_bias, "fsdp", axis=0, tiled=True),
        lax.all_gather(coarse_project, "fsdp", axis=0, tiled=True),
        lax.all_gather(coarse_output, "fsdp", axis=1, tiled=True),
        lax.all_gather(coarse_second_gain, "fsdp", axis=0, tiled=True),
        lax.all_gather(coarse_second_bias, "fsdp", axis=0, tiled=True),
        lax.all_gather(coarse_expand, "fsdp", axis=0, tiled=True),
        lax.all_gather(coarse_narrow, "fsdp", axis=1, tiled=True),
    )
    fine_full = (
        lax.all_gather(fine_first_gain, "fsdp", axis=0, tiled=True),
        lax.all_gather(fine_first_bias, "fsdp", axis=0, tiled=True),
        lax.all_gather(fine_project, "fsdp", axis=0, tiled=True),
        lax.all_gather(fine_output, "fsdp", axis=1, tiled=True),
        lax.all_gather(fine_second_gain, "fsdp", axis=0, tiled=True),
        lax.all_gather(fine_second_bias, "fsdp", axis=0, tiled=True),
        lax.all_gather(fine_expand, "fsdp", axis=0, tiled=True),
        lax.all_gather(fine_narrow, "fsdp", axis=1, tiled=True),
    )
    byte_rows = byte_inputs[0]
    bytes_here = byte_rows.shape[0]
    patches = bytes_here // PATCH
    segment_row = segment_ids[0]
    all_patches = segment_row.shape[0]
    places = jnp.arange(all_patches)
    coarse_allowed = (
        (places[:, None] >= places[None, :]) & (segment_row[:, None] == segment_row[None, :])
    )[None]
    inner = jnp.arange(PATCH)
    fine_allowed = (inner[:, None] >= inner[None, :])[None]

    def coarse_attend(triple):
        head_block = lax.all_to_all(
            triple.reshape(patches, 3, D), "seq", split_axis=2, concat_axis=0, tiled=True
        )
        all_rows = head_block.shape[0]
        columns = head_block.shape[2]
        local_heads = columns // HEAD_DIM
        queries = head_block[:, 0].reshape(1, all_rows, local_heads, HEAD_DIM)
        key_part = head_block[:, 1].reshape(1, all_rows, local_heads, HEAD_DIM)
        value_part = head_block[:, 2].reshape(1, all_rows, local_heads, HEAD_DIM)
        mixture, log_total = attend_forward(queries, key_part, value_part, coarse_allowed)
        merged = mixture.reshape(all_rows, columns).astype(jnp.bfloat16)
        back_rows = lax.all_to_all(merged, "seq", split_axis=0, concat_axis=1, tiled=True)
        return (back_rows, (queries, key_part, value_part, log_total))

    def coarse_back(grad_mixture, stored):
        queries, key_part, value_part, log_total = stored
        head_grad = lax.all_to_all(grad_mixture, "seq", split_axis=1, concat_axis=0, tiled=True)
        all_rows = head_grad.shape[0]
        columns = head_grad.shape[1]
        grad_queries, grad_keys, grad_values = attend_backward(
            queries,
            key_part,
            value_part,
            coarse_allowed,
            log_total,
            head_grad.reshape(1, all_rows, columns // HEAD_DIM, HEAD_DIM),
        )
        stacked = jnp.stack(
            [
                grad_queries.reshape(all_rows, columns),
                grad_keys.reshape(all_rows, columns),
                grad_values.reshape(all_rows, columns),
            ],
            1,
        ).astype(jnp.bfloat16)
        back_rows = lax.all_to_all(stacked, "seq", split_axis=0, concat_axis=2, tiled=True)
        return back_rows.reshape(back_rows.shape[0], 3 * D)

    def fine_attend(triple):
        grouped = triple.reshape(patches, PATCH, 3, D // HEAD_DIM, HEAD_DIM)
        queries = grouped[:, :, 0]
        key_part = grouped[:, :, 1]
        value_part = grouped[:, :, 2]
        mixture, log_total = attend_forward(queries, key_part, value_part, fine_allowed)
        return (
            mixture.reshape(bytes_here, D).astype(jnp.bfloat16),
            (queries, key_part, value_part, log_total),
        )

    def fine_back(grad_mixture, stored):
        queries, key_part, value_part, log_total = stored
        grad_queries, grad_keys, grad_values = attend_backward(
            queries,
            key_part,
            value_part,
            fine_allowed,
            log_total,
            grad_mixture.reshape(patches, PATCH, D // HEAD_DIM, HEAD_DIM),
        )
        stacked = jnp.stack([grad_queries, grad_keys, grad_values], 2).astype(jnp.bfloat16)
        return stacked.reshape(bytes_here, 3 * D)

    grouped_bytes = byte_rows.reshape(patches, PATCH * D)
    embedded = product(grouped_bytes, coarse_full[0])
    coarse_out, coarse_stored = block_forward(embedded, coarse_full[1:], coarse_attend)
    coarse_low = coarse_out.astype(jnp.bfloat16)
    arrived = shifted(coarse_low[-1:], "seq", 1)
    offset = lax.axis_index("seq") * patches
    padded = jnp.concatenate([segment_row[:1] - 1, segment_row])
    before = lax.dynamic_slice_in_dim(padded, offset, patches)
    current = lax.dynamic_slice_in_dim(segment_row, offset, patches)
    joined = (before == current).astype(jnp.float32)[:, None]
    previous = jnp.concatenate([arrived, coarse_low[:-1]]).astype(jnp.float32) * joined
    fine_in = (
        byte_rows.astype(jnp.float32).reshape(patches, PATCH, D) + previous[:, None, :]
    ).reshape(bytes_here, D)
    layer_rows, fine_stored = block_forward(fine_in, fine_full, fine_attend)
    fine_weights_back = (
        lax.all_gather(fine_first_gain, "fsdp", axis=0, tiled=True),
        lax.all_gather(fine_first_bias, "fsdp", axis=0, tiled=True),
        lax.all_gather(fine_project, "fsdp", axis=0, tiled=True),
        lax.all_gather(fine_output, "fsdp", axis=1, tiled=True),
        lax.all_gather(fine_second_gain, "fsdp", axis=0, tiled=True),
        lax.all_gather(fine_second_bias, "fsdp", axis=0, tiled=True),
        lax.all_gather(fine_expand, "fsdp", axis=0, tiled=True),
        lax.all_gather(fine_narrow, "fsdp", axis=1, tiled=True),
    )
    grad_fine_in, fine_grads = block_backward(
        cotangent[0].astype(jnp.float32), fine_weights_back, fine_stored, fine_back
    )
    grad_previous = jnp.sum(grad_fine_in.reshape(patches, PATCH, D), 1) * joined
    arrived_back = shifted(grad_previous[:1], "seq", -1)
    grad_coarse_out = jnp.concatenate([grad_previous[1:], arrived_back])
    coarse_weights_back = (
        lax.all_gather(patch_weight, "fsdp", axis=0, tiled=True),
        lax.all_gather(coarse_first_gain, "fsdp", axis=0, tiled=True),
        lax.all_gather(coarse_first_bias, "fsdp", axis=0, tiled=True),
        lax.all_gather(coarse_project, "fsdp", axis=0, tiled=True),
        lax.all_gather(coarse_output, "fsdp", axis=1, tiled=True),
        lax.all_gather(coarse_second_gain, "fsdp", axis=0, tiled=True),
        lax.all_gather(coarse_second_bias, "fsdp", axis=0, tiled=True),
        lax.all_gather(coarse_expand, "fsdp", axis=0, tiled=True),
        lax.all_gather(coarse_narrow, "fsdp", axis=1, tiled=True),
    )
    grad_embedded, coarse_grads = block_backward(
        grad_coarse_out, coarse_weights_back[1:], coarse_stored, coarse_back
    )
    grad_embed_low = grad_embedded.astype(jnp.bfloat16)
    grad_patch = left_product(grouped_bytes, grad_embed_low)
    grad_grouped = right_product(grad_embed_low, coarse_weights_back[0])
    input_gradient = (grad_fine_in + grad_grouped.reshape(bytes_here, D)).astype(jnp.bfloat16)
    shards = (
        lax.psum_scatter(grad_patch, "fsdp", scatter_dimension=0, tiled=True),
        lax.psum_scatter(coarse_grads[0], "fsdp", scatter_dimension=0, tiled=True),
        lax.psum_scatter(coarse_grads[1], "fsdp", scatter_dimension=0, tiled=True),
        lax.psum_scatter(coarse_grads[2], "fsdp", scatter_dimension=0, tiled=True),
        lax.psum_scatter(coarse_grads[3], "fsdp", scatter_dimension=1, tiled=True),
        lax.psum_scatter(coarse_grads[4], "fsdp", scatter_dimension=0, tiled=True),
        lax.psum_scatter(coarse_grads[5], "fsdp", scatter_dimension=0, tiled=True),
        lax.psum_scatter(coarse_grads[6], "fsdp", scatter_dimension=0, tiled=True),
        lax.psum_scatter(coarse_grads[7], "fsdp", scatter_dimension=1, tiled=True),
        lax.psum_scatter(fine_grads[0], "fsdp", scatter_dimension=0, tiled=True),
        lax.psum_scatter(fine_grads[1], "fsdp", scatter_dimension=0, tiled=True),
        lax.psum_scatter(fine_grads[2], "fsdp", scatter_dimension=0, tiled=True),
        lax.psum_scatter(fine_grads[3], "fsdp", scatter_dimension=1, tiled=True),
        lax.psum_scatter(fine_grads[4], "fsdp", scatter_dimension=0, tiled=True),
        lax.psum_scatter(fine_grads[5], "fsdp", scatter_dimension=0, tiled=True),
        lax.psum_scatter(fine_grads[6], "fsdp", scatter_dimension=0, tiled=True),
        lax.psum_scatter(fine_grads[7], "fsdp", scatter_dimension=1, tiled=True),
    )
    totals = (
        lax.psum(shards[0].astype(jnp.bfloat16), "seq").astype(jnp.float32),
        lax.psum(shards[1].astype(jnp.bfloat16), "seq").astype(jnp.float32),
        lax.psum(shards[2].astype(jnp.bfloat16), "seq").astype(jnp.float32),
        lax.psum(shards[3].astype(jnp.bfloat16), "seq").astype(jnp.float32),
        lax.psum(shards[4].astype(jnp.bfloat16), "seq").astype(jnp.float32),
        lax.psum(shards[5].astype(jnp.bfloat16), "seq").astype(jnp.float32),
        lax.psum(shards[6].astype(jnp.bfloat16), "seq").astype(jnp.float32),
        lax.psum(shards[7].astype(jnp.bfloat16), "seq").astype(jnp.float32),
        lax.psum(shards[8].astype(jnp.bfloat16), "seq").astype(jnp.float32),
        lax.psum(shards[9].astype(jnp.bfloat16), "seq").astype(jnp.float32),
        lax.psum(shards[10].astype(jnp.bfloat16), "seq").astype(jnp.float32),
        lax.psum(shards[11].astype(jnp.bfloat16), "seq").astype(jnp.float32),
        lax.psum(shards[12].astype(jnp.bfloat16), "seq").astype(jnp.float32),
        lax.psum(shards[13].astype(jnp.bfloat16), "seq").astype(jnp.float32),
        lax.psum(shards[14].astype(jnp.bfloat16), "seq").astype(jnp.float32),
        lax.psum(shards[15].astype(jnp.bfloat16), "seq").astype(jnp.float32),
        lax.psum(shards[16].astype(jnp.bfloat16), "seq").astype(jnp.float32),
    )
    layer_output = layer_rows.astype(jnp.bfloat16)[None]
    return (
        layer_output,
        input_gradient[None],
        totals[0],
        totals[1],
        totals[2],
        totals[3],
        totals[4],
        totals[5],
        totals[6],
        totals[7],
        totals[8],
        totals[9],
        totals[10],
        totals[11],
        totals[12],
        totals[13],
        totals[14],
        totals[15],
        totals[16],
    )


MESH = pl.DeviceIdType.MESH
HBM = pltpu.MemorySpace.HBM
VMEM = pltpu.MemorySpace.VMEM


class Place:
    def __init__(self):
        self.core = lax.axis_index("seq")
        self.at = lax.axis_index("fsdp")
        self.z = self.at // 4
        self.plane = self.at % 4
        self.near = 1 + self.core
        self.far = 2 - self.core

    def flip(self, mask):
        return self.at ^ mask

    def across(self, mask):
        return (self.core, self.at ^ mask)

    def partner(self):
        return (1 - self.core, self.at)


def enter(place, masks, partner=True):
    barrier = pltpu.get_barrier_semaphore()
    for mask in masks:
        pl.semaphore_signal(barrier, inc=1, device_id=place.across(mask), device_id_type=MESH)
    if partner:
        pl.semaphore_signal(barrier, inc=1, device_id=place.partner(), device_id_type=MESH)
    pl.semaphore_wait(barrier, len(masks) + (1 if partner else 0))


MASKS = (1, 2, 4, 8, 12)


class Gather:
    EVENTS = 12

    def __init__(self, place, source, buffer, rows, first, column, width, z_first, sends, receives, local):
        self.p, self.source, self.buffer, self.rows, self.first = place, source, buffer, rows, first
        self.z_first, self.sends, self.receives, self.local = z_first, sends, receives, local
        self.half = width // 2
        self.column, self.width = column, width
        self.mine = pl.ds(pl.multiple_of(column + place.core * self.half, 128), self.half)
        self.theirs = pl.ds(pl.multiple_of(column + (1 - place.core) * self.half, 128), self.half)
        self.started = []

    def group(self, plane, columns=None):
        return self.buffer.at[:, plane, self.rows, self.mine if columns is None else columns]

    def block(self, z, plane):
        return self.buffer.at[z, plane, self.rows, self.mine]

    def send(self, event, view, device, source=None):
        copy = pltpu.make_async_remote_copy(
            src_ref=view if source is None else source,
            dst_ref=view,
            send_sem=self.sends.at[event],
            recv_sem=self.receives.at[event],
            device_id=device,
            device_id_type=MESH,
        )
        copy.start()
        self.started.append(copy)

    def arrived(self, event, view):
        pltpu.make_async_remote_copy(
            src_ref=view,
            dst_ref=view,
            send_sem=self.sends.at[event],
            recv_sem=self.receives.at[event],
            device_id=self.p.partner(),
            device_id_type=MESH,
        ).wait_recv()

    def start(self):
        p = self.p
        own = self.source.at[self.rows, pl.ds(pl.multiple_of(self.first + p.core * self.half, 128), self.half)]
        self.copy = pltpu.make_async_copy(own, self.block(p.z, p.plane), self.local)
        self.copy.start()
        if not self.z_first:
            self.send(6, self.block(p.z, p.plane), p.across(p.near), own)
        for j in (1, 2, 3):
            self.send(j - 1, self.block(p.z, p.plane), p.across(4 * j), own)

    def one(self):
        p = self.p
        self.copy.wait()
        if self.z_first:
            for j in (1, 2, 3):
                self.arrived(j - 1, self.block(p.z ^ j, p.plane))
            self.send(6, self.group(p.plane), p.across(p.near))
            self.send(7, self.group(p.plane), p.across(p.far))
            self.send(9, self.group(p.plane), p.partner())
        else:
            self.arrived(6, self.block(p.z, p.plane ^ p.near))
            for j in (1, 2, 3):
                self.send(2 + j, self.block(p.z, p.plane ^ p.near), p.across(4 * j))

    def two(self):
        p = self.p
        if self.z_first:
            self.arrived(6, self.group(p.plane ^ p.near))
        else:
            for j in (1, 2, 3):
                self.arrived(j - 1, self.block(p.z ^ j, p.plane))
            self.send(7, self.group(p.plane), p.across(p.far))
            self.send(9, self.group(p.plane), p.partner())
            for j in (1, 2, 3):
                self.arrived(2 + j, self.block(p.z ^ j, p.plane ^ p.near))
        self.send(8, self.group(p.plane ^ p.near), p.across(p.far))
        self.send(10, self.group(p.plane ^ p.near), p.partner())

    def three(self):
        p = self.p
        self.arrived(7, self.group(p.plane ^ p.far))
        self.send(11, self.group(p.plane ^ p.far), p.partner())
        self.arrived(8, self.group(p.plane ^ 3))
        self.send(12, self.group(p.plane ^ 3), p.partner())

    def four(self):
        p = self.p
        self.arrived(9, self.group(p.plane, self.theirs))
        self.arrived(10, self.group(p.plane ^ p.far, self.theirs))
        self.arrived(11, self.group(p.plane ^ p.near, self.theirs))
        self.arrived(12, self.group(p.plane ^ 3, self.theirs))

    def drain(self):
        for copy in self.started:
            copy.wait_send()


def run_gathers(gathers, ahead, tick):
    n = len(gathers)
    for k in range(min(ahead, n)):
        gathers[k].start()
    for t in range(n + 3):
        if t < n:
            gathers[t].one()
            if t + ahead < n:
                gathers[t + ahead].start()
        if 0 <= t - 1 < n:
            gathers[t - 1].two()
        if 0 <= t - 2 < n:
            gathers[t - 2].three()
        if 0 <= t - 3 < n:
            gathers[t - 3].four()
        tick()
    for g in gathers:
        g.drain()


def gather_kernel(plan, ahead, *refs):
    sources, small, rows, rest = refs[:9], refs[9], refs[10], refs[11:]
    buffers, small_out, all_rows = rest[:3], rest[3], rest[4]
    sends, receives, local, value, arriving, small_sends, small_receives, row_sems = rest[5:]
    place = Place()
    enter(place, MASKS)
    value[0] = small[...]
    total = Total(place, (1, 2, 4, 8), value, arriving, small_sends, small_receives, small_out)
    stay = pltpu.make_async_copy(rows, all_rows.at[place.core], row_sems.at[0])
    stay.start()
    cross = pltpu.make_async_remote_copy(
        src_ref=rows, dst_ref=all_rows.at[place.core], send_sem=row_sems.at[1], recv_sem=row_sems.at[2],
        device_id=place.partner(), device_id_type=MESH,
    )
    cross.start()
    gathers = []
    for k, (source, buffer, first, rows, start, column, width, z_first) in enumerate(plan):
        gathers.append(
            Gather(place, sources[source], buffers[buffer], pl.ds(first, rows), start, column, width, z_first,
                   sends.at[k], receives.at[k], local.at[k])
        )
    run_gathers(gathers, ahead, total.advance)
    stay.wait()
    cross.wait()


def forward_plan(step=1536, patch_rows=96):
    plan = []
    for first in range(0, 384, patch_rows):
        plan.append((0, 0, first, patch_rows, 0, 0, 768))
    for block in (1, 2):
        column = 0
        for i, width in enumerate((2304, 768, 3072, 3072)):
            for start in range(0, width, step):
                plan.append((4 * block - 3 + i, block, 0, 48, start, column + start, min(step, width - start)))
            column += width
    return tuple(p + (i % 5 != 4,) for i, p in enumerate(plan))


PLAN = forward_plan()


def gather_all(sources, small, rows, ahead=3, plan=PLAN):
    n = len(plan)
    bf = jnp.bfloat16
    return pl.pallas_call(
        functools.partial(gather_kernel, plan, ahead),
        out_shape=(
            jax.ShapeDtypeStruct((4, 4, 384, 768), bf),
            jax.ShapeDtypeStruct((4, 4, 48, 9216), bf),
            jax.ShapeDtypeStruct((4, 4, 48, 9216), bf),
            jax.ShapeDtypeStruct((8, 768), jnp.float32),
            jax.ShapeDtypeStruct((2,) + rows.shape, bf),
        ),
        in_specs=[pl.BlockSpec(memory_space=VMEM)] * 10 + [pl.BlockSpec(memory_space=HBM)],
        out_specs=[pl.BlockSpec(memory_space=HBM)] * 3 + [pl.BlockSpec(memory_space=VMEM), pl.BlockSpec(memory_space=HBM)],
        scratch_shapes=[
            pltpu.SemaphoreType.DMA((n, 13)),
            pltpu.SemaphoreType.DMA((n, 13)),
            pltpu.SemaphoreType.DMA((n,)),
            pltpu.VMEM((5, 8, 768), jnp.float32),
            pltpu.VMEM((4, 8, 768), jnp.float32),
            pltpu.SemaphoreType.DMA((4,)),
            pltpu.SemaphoreType.DMA((4,)),
            pltpu.SemaphoreType.DMA((3,)),
        ],
        compiler_params=pltpu.CompilerParams(collective_id=0, has_side_effects=True),
        name="gather_all",
    )(*sources, small, rows)


class Total:
    def __init__(self, place, masks, value, arriving, sends, receives, result):
        self.p, self.masks, self.value, self.arriving = place, masks, value, arriving
        self.sends, self.receives, self.result = sends, receives, result
        self.step, self.copy = 0, None

    def advance(self):
        if self.step > len(self.masks):
            return
        if self.copy is not None:
            self.copy.wait()
            i = self.step - 1
            self.value[i + 1] = self.value[i] + self.arriving[i]
        if self.step < len(self.masks):
            i = self.step
            mask = self.masks[i]
            self.copy = pltpu.make_async_remote_copy(
                src_ref=self.value.at[i],
                dst_ref=self.arriving.at[i],
                send_sem=self.sends.at[i],
                recv_sem=self.receives.at[i],
                device_id=self.p.across(mask) if mask else self.p.partner(),
                device_id_type=MESH,
            )
            self.copy.start()
        else:
            self.result[...] = self.value[len(self.masks)]
        self.step += 1


def add(left, right):
    return left.astype(jnp.float32) + right.astype(jnp.float32)


class Reduce:
    def __init__(self, place, held, paired, far, near, line, out, rows, column, width, z_last, sends, receives):
        self.p, self.held, self.from_partner, self.from_far = place, held, paired, far
        self.from_near, self.from_line, self.out, self.rows = near, line, out, rows
        self.z_last, self.sends, self.receives = z_last, sends, receives
        self.half = width // 2
        self.mine = pl.ds(pl.multiple_of(column + place.core * self.half, 128), self.half)
        self.theirs = pl.ds(pl.multiple_of(column + (1 - place.core) * self.half, 128), self.half)
        self.started = []

    def send(self, event, source, target, device):
        copy = pltpu.make_async_remote_copy(
            src_ref=source, dst_ref=target, send_sem=self.sends.at[event], recv_sem=self.receives.at[event],
            device_id=device, device_id_type=MESH,
        )
        copy.start()
        self.started.append(copy)

    def arrived(self, event, target):
        pltpu.make_async_remote_copy(
            src_ref=target, dst_ref=target, send_sem=self.sends.at[event], recv_sem=self.receives.at[event],
            device_id=self.p.partner(), device_id_type=MESH,
        ).wait_recv()

    def pair(self, theirs):
        self.send(0, theirs, self.from_partner, self.p.partner())

    def fold(self, plane, others):
        def step(z, _):
            self.held[z, plane] = add(self.held[z, plane], others[z]).astype(jnp.bfloat16)
            return 0

        lax.fori_loop(0, 4, step, 0)

    def one(self):
        p = self.p
        if self.from_partner is not None:
            self.arrived(0, self.from_partner)
            self.fold(p.plane ^ p.far, self.from_partner.at[:, p.plane ^ p.far])
        self.send(1, self.held.at[:, p.plane ^ p.far], self.from_far.at[0], p.across(p.far))
        if self.from_partner is not None:
            self.fold(p.plane ^ 3, self.from_partner.at[:, p.plane ^ 3])
        self.send(2, self.held.at[:, p.plane ^ 3], self.from_far.at[1], p.across(p.far))
        if self.from_partner is not None:
            self.fold(p.plane, self.from_partner.at[:, p.plane])
            self.fold(p.plane ^ p.near, self.from_partner.at[:, p.plane ^ p.near])

    def two(self):
        p = self.p
        self.arrived(2, self.from_far.at[1])
        self.fold(p.plane ^ p.near, self.from_far.at[1])
        if self.z_last:
            self.send(3, self.held.at[:, p.plane ^ p.near], self.from_near, p.across(p.near))
        else:
            for j in (1, 2, 3):
                self.send(6 + j, self.held.at[p.z ^ j, p.plane ^ p.near], self.from_line.at[2 + j], p.across(4 * j))
        self.arrived(1, self.from_far.at[0])
        self.fold(p.plane, self.from_far.at[0])
        if not self.z_last:
            for j in (1, 2, 3):
                self.send(3 + j, self.held.at[p.z ^ j, p.plane], self.from_line.at[j - 1], p.across(4 * j))

    def three(self):
        p = self.p
        if self.z_last:
            self.arrived(3, self.from_near)
            self.fold(p.plane, self.from_near)
            for j in (1, 2, 3):
                self.send(3 + j, self.held.at[p.z ^ j, p.plane], self.from_line.at[j - 1], p.across(4 * j))
        else:
            for j in (1, 2, 3):
                self.arrived(6 + j, self.from_line.at[2 + j])
            near = (add(self.held[p.z, p.plane ^ p.near], self.from_line[3]) + add(self.from_line[4], self.from_line[5]))
            self.held[p.z, p.plane ^ p.near] = near.astype(jnp.bfloat16)
            self.send(3, self.held.at[p.z, p.plane ^ p.near], self.from_near.at[0], p.across(p.near))

    def four(self):
        p = self.p
        for j in (1, 2, 3):
            self.arrived(3 + j, self.from_line.at[j - 1])
        total = add(self.held[p.z, p.plane], self.from_line[0]) + add(self.from_line[1], self.from_line[2])
        if not self.z_last:
            self.arrived(3, self.from_near.at[0])
            total = total + self.from_near[0].astype(jnp.float32)
        self.out[self.rows, self.mine] = total
        view = self.out.at[self.rows, self.mine]
        self.send(10, view, view, p.partner())

    def drain(self):
        for copy in self.started:
            copy.wait_send()
        self.started = []

    def five(self):
        self.arrived(10, self.out.at[self.rows, self.theirs])


def backward_plan(step=1536, patch_rows=96):
    plan = []
    for array, width in ((8, 3072), (7, 3072), (6, 768), (5, 2304), (4, 3072), (3, 3072), (2, 768), (1, 2304)):
        for start in range(0, width, step):
            plan.append((array, 0, 48, start, min(step, width - start)))
    for first in range(0, 384, patch_rows):
        plan.append((0, first, patch_rows, 0, 768))
    return tuple(p + (i % 5 != 4,) for i, p in enumerate(plan))


BACK_PLAN = backward_plan()
SLOTS = 8
LAGS = (2, 3, 4, 5)
ARRAYS = 9


def reduce_kernel(plan, grads, small, outs, small_out, slots, pairs, fars, nears, lines, sends, receives, loads,
                  value, arriving, small_sends, small_receives):
    place = Place()
    enter(place, MASKS)
    n = len(plan)
    value[0] = small[...]
    total = Total(place, (0, 1, 2, 4, 8), value, arriving, small_sends, small_receives, small_out)
    used = [0, 0]
    reduces, copies = [], []
    for k, (array, first, rows, column, width, z_last) in enumerate(plan):
        kind = 0 if array == 0 else 1
        slot = used[kind] % SLOTS
        used[kind] += 1
        half = width // 2
        cut = (lambda ref, half=half: ref if half == ref.shape[-1] else ref.at[..., pl.ds(0, half)])
        reduces.append(
            Reduce(place, cut(slots[kind].at[slot]), cut(pairs.at[used[kind] - 1]) if array > 4 else None, cut(fars[kind].at[used[kind] - 1]),
                   cut(nears[kind].at[used[kind] - 1]), cut(lines[kind].at[used[kind] - 1]), outs[array],
                   pl.ds(first, rows), column, width, z_last, sends.at[k], receives.at[k])
        )

    def load(k):
        array = plan[k][0]
        r = reduces[k]
        if k - SLOTS >= 0:
            reduces[k - SLOTS].drain()
        copy = pltpu.make_async_copy(grads[array].at[:, :, r.rows, r.mine], r.held, loads.at[k])
        copy.start()
        copies.append(copy)
        if array > 4:
            r.pair(grads[array].at[:, :, r.rows, r.theirs])

    load(0)
    for t in range(n + LAGS[-1]):
        if t + 1 < n:
            load(t + 1)
        if t < n:
            copies[t].wait()
            reduces[t].one()
        for lag, name in zip(LAGS, ("two", "three", "four", "five")):
            if 0 <= t - lag < n:
                getattr(reduces[t - lag], name)()
        total.advance()
    for r in reduces:
        r.drain()


def reduce_all(grads, small, plan=BACK_PLAN):
    n = len(plan)
    bf = jnp.bfloat16
    counts = [sum(p[0] == 0 for p in plan), sum(p[0] > 0 for p in plan), sum(p[0] > 4 for p in plan)]
    shapes = tuple((max(p[2] for p in plan if c(p[0])), max(p[4] for p in plan if c(p[0])) // 2) for c in (lambda a: a == 0, lambda a: a > 0))

    def kernel(*refs):
        grads, small, outs, small_out = refs[:ARRAYS], refs[ARRAYS], refs[ARRAYS + 1 : 2 * ARRAYS + 1], refs[2 * ARRAYS + 1]
        pairs, rest = refs[2 * ARRAYS + 2], refs[2 * ARRAYS + 3 :]
        slots, fars, nears, lines = (rest[2 * i : 2 * i + 2] for i in range(4))
        reduce_kernel(plan, grads, small, outs, small_out, slots, pairs, fars, nears, lines, *rest[8:])

    scratch = [pltpu.VMEM((counts[2], 4, 4) + shapes[1], bf)]
    scratch += [pltpu.VMEM((min(SLOTS, counts[i]), 4, 4) + shapes[i], bf) for i in (0, 1)]
    for lead in ((2, 4), (4,), (6,)):
        scratch += [pltpu.VMEM((counts[i],) + lead + shapes[i], bf) for i in (0, 1)]
    scratch += [
        pltpu.SemaphoreType.DMA((n, 11)),
        pltpu.SemaphoreType.DMA((n, 11)),
        pltpu.SemaphoreType.DMA((n,)),
        pltpu.VMEM((6, 8, 768), jnp.float32),
        pltpu.VMEM((5, 8, 768), jnp.float32),
        pltpu.SemaphoreType.DMA((5,)),
        pltpu.SemaphoreType.DMA((5,)),
    ]
    grads = [g.reshape(4, 4, g.shape[0] // 16, g.shape[1]) for g in grads]
    return pl.pallas_call(
        kernel,
        out_shape=[jax.ShapeDtypeStruct(g.shape[2:], jnp.float32) for g in grads] + [jax.ShapeDtypeStruct((8, 768), jnp.float32)],
        in_specs=[pl.BlockSpec(memory_space=HBM)] * ARRAYS + [pl.BlockSpec(memory_space=VMEM)],
        out_specs=[pl.BlockSpec(memory_space=VMEM)] * (ARRAYS + 1),
        scratch_shapes=scratch,
        compiler_params=pltpu.CompilerParams(collective_id=1, has_side_effects=True, vmem_limit_bytes=66_000_000),
        name="reduce_all",
    )(*grads, small)


def fast_body(byte_inputs, segment_ids, cotangent, patch_weight, *weights):
    coarse, fine = weights[:8], weights[8:]
    core, at = lax.axis_index("seq"), lax.axis_index("fsdp")
    vectors = jnp.stack([w[i] for w in (coarse, fine) for i in (0, 1, 4, 5)]).astype(jnp.float32)
    small = lax.dynamic_update_slice(jnp.zeros((8, D), jnp.float32), vectors, (0, at * vectors.shape[1]))
    sources = [patch_weight]
    for w in (coarse, fine):
        sources += [w[2], w[3].T, w[6], w[7].T]
    byte_rows = byte_inputs[0]
    bytes_here = byte_rows.shape[0]
    patches = bytes_here // PATCH
    patch_full, coarse_full, fine_full, small, all_rows = gather_all(sources, small, byte_rows)
    patch_full = patch_full.reshape(-1, D)

    def unpack(full, first):
        full = full.reshape(D, -1)
        return (small[first], small[first + 1], full[:, : 3 * D], full[:, 3 * D : 4 * D], small[first + 2], small[first + 3],
                full[:, 4 * D : 8 * D], full[:, 8 * D :])

    coarse_w = unpack(coarse_full, 0)
    segment_row = segment_ids[0]
    all_patches = segment_row.shape[0]
    places = jnp.arange(all_patches)
    coarse_allowed = (
        (places[:, None] >= places[None, :]) & (segment_row[:, None] == segment_row[None, :])
    )[None]

    def attend(shape, allowed):
        rows = shape[0] * shape[1]

        def forward(triple):
            grouped = triple.reshape(shape + (3, D // HEAD_DIM, HEAD_DIM))
            parts = grouped[:, :, 0], grouped[:, :, 1], grouped[:, :, 2]
            mixture, log_total = attend_forward(*parts, allowed)
            return (mixture.reshape(rows, D).astype(jnp.bfloat16), parts + (log_total,))

        def backward(grad_mixture, stored):
            queries, key_part, value_part, log_total = stored
            grads = attend_backward(
                queries, key_part, value_part, allowed, log_total,
                grad_mixture.reshape(shape + (D // HEAD_DIM, HEAD_DIM)),
            )
            return jnp.stack(grads, 2).astype(jnp.bfloat16).reshape(rows, 3 * D)

        return forward, backward

    coarse_attend, coarse_back = attend((1, all_patches), coarse_allowed)
    grouped_bytes = all_rows.reshape(all_patches, PATCH * D)
    embedded = product(grouped_bytes, patch_full)
    coarse_out, coarse_stored = block_forward_t(embedded, coarse_w, coarse_attend)
    coarse_low = coarse_out.astype(jnp.bfloat16)
    joined = jnp.concatenate([jnp.zeros((1,), bool), segment_row[1:] == segment_row[:-1]]).astype(jnp.float32)[:, None]
    previous = jnp.concatenate([jnp.zeros((1, D), jnp.bfloat16), coarse_low[:-1]]).astype(jnp.float32) * joined
    previous = lax.dynamic_slice_in_dim(previous, core * patches, patches)
    (layer_rows, grad_fine_in, grad_previous, fine_vectors, normed, mixture, second, hidden, grad_middle, grad_lifted,
     grad_triple) = fine_block(byte_rows, previous, cotangent[0], small, fine_full.reshape(D, -1))
    fine_grads = [
        left_product(*pair).astype(jnp.bfloat16)
        for pair in ((normed, grad_triple), (grad_middle, mixture), (second, grad_lifted), (cotangent[0], hidden))
    ]
    grad_previous = lax.all_gather(grad_previous, "seq", axis=0, tiled=True) * joined
    grad_coarse_out = jnp.concatenate([grad_previous[1:], jnp.zeros((1, D), jnp.float32)])
    grad_embedded, coarse_grads = block_backward_t(grad_coarse_out, coarse_w, coarse_stored, coarse_back)
    grad_embed_low = grad_embedded.astype(jnp.bfloat16)
    grad_patch = left_product(grouped_bytes, grad_embed_low).astype(jnp.bfloat16)
    grad_here = lax.dynamic_slice_in_dim(grad_embed_low, core * patches, patches)
    grad_grouped = right_product(grad_here, patch_full)
    input_gradient = (grad_fine_in + grad_grouped.reshape(bytes_here, D)).astype(jnp.bfloat16)
    once = (core == 0).astype(jnp.float32)
    small = jnp.concatenate([jnp.stack([coarse_grads[i] * once for i in (0, 1, 4, 5)]), fine_vectors[4:]])
    *shards, small = reduce_all(
        [grad_patch] + [coarse_grads[i].astype(jnp.bfloat16) for i in (2, 3, 6, 7)] + fine_grads, small
    )
    small = lax.dynamic_slice_in_dim(small, at * vectors.shape[1], vectors.shape[1], 1)

    def gradients(parts, first):
        return (small[first], small[first + 1], parts[0], parts[1].T, small[first + 2], small[first + 3], parts[2], parts[3].T)

    return (layer_rows[None], input_gradient[None], shards[0]) + gradients(shards[1:5], 0) + gradients(shards[5:], 4)


def block_forward_t(inputs, weights, attend):
    first_gain, first_bias, project, output_t, second_gain, second_bias, expand, narrow_t = weights
    normed = layer_norm(inputs, first_gain, first_bias).astype(jnp.bfloat16)
    triple = product(normed, project).astype(jnp.bfloat16)
    mixture, attend_stored = attend(triple)
    middle = inputs + right_product(mixture, output_t)
    second = layer_norm(middle, second_gain, second_bias).astype(jnp.bfloat16)
    lifted = product(second, expand)
    hidden = smooth_gate(lifted).astype(jnp.bfloat16)
    result = middle + right_product(hidden, narrow_t)
    stored = (inputs, normed, attend_stored, mixture, middle, second, lifted, hidden)
    return (result, stored)


def block_backward_t(grad_result, weights, stored, attend_back):
    first_gain, first_bias, project, output_t, second_gain, second_bias, expand, narrow_t = weights
    inputs, normed, attend_stored, mixture, middle, second, lifted, hidden = stored
    grad_branch = grad_result.astype(jnp.bfloat16)
    grad_narrow_t = left_product(grad_branch, hidden)
    grad_hidden = product(grad_branch, narrow_t)
    grad_lifted = jax.vjp(smooth_gate, lifted)[1](grad_hidden)[0].astype(jnp.bfloat16)
    grad_expand = left_product(second, grad_lifted)
    grad_second = right_product(grad_lifted, expand)
    pullback = jax.vjp(layer_norm, middle, second_gain, second_bias)[1]
    grad_middle, grad_gain_two, grad_bias_two = pullback(grad_second)
    grad_middle = grad_middle + grad_result
    grad_attended = grad_middle.astype(jnp.bfloat16)
    grad_output_t = left_product(grad_attended, mixture)
    grad_mixture = product(grad_attended, output_t).astype(jnp.bfloat16)
    grad_triple = attend_back(grad_mixture, attend_stored)
    grad_project = left_product(normed, grad_triple)
    grad_normed = right_product(grad_triple, project)
    pullback = jax.vjp(layer_norm, inputs, first_gain, first_bias)[1]
    grad_inputs, grad_gain_one, grad_bias_one = pullback(grad_normed)
    grad_inputs = grad_inputs + grad_middle
    return (
        grad_inputs,
        (grad_gain_one, grad_bias_one, grad_project, grad_output_t, grad_gain_two, grad_bias_two, grad_expand, grad_narrow_t),
    )


def normalize(values):
    centred = values - jnp.mean(values, -1, keepdims=True)
    scale = lax.rsqrt(jnp.mean(centred * centred, -1, keepdims=True) + epsilon)
    return centred * scale, scale


def normalize_back(grad, unit, scale, norm_gain):
    scaled = grad * norm_gain
    return scale * (
        scaled - jnp.mean(scaled, -1, keepdims=True) - unit * jnp.mean(scaled * unit, -1, keepdims=True)
    )


def gate_both(values):
    root = math.sqrt(2.0 / math.pi)
    square = values * values
    bend = jnp.tanh(root * values * (1.0 + 0.044715 * square))
    half = 0.5 + 0.5 * bend
    slope = half + 0.5 * values * (1.0 - bend * bend) * (root * (1.0 + 3.0 * 0.044715 * square))
    return values * half, slope


def head_lanes(pair):
    lane = lax.broadcasted_iota(jnp.int32, pair.shape, 1)
    zero = jnp.zeros_like(pair)
    return jnp.where(lane < HEAD_DIM, pair, zero), jnp.where(lane < HEAD_DIM, zero, pair)


def chances_of(queries, keys, allowed):
    scores = right_product(queries, keys) * (1.0 / math.sqrt(HEAD_DIM))
    scores = jnp.where(allowed, scores, -1e30)
    powers = jnp.exp(scores - jnp.max(scores, -1, keepdims=True))
    return powers * (1.0 / jnp.sum(powers, -1, keepdims=True))


TILE = 128
PAIRS = 6


def fine_kernel(byte_ref, previous_ref, cotangent_ref, small_ref, w_ref,
                out_ref, grad_in_ref, patch_grad_ref, vectors_ref,
                normed_ref, mixture_ref, second_ref, hidden_ref, low_ref, lifted_grad_ref, triple_grad_ref,
                triple, chances, result, grad_second):
    rows = byte_ref.shape[0]
    bf = jnp.bfloat16
    first_gain, first_bias, second_gain, second_bias = (small_ref[i : i + 1] for i in (4, 5, 6, 7))
    previous = previous_ref[...]
    inputs = (
        byte_ref[...].astype(jnp.float32).reshape(rows // PATCH, PATCH, D) + previous[:, None, :]
    ).reshape(rows, D)
    unit_one, scale_one = normalize(inputs)
    normed = (unit_one * first_gain + first_bias).astype(bf)
    normed_ref[...] = normed
    triple[...] = product(normed, w_ref[:, : 3 * D]).astype(bf)
    row = lax.broadcasted_iota(jnp.int32, (TILE, TILE), 0)
    column = lax.broadcasted_iota(jnp.int32, (TILE, TILE), 1)
    allowed = (row // PATCH == column // PATCH) & (column <= row)
    tiles = rows // TILE

    def attend(pair, _):
        lanes = [pl.ds(pl.multiple_of(i * D + pair * 128, 128), 128) for i in range(3)]
        for tile in range(tiles):
            here = slice(tile * TILE, tile * TILE + TILE)
            queries = head_lanes(triple[here, lanes[0]])
            keys = triple[here, lanes[1]]
            values = head_lanes(triple[here, lanes[2]])
            mixed = None
            for head in range(2):
                found = chances_of(queries[head], keys, allowed)
                chances[pair * 2 + head, here] = found
                term = product(found.astype(bf), values[head])
                mixed = term if mixed is None else mixed + term
            mixture_ref[here, lanes[0]] = mixed.astype(bf)
        return 0

    lax.fori_loop(0, PAIRS, attend, 0)
    middle = inputs + right_product(mixture_ref[...], w_ref[:, 3 * D : 4 * D])
    unit_two, scale_two = normalize(middle)
    second = (unit_two * second_gain + second_bias).astype(bf)
    second_ref[...] = second
    grad_low = cotangent_ref[...]
    result[...] = middle
    for j in range(4):
        here = slice(j * D, j * D + D)
        expand = w_ref[:, 4 * D + j * D : 5 * D + j * D]
        narrow_t = w_ref[:, 8 * D + j * D : 9 * D + j * D]
        hidden, slope = gate_both(product(second, expand))
        hidden = hidden.astype(bf)
        hidden_ref[:, here] = hidden
        lifted_grad = (product(grad_low, narrow_t) * slope).astype(bf)
        lifted_grad_ref[:, here] = lifted_grad
        result[...] += right_product(hidden, narrow_t)
        term = right_product(lifted_grad, expand)
        if j:
            grad_second[...] += term
        else:
            grad_second[...] = term
    out_ref[...] = result[...].astype(bf)
    grad_two = grad_second[...]
    grad_middle = grad_low.astype(jnp.float32) + normalize_back(grad_two, unit_two, scale_two, second_gain)
    low = grad_middle.astype(bf)
    low_ref[...] = low
    grad_second[...] = grad_middle
    grad_mixture = product(low, w_ref[:, 3 * D : 4 * D]).astype(bf)
    result[...] = grad_mixture.astype(jnp.float32)

    def attend_back(pair, _):
        lanes = [pl.ds(pl.multiple_of(i * D + pair * 128, 128), 128) for i in range(3)]
        factor = 1.0 / math.sqrt(HEAD_DIM)
        for tile in range(tiles):
            here = slice(tile * TILE, tile * TILE + TILE)
            queries = head_lanes(triple[here, lanes[0]])
            keys = head_lanes(triple[here, lanes[1]])
            values = triple[here, lanes[2]]
            mixed = head_lanes(result[here, lanes[0]].astype(bf))
            sums = [None, None, None]
            for head in range(2):
                found = chances[pair * 2 + head, here]
                grad = right_product(mixed[head], values)
                scores = (found * (grad - jnp.sum(grad * found, -1, keepdims=True))).astype(bf)
                terms = (
                    product(scores, keys[head]),
                    left_product(scores, queries[head]),
                    left_product(found.astype(bf), mixed[head]),
                )
                sums = [t if s is None else s + t for s, t in zip(sums, terms)]
            triple_grad_ref[here, lanes[0]] = (sums[0] * factor).astype(bf)
            triple_grad_ref[here, lanes[1]] = (sums[1] * factor).astype(bf)
            triple_grad_ref[here, lanes[2]] = sums[2].astype(bf)
        return 0

    lax.fori_loop(0, PAIRS, attend_back, 0)
    grad_one = right_product(triple_grad_ref[...], w_ref[:, : 3 * D])
    grad_in = grad_second[...] + normalize_back(grad_one, unit_one, scale_one, first_gain)
    grad_in_ref[...] = grad_in
    patch_grad_ref[...] = jnp.sum(grad_in.reshape(rows // PATCH, PATCH, D), 1)
    terms = [jnp.sum(t, 0, keepdims=True) for t in (grad_one * unit_one, grad_one, grad_two * unit_two, grad_two)]

    @pl.when(pl.program_id(0) == 0)
    def _():
        vectors_ref[...] = jnp.zeros_like(vectors_ref)

    for i, term in enumerate(terms):
        vectors_ref[4 + i : 5 + i] += term


def fine_block(byte_rows, previous, cotangent, small, full, rows=256):
    count = byte_rows.shape[0]
    bf, f32 = jnp.bfloat16, jnp.float32

    def spec(height, width):
        return pl.BlockSpec((height, width), lambda i: (i, 0))

    def whole(shape):
        return pl.BlockSpec(shape, lambda i: (0, 0), pipeline_mode=pl.Buffered(1))

    outs = [(rows, D, bf), (rows, D, f32), (rows // PATCH, D, f32), None]
    outs += [(rows, D, bf)] * 3 + [(rows, 4 * D, bf), (rows, D, bf), (rows, 4 * D, bf), (rows, 3 * D, bf)]
    steps = count // rows
    return pl.pallas_call(
        fine_kernel,
        grid=(steps,),
        out_shape=[
            jax.ShapeDtypeStruct((o[0] * steps, o[1]), o[2]) if o else jax.ShapeDtypeStruct((8, D), f32) for o in outs
        ],
        in_specs=[spec(rows, D), spec(rows // PATCH, D), spec(rows, D), whole((8, D)), whole(full.shape)],
        out_specs=[spec(o[0], o[1]) if o else pl.BlockSpec((8, D), lambda i: (0, 0)) for o in outs],
        scratch_shapes=[
            pltpu.VMEM((rows, 3 * D), bf),
            pltpu.VMEM((2 * PAIRS, rows, TILE), f32),
            pltpu.VMEM((rows, D), f32),
            pltpu.VMEM((rows, D), f32),
        ],
        compiler_params=pltpu.CompilerParams(dimension_semantics=("arbitrary",), vmem_limit_bytes=64_000_000),
        name="fine_block",
    )(byte_rows, previous, cotangent, small, full)


def solution(mesh):
    return jax.shard_map(
        fast_body if (mesh.shape["seq"], mesh.shape["fsdp"]) == (2, 16) else body,
        mesh=mesh,
        in_specs=(
            P("fsdp", "seq", None),
            P("fsdp", None),
            P("fsdp", "seq", None),
            P("fsdp", None),
            P("fsdp"),
            P("fsdp"),
            P("fsdp", None),
            P(None, "fsdp"),
            P("fsdp"),
            P("fsdp"),
            P("fsdp", None),
            P(None, "fsdp"),
            P("fsdp"),
            P("fsdp"),
            P("fsdp", None),
            P(None, "fsdp"),
            P("fsdp"),
            P("fsdp"),
            P("fsdp", None),
            P(None, "fsdp"),
        ),
        out_specs=(
            P("fsdp", "seq", None),
            P("fsdp", "seq", None),
            P("fsdp", None),
            P("fsdp"),
            P("fsdp"),
            P("fsdp", None),
            P(None, "fsdp"),
            P("fsdp"),
            P("fsdp"),
            P("fsdp", None),
            P(None, "fsdp"),
            P("fsdp"),
            P("fsdp"),
            P("fsdp", None),
            P(None, "fsdp"),
            P("fsdp"),
            P("fsdp"),
            P("fsdp", None),
            P(None, "fsdp"),
        ),
        check_vma=False,
    )
```

```python
import functools
import math

import jax
import jax.numpy as jnp
from jax import lax
from jax.experimental import pallas as pl
from jax.experimental.pallas import tpu as pltpu
from jax.sharding import PartitionSpec as P


D = 768
HEAD_DIM = 64
PATCH = 8


epsilon = 1e-05


def shifted(block, axis, distance):
    devices = range(lax.axis_size(axis))
    route = [(i - distance, i) for i in devices if i - distance in devices]
    return lax.ppermute(block, axis, route)


def layer_norm(values, norm_gain, norm_bias):
    center = jnp.mean(values, -1, keepdims=True)
    centred = values - center
    spread = jnp.mean(centred * centred, -1, keepdims=True)
    return centred * lax.rsqrt(spread + epsilon) * norm_gain + norm_bias


def smooth_gate(values):
    return jax.nn.gelu(values, approximate=True)


def product(left_side, right_side):
    return jnp.dot(left_side, right_side, preferred_element_type=jnp.float32)


def left_product(left_side, right_side):
    return lax.dot_general(
        left_side, right_side, (((0,), (0,)), ((), ())), preferred_element_type=jnp.float32
    )


def right_product(left_side, right_side):
    return lax.dot_general(
        left_side, right_side, (((1,), (1,)), ((), ())), preferred_element_type=jnp.float32
    )


def attend_forward(queries, key_part, value_part, allowed):
    factor = 1.0 / math.sqrt(HEAD_DIM)
    scores = (
        jnp.einsum("bqhd,bkhd->bhqk", queries, key_part, preferred_element_type=jnp.float32)
        * factor
    )
    scores = jnp.where(allowed[:, None], scores, -1e30)
    highest = jnp.max(scores, -1, keepdims=True)
    log_total = highest + jnp.log(jnp.sum(jnp.exp(scores - highest), -1, keepdims=True))
    rounded = jnp.exp(scores - log_total).astype(jnp.bfloat16)
    mixture = jnp.einsum("bhqk,bkhd->bqhd", rounded, value_part, preferred_element_type=jnp.float32)
    return (mixture, log_total)


def attend_backward(queries, key_part, value_part, allowed, log_total, grad_mixture):
    factor = 1.0 / math.sqrt(HEAD_DIM)
    scores = (
        jnp.einsum("bqhd,bkhd->bhqk", queries, key_part, preferred_element_type=jnp.float32)
        * factor
    )
    scores = jnp.where(allowed[:, None], scores, -1e30)
    chances = jnp.exp(scores - log_total)
    rounded = chances.astype(jnp.bfloat16)
    grad_values = jnp.einsum(
        "bhqk,bqhd->bkhd", rounded, grad_mixture, preferred_element_type=jnp.float32
    )
    grad_chances = jnp.einsum(
        "bqhd,bkhd->bhqk", grad_mixture, value_part, preferred_element_type=jnp.float32
    )
    grad_scores = (
        chances * (grad_chances - jnp.sum(grad_chances * chances, -1, keepdims=True))
    ).astype(jnp.bfloat16)
    grad_queries = (
        jnp.einsum("bhqk,bkhd->bqhd", grad_scores, key_part, preferred_element_type=jnp.float32)
        * factor
    )
    grad_keys = (
        jnp.einsum("bhqk,bqhd->bkhd", grad_scores, queries, preferred_element_type=jnp.float32)
        * factor
    )
    return (grad_queries, grad_keys, grad_values)


def block_forward(inputs, weights, attend):
    first_gain, first_bias, project, output, second_gain, second_bias, expand, narrow = weights
    normed = layer_norm(
        inputs, first_gain.astype(jnp.float32), first_bias.astype(jnp.float32)
    ).astype(jnp.bfloat16)
    triple = product(normed, project).astype(jnp.bfloat16)
    mixture, attend_stored = attend(triple)
    middle = inputs + product(mixture, output)
    second = layer_norm(
        middle, second_gain.astype(jnp.float32), second_bias.astype(jnp.float32)
    ).astype(jnp.bfloat16)
    lifted = product(second, expand)
    hidden = smooth_gate(lifted).astype(jnp.bfloat16)
    result = middle + product(hidden, narrow)
    stored = (inputs, normed, attend_stored, mixture, middle, second, lifted, hidden)
    return (result, stored)


def block_backward(grad_result, weights, stored, attend_back):
    first_gain, first_bias, project, output, second_gain, second_bias, expand, narrow = weights
    inputs, normed, attend_stored, mixture, middle, second, lifted, hidden = stored
    grad_branch = grad_result.astype(jnp.bfloat16)
    grad_narrow = left_product(hidden, grad_branch)
    grad_hidden = right_product(grad_branch, narrow)
    grad_lifted = jax.vjp(smooth_gate, lifted)[1](grad_hidden)[0].astype(jnp.bfloat16)
    grad_expand = left_product(second, grad_lifted)
    grad_second = right_product(grad_lifted, expand)
    pullback = jax.vjp(
        layer_norm, middle, second_gain.astype(jnp.float32), second_bias.astype(jnp.float32)
    )[1]
    grad_middle, grad_gain_two, grad_bias_two = pullback(grad_second)
    grad_middle = grad_middle + grad_result
    grad_attended = grad_middle.astype(jnp.bfloat16)
    grad_output = left_product(mixture, grad_attended)
    grad_mixture = right_product(grad_attended, output).astype(jnp.bfloat16)
    grad_triple = attend_back(grad_mixture, attend_stored)
    grad_project = left_product(normed, grad_triple)
    grad_normed = right_product(grad_triple, project)
    pullback = jax.vjp(
        layer_norm, inputs, first_gain.astype(jnp.float32), first_bias.astype(jnp.float32)
    )[1]
    grad_inputs, grad_gain_one, grad_bias_one = pullback(grad_normed)
    grad_inputs = grad_inputs + grad_middle
    return (
        grad_inputs,
        (
            grad_gain_one,
            grad_bias_one,
            grad_project,
            grad_output,
            grad_gain_two,
            grad_bias_two,
            grad_expand,
            grad_narrow,
        ),
    )


def body(
    byte_inputs,
    segment_ids,
    cotangent,
    patch_weight,
    coarse_first_gain,
    coarse_first_bias,
    coarse_project,
    coarse_output,
    coarse_second_gain,
    coarse_second_bias,
    coarse_expand,
    coarse_narrow,
    fine_first_gain,
    fine_first_bias,
    fine_project,
    fine_output,
    fine_second_gain,
    fine_second_bias,
    fine_expand,
    fine_narrow,
):
    coarse_full = (
        lax.all_gather(patch_weight, "fsdp", axis=0, tiled=True),
        lax.all_gather(coarse_first_gain, "fsdp", axis=0, tiled=True),
        lax.all_gather(coarse_first_bias, "fsdp", axis=0, tiled=True),
        lax.all_gather(coarse_project, "fsdp", axis=0, tiled=True),
        lax.all_gather(coarse_output, "fsdp", axis=1, tiled=True),
        lax.all_gather(coarse_second_gain, "fsdp", axis=0, tiled=True),
        lax.all_gather(coarse_second_bias, "fsdp", axis=0, tiled=True),
        lax.all_gather(coarse_expand, "fsdp", axis=0, tiled=True),
        lax.all_gather(coarse_narrow, "fsdp", axis=1, tiled=True),
    )
    fine_full = (
        lax.all_gather(fine_first_gain, "fsdp", axis=0, tiled=True),
        lax.all_gather(fine_first_bias, "fsdp", axis=0, tiled=True),
        lax.all_gather(fine_project, "fsdp", axis=0, tiled=True),
        lax.all_gather(fine_output, "fsdp", axis=1, tiled=True),
        lax.all_gather(fine_second_gain, "fsdp", axis=0, tiled=True),
        lax.all_gather(fine_second_bias, "fsdp", axis=0, tiled=True),
        lax.all_gather(fine_expand, "fsdp", axis=0, tiled=True),
        lax.all_gather(fine_narrow, "fsdp", axis=1, tiled=True),
    )
    byte_rows = byte_inputs[0]
    bytes_here = byte_rows.shape[0]
    patches = bytes_here // PATCH
    segment_row = segment_ids[0]
    all_patches = segment_row.shape[0]
    places = jnp.arange(all_patches)
    coarse_allowed = (
        (places[:, None] >= places[None, :]) & (segment_row[:, None] == segment_row[None, :])
    )[None]
    inner = jnp.arange(PATCH)
    fine_allowed = (inner[:, None] >= inner[None, :])[None]

    def coarse_attend(triple):
        head_block = lax.all_to_all(
            triple.reshape(patches, 3, D), "seq", split_axis=2, concat_axis=0, tiled=True
        )
        all_rows = head_block.shape[0]
        columns = head_block.shape[2]
        local_heads = columns // HEAD_DIM
        queries = head_block[:, 0].reshape(1, all_rows, local_heads, HEAD_DIM)
        key_part = head_block[:, 1].reshape(1, all_rows, local_heads, HEAD_DIM)
        value_part = head_block[:, 2].reshape(1, all_rows, local_heads, HEAD_DIM)
        mixture, log_total = attend_forward(queries, key_part, value_part, coarse_allowed)
        merged = mixture.reshape(all_rows, columns).astype(jnp.bfloat16)
        back_rows = lax.all_to_all(merged, "seq", split_axis=0, concat_axis=1, tiled=True)
        return (back_rows, (queries, key_part, value_part, log_total))

    def coarse_back(grad_mixture, stored):
        queries, key_part, value_part, log_total = stored
        head_grad = lax.all_to_all(grad_mixture, "seq", split_axis=1, concat_axis=0, tiled=True)
        all_rows = head_grad.shape[0]
        columns = head_grad.shape[1]
        grad_queries, grad_keys, grad_values = attend_backward(
            queries,
            key_part,
            value_part,
            coarse_allowed,
            log_total,
            head_grad.reshape(1, all_rows, columns // HEAD_DIM, HEAD_DIM),
        )
        stacked = jnp.stack(
            [
                grad_queries.reshape(all_rows, columns),
                grad_keys.reshape(all_rows, columns),
                grad_values.reshape(all_rows, columns),
            ],
            1,
        ).astype(jnp.bfloat16)
        back_rows = lax.all_to_all(stacked, "seq", split_axis=0, concat_axis=2, tiled=True)
        return back_rows.reshape(back_rows.shape[0], 3 * D)

    def fine_attend(triple):
        grouped = triple.reshape(patches, PATCH, 3, D // HEAD_DIM, HEAD_DIM)
        queries = grouped[:, :, 0]
        key_part = grouped[:, :, 1]
        value_part = grouped[:, :, 2]
        mixture, log_total = attend_forward(queries, key_part, value_part, fine_allowed)
        return (
            mixture.reshape(bytes_here, D).astype(jnp.bfloat16),
            (queries, key_part, value_part, log_total),
        )

    def fine_back(grad_mixture, stored):
        queries, key_part, value_part, log_total = stored
        grad_queries, grad_keys, grad_values = attend_backward(
            queries,
            key_part,
            value_part,
            fine_allowed,
            log_total,
            grad_mixture.reshape(patches, PATCH, D // HEAD_DIM, HEAD_DIM),
        )
        stacked = jnp.stack([grad_queries, grad_keys, grad_values], 2).astype(jnp.bfloat16)
        return stacked.reshape(bytes_here, 3 * D)

    grouped_bytes = byte_rows.reshape(patches, PATCH * D)
    embedded = product(grouped_bytes, coarse_full[0])
    coarse_out, coarse_stored = block_forward(embedded, coarse_full[1:], coarse_attend)
    coarse_low = coarse_out.astype(jnp.bfloat16)
    arrived = shifted(coarse_low[-1:], "seq", 1)
    offset = lax.axis_index("seq") * patches
    padded = jnp.concatenate([segment_row[:1] - 1, segment_row])
    before = lax.dynamic_slice_in_dim(padded, offset, patches)
    current = lax.dynamic_slice_in_dim(segment_row, offset, patches)
    joined = (before == current).astype(jnp.float32)[:, None]
    previous = jnp.concatenate([arrived, coarse_low[:-1]]).astype(jnp.float32) * joined
    fine_in = (
        byte_rows.astype(jnp.float32).reshape(patches, PATCH, D) + previous[:, None, :]
    ).reshape(bytes_here, D)
    layer_rows, fine_stored = block_forward(fine_in, fine_full, fine_attend)
    fine_weights_back = (
        lax.all_gather(fine_first_gain, "fsdp", axis=0, tiled=True),
        lax.all_gather(fine_first_bias, "fsdp", axis=0, tiled=True),
        lax.all_gather(fine_project, "fsdp", axis=0, tiled=True),
        lax.all_gather(fine_output, "fsdp", axis=1, tiled=True),
        lax.all_gather(fine_second_gain, "fsdp", axis=0, tiled=True),
        lax.all_gather(fine_second_bias, "fsdp", axis=0, tiled=True),
        lax.all_gather(fine_expand, "fsdp", axis=0, tiled=True),
        lax.all_gather(fine_narrow, "fsdp", axis=1, tiled=True),
    )
    grad_fine_in, fine_grads = block_backward(
        cotangent[0].astype(jnp.float32), fine_weights_back, fine_stored, fine_back
    )
    grad_previous = jnp.sum(grad_fine_in.reshape(patches, PATCH, D), 1) * joined
    arrived_back = shifted(grad_previous[:1], "seq", -1)
    grad_coarse_out = jnp.concatenate([grad_previous[1:], arrived_back])
    coarse_weights_back = (
        lax.all_gather(patch_weight, "fsdp", axis=0, tiled=True),
        lax.all_gather(coarse_first_gain, "fsdp", axis=0, tiled=True),
        lax.all_gather(coarse_first_bias, "fsdp", axis=0, tiled=True),
        lax.all_gather(coarse_project, "fsdp", axis=0, tiled=True),
        lax.all_gather(coarse_output, "fsdp", axis=1, tiled=True),
        lax.all_gather(coarse_second_gain, "fsdp", axis=0, tiled=True),
        lax.all_gather(coarse_second_bias, "fsdp", axis=0, tiled=True),
        lax.all_gather(coarse_expand, "fsdp", axis=0, tiled=True),
        lax.all_gather(coarse_narrow, "fsdp", axis=1, tiled=True),
    )
    grad_embedded, coarse_grads = block_backward(
        grad_coarse_out, coarse_weights_back[1:], coarse_stored, coarse_back
    )
    grad_embed_low = grad_embedded.astype(jnp.bfloat16)
    grad_patch = left_product(grouped_bytes, grad_embed_low)
    grad_grouped = right_product(grad_embed_low, coarse_weights_back[0])
    input_gradient = (grad_fine_in + grad_grouped.reshape(bytes_here, D)).astype(jnp.bfloat16)
    shards = (
        lax.psum_scatter(grad_patch, "fsdp", scatter_dimension=0, tiled=True),
        lax.psum_scatter(coarse_grads[0], "fsdp", scatter_dimension=0, tiled=True),
        lax.psum_scatter(coarse_grads[1], "fsdp", scatter_dimension=0, tiled=True),
        lax.psum_scatter(coarse_grads[2], "fsdp", scatter_dimension=0, tiled=True),
        lax.psum_scatter(coarse_grads[3], "fsdp", scatter_dimension=1, tiled=True),
        lax.psum_scatter(coarse_grads[4], "fsdp", scatter_dimension=0, tiled=True),
        lax.psum_scatter(coarse_grads[5], "fsdp", scatter_dimension=0, tiled=True),
        lax.psum_scatter(coarse_grads[6], "fsdp", scatter_dimension=0, tiled=True),
        lax.psum_scatter(coarse_grads[7], "fsdp", scatter_dimension=1, tiled=True),
        lax.psum_scatter(fine_grads[0], "fsdp", scatter_dimension=0, tiled=True),
        lax.psum_scatter(fine_grads[1], "fsdp", scatter_dimension=0, tiled=True),
        lax.psum_scatter(fine_grads[2], "fsdp", scatter_dimension=0, tiled=True),
        lax.psum_scatter(fine_grads[3], "fsdp", scatter_dimension=1, tiled=True),
        lax.psum_scatter(fine_grads[4], "fsdp", scatter_dimension=0, tiled=True),
        lax.psum_scatter(fine_grads[5], "fsdp", scatter_dimension=0, tiled=True),
        lax.psum_scatter(fine_grads[6], "fsdp", scatter_dimension=0, tiled=True),
        lax.psum_scatter(fine_grads[7], "fsdp", scatter_dimension=1, tiled=True),
    )
    totals = (
        lax.psum(shards[0].astype(jnp.bfloat16), "seq").astype(jnp.float32),
        lax.psum(shards[1].astype(jnp.bfloat16), "seq").astype(jnp.float32),
        lax.psum(shards[2].astype(jnp.bfloat16), "seq").astype(jnp.float32),
        lax.psum(shards[3].astype(jnp.bfloat16), "seq").astype(jnp.float32),
        lax.psum(shards[4].astype(jnp.bfloat16), "seq").astype(jnp.float32),
        lax.psum(shards[5].astype(jnp.bfloat16), "seq").astype(jnp.float32),
        lax.psum(shards[6].astype(jnp.bfloat16), "seq").astype(jnp.float32),
        lax.psum(shards[7].astype(jnp.bfloat16), "seq").astype(jnp.float32),
        lax.psum(shards[8].astype(jnp.bfloat16), "seq").astype(jnp.float32),
        lax.psum(shards[9].astype(jnp.bfloat16), "seq").astype(jnp.float32),
        lax.psum(shards[10].astype(jnp.bfloat16), "seq").astype(jnp.float32),
        lax.psum(shards[11].astype(jnp.bfloat16), "seq").astype(jnp.float32),
        lax.psum(shards[12].astype(jnp.bfloat16), "seq").astype(jnp.float32),
        lax.psum(shards[13].astype(jnp.bfloat16), "seq").astype(jnp.float32),
        lax.psum(shards[14].astype(jnp.bfloat16), "seq").astype(jnp.float32),
        lax.psum(shards[15].astype(jnp.bfloat16), "seq").astype(jnp.float32),
        lax.psum(shards[16].astype(jnp.bfloat16), "seq").astype(jnp.float32),
    )
    layer_output = layer_rows.astype(jnp.bfloat16)[None]
    return (
        layer_output,
        input_gradient[None],
        totals[0],
        totals[1],
        totals[2],
        totals[3],
        totals[4],
        totals[5],
        totals[6],
        totals[7],
        totals[8],
        totals[9],
        totals[10],
        totals[11],
        totals[12],
        totals[13],
        totals[14],
        totals[15],
        totals[16],
    )


MESH = pl.DeviceIdType.MESH
HBM = pltpu.MemorySpace.HBM
VMEM = pltpu.MemorySpace.VMEM


class Place:
    def __init__(self):
        self.core = lax.axis_index("seq")
        self.at = lax.axis_index("fsdp")
        self.z = self.at // 4
        self.plane = self.at % 4
        self.near = 1 + self.core
        self.far = 2 - self.core

    def flip(self, mask):
        return self.at ^ mask

    def across(self, mask):
        return (self.core, self.at ^ mask)

    def partner(self):
        return (1 - self.core, self.at)


def enter(place, masks, partner=True):
    barrier = pltpu.get_barrier_semaphore()
    for mask in masks:
        pl.semaphore_signal(barrier, inc=1, device_id=place.across(mask), device_id_type=MESH)
    if partner:
        pl.semaphore_signal(barrier, inc=1, device_id=place.partner(), device_id_type=MESH)
    pl.semaphore_wait(barrier, len(masks) + (1 if partner else 0))


MASKS = (1, 2, 4, 8, 12)


class Gather:
    EVENTS = 12

    def __init__(self, place, source, buffer, rows, first, column, width, z_first, sends, receives, local):
        self.p, self.source, self.buffer, self.rows, self.first = place, source, buffer, rows, first
        self.z_first, self.sends, self.receives, self.local = z_first, sends, receives, local
        self.half = width // 2
        self.column, self.width = column, width
        self.mine = pl.ds(pl.multiple_of(column + place.core * self.half, 128), self.half)
        self.theirs = pl.ds(pl.multiple_of(column + (1 - place.core) * self.half, 128), self.half)
        self.started = []

    def group(self, plane, columns=None):
        return self.buffer.at[:, plane, self.rows, self.mine if columns is None else columns]

    def block(self, z, plane):
        return self.buffer.at[z, plane, self.rows, self.mine]

    def send(self, event, view, device, source=None):
        copy = pltpu.make_async_remote_copy(
            src_ref=view if source is None else source,
            dst_ref=view,
            send_sem=self.sends.at[event],
            recv_sem=self.receives.at[event],
            device_id=device,
            device_id_type=MESH,
        )
        copy.start()
        self.started.append(copy)

    def arrived(self, event, view):
        pltpu.make_async_remote_copy(
            src_ref=view,
            dst_ref=view,
            send_sem=self.sends.at[event],
            recv_sem=self.receives.at[event],
            device_id=self.p.partner(),
            device_id_type=MESH,
        ).wait_recv()

    def start(self):
        p = self.p
        own = self.source.at[self.rows, pl.ds(pl.multiple_of(self.first + p.core * self.half, 128), self.half)]
        self.copy = pltpu.make_async_copy(own, self.block(p.z, p.plane), self.local)
        self.copy.start()
        if not self.z_first:
            self.send(6, self.block(p.z, p.plane), p.across(p.near), own)
        for j in (1, 2, 3):
            self.send(j - 1, self.block(p.z, p.plane), p.across(4 * j), own)

    def one(self):
        p = self.p
        self.copy.wait()
        if self.z_first:
            for j in (1, 2, 3):
                self.arrived(j - 1, self.block(p.z ^ j, p.plane))
            self.send(6, self.group(p.plane), p.across(p.near))
            self.send(7, self.group(p.plane), p.across(p.far))
            self.send(9, self.group(p.plane), p.partner())
        else:
            self.arrived(6, self.block(p.z, p.plane ^ p.near))
            for j in (1, 2, 3):
                self.send(2 + j, self.block(p.z, p.plane ^ p.near), p.across(4 * j))

    def two(self):
        p = self.p
        if self.z_first:
            self.arrived(6, self.group(p.plane ^ p.near))
        else:
            for j in (1, 2, 3):
                self.arrived(j - 1, self.block(p.z ^ j, p.plane))
            self.send(7, self.group(p.plane), p.across(p.far))
            self.send(9, self.group(p.plane), p.partner())
            for j in (1, 2, 3):
                self.arrived(2 + j, self.block(p.z ^ j, p.plane ^ p.near))
        self.send(8, self.group(p.plane ^ p.near), p.across(p.far))
        self.send(10, self.group(p.plane ^ p.near), p.partner())

    def three(self):
        p = self.p
        self.arrived(7, self.group(p.plane ^ p.far))
        self.send(11, self.group(p.plane ^ p.far), p.partner())
        self.arrived(8, self.group(p.plane ^ 3))
        self.send(12, self.group(p.plane ^ 3), p.partner())

    def four(self):
        p = self.p
        self.arrived(9, self.group(p.plane, self.theirs))
        self.arrived(10, self.group(p.plane ^ p.far, self.theirs))
        self.arrived(11, self.group(p.plane ^ p.near, self.theirs))
        self.arrived(12, self.group(p.plane ^ 3, self.theirs))

    def drain(self):
        for copy in self.started:
            copy.wait_send()


def run_gathers(gathers, ahead, tick):
    n = len(gathers)
    for k in range(min(ahead, n)):
        gathers[k].start()
    for t in range(n + 3):
        if t < n:
            gathers[t].one()
            if t + ahead < n:
                gathers[t + ahead].start()
        if 0 <= t - 1 < n:
            gathers[t - 1].two()
        if 0 <= t - 2 < n:
            gathers[t - 2].three()
        if 0 <= t - 3 < n:
            gathers[t - 3].four()
        tick(t)
    for g in gathers:
        g.drain()


class PatchForward:
    def __init__(self, small, rows, patch, w, segments, outs):
        self.small, self.rows, self.patch, self.w, self.segments = small, rows, patch, w, segments
        self.embedded, self.normed, self.triple, self.chances, self.mixture = outs[:5]
        self.middle, self.second, self.lifted, self.hidden, self.result = outs[5:]

    def weight(self, column, width):
        return self.w[:, :, :, column : column + width].reshape(D, width)

    def embed(self, first):
        def step(z, _):
            columns = pl.ds(pl.multiple_of(z * 2 * D, 128), 2 * D)
            rows = self.rows[:, :, columns].reshape(self.embedded.shape[0], 2 * D)
            term = product(rows, self.patch[z].reshape(2 * D, D))
            self.embedded[...] += term
            return 0

        if first == 0:
            self.embedded[...] = jnp.zeros_like(self.embedded)
        lax.fori_loop(first, first + 2, step, 0)

    def project(self):
        unit, _ = normalize(self.embedded[...])
        self.normed[...] = (unit * self.small[0:1] + self.small[1:2]).astype(jnp.bfloat16)
        self.triple[...] = product(self.normed[...], self.weight(0, 3 * D)).astype(jnp.bfloat16)

    def attend(self, first):
        count = self.triple.shape[0]
        row = lax.broadcasted_iota(jnp.int32, (count, count), 0)
        column = lax.broadcasted_iota(jnp.int32, (count, count), 1)
        allowed = (column <= row) & (self.segments[1][...] == self.segments[0][...])

        def step(pair, _):
            lanes = [pl.ds(pl.multiple_of(i * D + pair * 128, 128), 128) for i in range(3)]
            queries = head_lanes(self.triple[:, lanes[0]])
            keys = self.triple[:, lanes[1]]
            values = head_lanes(self.triple[:, lanes[2]])
            mixed = None
            for head in range(2):
                found = chances_of(queries[head], keys, allowed)
                self.chances[pair * 2 + head] = found
                term = product(found.astype(jnp.bfloat16), values[head])
                mixed = term if mixed is None else mixed + term
            self.mixture[:, lanes[0]] = mixed.astype(jnp.bfloat16)
            return 0

        lax.fori_loop(first, first + 3, step, 0)

    def join(self):
        middle = self.embedded[...] + right_product(self.mixture[...], self.weight(3 * D, D))
        self.middle[...] = middle
        self.result[...] = middle
        unit, _ = normalize(middle)
        self.second[...] = (unit * self.small[2:3] + self.small[3:4]).astype(jnp.bfloat16)

    def lift(self, half):
        here = slice(half * 2 * D, half * 2 * D + 2 * D)
        lifted = product(self.second[...], self.weight(4 * D + half * 2 * D, 2 * D))
        self.lifted[:, here] = lifted
        self.hidden[:, here] = smooth_gate(lifted).astype(jnp.bfloat16)

    def lower(self, half):
        here = slice(half * 2 * D, half * 2 * D + 2 * D)
        self.result[...] += right_product(self.hidden[:, here], self.weight(8 * D + half * 2 * D, 2 * D))


def gather_kernel(plan, ahead, *refs):
    sources, small, rows, segments, rest = refs[:9], refs[9], refs[10], refs[11:13], refs[13:]
    buffers, small_out, all_rows, patch_outs, rest = rest[:3], rest[3], rest[4], rest[5:15], rest[15:]
    sends, receives, local, value, arriving, small_sends, small_receives, row_sems, patch, w, loads = rest
    place = Place()
    enter(place, MASKS)
    value[0] = small[...]
    total = Total(place, (1, 2, 4, 8), value, arriving, small_sends, small_receives, small_out)
    stay = pltpu.make_async_copy(rows, all_rows.at[place.core], row_sems.at[0])
    stay.start()
    cross = pltpu.make_async_remote_copy(
        src_ref=rows, dst_ref=all_rows.at[place.core], send_sem=row_sems.at[1], recv_sem=row_sems.at[2],
        device_id=place.partner(), device_id_type=MESH,
    )
    cross.start()
    gathers = []
    for k, (source, buffer, first, rows_here, start, column, width, z_first) in enumerate(plan):
        gathers.append(
            Gather(place, sources[source], buffers[buffer], pl.ds(first, rows_here), start, column, width, z_first,
                   sends.at[k], receives.at[k], local.at[k])
        )
    forward = PatchForward(small_out, all_rows, patch, w, segments, patch_outs)
    waiting = []
    patches = sum(p[1] == 0 for p in plan)
    held = sum(p[1] < 2 for p in plan)

    def fetched():
        while waiting:
            waiting.pop().wait()

    def rows_there():
        stay.wait()
        cross.wait()

    base = patches + 4
    pieces = {
        base: (rows_there, fetched, functools.partial(forward.embed, 0)),
        base + 1: (functools.partial(forward.embed, 2),),
        base + 2: (fetched, forward.project),
        base + 3: (functools.partial(forward.attend, 0),),
        base + 4: (functools.partial(forward.attend, 3),),
        base + 5: (fetched, forward.join),
        base + 6: (functools.partial(forward.lift, 0),),
        base + 7: (functools.partial(forward.lift, 1),),
        base + 8: (fetched, functools.partial(forward.lower, 0)),
        base + 9: (functools.partial(forward.lower, 1),),
    }

    def tick(t):
        total.advance()
        for piece in pieces.get(t, ()):
            piece()
        k = t - 3
        if 0 <= k < held:
            _, buffer, first, count, _, column, width, _ = plan[k]
            part = (slice(None), slice(None), pl.ds(first, count), pl.ds(column, width))
            copy = pltpu.make_async_copy(buffers[buffer].at[part], (patch, w)[buffer].at[part], loads.at[k])
            copy.start()
            waiting.append(copy)

    run_gathers(gathers, ahead, tick)


def forward_plan(step=1536, patch_rows=96):
    plan = []
    for first in range(0, 384, patch_rows):
        plan.append((0, 0, first, patch_rows, 0, 0, 768))
    for block in (1, 2):
        column = 0
        for i, width in enumerate((2304, 768, 3072, 3072)):
            for start in range(0, width, step):
                plan.append((4 * block - 3 + i, block, 0, 48, start, column + start, min(step, width - start)))
            column += width
    return tuple(p + (i % 5 != 4,) for i, p in enumerate(plan))


PLAN = forward_plan()


def gather_all(sources, small, rows, segments, ahead=3, plan=PLAN):
    n = len(plan)
    bf, f32 = jnp.bfloat16, jnp.float32
    count = 2 * rows.shape[0]
    outs = [((8, D), f32), ((2,) + rows.shape, bf), ((count, D), f32), ((count, D), bf), ((count, 3 * D), bf),
            ((D // HEAD_DIM, count, count), f32), ((count, D), bf), ((count, D), f32), ((count, D), bf), ((count, 4 * D), f32),
            ((count, 4 * D), bf), ((count, D), f32)]
    shapes = ((4, 4, 384, D), (4, 4, 48, 12 * D))
    return pl.pallas_call(
        functools.partial(gather_kernel, plan, ahead),
        out_shape=[jax.ShapeDtypeStruct(shape, bf) for shape in shapes + shapes[1:]]
        + [jax.ShapeDtypeStruct(*out) for out in outs],
        in_specs=[pl.BlockSpec(memory_space=VMEM)] * 10 + [pl.BlockSpec(memory_space=HBM)] + [pl.BlockSpec(memory_space=VMEM)] * 2,
        out_specs=[pl.BlockSpec(memory_space=HBM)] * 3 + [pl.BlockSpec(memory_space=VMEM)] * len(outs),
        scratch_shapes=[
            pltpu.SemaphoreType.DMA((n, 13)),
            pltpu.SemaphoreType.DMA((n, 13)),
            pltpu.SemaphoreType.DMA((n,)),
            pltpu.VMEM((5, 8, 768), jnp.float32),
            pltpu.VMEM((4, 8, 768), jnp.float32),
            pltpu.SemaphoreType.DMA((4,)),
            pltpu.SemaphoreType.DMA((4,)),
            pltpu.SemaphoreType.DMA((3,)),
            pltpu.VMEM(shapes[0], bf),
            pltpu.VMEM(shapes[1], bf),
            pltpu.SemaphoreType.DMA((n,)),
        ],
        compiler_params=pltpu.CompilerParams(collective_id=0, has_side_effects=True, vmem_limit_bytes=64_000_000),
        name="gather_all",
    )(*sources, small, rows, *segments)


class Total:
    def __init__(self, place, masks, value, arriving, sends, receives, result):
        self.p, self.masks, self.value, self.arriving = place, masks, value, arriving
        self.sends, self.receives, self.result = sends, receives, result
        self.step, self.copy = 0, None

    def advance(self):
        if self.step > len(self.masks):
            return
        if self.copy is not None:
            self.copy.wait()
            i = self.step - 1
            self.value[i + 1] = self.value[i] + self.arriving[i]
        if self.step < len(self.masks):
            i = self.step
            mask = self.masks[i]
            self.copy = pltpu.make_async_remote_copy(
                src_ref=self.value.at[i],
                dst_ref=self.arriving.at[i],
                send_sem=self.sends.at[i],
                recv_sem=self.receives.at[i],
                device_id=self.p.across(mask) if mask else self.p.partner(),
                device_id_type=MESH,
            )
            self.copy.start()
        else:
            self.result[...] = self.value[len(self.masks)]
        self.step += 1


def add(left, right):
    return left.astype(jnp.float32) + right.astype(jnp.float32)


class Reduce:
    def __init__(self, place, held, paired, far, near, line, out, rows, column, width, z_last, sends, receives):
        self.p, self.held, self.from_partner, self.from_far = place, held, paired, far
        self.from_near, self.from_line, self.out, self.rows = near, line, out, rows
        self.z_last, self.sends, self.receives = z_last, sends, receives
        self.half = width // 2
        whole = out.shape[1] // 2
        self.own = pl.ds(column // 2, self.half)
        self.mine = pl.ds(pl.multiple_of(column // 2 + place.core * whole, 128), self.half)
        self.theirs = pl.ds(pl.multiple_of(column // 2 + (1 - place.core) * whole, 128), self.half)
        self.started = []

    def send(self, event, source, target, device):
        copy = pltpu.make_async_remote_copy(
            src_ref=source, dst_ref=target, send_sem=self.sends.at[event], recv_sem=self.receives.at[event],
            device_id=device, device_id_type=MESH,
        )
        copy.start()
        self.started.append(copy)

    def arrived(self, event, target):
        pltpu.make_async_remote_copy(
            src_ref=target, dst_ref=target, send_sem=self.sends.at[event], recv_sem=self.receives.at[event],
            device_id=self.p.partner(), device_id_type=MESH,
        ).wait_recv()

    def pair(self, theirs):
        self.send(0, theirs, self.from_partner, self.p.partner())

    def fold(self, plane, others):
        def step(z, _):
            self.held[z, plane] = add(self.held[z, plane], others[z]).astype(jnp.bfloat16)
            return 0

        lax.fori_loop(0, 4, step, 0)

    def one(self):
        p = self.p
        if self.from_partner is not None:
            self.arrived(0, self.from_partner)
            self.fold(p.plane ^ p.far, self.from_partner.at[:, p.plane ^ p.far])
        self.send(1, self.held.at[:, p.plane ^ p.far], self.from_far.at[0], p.across(p.far))
        if self.from_partner is not None:
            self.fold(p.plane ^ 3, self.from_partner.at[:, p.plane ^ 3])
        self.send(2, self.held.at[:, p.plane ^ 3], self.from_far.at[1], p.across(p.far))
        if self.from_partner is not None:
            self.fold(p.plane, self.from_partner.at[:, p.plane])
            self.fold(p.plane ^ p.near, self.from_partner.at[:, p.plane ^ p.near])

    def two(self):
        p = self.p
        self.arrived(2, self.from_far.at[1])
        self.fold(p.plane ^ p.near, self.from_far.at[1])
        if self.z_last:
            self.send(3, self.held.at[:, p.plane ^ p.near], self.from_near, p.across(p.near))
        else:
            for j in (1, 2, 3):
                self.send(6 + j, self.held.at[p.z ^ j, p.plane ^ p.near], self.from_line.at[2 + j], p.across(4 * j))
        self.arrived(1, self.from_far.at[0])
        self.fold(p.plane, self.from_far.at[0])
        if not self.z_last:
            for j in (1, 2, 3):
                self.send(3 + j, self.held.at[p.z ^ j, p.plane], self.from_line.at[j - 1], p.across(4 * j))

    def three(self):
        p = self.p
        if self.z_last:
            self.arrived(3, self.from_near)
            self.fold(p.plane, self.from_near)
            for j in (1, 2, 3):
                self.send(3 + j, self.held.at[p.z ^ j, p.plane], self.from_line.at[j - 1], p.across(4 * j))
        else:
            for j in (1, 2, 3):
                self.arrived(6 + j, self.from_line.at[2 + j])
            near = (add(self.held[p.z, p.plane ^ p.near], self.from_line[3]) + add(self.from_line[4], self.from_line[5]))
            self.held[p.z, p.plane ^ p.near] = near.astype(jnp.bfloat16)
            self.send(3, self.held.at[p.z, p.plane ^ p.near], self.from_near.at[0], p.across(p.near))

    def four(self):
        p = self.p
        for j in (1, 2, 3):
            self.arrived(3 + j, self.from_line.at[j - 1])
        total = add(self.held[p.z, p.plane], self.from_line[0]) + add(self.from_line[1], self.from_line[2])
        if not self.z_last:
            self.arrived(3, self.from_near.at[0])
            total = total + self.from_near[0].astype(jnp.float32)
        self.out[self.rows, self.mine] = total
        view = self.out.at[self.rows, self.mine]
        self.send(10, view, view, p.partner())

    def drain(self):
        for copy in self.started:
            copy.wait_send()
        self.started = []

    def five(self):
        self.arrived(10, self.out.at[self.rows, self.theirs])


def backward_plan(step=1536, patch_rows=96):
    plan = []
    for array, width in ((8, 3072), (7, 3072), (6, 768), (5, 2304), (4, 3072), (3, 3072), (2, 768), (1, 2304)):
        for start in range(0, width, step):
            plan.append((array, 0, 48, start, min(step, width - start)))
    for first in range(0, 384, patch_rows):
        plan.append((0, first, patch_rows, 0, 768))
    return tuple(p + (i % 5 != 4,) for i, p in enumerate(plan))


BACK_PLAN = backward_plan()
SLOTS = 8
LAGS = (2, 3, 4, 5)
ARRAYS = 9


def reduce_kernel(plan, grads, small, outs, small_out, slots, pairs, fars, nears, lines, sends, receives, loads,
                  value, arriving, small_sends, small_receives):
    place = Place()
    enter(place, MASKS)
    n = len(plan)
    value[0] = small[...]
    total = Total(place, (0, 1, 2, 4, 8), value, arriving, small_sends, small_receives, small_out)
    used = [0, 0]
    reduces, copies = [], []
    for k, (array, first, rows, column, width, z_last) in enumerate(plan):
        kind = 0 if array == 0 else 1
        slot = used[kind] % SLOTS
        used[kind] += 1
        half = width // 2
        cut = (lambda ref, half=half: ref if half == ref.shape[-1] else ref.at[..., pl.ds(0, half)])
        reduces.append(
            Reduce(place, cut(slots[kind].at[slot]), cut(pairs.at[used[kind] - 1]) if array > 4 else None, cut(fars[kind].at[used[kind] - 1]),
                   cut(nears[kind].at[used[kind] - 1]), cut(lines[kind].at[used[kind] - 1]), outs[array],
                   pl.ds(first, rows), column, width, z_last, sends.at[k], receives.at[k])
        )

    def load(k):
        array = plan[k][0]
        r = reduces[k]
        if k - SLOTS >= 0:
            reduces[k - SLOTS].drain()
        copy = pltpu.make_async_copy(grads[array].at[:, :, r.rows, r.mine if array > 4 else r.own], r.held, loads.at[k])
        copy.start()
        copies.append(copy)
        if array > 4:
            r.pair(grads[array].at[:, :, r.rows, r.theirs])

    load(0)
    for t in range(n + LAGS[-1]):
        if t + 1 < n:
            load(t + 1)
        if t < n:
            copies[t].wait()
            reduces[t].one()
        for lag, name in zip(LAGS, ("two", "three", "four", "five")):
            if 0 <= t - lag < n:
                getattr(reduces[t - lag], name)()
        total.advance()
    for r in reduces:
        r.drain()


def reduce_all(grads, small, plan=BACK_PLAN):
    n = len(plan)
    bf = jnp.bfloat16
    counts = [sum(p[0] == 0 for p in plan), sum(p[0] > 0 for p in plan), sum(p[0] > 4 for p in plan)]
    shapes = tuple((max(p[2] for p in plan if c(p[0])), max(p[4] for p in plan if c(p[0])) // 2) for c in (lambda a: a == 0, lambda a: a > 0))

    def kernel(*refs):
        grads, small, outs, small_out = refs[:ARRAYS], refs[ARRAYS], refs[ARRAYS + 1 : 2 * ARRAYS + 1], refs[2 * ARRAYS + 1]
        pairs, rest = refs[2 * ARRAYS + 2], refs[2 * ARRAYS + 3 :]
        slots, fars, nears, lines = (rest[2 * i : 2 * i + 2] for i in range(4))
        reduce_kernel(plan, grads, small, outs, small_out, slots, pairs, fars, nears, lines, *rest[8:])

    scratch = [pltpu.VMEM((counts[2], 4, 4) + shapes[1], bf)]
    scratch += [pltpu.VMEM((min(SLOTS, counts[i]), 4, 4) + shapes[i], bf) for i in (0, 1)]
    for lead in ((2, 4), (4,), (6,)):
        scratch += [pltpu.VMEM((counts[i],) + lead + shapes[i], bf) for i in (0, 1)]
    scratch += [
        pltpu.SemaphoreType.DMA((n, 11)),
        pltpu.SemaphoreType.DMA((n, 11)),
        pltpu.SemaphoreType.DMA((n,)),
        pltpu.VMEM((6, 8, 768), jnp.float32),
        pltpu.VMEM((5, 8, 768), jnp.float32),
        pltpu.SemaphoreType.DMA((5,)),
        pltpu.SemaphoreType.DMA((5,)),
    ]
    grads = [g.reshape(4, 4, g.shape[0] // 16, g.shape[1]) for g in grads]
    return pl.pallas_call(
        kernel,
        out_shape=[
            jax.ShapeDtypeStruct((g.shape[2], g.shape[3] if i > 4 else 2 * g.shape[3]), jnp.float32) for i, g in enumerate(grads)
        ] + [jax.ShapeDtypeStruct((8, 768), jnp.float32)],
        in_specs=[pl.BlockSpec(memory_space=HBM)] * ARRAYS + [pl.BlockSpec(memory_space=VMEM)],
        out_specs=[pl.BlockSpec(memory_space=VMEM)] * (ARRAYS + 1),
        scratch_shapes=scratch,
        compiler_params=pltpu.CompilerParams(collective_id=1, has_side_effects=True, vmem_limit_bytes=66_000_000),
        name="reduce_all",
    )(*grads, small)


def fast_body(byte_inputs, segment_ids, cotangent, patch_weight, *weights):
    coarse, fine = weights[:8], weights[8:]
    core, at = lax.axis_index("seq"), lax.axis_index("fsdp")
    vectors = jnp.stack([w[i] for w in (coarse, fine) for i in (0, 1, 4, 5)]).astype(jnp.float32)
    small = lax.dynamic_update_slice(jnp.zeros((8, D), jnp.float32), vectors, (0, at * vectors.shape[1]))
    sources = [patch_weight]
    for w in (coarse, fine):
        sources += [w[2], w[3].T, w[6], w[7].T]
    byte_rows = byte_inputs[0]
    bytes_here = byte_rows.shape[0]
    patches = bytes_here // PATCH
    segment_row = segment_ids[0]
    all_patches = segment_row.shape[0]
    patch_full, coarse_full, fine_full, small, all_rows, *stored, coarse_out = gather_all(
        sources, small, byte_rows.reshape(patches, PATCH * D), (segment_row[None], segment_row[:, None])
    )
    patch_full = patch_full.reshape(-1, D)

    def unpack(full, first):
        full = full.reshape(D, -1)
        return (small[first], small[first + 1], full[:, : 3 * D], full[:, 3 * D : 4 * D], small[first + 2], small[first + 3],
                full[:, 4 * D : 8 * D], full[:, 8 * D :])

    def mine(values):
        width = values.shape[1] // 2
        return lax.dynamic_slice_in_dim(values, core * width, width, 1)

    def coarse_back(grad_mixture, stored):
        triple, chances = stored
        parts = triple.reshape(1, all_patches, 3, D // HEAD_DIM, HEAD_DIM)
        grads = attend_backward_known(
            parts[:, :, 0], parts[:, :, 1], parts[:, :, 2], chances[None],
            grad_mixture.reshape(1, all_patches, D // HEAD_DIM, HEAD_DIM),
        )
        return jnp.stack(grads, 2).astype(jnp.bfloat16).reshape(all_patches, 3 * D)

    coarse_w = unpack(coarse_full, 0)
    coarse_stored = tuple(stored[:2]) + (tuple(stored[2:4]),) + tuple(stored[4:])
    grouped_bytes = all_rows.reshape(all_patches, PATCH * D)
    coarse_low = coarse_out.astype(jnp.bfloat16)
    joined = jnp.concatenate([jnp.zeros((1,), bool), segment_row[1:] == segment_row[:-1]]).astype(jnp.float32)[:, None]
    previous = jnp.concatenate([jnp.zeros((1, D), jnp.bfloat16), coarse_low[:-1]]).astype(jnp.float32) * joined
    previous = lax.dynamic_slice_in_dim(previous, core * patches, patches)
    (layer_rows, grad_fine_in, grad_previous, fine_vectors, normed, mixture, second, hidden, grad_middle, grad_lifted,
     grad_triple) = fine_block(byte_rows, previous, cotangent[0], small, fine_full.reshape(D, -1))
    fine_grads = [
        left_product(*pair).astype(jnp.bfloat16)
        for pair in ((normed, grad_triple), (grad_middle, mixture), (second, grad_lifted), (cotangent[0], hidden))
    ]
    grad_previous = lax.all_gather(grad_previous, "seq", axis=0, tiled=True) * joined
    grad_coarse_out = jnp.concatenate([grad_previous[1:], jnp.zeros((1, D), jnp.float32)])
    grad_embedded, coarse_grads = block_backward_t(grad_coarse_out, coarse_w, coarse_stored, coarse_back, mine)
    grad_embed_low = grad_embedded.astype(jnp.bfloat16)
    grad_patch = left_product(grouped_bytes, mine(grad_embed_low)).astype(jnp.bfloat16)
    grad_here = lax.dynamic_slice_in_dim(grad_embed_low, core * patches, patches)
    grad_grouped = right_product(grad_here, patch_full)
    input_gradient = (grad_fine_in + grad_grouped.reshape(bytes_here, D)).astype(jnp.bfloat16)
    once = (core == 0).astype(jnp.float32)
    small = jnp.concatenate([jnp.stack([coarse_grads[i] * once for i in (0, 1, 4, 5)]), fine_vectors[4:]])
    *shards, small = reduce_all(
        [grad_patch] + [coarse_grads[i].astype(jnp.bfloat16) for i in (2, 3, 6, 7)] + fine_grads, small
    )
    small = lax.dynamic_slice_in_dim(small, at * vectors.shape[1], vectors.shape[1], 1)

    def gradients(parts, first):
        return (small[first], small[first + 1], parts[0], parts[1].T, small[first + 2], small[first + 3], parts[2], parts[3].T)

    return (layer_rows[None], input_gradient[None], shards[0]) + gradients(shards[1:5], 0) + gradients(shards[5:], 4)


def attend_backward_known(queries, key_part, value_part, chances, grad_mixture):
    factor = 1.0 / math.sqrt(HEAD_DIM)
    grad_values = jnp.einsum(
        "bhqk,bqhd->bkhd", chances.astype(jnp.bfloat16), grad_mixture, preferred_element_type=jnp.float32
    )
    grad_chances = jnp.einsum(
        "bqhd,bkhd->bhqk", grad_mixture, value_part, preferred_element_type=jnp.float32
    )
    grad_scores = (
        chances * (grad_chances - jnp.sum(grad_chances * chances, -1, keepdims=True))
    ).astype(jnp.bfloat16)
    grad_queries = (
        jnp.einsum("bhqk,bkhd->bqhd", grad_scores, key_part, preferred_element_type=jnp.float32)
        * factor
    )
    grad_keys = (
        jnp.einsum("bhqk,bqhd->bkhd", grad_scores, queries, preferred_element_type=jnp.float32)
        * factor
    )
    return (grad_queries, grad_keys, grad_values)


def block_backward_t(grad_result, weights, stored, attend_back, mine):
    first_gain, first_bias, project, output_t, second_gain, second_bias, expand, narrow_t = weights
    inputs, normed, attend_stored, mixture, middle, second, lifted, hidden = stored
    grad_branch = grad_result.astype(jnp.bfloat16)
    grad_narrow_t = left_product(grad_branch, mine(hidden))
    grad_hidden = product(grad_branch, narrow_t)
    grad_lifted = jax.vjp(smooth_gate, lifted)[1](grad_hidden)[0].astype(jnp.bfloat16)
    grad_expand = left_product(second, mine(grad_lifted))
    grad_second = right_product(grad_lifted, expand)
    pullback = jax.vjp(layer_norm, middle, second_gain, second_bias)[1]
    grad_middle, grad_gain_two, grad_bias_two = pullback(grad_second)
    grad_middle = grad_middle + grad_result
    grad_attended = grad_middle.astype(jnp.bfloat16)
    grad_output_t = left_product(grad_attended, mine(mixture))
    grad_mixture = product(grad_attended, output_t).astype(jnp.bfloat16)
    grad_triple = attend_back(grad_mixture, attend_stored)
    grad_project = left_product(normed, mine(grad_triple))
    grad_normed = right_product(grad_triple, project)
    pullback = jax.vjp(layer_norm, inputs, first_gain, first_bias)[1]
    grad_inputs, grad_gain_one, grad_bias_one = pullback(grad_normed)
    grad_inputs = grad_inputs + grad_middle
    return (
        grad_inputs,
        (grad_gain_one, grad_bias_one, grad_project, grad_output_t, grad_gain_two, grad_bias_two, grad_expand, grad_narrow_t),
    )


def normalize(values):
    centred = values - jnp.mean(values, -1, keepdims=True)
    scale = lax.rsqrt(jnp.mean(centred * centred, -1, keepdims=True) + epsilon)
    return centred * scale, scale


def normalize_back(grad, unit, scale, norm_gain):
    scaled = grad * norm_gain
    return scale * (
        scaled - jnp.mean(scaled, -1, keepdims=True) - unit * jnp.mean(scaled * unit, -1, keepdims=True)
    )


def gate_both(values):
    root = math.sqrt(2.0 / math.pi)
    square = values * values
    bend = jnp.tanh(root * values * (1.0 + 0.044715 * square))
    half = 0.5 + 0.5 * bend
    slope = half + 0.5 * values * (1.0 - bend * bend) * (root * (1.0 + 3.0 * 0.044715 * square))
    return values * half, slope


def head_lanes(pair):
    lane = lax.broadcasted_iota(jnp.int32, pair.shape, 1)
    zero = jnp.zeros_like(pair)
    return jnp.where(lane < HEAD_DIM, pair, zero), jnp.where(lane < HEAD_DIM, zero, pair)


def chances_of(queries, keys, allowed):
    scores = right_product(queries, keys) * (1.0 / math.sqrt(HEAD_DIM))
    scores = jnp.where(allowed, scores, -1e30)
    powers = jnp.exp(scores - jnp.max(scores, -1, keepdims=True))
    return powers * (1.0 / jnp.sum(powers, -1, keepdims=True))


TILE = 128
PAIRS = 6


def fine_kernel(byte_ref, previous_ref, cotangent_ref, small_ref, w_ref,
                out_ref, grad_in_ref, patch_grad_ref, vectors_ref,
                normed_ref, mixture_ref, second_ref, hidden_ref, low_ref, lifted_grad_ref, triple_grad_ref,
                triple, chances, result, grad_second):
    rows = byte_ref.shape[0]
    bf = jnp.bfloat16
    first_gain, first_bias, second_gain, second_bias = (small_ref[i : i + 1] for i in (4, 5, 6, 7))
    previous = previous_ref[...]
    inputs = (
        byte_ref[...].astype(jnp.float32).reshape(rows // PATCH, PATCH, D) + previous[:, None, :]
    ).reshape(rows, D)
    unit_one, scale_one = normalize(inputs)
    normed = (unit_one * first_gain + first_bias).astype(bf)
    normed_ref[...] = normed
    triple[...] = product(normed, w_ref[:, : 3 * D]).astype(bf)
    row = lax.broadcasted_iota(jnp.int32, (TILE, TILE), 0)
    column = lax.broadcasted_iota(jnp.int32, (TILE, TILE), 1)
    allowed = (row // PATCH == column // PATCH) & (column <= row)
    tiles = rows // TILE

    def attend(pair, _):
        lanes = [pl.ds(pl.multiple_of(i * D + pair * 128, 128), 128) for i in range(3)]
        for tile in range(tiles):
            here = slice(tile * TILE, tile * TILE + TILE)
            queries = head_lanes(triple[here, lanes[0]])
            keys = triple[here, lanes[1]]
            values = head_lanes(triple[here, lanes[2]])
            mixed = None
            for head in range(2):
                found = chances_of(queries[head], keys, allowed)
                chances[pair * 2 + head, here] = found
                term = product(found.astype(bf), values[head])
                mixed = term if mixed is None else mixed + term
            mixture_ref[here, lanes[0]] = mixed.astype(bf)
        return 0

    lax.fori_loop(0, PAIRS, attend, 0)
    middle = inputs + right_product(mixture_ref[...], w_ref[:, 3 * D : 4 * D])
    unit_two, scale_two = normalize(middle)
    second = (unit_two * second_gain + second_bias).astype(bf)
    second_ref[...] = second
    grad_low = cotangent_ref[...]
    result[...] = middle
    for j in range(4):
        here = slice(j * D, j * D + D)
        expand = w_ref[:, 4 * D + j * D : 5 * D + j * D]
        narrow_t = w_ref[:, 8 * D + j * D : 9 * D + j * D]
        hidden, slope = gate_both(product(second, expand))
        hidden = hidden.astype(bf)
        hidden_ref[:, here] = hidden
        lifted_grad = (product(grad_low, narrow_t) * slope).astype(bf)
        lifted_grad_ref[:, here] = lifted_grad
        result[...] += right_product(hidden, narrow_t)
        term = right_product(lifted_grad, expand)
        if j:
            grad_second[...] += term
        else:
            grad_second[...] = term
    out_ref[...] = result[...].astype(bf)
    grad_two = grad_second[...]
    grad_middle = grad_low.astype(jnp.float32) + normalize_back(grad_two, unit_two, scale_two, second_gain)
    low = grad_middle.astype(bf)
    low_ref[...] = low
    grad_second[...] = grad_middle
    grad_mixture = product(low, w_ref[:, 3 * D : 4 * D]).astype(bf)
    result[...] = grad_mixture.astype(jnp.float32)

    def attend_back(pair, _):
        lanes = [pl.ds(pl.multiple_of(i * D + pair * 128, 128), 128) for i in range(3)]
        factor = 1.0 / math.sqrt(HEAD_DIM)
        for tile in range(tiles):
            here = slice(tile * TILE, tile * TILE + TILE)
            queries = head_lanes(triple[here, lanes[0]])
            keys = head_lanes(triple[here, lanes[1]])
            values = triple[here, lanes[2]]
            mixed = head_lanes(result[here, lanes[0]].astype(bf))
            sums = [None, None, None]
            for head in range(2):
                found = chances[pair * 2 + head, here]
                grad = right_product(mixed[head], values)
                scores = (found * (grad - jnp.sum(grad * found, -1, keepdims=True))).astype(bf)
                terms = (
                    product(scores, keys[head]),
                    left_product(scores, queries[head]),
                    left_product(found.astype(bf), mixed[head]),
                )
                sums = [t if s is None else s + t for s, t in zip(sums, terms)]
            triple_grad_ref[here, lanes[0]] = (sums[0] * factor).astype(bf)
            triple_grad_ref[here, lanes[1]] = (sums[1] * factor).astype(bf)
            triple_grad_ref[here, lanes[2]] = sums[2].astype(bf)
        return 0

    lax.fori_loop(0, PAIRS, attend_back, 0)
    grad_one = right_product(triple_grad_ref[...], w_ref[:, : 3 * D])
    grad_in = grad_second[...] + normalize_back(grad_one, unit_one, scale_one, first_gain)
    grad_in_ref[...] = grad_in
    patch_grad_ref[...] = jnp.sum(grad_in.reshape(rows // PATCH, PATCH, D), 1)
    terms = [jnp.sum(t, 0, keepdims=True) for t in (grad_one * unit_one, grad_one, grad_two * unit_two, grad_two)]

    @pl.when(pl.program_id(0) == 0)
    def _():
        vectors_ref[...] = jnp.zeros_like(vectors_ref)

    for i, term in enumerate(terms):
        vectors_ref[4 + i : 5 + i] += term


def fine_block(byte_rows, previous, cotangent, small, full, rows=256):
    count = byte_rows.shape[0]
    bf, f32 = jnp.bfloat16, jnp.float32

    def spec(height, width):
        return pl.BlockSpec((height, width), lambda i: (i, 0))

    def whole(shape):
        return pl.BlockSpec(shape, lambda i: (0, 0), pipeline_mode=pl.Buffered(1))

    outs = [(rows, D, bf), (rows, D, f32), (rows // PATCH, D, f32), None]
    outs += [(rows, D, bf)] * 3 + [(rows, 4 * D, bf), (rows, D, bf), (rows, 4 * D, bf), (rows, 3 * D, bf)]
    steps = count // rows
    return pl.pallas_call(
        fine_kernel,
        grid=(steps,),
        out_shape=[
            jax.ShapeDtypeStruct((o[0] * steps, o[1]), o[2]) if o else jax.ShapeDtypeStruct((8, D), f32) for o in outs
        ],
        in_specs=[spec(rows, D), spec(rows // PATCH, D), spec(rows, D), whole((8, D)), whole(full.shape)],
        out_specs=[spec(o[0], o[1]) if o else pl.BlockSpec((8, D), lambda i: (0, 0)) for o in outs],
        scratch_shapes=[
            pltpu.VMEM((rows, 3 * D), bf),
            pltpu.VMEM((2 * PAIRS, rows, TILE), f32),
            pltpu.VMEM((rows, D), f32),
            pltpu.VMEM((rows, D), f32),
        ],
        compiler_params=pltpu.CompilerParams(dimension_semantics=("arbitrary",), vmem_limit_bytes=64_000_000),
        name="fine_block",
    )(byte_rows, previous, cotangent, small, full)


def solution(mesh):
    return jax.shard_map(
        fast_body if (mesh.shape["seq"], mesh.shape["fsdp"]) == (2, 16) else body,
        mesh=mesh,
        in_specs=(
            P("fsdp", "seq", None),
            P("fsdp", None),
            P("fsdp", "seq", None),
            P("fsdp", None),
            P("fsdp"),
            P("fsdp"),
            P("fsdp", None),
            P(None, "fsdp"),
            P("fsdp"),
            P("fsdp"),
            P("fsdp", None),
            P(None, "fsdp"),
            P("fsdp"),
            P("fsdp"),
            P("fsdp", None),
            P(None, "fsdp"),
            P("fsdp"),
            P("fsdp"),
            P("fsdp", None),
            P(None, "fsdp"),
        ),
        out_specs=(
            P("fsdp", "seq", None),
            P("fsdp", "seq", None),
            P("fsdp", None),
            P("fsdp"),
            P("fsdp"),
            P("fsdp", None),
            P(None, "fsdp"),
            P("fsdp"),
            P("fsdp"),
            P("fsdp", None),
            P(None, "fsdp"),
            P("fsdp"),
            P("fsdp"),
            P("fsdp", None),
            P(None, "fsdp"),
            P("fsdp"),
            P("fsdp"),
            P("fsdp", None),
            P(None, "fsdp"),
        ),
        check_vma=False,
    )
```

```python
import functools
import math

import jax
import jax.numpy as jnp
from jax import lax
from jax.experimental import pallas as pl
from jax.experimental.pallas import tpu as pltpu
from jax.sharding import PartitionSpec as P


D = 768
HEAD_DIM = 64
PATCH = 8


epsilon = 1e-05


def shifted(block, axis, distance):
    devices = range(lax.axis_size(axis))
    route = [(i - distance, i) for i in devices if i - distance in devices]
    return lax.ppermute(block, axis, route)


def layer_norm(values, norm_gain, norm_bias):
    center = jnp.mean(values, -1, keepdims=True)
    centred = values - center
    spread = jnp.mean(centred * centred, -1, keepdims=True)
    return centred * lax.rsqrt(spread + epsilon) * norm_gain + norm_bias


def smooth_gate(values):
    return jax.nn.gelu(values, approximate=True)


def product(left_side, right_side):
    return jnp.dot(left_side, right_side, preferred_element_type=jnp.float32)


def left_product(left_side, right_side):
    return lax.dot_general(
        left_side, right_side, (((0,), (0,)), ((), ())), preferred_element_type=jnp.float32
    )


def right_product(left_side, right_side):
    return lax.dot_general(
        left_side, right_side, (((1,), (1,)), ((), ())), preferred_element_type=jnp.float32
    )


def attend_forward(queries, key_part, value_part, allowed):
    factor = 1.0 / math.sqrt(HEAD_DIM)
    scores = (
        jnp.einsum("bqhd,bkhd->bhqk", queries, key_part, preferred_element_type=jnp.float32)
        * factor
    )
    scores = jnp.where(allowed[:, None], scores, -1e30)
    highest = jnp.max(scores, -1, keepdims=True)
    log_total = highest + jnp.log(jnp.sum(jnp.exp(scores - highest), -1, keepdims=True))
    rounded = jnp.exp(scores - log_total).astype(jnp.bfloat16)
    mixture = jnp.einsum("bhqk,bkhd->bqhd", rounded, value_part, preferred_element_type=jnp.float32)
    return (mixture, log_total)


def attend_backward(queries, key_part, value_part, allowed, log_total, grad_mixture):
    factor = 1.0 / math.sqrt(HEAD_DIM)
    scores = (
        jnp.einsum("bqhd,bkhd->bhqk", queries, key_part, preferred_element_type=jnp.float32)
        * factor
    )
    scores = jnp.where(allowed[:, None], scores, -1e30)
    chances = jnp.exp(scores - log_total)
    rounded = chances.astype(jnp.bfloat16)
    grad_values = jnp.einsum(
        "bhqk,bqhd->bkhd", rounded, grad_mixture, preferred_element_type=jnp.float32
    )
    grad_chances = jnp.einsum(
        "bqhd,bkhd->bhqk", grad_mixture, value_part, preferred_element_type=jnp.float32
    )
    grad_scores = (
        chances * (grad_chances - jnp.sum(grad_chances * chances, -1, keepdims=True))
    ).astype(jnp.bfloat16)
    grad_queries = (
        jnp.einsum("bhqk,bkhd->bqhd", grad_scores, key_part, preferred_element_type=jnp.float32)
        * factor
    )
    grad_keys = (
        jnp.einsum("bhqk,bqhd->bkhd", grad_scores, queries, preferred_element_type=jnp.float32)
        * factor
    )
    return (grad_queries, grad_keys, grad_values)


def block_forward(inputs, weights, attend):
    first_gain, first_bias, project, output, second_gain, second_bias, expand, narrow = weights
    normed = layer_norm(
        inputs, first_gain.astype(jnp.float32), first_bias.astype(jnp.float32)
    ).astype(jnp.bfloat16)
    triple = product(normed, project).astype(jnp.bfloat16)
    mixture, attend_stored = attend(triple)
    middle = inputs + product(mixture, output)
    second = layer_norm(
        middle, second_gain.astype(jnp.float32), second_bias.astype(jnp.float32)
    ).astype(jnp.bfloat16)
    lifted = product(second, expand)
    hidden = smooth_gate(lifted).astype(jnp.bfloat16)
    result = middle + product(hidden, narrow)
    stored = (inputs, normed, attend_stored, mixture, middle, second, lifted, hidden)
    return (result, stored)


def block_backward(grad_result, weights, stored, attend_back):
    first_gain, first_bias, project, output, second_gain, second_bias, expand, narrow = weights
    inputs, normed, attend_stored, mixture, middle, second, lifted, hidden = stored
    grad_branch = grad_result.astype(jnp.bfloat16)
    grad_narrow = left_product(hidden, grad_branch)
    grad_hidden = right_product(grad_branch, narrow)
    grad_lifted = jax.vjp(smooth_gate, lifted)[1](grad_hidden)[0].astype(jnp.bfloat16)
    grad_expand = left_product(second, grad_lifted)
    grad_second = right_product(grad_lifted, expand)
    pullback = jax.vjp(
        layer_norm, middle, second_gain.astype(jnp.float32), second_bias.astype(jnp.float32)
    )[1]
    grad_middle, grad_gain_two, grad_bias_two = pullback(grad_second)
    grad_middle = grad_middle + grad_result
    grad_attended = grad_middle.astype(jnp.bfloat16)
    grad_output = left_product(mixture, grad_attended)
    grad_mixture = right_product(grad_attended, output).astype(jnp.bfloat16)
    grad_triple = attend_back(grad_mixture, attend_stored)
    grad_project = left_product(normed, grad_triple)
    grad_normed = right_product(grad_triple, project)
    pullback = jax.vjp(
        layer_norm, inputs, first_gain.astype(jnp.float32), first_bias.astype(jnp.float32)
    )[1]
    grad_inputs, grad_gain_one, grad_bias_one = pullback(grad_normed)
    grad_inputs = grad_inputs + grad_middle
    return (
        grad_inputs,
        (
            grad_gain_one,
            grad_bias_one,
            grad_project,
            grad_output,
            grad_gain_two,
            grad_bias_two,
            grad_expand,
            grad_narrow,
        ),
    )


def body(
    byte_inputs,
    segment_ids,
    cotangent,
    patch_weight,
    coarse_first_gain,
    coarse_first_bias,
    coarse_project,
    coarse_output,
    coarse_second_gain,
    coarse_second_bias,
    coarse_expand,
    coarse_narrow,
    fine_first_gain,
    fine_first_bias,
    fine_project,
    fine_output,
    fine_second_gain,
    fine_second_bias,
    fine_expand,
    fine_narrow,
):
    coarse_full = (
        lax.all_gather(patch_weight, "fsdp", axis=0, tiled=True),
        lax.all_gather(coarse_first_gain, "fsdp", axis=0, tiled=True),
        lax.all_gather(coarse_first_bias, "fsdp", axis=0, tiled=True),
        lax.all_gather(coarse_project, "fsdp", axis=0, tiled=True),
        lax.all_gather(coarse_output, "fsdp", axis=1, tiled=True),
        lax.all_gather(coarse_second_gain, "fsdp", axis=0, tiled=True),
        lax.all_gather(coarse_second_bias, "fsdp", axis=0, tiled=True),
        lax.all_gather(coarse_expand, "fsdp", axis=0, tiled=True),
        lax.all_gather(coarse_narrow, "fsdp", axis=1, tiled=True),
    )
    fine_full = (
        lax.all_gather(fine_first_gain, "fsdp", axis=0, tiled=True),
        lax.all_gather(fine_first_bias, "fsdp", axis=0, tiled=True),
        lax.all_gather(fine_project, "fsdp", axis=0, tiled=True),
        lax.all_gather(fine_output, "fsdp", axis=1, tiled=True),
        lax.all_gather(fine_second_gain, "fsdp", axis=0, tiled=True),
        lax.all_gather(fine_second_bias, "fsdp", axis=0, tiled=True),
        lax.all_gather(fine_expand, "fsdp", axis=0, tiled=True),
        lax.all_gather(fine_narrow, "fsdp", axis=1, tiled=True),
    )
    byte_rows = byte_inputs[0]
    bytes_here = byte_rows.shape[0]
    patches = bytes_here // PATCH
    segment_row = segment_ids[0]
    all_patches = segment_row.shape[0]
    places = jnp.arange(all_patches)
    coarse_allowed = (
        (places[:, None] >= places[None, :]) & (segment_row[:, None] == segment_row[None, :])
    )[None]
    inner = jnp.arange(PATCH)
    fine_allowed = (inner[:, None] >= inner[None, :])[None]

    def coarse_attend(triple):
        head_block = lax.all_to_all(
            triple.reshape(patches, 3, D), "seq", split_axis=2, concat_axis=0, tiled=True
        )
        all_rows = head_block.shape[0]
        columns = head_block.shape[2]
        local_heads = columns // HEAD_DIM
        queries = head_block[:, 0].reshape(1, all_rows, local_heads, HEAD_DIM)
        key_part = head_block[:, 1].reshape(1, all_rows, local_heads, HEAD_DIM)
        value_part = head_block[:, 2].reshape(1, all_rows, local_heads, HEAD_DIM)
        mixture, log_total = attend_forward(queries, key_part, value_part, coarse_allowed)
        merged = mixture.reshape(all_rows, columns).astype(jnp.bfloat16)
        back_rows = lax.all_to_all(merged, "seq", split_axis=0, concat_axis=1, tiled=True)
        return (back_rows, (queries, key_part, value_part, log_total))

    def coarse_back(grad_mixture, stored):
        queries, key_part, value_part, log_total = stored
        head_grad = lax.all_to_all(grad_mixture, "seq", split_axis=1, concat_axis=0, tiled=True)
        all_rows = head_grad.shape[0]
        columns = head_grad.shape[1]
        grad_queries, grad_keys, grad_values = attend_backward(
            queries,
            key_part,
            value_part,
            coarse_allowed,
            log_total,
            head_grad.reshape(1, all_rows, columns // HEAD_DIM, HEAD_DIM),
        )
        stacked = jnp.stack(
            [
                grad_queries.reshape(all_rows, columns),
                grad_keys.reshape(all_rows, columns),
                grad_values.reshape(all_rows, columns),
            ],
            1,
        ).astype(jnp.bfloat16)
        back_rows = lax.all_to_all(stacked, "seq", split_axis=0, concat_axis=2, tiled=True)
        return back_rows.reshape(back_rows.shape[0], 3 * D)

    def fine_attend(triple):
        grouped = triple.reshape(patches, PATCH, 3, D // HEAD_DIM, HEAD_DIM)
        queries = grouped[:, :, 0]
        key_part = grouped[:, :, 1]
        value_part = grouped[:, :, 2]
        mixture, log_total = attend_forward(queries, key_part, value_part, fine_allowed)
        return (
            mixture.reshape(bytes_here, D).astype(jnp.bfloat16),
            (queries, key_part, value_part, log_total),
        )

    def fine_back(grad_mixture, stored):
        queries, key_part, value_part, log_total = stored
        grad_queries, grad_keys, grad_values = attend_backward(
            queries,
            key_part,
            value_part,
            fine_allowed,
            log_total,
            grad_mixture.reshape(patches, PATCH, D // HEAD_DIM, HEAD_DIM),
        )
        stacked = jnp.stack([grad_queries, grad_keys, grad_values], 2).astype(jnp.bfloat16)
        return stacked.reshape(bytes_here, 3 * D)

    grouped_bytes = byte_rows.reshape(patches, PATCH * D)
    embedded = product(grouped_bytes, coarse_full[0])
    coarse_out, coarse_stored = block_forward(embedded, coarse_full[1:], coarse_attend)
    coarse_low = coarse_out.astype(jnp.bfloat16)
    arrived = shifted(coarse_low[-1:], "seq", 1)
    offset = lax.axis_index("seq") * patches
    padded = jnp.concatenate([segment_row[:1] - 1, segment_row])
    before = lax.dynamic_slice_in_dim(padded, offset, patches)
    current = lax.dynamic_slice_in_dim(segment_row, offset, patches)
    joined = (before == current).astype(jnp.float32)[:, None]
    previous = jnp.concatenate([arrived, coarse_low[:-1]]).astype(jnp.float32) * joined
    fine_in = (
        byte_rows.astype(jnp.float32).reshape(patches, PATCH, D) + previous[:, None, :]
    ).reshape(bytes_here, D)
    layer_rows, fine_stored = block_forward(fine_in, fine_full, fine_attend)
    fine_weights_back = (
        lax.all_gather(fine_first_gain, "fsdp", axis=0, tiled=True),
        lax.all_gather(fine_first_bias, "fsdp", axis=0, tiled=True),
        lax.all_gather(fine_project, "fsdp", axis=0, tiled=True),
        lax.all_gather(fine_output, "fsdp", axis=1, tiled=True),
        lax.all_gather(fine_second_gain, "fsdp", axis=0, tiled=True),
        lax.all_gather(fine_second_bias, "fsdp", axis=0, tiled=True),
        lax.all_gather(fine_expand, "fsdp", axis=0, tiled=True),
        lax.all_gather(fine_narrow, "fsdp", axis=1, tiled=True),
    )
    grad_fine_in, fine_grads = block_backward(
        cotangent[0].astype(jnp.float32), fine_weights_back, fine_stored, fine_back
    )
    grad_previous = jnp.sum(grad_fine_in.reshape(patches, PATCH, D), 1) * joined
    arrived_back = shifted(grad_previous[:1], "seq", -1)
    grad_coarse_out = jnp.concatenate([grad_previous[1:], arrived_back])
    coarse_weights_back = (
        lax.all_gather(patch_weight, "fsdp", axis=0, tiled=True),
        lax.all_gather(coarse_first_gain, "fsdp", axis=0, tiled=True),
        lax.all_gather(coarse_first_bias, "fsdp", axis=0, tiled=True),
        lax.all_gather(coarse_project, "fsdp", axis=0, tiled=True),
        lax.all_gather(coarse_output, "fsdp", axis=1, tiled=True),
        lax.all_gather(coarse_second_gain, "fsdp", axis=0, tiled=True),
        lax.all_gather(coarse_second_bias, "fsdp", axis=0, tiled=True),
        lax.all_gather(coarse_expand, "fsdp", axis=0, tiled=True),
        lax.all_gather(coarse_narrow, "fsdp", axis=1, tiled=True),
    )
    grad_embedded, coarse_grads = block_backward(
        grad_coarse_out, coarse_weights_back[1:], coarse_stored, coarse_back
    )
    grad_embed_low = grad_embedded.astype(jnp.bfloat16)
    grad_patch = left_product(grouped_bytes, grad_embed_low)
    grad_grouped = right_product(grad_embed_low, coarse_weights_back[0])
    input_gradient = (grad_fine_in + grad_grouped.reshape(bytes_here, D)).astype(jnp.bfloat16)
    shards = (
        lax.psum_scatter(grad_patch, "fsdp", scatter_dimension=0, tiled=True),
        lax.psum_scatter(coarse_grads[0], "fsdp", scatter_dimension=0, tiled=True),
        lax.psum_scatter(coarse_grads[1], "fsdp", scatter_dimension=0, tiled=True),
        lax.psum_scatter(coarse_grads[2], "fsdp", scatter_dimension=0, tiled=True),
        lax.psum_scatter(coarse_grads[3], "fsdp", scatter_dimension=1, tiled=True),
        lax.psum_scatter(coarse_grads[4], "fsdp", scatter_dimension=0, tiled=True),
        lax.psum_scatter(coarse_grads[5], "fsdp", scatter_dimension=0, tiled=True),
        lax.psum_scatter(coarse_grads[6], "fsdp", scatter_dimension=0, tiled=True),
        lax.psum_scatter(coarse_grads[7], "fsdp", scatter_dimension=1, tiled=True),
        lax.psum_scatter(fine_grads[0], "fsdp", scatter_dimension=0, tiled=True),
        lax.psum_scatter(fine_grads[1], "fsdp", scatter_dimension=0, tiled=True),
        lax.psum_scatter(fine_grads[2], "fsdp", scatter_dimension=0, tiled=True),
        lax.psum_scatter(fine_grads[3], "fsdp", scatter_dimension=1, tiled=True),
        lax.psum_scatter(fine_grads[4], "fsdp", scatter_dimension=0, tiled=True),
        lax.psum_scatter(fine_grads[5], "fsdp", scatter_dimension=0, tiled=True),
        lax.psum_scatter(fine_grads[6], "fsdp", scatter_dimension=0, tiled=True),
        lax.psum_scatter(fine_grads[7], "fsdp", scatter_dimension=1, tiled=True),
    )
    totals = (
        lax.psum(shards[0].astype(jnp.bfloat16), "seq").astype(jnp.float32),
        lax.psum(shards[1].astype(jnp.bfloat16), "seq").astype(jnp.float32),
        lax.psum(shards[2].astype(jnp.bfloat16), "seq").astype(jnp.float32),
        lax.psum(shards[3].astype(jnp.bfloat16), "seq").astype(jnp.float32),
        lax.psum(shards[4].astype(jnp.bfloat16), "seq").astype(jnp.float32),
        lax.psum(shards[5].astype(jnp.bfloat16), "seq").astype(jnp.float32),
        lax.psum(shards[6].astype(jnp.bfloat16), "seq").astype(jnp.float32),
        lax.psum(shards[7].astype(jnp.bfloat16), "seq").astype(jnp.float32),
        lax.psum(shards[8].astype(jnp.bfloat16), "seq").astype(jnp.float32),
        lax.psum(shards[9].astype(jnp.bfloat16), "seq").astype(jnp.float32),
        lax.psum(shards[10].astype(jnp.bfloat16), "seq").astype(jnp.float32),
        lax.psum(shards[11].astype(jnp.bfloat16), "seq").astype(jnp.float32),
        lax.psum(shards[12].astype(jnp.bfloat16), "seq").astype(jnp.float32),
        lax.psum(shards[13].astype(jnp.bfloat16), "seq").astype(jnp.float32),
        lax.psum(shards[14].astype(jnp.bfloat16), "seq").astype(jnp.float32),
        lax.psum(shards[15].astype(jnp.bfloat16), "seq").astype(jnp.float32),
        lax.psum(shards[16].astype(jnp.bfloat16), "seq").astype(jnp.float32),
    )
    layer_output = layer_rows.astype(jnp.bfloat16)[None]
    return (
        layer_output,
        input_gradient[None],
        totals[0],
        totals[1],
        totals[2],
        totals[3],
        totals[4],
        totals[5],
        totals[6],
        totals[7],
        totals[8],
        totals[9],
        totals[10],
        totals[11],
        totals[12],
        totals[13],
        totals[14],
        totals[15],
        totals[16],
    )


MESH = pl.DeviceIdType.MESH
HBM = pltpu.MemorySpace.HBM
VMEM = pltpu.MemorySpace.VMEM


class Place:
    def __init__(self):
        self.core = lax.axis_index("seq")
        self.at = lax.axis_index("fsdp")
        self.z = self.at // 4
        self.plane = self.at % 4
        self.near = 1 + self.core
        self.far = 2 - self.core

    def flip(self, mask):
        return self.at ^ mask

    def across(self, mask):
        return (self.core, self.at ^ mask)

    def partner(self):
        return (1 - self.core, self.at)


def enter(place, masks, partner=True):
    barrier = pltpu.get_barrier_semaphore()
    for mask in masks:
        pl.semaphore_signal(barrier, inc=1, device_id=place.across(mask), device_id_type=MESH)
    if partner:
        pl.semaphore_signal(barrier, inc=1, device_id=place.partner(), device_id_type=MESH)
    pl.semaphore_wait(barrier, len(masks) + (1 if partner else 0))


MASKS = (1, 2, 4, 8, 12)


class Gather:
    EVENTS = 12

    def __init__(self, place, source, buffer, rows, first, column, width, z_first, sends, receives, local):
        self.p, self.source, self.buffer, self.rows, self.first = place, source, buffer, rows, first
        self.z_first, self.sends, self.receives, self.local = z_first, sends, receives, local
        self.half = width // 2
        self.column, self.width = column, width
        self.mine = pl.ds(pl.multiple_of(column + place.core * self.half, 128), self.half)
        self.theirs = pl.ds(pl.multiple_of(column + (1 - place.core) * self.half, 128), self.half)
        self.started = []

    def group(self, plane, columns=None):
        return self.buffer.at[:, plane, self.rows, self.mine if columns is None else columns]

    def block(self, z, plane):
        return self.buffer.at[z, plane, self.rows, self.mine]

    def send(self, event, view, device, source=None):
        copy = pltpu.make_async_remote_copy(
            src_ref=view if source is None else source,
            dst_ref=view,
            send_sem=self.sends.at[event],
            recv_sem=self.receives.at[event],
            device_id=device,
            device_id_type=MESH,
        )
        copy.start()
        self.started.append(copy)

    def arrived(self, event, view):
        pltpu.make_async_remote_copy(
            src_ref=view,
            dst_ref=view,
            send_sem=self.sends.at[event],
            recv_sem=self.receives.at[event],
            device_id=self.p.partner(),
            device_id_type=MESH,
        ).wait_recv()

    def start(self):
        p = self.p
        own = self.source.at[self.rows, pl.ds(pl.multiple_of(self.first + p.core * self.half, 128), self.half)]
        self.copy = pltpu.make_async_copy(own, self.block(p.z, p.plane), self.local)
        self.copy.start()
        if not self.z_first:
            self.send(6, self.block(p.z, p.plane), p.across(p.near), own)
        for j in (1, 2, 3):
            self.send(j - 1, self.block(p.z, p.plane), p.across(4 * j), own)

    def one(self):
        p = self.p
        self.copy.wait()
        if self.z_first:
            for j in (1, 2, 3):
                self.arrived(j - 1, self.block(p.z ^ j, p.plane))
            self.send(6, self.group(p.plane), p.across(p.near))
            self.send(7, self.group(p.plane), p.across(p.far))
            self.send(9, self.group(p.plane), p.partner())
        else:
            self.arrived(6, self.block(p.z, p.plane ^ p.near))
            for j in (1, 2, 3):
                self.send(2 + j, self.block(p.z, p.plane ^ p.near), p.across(4 * j))

    def two(self):
        p = self.p
        if self.z_first:
            self.arrived(6, self.group(p.plane ^ p.near))
        else:
            for j in (1, 2, 3):
                self.arrived(j - 1, self.block(p.z ^ j, p.plane))
            self.send(7, self.group(p.plane), p.across(p.far))
            self.send(9, self.group(p.plane), p.partner())
            for j in (1, 2, 3):
                self.arrived(2 + j, self.block(p.z ^ j, p.plane ^ p.near))
        self.send(8, self.group(p.plane ^ p.near), p.across(p.far))
        self.send(10, self.group(p.plane ^ p.near), p.partner())

    def three(self):
        p = self.p
        self.arrived(7, self.group(p.plane ^ p.far))
        self.send(11, self.group(p.plane ^ p.far), p.partner())
        self.arrived(8, self.group(p.plane ^ 3))
        self.send(12, self.group(p.plane ^ 3), p.partner())

    def four(self):
        p = self.p
        self.arrived(9, self.group(p.plane, self.theirs))
        self.arrived(10, self.group(p.plane ^ p.far, self.theirs))
        self.arrived(11, self.group(p.plane ^ p.near, self.theirs))
        self.arrived(12, self.group(p.plane ^ 3, self.theirs))

    def drain(self):
        for copy in self.started:
            copy.wait_send()


def run_gathers(gathers, ahead, tick):
    n = len(gathers)
    for k in range(min(ahead, n)):
        gathers[k].start()
    for t in range(n + 3):
        if t < n:
            gathers[t].one()
            if t + ahead < n:
                gathers[t + ahead].start()
        if 0 <= t - 1 < n:
            gathers[t - 1].two()
        if 0 <= t - 2 < n:
            gathers[t - 2].three()
        if 0 <= t - 3 < n:
            gathers[t - 3].four()
        tick(t)
    for g in gathers:
        g.drain()


class PatchForward:
    def __init__(self, small, rows, patch, w, segments, outs):
        self.small, self.rows, self.patch, self.w, self.segments = small, rows, patch, w, segments
        self.embedded, self.normed, self.triple, self.chances, self.mixture = outs[:5]
        self.middle, self.second, self.lifted, self.hidden, self.result = outs[5:]

    def weight(self, column, width):
        return self.w[:, :, :, column : column + width].reshape(D, width)

    def embed(self, first):
        def step(z, _):
            columns = pl.ds(pl.multiple_of(z * 2 * D, 128), 2 * D)
            rows = self.rows[:, :, columns].reshape(self.embedded.shape[0], 2 * D)
            term = product(rows, self.patch[z].reshape(2 * D, D))
            self.embedded[...] += term
            return 0

        if first == 0:
            self.embedded[...] = jnp.zeros_like(self.embedded)
        lax.fori_loop(first, first + 2, step, 0)

    def project(self):
        unit, _ = normalize(self.embedded[...])
        self.normed[...] = (unit * self.small[0:1] + self.small[1:2]).astype(jnp.bfloat16)
        self.triple[...] = product(self.normed[...], self.weight(0, 3 * D)).astype(jnp.bfloat16)

    def attend(self, first):
        count = self.triple.shape[0]
        row = lax.broadcasted_iota(jnp.int32, (count, count), 0)
        column = lax.broadcasted_iota(jnp.int32, (count, count), 1)
        allowed = (column <= row) & (self.segments[1][...] == self.segments[0][...])

        def step(pair, _):
            lanes = [pl.ds(pl.multiple_of(i * D + pair * 128, 128), 128) for i in range(3)]
            queries = head_lanes(self.triple[:, lanes[0]])
            keys = self.triple[:, lanes[1]]
            values = head_lanes(self.triple[:, lanes[2]])
            mixed = None
            for head in range(2):
                found = chances_of(queries[head], keys, allowed)
                self.chances[pair * 2 + head] = found
                term = product(found.astype(jnp.bfloat16), values[head])
                mixed = term if mixed is None else mixed + term
            self.mixture[:, lanes[0]] = mixed.astype(jnp.bfloat16)
            return 0

        lax.fori_loop(first, first + 3, step, 0)

    def join(self):
        middle = self.embedded[...] + right_product(self.mixture[...], self.weight(3 * D, D))
        self.middle[...] = middle
        self.result[...] = middle
        unit, _ = normalize(middle)
        self.second[...] = (unit * self.small[2:3] + self.small[3:4]).astype(jnp.bfloat16)

    def lift(self, half):
        here = slice(half * 2 * D, half * 2 * D + 2 * D)
        lifted = product(self.second[...], self.weight(4 * D + half * 2 * D, 2 * D))
        self.lifted[:, here] = lifted
        self.hidden[:, here] = smooth_gate(lifted).astype(jnp.bfloat16)

    def lower(self, half):
        here = slice(half * 2 * D, half * 2 * D + 2 * D)
        self.result[...] += right_product(self.hidden[:, here], self.weight(8 * D + half * 2 * D, 2 * D))


def gather_kernel(plan, ahead, *refs):
    sources, small, rows, segments, rest = refs[:9], refs[9], refs[10], refs[11:13], refs[13:]
    buffers, small_out, all_rows, patch_outs, rest = rest[:3], rest[3], rest[4], rest[5:15], rest[15:]
    sends, receives, local, value, arriving, small_sends, small_receives, row_sems, patch, w, loads = rest
    place = Place()
    enter(place, MASKS)
    value[0] = small[...]
    total = Total(place, (1, 2, 4, 8), value, arriving, small_sends, small_receives, small_out)
    stay = pltpu.make_async_copy(rows, all_rows.at[place.core], row_sems.at[0])
    stay.start()
    cross = pltpu.make_async_remote_copy(
        src_ref=rows, dst_ref=all_rows.at[place.core], send_sem=row_sems.at[1], recv_sem=row_sems.at[2],
        device_id=place.partner(), device_id_type=MESH,
    )
    cross.start()
    gathers = []
    for k, (source, buffer, first, rows_here, start, column, width, z_first) in enumerate(plan):
        gathers.append(
            Gather(place, sources[source], buffers[buffer], pl.ds(first, rows_here), start, column, width, z_first,
                   sends.at[k], receives.at[k], local.at[k])
        )
    forward = PatchForward(small_out, all_rows, patch, w, segments, patch_outs)
    waiting = []
    patches = sum(p[1] == 0 for p in plan)
    held = sum(p[1] < 2 for p in plan)

    def fetched():
        while waiting:
            waiting.pop().wait()

    def rows_there():
        stay.wait()
        cross.wait()

    base = patches + 4
    pieces = {
        base: (rows_there, fetched, functools.partial(forward.embed, 0)),
        base + 1: (functools.partial(forward.embed, 2),),
        base + 2: (fetched, forward.project),
        base + 3: (functools.partial(forward.attend, 0),),
        base + 4: (functools.partial(forward.attend, 3),),
        base + 5: (fetched, forward.join),
        base + 6: (functools.partial(forward.lift, 0),),
        base + 7: (functools.partial(forward.lift, 1),),
        base + 8: (fetched, functools.partial(forward.lower, 0)),
        base + 9: (functools.partial(forward.lower, 1),),
    }

    def tick(t):
        total.advance()
        for piece in pieces.get(t, ()):
            piece()
        k = t - 3
        if 0 <= k < held:
            _, buffer, first, count, _, column, width, _ = plan[k]
            part = (slice(None), slice(None), pl.ds(first, count), pl.ds(column, width))
            copy = pltpu.make_async_copy(buffers[buffer].at[part], (patch, w)[buffer].at[part], loads.at[k])
            copy.start()
            waiting.append(copy)

    run_gathers(gathers, ahead, tick)


def forward_plan(step=1536, patch_rows=96):
    plan = []
    for first in range(0, 384, patch_rows):
        plan.append((0, 0, first, patch_rows, 0, 0, 768))
    for block in (1, 2):
        column = 0
        for i, width in enumerate((2304, 768, 3072, 3072)):
            for start in range(0, width, step):
                plan.append((4 * block - 3 + i, block, 0, 48, start, column + start, min(step, width - start)))
            column += width
    return tuple(p + (i % 5 != 4,) for i, p in enumerate(plan))


PLAN = forward_plan()


def gather_all(sources, small, rows, segments, ahead=3, plan=PLAN):
    n = len(plan)
    bf, f32 = jnp.bfloat16, jnp.float32
    count = 2 * rows.shape[0]
    outs = [((8, D), f32), ((2,) + rows.shape, bf), ((count, D), f32), ((count, D), bf), ((count, 3 * D), bf),
            ((D // HEAD_DIM, count, count), f32), ((count, D), bf), ((count, D), f32), ((count, D), bf), ((count, 4 * D), f32),
            ((count, 4 * D), bf), ((count, D), f32)]
    shapes = ((4, 4, 384, D), (4, 4, 48, 12 * D))
    return pl.pallas_call(
        functools.partial(gather_kernel, plan, ahead),
        out_shape=[jax.ShapeDtypeStruct(shape, bf) for shape in shapes + shapes[1:]]
        + [jax.ShapeDtypeStruct(*out) for out in outs],
        in_specs=[pl.BlockSpec(memory_space=VMEM)] * 10 + [pl.BlockSpec(memory_space=HBM)] + [pl.BlockSpec(memory_space=VMEM)] * 2,
        out_specs=[pl.BlockSpec(memory_space=HBM)] * 3 + [pl.BlockSpec(memory_space=VMEM)] * len(outs),
        scratch_shapes=[
            pltpu.SemaphoreType.DMA((n, 13)),
            pltpu.SemaphoreType.DMA((n, 13)),
            pltpu.SemaphoreType.DMA((n,)),
            pltpu.VMEM((5, 8, 768), jnp.float32),
            pltpu.VMEM((4, 8, 768), jnp.float32),
            pltpu.SemaphoreType.DMA((4,)),
            pltpu.SemaphoreType.DMA((4,)),
            pltpu.SemaphoreType.DMA((3,)),
            pltpu.VMEM(shapes[0], bf),
            pltpu.VMEM(shapes[1], bf),
            pltpu.SemaphoreType.DMA((n,)),
        ],
        compiler_params=pltpu.CompilerParams(collective_id=0, has_side_effects=True, vmem_limit_bytes=64_000_000),
        name="gather_all",
    )(*sources, small, rows, *segments)


class Total:
    def __init__(self, place, masks, value, arriving, sends, receives, result):
        self.p, self.masks, self.value, self.arriving = place, masks, value, arriving
        self.sends, self.receives, self.result = sends, receives, result
        self.step, self.copy = 0, None

    def advance(self):
        if self.step > len(self.masks):
            return
        if self.copy is not None:
            self.copy.wait()
            i = self.step - 1
            self.value[i + 1] = self.value[i] + self.arriving[i]
        if self.step < len(self.masks):
            i = self.step
            mask = self.masks[i]
            self.copy = pltpu.make_async_remote_copy(
                src_ref=self.value.at[i],
                dst_ref=self.arriving.at[i],
                send_sem=self.sends.at[i],
                recv_sem=self.receives.at[i],
                device_id=self.p.across(mask) if mask else self.p.partner(),
                device_id_type=MESH,
            )
            self.copy.start()
        else:
            self.result[...] = self.value[len(self.masks)]
        self.step += 1


def add(left, right):
    return left.astype(jnp.float32) + right.astype(jnp.float32)


class Reduce:
    def __init__(self, place, held, paired, far, near, line, out, rows, column, width, z_last, sends, receives):
        self.p, self.held, self.from_partner, self.from_far = place, held, paired, far
        self.from_near, self.from_line, self.out, self.rows = near, line, out, rows
        self.z_last, self.sends, self.receives = z_last, sends, receives
        self.half = width // 2
        whole = out.shape[1] // 2
        self.own = pl.ds(column // 2, self.half)
        self.mine = pl.ds(pl.multiple_of(column // 2 + place.core * whole, 128), self.half)
        self.theirs = pl.ds(pl.multiple_of(column // 2 + (1 - place.core) * whole, 128), self.half)
        self.started = []

    def send(self, event, source, target, device):
        copy = pltpu.make_async_remote_copy(
            src_ref=source, dst_ref=target, send_sem=self.sends.at[event], recv_sem=self.receives.at[event],
            device_id=device, device_id_type=MESH,
        )
        copy.start()
        self.started.append(copy)

    def arrived(self, event, target):
        pltpu.make_async_remote_copy(
            src_ref=target, dst_ref=target, send_sem=self.sends.at[event], recv_sem=self.receives.at[event],
            device_id=self.p.partner(), device_id_type=MESH,
        ).wait_recv()

    def pair(self, theirs):
        self.send(0, theirs, self.from_partner, self.p.partner())
        self.paired = self.started.pop()

    def fold(self, plane, others):
        def step(z, _):
            self.held[z, plane] = add(self.held[z, plane], others[z]).astype(jnp.bfloat16)
            return 0

        lax.fori_loop(0, 4, step, 0)

    def one(self):
        p = self.p
        if self.from_partner is not None:
            self.arrived(0, self.from_partner)
            self.fold(p.plane ^ p.far, self.from_partner.at[:, p.plane ^ p.far])
        self.send(1, self.held.at[:, p.plane ^ p.far], self.from_far.at[0], p.across(p.far))
        if self.from_partner is not None:
            self.fold(p.plane ^ 3, self.from_partner.at[:, p.plane ^ 3])
        self.send(2, self.held.at[:, p.plane ^ 3], self.from_far.at[1], p.across(p.far))
        if self.from_partner is not None:
            self.fold(p.plane, self.from_partner.at[:, p.plane])
            self.fold(p.plane ^ p.near, self.from_partner.at[:, p.plane ^ p.near])

    def two(self):
        p = self.p
        self.arrived(2, self.from_far.at[1])
        self.fold(p.plane ^ p.near, self.from_far.at[1])
        if self.z_last:
            self.send(3, self.held.at[:, p.plane ^ p.near], self.from_near, p.across(p.near))
        else:
            for j in (1, 2, 3):
                self.send(6 + j, self.held.at[p.z ^ j, p.plane ^ p.near], self.from_line.at[2 + j], p.across(4 * j))
        self.arrived(1, self.from_far.at[0])
        self.fold(p.plane, self.from_far.at[0])
        if not self.z_last:
            for j in (1, 2, 3):
                self.send(3 + j, self.held.at[p.z ^ j, p.plane], self.from_line.at[j - 1], p.across(4 * j))

    def three(self):
        p = self.p
        if self.z_last:
            self.arrived(3, self.from_near)
            self.fold(p.plane, self.from_near)
            for j in (1, 2, 3):
                self.send(3 + j, self.held.at[p.z ^ j, p.plane], self.from_line.at[j - 1], p.across(4 * j))
        else:
            for j in (1, 2, 3):
                self.arrived(6 + j, self.from_line.at[2 + j])
            near = (add(self.held[p.z, p.plane ^ p.near], self.from_line[3]) + add(self.from_line[4], self.from_line[5]))
            self.held[p.z, p.plane ^ p.near] = near.astype(jnp.bfloat16)
            self.send(3, self.held.at[p.z, p.plane ^ p.near], self.from_near.at[0], p.across(p.near))

    def four(self):
        p = self.p
        for j in (1, 2, 3):
            self.arrived(3 + j, self.from_line.at[j - 1])
        total = add(self.held[p.z, p.plane], self.from_line[0]) + add(self.from_line[1], self.from_line[2])
        if not self.z_last:
            self.arrived(3, self.from_near.at[0])
            total = total + self.from_near[0].astype(jnp.float32)
        self.out[self.rows, self.mine] = total
        view = self.out.at[self.rows, self.mine]
        self.send(10, view, view, p.partner())

    def drain(self):
        for copy in self.started:
            copy.wait_send()
        self.started = []

    def five(self):
        self.arrived(10, self.out.at[self.rows, self.theirs])


def backward_plan(step=1536, patch_rows=96):
    plan = []
    for array, width in ((6, 768), (8, 3072), (7, 3072), (5, 2304), (4, 3072), (3, 3072), (2, 768), (1, 2304)):
        for start in range(0, width, step):
            plan.append((array, 0, 48, start, min(step, width - start)))
    for first in range(0, 384, patch_rows):
        plan.append((0, first, patch_rows, 0, 768))
    return tuple(p + (i % 5 != 4,) for i, p in enumerate(plan))


BACK_PLAN = backward_plan()
SLOTS = 8
LAGS = (2, 3, 4, 5)
ARRAYS = 9


def reduce_kernel(plan, patch, lefts, rights, small, outs, small_out, slots, pairs, fars, nears, lines, staging, left_held,
                  right_held, sends, receives, loads, left_sems, right_sems, value, arriving, small_sends, small_receives):
    place = Place()
    enter(place, MASKS)
    n = len(plan)
    value[0] = small[...]
    total = Total(place, (0, 1, 2, 4, 8), value, arriving, small_sends, small_receives, small_out)
    used = [0, 0]
    reduces, copies, staged, steps, order = [], {}, [], [], []
    for k, (array, first, rows, column, width, z_last) in enumerate(plan):
        kind = 0 if array == 0 else 1
        slot = used[kind] % SLOTS
        used[kind] += 1
        half = width // 2
        cut = (lambda ref, half=half: ref if half == ref.shape[-1] else ref.at[..., pl.ds(0, half)])
        r = Reduce(place, cut(slots[kind].at[slot]), cut(pairs.at[used[kind] - 1]) if array > 4 else None, cut(fars[kind].at[used[kind] - 1]),
                   cut(nears[kind].at[used[kind] - 1]), cut(lines[kind].at[used[kind] - 1]), outs[array],
                   pl.ds(first, rows), column, width, z_last, sends.at[k], receives.at[k])
        r.staging = cut(staging.at[(used[kind] - 1) % 2])
        r.paired = None
        reduces.append(r)
        if array > 4:
            steps.append((k, r.theirs))
        if array:
            steps.append((k, r.mine))
            if array not in order:
                order.append(array)

    def left_view(index):
        return left_held.at[index % 2, pl.ds(0, lefts[order[index] - 1].shape[0])]

    def left_copy(index):
        return pltpu.make_async_copy(lefts[order[index] - 1], left_view(index), left_sems.at[index % 2])

    def right_view(index):
        k = steps[index][0]
        return right_held.at[index % 3, pl.ds(0, rights[plan[k][0] - 1].shape[0]), pl.ds(0, reduces[k].half)]

    def right_copy(index):
        k, columns = steps[index]
        return pltpu.make_async_copy(rights[plan[k][0] - 1].at[:, columns], right_view(index), right_sems.at[index % 3])

    done, begun = [0], [0]

    def make(target, k):
        index = done[0]
        if plan[k][0] != order[begun[0] - 1] or begun[0] == 0:
            left_copy(begun[0]).wait()
            begun[0] += 1
            if begun[0] < len(order):
                left_copy(begun[0]).start()
        left, right = left_view(begun[0] - 1), right_view(index)
        right_copy(index).wait()
        rows = D // 2

        def part(i, _):
            columns = pl.ds(pl.multiple_of(i * rows, 128), rows)
            term = left_product(left[:, columns], right[...]).astype(jnp.bfloat16)
            target[pl.ds(i * 2, 2)] = term.reshape((2,) + target.shape[1:])
            return 0

        lax.fori_loop(0, 2, part, 0)
        done[0] += 1
        if index + 3 < len(steps):
            right_copy(index + 3).start()

    left_copy(0).start()
    for index in range(3):
        right_copy(index).start()

    def load(k):
        array = plan[k][0]
        r = reduces[k]
        if k - SLOTS >= 0:
            reduces[k - SLOTS].drain()
        if array == 0:
            copies[k] = pltpu.make_async_copy(patch.at[:, :, r.rows, r.own], r.held, loads.at[k])
            copies[k].start()
            return
        if array > 4:
            if len(staged) > 1:
                staged[-2].paired.wait_send()
            make(r.staging, k)
            r.pair(r.staging)
            staged.append(r)
        make(r.held, k)

    load(0)
    for t in range(n + LAGS[-1]):
        if t + 1 < n:
            load(t + 1)
        if t < n:
            if t in copies:
                copies[t].wait()
            reduces[t].one()
        for lag, name in zip(LAGS, ("two", "three", "four", "five")):
            if 0 <= t - lag < n:
                getattr(reduces[t - lag], name)()
        total.advance()
    for r in reduces:
        r.drain()
    for r in staged[-2:]:
        r.paired.wait_send()


def reduce_all(patch, terms, small, plan=BACK_PLAN):
    n = len(plan)
    bf = jnp.bfloat16
    counts = [sum(p[0] == 0 for p in plan), sum(p[0] > 0 for p in plan), sum(p[0] > 4 for p in plan)]
    shapes = tuple((max(p[2] for p in plan if c(p[0])), max(p[4] for p in plan if c(p[0])) // 2) for c in (lambda a: a == 0, lambda a: a > 0))

    inputs = 2 * ARRAYS

    def kernel(*refs):
        patch, lefts, rights, small = refs[0], refs[1:ARRAYS], refs[ARRAYS : inputs - 1], refs[inputs - 1]
        outs, small_out = refs[inputs : inputs + ARRAYS], refs[inputs + ARRAYS]
        pairs, rest = refs[inputs + ARRAYS + 1], refs[inputs + ARRAYS + 2 :]
        slots, fars, nears, lines = (rest[2 * i : 2 * i + 2] for i in range(4))
        reduce_kernel(plan, patch, lefts, rights, small, outs, small_out, slots, pairs, fars, nears, lines, *rest[8:])

    scratch = [pltpu.VMEM((counts[2], 4, 4) + shapes[1], bf)]
    scratch += [pltpu.VMEM((min(SLOTS, counts[i]), 4, 4) + shapes[i], bf) for i in (0, 1)]
    for lead in ((2, 4), (4,), (6,)):
        scratch += [pltpu.VMEM((counts[i],) + lead + shapes[i], bf) for i in (0, 1)]
    depth = max(left.shape[0] for left, _ in terms)
    scratch += [
        pltpu.VMEM((2, 4, 4) + shapes[1], bf),
        pltpu.VMEM((2, depth, D), bf),
        pltpu.VMEM((3, depth, shapes[1][1]), bf),
        pltpu.SemaphoreType.DMA((n, 11)),
        pltpu.SemaphoreType.DMA((n, 11)),
        pltpu.SemaphoreType.DMA((n,)),
        pltpu.SemaphoreType.DMA((2,)),
        pltpu.SemaphoreType.DMA((3,)),
        pltpu.VMEM((6, 8, 768), jnp.float32),
        pltpu.VMEM((5, 8, 768), jnp.float32),
        pltpu.SemaphoreType.DMA((5,)),
        pltpu.SemaphoreType.DMA((5,)),
    ]
    patch = patch.reshape(4, 4, patch.shape[0] // 16, patch.shape[1])
    outs = [(patch.shape[2], 2 * patch.shape[3])] + [(left.shape[1] // 16, right.shape[1]) for left, right in terms] + [(8, 768)]
    return pl.pallas_call(
        kernel,
        out_shape=[jax.ShapeDtypeStruct(out, jnp.float32) for out in outs],
        in_specs=[pl.BlockSpec(memory_space=HBM)] * (inputs - 1) + [pl.BlockSpec(memory_space=VMEM)],
        out_specs=[pl.BlockSpec(memory_space=VMEM)] * (ARRAYS + 1),
        scratch_shapes=scratch,
        compiler_params=pltpu.CompilerParams(collective_id=1, has_side_effects=True, vmem_limit_bytes=67_000_000),
        name="reduce_all",
    )(patch, *[left for left, _ in terms], *[right for _, right in terms], small)


def fast_body(byte_inputs, segment_ids, cotangent, patch_weight, *weights):
    coarse, fine = weights[:8], weights[8:]
    core, at = lax.axis_index("seq"), lax.axis_index("fsdp")
    vectors = jnp.stack([w[i] for w in (coarse, fine) for i in (0, 1, 4, 5)]).astype(jnp.float32)
    small = lax.dynamic_update_slice(jnp.zeros((8, D), jnp.float32), vectors, (0, at * vectors.shape[1]))
    sources = [patch_weight]
    for w in (coarse, fine):
        sources += [w[2], w[3].T, w[6], w[7].T]
    byte_rows = byte_inputs[0]
    bytes_here = byte_rows.shape[0]
    patches = bytes_here // PATCH
    segment_row = segment_ids[0]
    all_patches = segment_row.shape[0]
    patch_full, coarse_full, fine_full, small, all_rows, *stored, coarse_out = gather_all(
        sources, small, byte_rows.reshape(patches, PATCH * D), (segment_row[None], segment_row[:, None])
    )
    patch_full = patch_full.reshape(-1, D)

    def unpack(full, first):
        full = full.reshape(D, -1)
        return (small[first], small[first + 1], full[:, : 3 * D], full[:, 3 * D : 4 * D], small[first + 2], small[first + 3],
                full[:, 4 * D : 8 * D], full[:, 8 * D :])

    def mine(values):
        width = values.shape[1] // 2
        return lax.dynamic_slice_in_dim(values, core * width, width, 1)

    def coarse_back(grad_mixture, stored):
        triple, chances = stored
        parts = triple.reshape(1, all_patches, 3, D // HEAD_DIM, HEAD_DIM)
        grads = attend_backward_known(
            parts[:, :, 0], parts[:, :, 1], parts[:, :, 2], chances[None],
            grad_mixture.reshape(1, all_patches, D // HEAD_DIM, HEAD_DIM),
        )
        return jnp.stack(grads, 2).astype(jnp.bfloat16).reshape(all_patches, 3 * D)

    coarse_w = unpack(coarse_full, 0)
    coarse_stored = tuple(stored[:2]) + (tuple(stored[2:4]),) + tuple(stored[4:])
    grouped_bytes = all_rows.reshape(all_patches, PATCH * D)
    coarse_low = coarse_out.astype(jnp.bfloat16)
    joined = jnp.concatenate([jnp.zeros((1,), bool), segment_row[1:] == segment_row[:-1]]).astype(jnp.float32)[:, None]
    previous = jnp.concatenate([jnp.zeros((1, D), jnp.bfloat16), coarse_low[:-1]]).astype(jnp.float32) * joined
    previous = lax.dynamic_slice_in_dim(previous, core * patches, patches)
    (layer_rows, grad_fine_in, grad_previous, fine_vectors, normed, mixture, second, hidden, grad_middle, grad_lifted,
     grad_triple) = fine_block(byte_rows, previous, cotangent[0], small, fine_full.reshape(D, -1))
    fine_terms = [(normed, grad_triple), (grad_middle, mixture), (second, grad_lifted), (cotangent[0], hidden)]
    grad_previous = lax.all_gather(grad_previous, "seq", axis=0, tiled=True) * joined
    grad_coarse_out = jnp.concatenate([grad_previous[1:], jnp.zeros((1, D), jnp.float32)])
    grad_embedded, coarse_vectors, coarse_terms = block_backward_t(grad_coarse_out, coarse_w, coarse_stored, coarse_back)
    grad_embed_low = grad_embedded.astype(jnp.bfloat16)
    grad_patch = left_product(grouped_bytes, mine(grad_embed_low)).astype(jnp.bfloat16)
    grad_here = lax.dynamic_slice_in_dim(grad_embed_low, core * patches, patches)
    grad_grouped = right_product(grad_here, patch_full)
    input_gradient = (grad_fine_in + grad_grouped.reshape(bytes_here, D)).astype(jnp.bfloat16)
    once = (core == 0).astype(jnp.float32)
    small = jnp.concatenate([jnp.stack(coarse_vectors) * once, fine_vectors[4:]])
    *shards, small = reduce_all(grad_patch, coarse_terms + fine_terms, small)
    small = lax.dynamic_slice_in_dim(small, at * vectors.shape[1], vectors.shape[1], 1)

    def gradients(parts, first):
        return (small[first], small[first + 1], parts[0], parts[1].T, small[first + 2], small[first + 3], parts[2], parts[3].T)

    return (layer_rows[None], input_gradient[None], shards[0]) + gradients(shards[1:5], 0) + gradients(shards[5:], 4)


def attend_backward_known(queries, key_part, value_part, chances, grad_mixture):
    factor = 1.0 / math.sqrt(HEAD_DIM)
    grad_values = jnp.einsum(
        "bhqk,bqhd->bkhd", chances.astype(jnp.bfloat16), grad_mixture, preferred_element_type=jnp.float32
    )
    grad_chances = jnp.einsum(
        "bqhd,bkhd->bhqk", grad_mixture, value_part, preferred_element_type=jnp.float32
    )
    grad_scores = (
        chances * (grad_chances - jnp.sum(grad_chances * chances, -1, keepdims=True))
    ).astype(jnp.bfloat16)
    grad_queries = (
        jnp.einsum("bhqk,bkhd->bqhd", grad_scores, key_part, preferred_element_type=jnp.float32)
        * factor
    )
    grad_keys = (
        jnp.einsum("bhqk,bqhd->bkhd", grad_scores, queries, preferred_element_type=jnp.float32)
        * factor
    )
    return (grad_queries, grad_keys, grad_values)


def block_backward_t(grad_result, weights, stored, attend_back):
    first_gain, first_bias, project, output_t, second_gain, second_bias, expand, narrow_t = weights
    inputs, normed, attend_stored, mixture, middle, second, lifted, hidden = stored
    grad_branch = grad_result.astype(jnp.bfloat16)
    grad_hidden = product(grad_branch, narrow_t)
    grad_lifted = jax.vjp(smooth_gate, lifted)[1](grad_hidden)[0].astype(jnp.bfloat16)
    grad_second = right_product(grad_lifted, expand)
    pullback = jax.vjp(layer_norm, middle, second_gain, second_bias)[1]
    grad_middle, grad_gain_two, grad_bias_two = pullback(grad_second)
    grad_middle = grad_middle + grad_result
    grad_attended = grad_middle.astype(jnp.bfloat16)
    grad_mixture = product(grad_attended, output_t).astype(jnp.bfloat16)
    grad_triple = attend_back(grad_mixture, attend_stored)
    grad_normed = right_product(grad_triple, project)
    pullback = jax.vjp(layer_norm, inputs, first_gain, first_bias)[1]
    grad_inputs, grad_gain_one, grad_bias_one = pullback(grad_normed)
    grad_inputs = grad_inputs + grad_middle
    return (
        grad_inputs,
        (grad_gain_one, grad_bias_one, grad_gain_two, grad_bias_two),
        [(normed, grad_triple), (grad_attended, mixture), (second, grad_lifted), (grad_branch, hidden)],
    )


def normalize(values):
    centred = values - jnp.mean(values, -1, keepdims=True)
    scale = lax.rsqrt(jnp.mean(centred * centred, -1, keepdims=True) + epsilon)
    return centred * scale, scale


def normalize_back(grad, unit, scale, norm_gain):
    scaled = grad * norm_gain
    return scale * (
        scaled - jnp.mean(scaled, -1, keepdims=True) - unit * jnp.mean(scaled * unit, -1, keepdims=True)
    )


def gate_both(values):
    root = math.sqrt(2.0 / math.pi)
    square = values * values
    bend = jnp.tanh(root * values * (1.0 + 0.044715 * square))
    half = 0.5 + 0.5 * bend
    slope = half + 0.5 * values * (1.0 - bend * bend) * (root * (1.0 + 3.0 * 0.044715 * square))
    return values * half, slope


def head_lanes(pair):
    lane = lax.broadcasted_iota(jnp.int32, pair.shape, 1)
    zero = jnp.zeros_like(pair)
    return jnp.where(lane < HEAD_DIM, pair, zero), jnp.where(lane < HEAD_DIM, zero, pair)


def chances_of(queries, keys, allowed):
    scores = right_product(queries, keys) * (1.0 / math.sqrt(HEAD_DIM))
    scores = jnp.where(allowed, scores, -1e30)
    powers = jnp.exp(scores - jnp.max(scores, -1, keepdims=True))
    return powers * (1.0 / jnp.sum(powers, -1, keepdims=True))


TILE = 128
PAIRS = 6


def fine_kernel(byte_ref, previous_ref, cotangent_ref, small_ref, w_ref,
                out_ref, grad_in_ref, patch_grad_ref, vectors_ref,
                normed_ref, mixture_ref, second_ref, hidden_ref, low_ref, lifted_grad_ref, triple_grad_ref,
                triple, chances, result, grad_second):
    rows = byte_ref.shape[0]
    bf = jnp.bfloat16
    first_gain, first_bias, second_gain, second_bias = (small_ref[i : i + 1] for i in (4, 5, 6, 7))
    previous = previous_ref[...]
    inputs = (
        byte_ref[...].astype(jnp.float32).reshape(rows // PATCH, PATCH, D) + previous[:, None, :]
    ).reshape(rows, D)
    unit_one, scale_one = normalize(inputs)
    normed = (unit_one * first_gain + first_bias).astype(bf)
    normed_ref[...] = normed
    triple[...] = product(normed, w_ref[:, : 3 * D]).astype(bf)
    row = lax.broadcasted_iota(jnp.int32, (TILE, TILE), 0)
    column = lax.broadcasted_iota(jnp.int32, (TILE, TILE), 1)
    allowed = (row // PATCH == column // PATCH) & (column <= row)
    tiles = rows // TILE

    def attend(pair, _):
        lanes = [pl.ds(pl.multiple_of(i * D + pair * 128, 128), 128) for i in range(3)]
        for tile in range(tiles):
            here = slice(tile * TILE, tile * TILE + TILE)
            queries = head_lanes(triple[here, lanes[0]])
            keys = triple[here, lanes[1]]
            values = head_lanes(triple[here, lanes[2]])
            mixed = None
            for head in range(2):
                found = chances_of(queries[head], keys, allowed)
                chances[pair * 2 + head, here] = found
                term = product(found.astype(bf), values[head])
                mixed = term if mixed is None else mixed + term
            mixture_ref[here, lanes[0]] = mixed.astype(bf)
        return 0

    lax.fori_loop(0, PAIRS, attend, 0)
    middle = inputs + right_product(mixture_ref[...], w_ref[:, 3 * D : 4 * D])
    unit_two, scale_two = normalize(middle)
    second = (unit_two * second_gain + second_bias).astype(bf)
    second_ref[...] = second
    grad_low = cotangent_ref[...]
    result[...] = middle
    for j in range(4):
        here = slice(j * D, j * D + D)
        expand = w_ref[:, 4 * D + j * D : 5 * D + j * D]
        narrow_t = w_ref[:, 8 * D + j * D : 9 * D + j * D]
        hidden, slope = gate_both(product(second, expand))
        hidden = hidden.astype(bf)
        hidden_ref[:, here] = hidden
        lifted_grad = (product(grad_low, narrow_t) * slope).astype(bf)
        lifted_grad_ref[:, here] = lifted_grad
        result[...] += right_product(hidden, narrow_t)
        term = right_product(lifted_grad, expand)
        if j:
            grad_second[...] += term
        else:
            grad_second[...] = term
    out_ref[...] = result[...].astype(bf)
    grad_two = grad_second[...]
    grad_middle = grad_low.astype(jnp.float32) + normalize_back(grad_two, unit_two, scale_two, second_gain)
    low = grad_middle.astype(bf)
    low_ref[...] = low
    grad_second[...] = grad_middle
    grad_mixture = product(low, w_ref[:, 3 * D : 4 * D]).astype(bf)
    result[...] = grad_mixture.astype(jnp.float32)

    def attend_back(pair, _):
        lanes = [pl.ds(pl.multiple_of(i * D + pair * 128, 128), 128) for i in range(3)]
        factor = 1.0 / math.sqrt(HEAD_DIM)
        for tile in range(tiles):
            here = slice(tile * TILE, tile * TILE + TILE)
            queries = head_lanes(triple[here, lanes[0]])
            keys = head_lanes(triple[here, lanes[1]])
            values = triple[here, lanes[2]]
            mixed = head_lanes(result[here, lanes[0]].astype(bf))
            sums = [None, None, None]
            for head in range(2):
                found = chances[pair * 2 + head, here]
                grad = right_product(mixed[head], values)
                scores = (found * (grad - jnp.sum(grad * found, -1, keepdims=True))).astype(bf)
                terms = (
                    product(scores, keys[head]),
                    left_product(scores, queries[head]),
                    left_product(found.astype(bf), mixed[head]),
                )
                sums = [t if s is None else s + t for s, t in zip(sums, terms)]
            triple_grad_ref[here, lanes[0]] = (sums[0] * factor).astype(bf)
            triple_grad_ref[here, lanes[1]] = (sums[1] * factor).astype(bf)
            triple_grad_ref[here, lanes[2]] = sums[2].astype(bf)
        return 0

    lax.fori_loop(0, PAIRS, attend_back, 0)
    grad_one = right_product(triple_grad_ref[...], w_ref[:, : 3 * D])
    grad_in = grad_second[...] + normalize_back(grad_one, unit_one, scale_one, first_gain)
    grad_in_ref[...] = grad_in
    patch_grad_ref[...] = jnp.sum(grad_in.reshape(rows // PATCH, PATCH, D), 1)
    terms = [jnp.sum(t, 0, keepdims=True) for t in (grad_one * unit_one, grad_one, grad_two * unit_two, grad_two)]

    @pl.when(pl.program_id(0) == 0)
    def _():
        vectors_ref[...] = jnp.zeros_like(vectors_ref)

    for i, term in enumerate(terms):
        vectors_ref[4 + i : 5 + i] += term


def fine_block(byte_rows, previous, cotangent, small, full, rows=256):
    count = byte_rows.shape[0]
    bf, f32 = jnp.bfloat16, jnp.float32

    def spec(height, width):
        return pl.BlockSpec((height, width), lambda i: (i, 0))

    def whole(shape):
        return pl.BlockSpec(shape, lambda i: (0, 0), pipeline_mode=pl.Buffered(1))

    outs = [(rows, D, bf), (rows, D, f32), (rows // PATCH, D, f32), None]
    outs += [(rows, D, bf)] * 3 + [(rows, 4 * D, bf), (rows, D, bf), (rows, 4 * D, bf), (rows, 3 * D, bf)]
    steps = count // rows
    return pl.pallas_call(
        fine_kernel,
        grid=(steps,),
        out_shape=[
            jax.ShapeDtypeStruct((o[0] * steps, o[1]), o[2]) if o else jax.ShapeDtypeStruct((8, D), f32) for o in outs
        ],
        in_specs=[spec(rows, D), spec(rows // PATCH, D), spec(rows, D), whole((8, D)), whole(full.shape)],
        out_specs=[spec(o[0], o[1]) if o else pl.BlockSpec((8, D), lambda i: (0, 0)) for o in outs],
        scratch_shapes=[
            pltpu.VMEM((rows, 3 * D), bf),
            pltpu.VMEM((2 * PAIRS, rows, TILE), f32),
            pltpu.VMEM((rows, D), f32),
            pltpu.VMEM((rows, D), f32),
        ],
        compiler_params=pltpu.CompilerParams(dimension_semantics=("arbitrary",), vmem_limit_bytes=64_000_000),
        name="fine_block",
    )(byte_rows, previous, cotangent, small, full)


def solution(mesh):
    return jax.shard_map(
        fast_body if (mesh.shape["seq"], mesh.shape["fsdp"]) == (2, 16) else body,
        mesh=mesh,
        in_specs=(
            P("fsdp", "seq", None),
            P("fsdp", None),
            P("fsdp", "seq", None),
            P("fsdp", None),
            P("fsdp"),
            P("fsdp"),
            P("fsdp", None),
            P(None, "fsdp"),
            P("fsdp"),
            P("fsdp"),
            P("fsdp", None),
            P(None, "fsdp"),
            P("fsdp"),
            P("fsdp"),
            P("fsdp", None),
            P(None, "fsdp"),
            P("fsdp"),
            P("fsdp"),
            P("fsdp", None),
            P(None, "fsdp"),
        ),
        out_specs=(
            P("fsdp", "seq", None),
            P("fsdp", "seq", None),
            P("fsdp", None),
            P("fsdp"),
            P("fsdp"),
            P("fsdp", None),
            P(None, "fsdp"),
            P("fsdp"),
            P("fsdp"),
            P("fsdp", None),
            P(None, "fsdp"),
            P("fsdp"),
            P("fsdp"),
            P("fsdp", None),
            P(None, "fsdp"),
            P("fsdp"),
            P("fsdp"),
            P("fsdp", None),
            P(None, "fsdp"),
        ),
        check_vma=False,
    )
```

```python
import functools
import math

import jax
import jax.numpy as jnp
from jax import lax
from jax.experimental import pallas as pl
from jax.experimental.pallas import tpu as pltpu
from jax.sharding import PartitionSpec as P


D = 768
HEAD_DIM = 64
PATCH = 8


epsilon = 1e-05


def shifted(block, axis, distance):
    devices = range(lax.axis_size(axis))
    route = [(i - distance, i) for i in devices if i - distance in devices]
    return lax.ppermute(block, axis, route)


def layer_norm(values, norm_gain, norm_bias):
    center = jnp.mean(values, -1, keepdims=True)
    centred = values - center
    spread = jnp.mean(centred * centred, -1, keepdims=True)
    return centred * lax.rsqrt(spread + epsilon) * norm_gain + norm_bias


def smooth_gate(values):
    return jax.nn.gelu(values, approximate=True)


def product(left_side, right_side):
    return jnp.dot(left_side, right_side, preferred_element_type=jnp.float32)


def left_product(left_side, right_side):
    return lax.dot_general(
        left_side, right_side, (((0,), (0,)), ((), ())), preferred_element_type=jnp.float32
    )


def right_product(left_side, right_side):
    return lax.dot_general(
        left_side, right_side, (((1,), (1,)), ((), ())), preferred_element_type=jnp.float32
    )


def attend_forward(queries, key_part, value_part, allowed):
    factor = 1.0 / math.sqrt(HEAD_DIM)
    scores = (
        jnp.einsum("bqhd,bkhd->bhqk", queries, key_part, preferred_element_type=jnp.float32)
        * factor
    )
    scores = jnp.where(allowed[:, None], scores, -1e30)
    highest = jnp.max(scores, -1, keepdims=True)
    log_total = highest + jnp.log(jnp.sum(jnp.exp(scores - highest), -1, keepdims=True))
    rounded = jnp.exp(scores - log_total).astype(jnp.bfloat16)
    mixture = jnp.einsum("bhqk,bkhd->bqhd", rounded, value_part, preferred_element_type=jnp.float32)
    return (mixture, log_total)


def attend_backward(queries, key_part, value_part, allowed, log_total, grad_mixture):
    factor = 1.0 / math.sqrt(HEAD_DIM)
    scores = (
        jnp.einsum("bqhd,bkhd->bhqk", queries, key_part, preferred_element_type=jnp.float32)
        * factor
    )
    scores = jnp.where(allowed[:, None], scores, -1e30)
    chances = jnp.exp(scores - log_total)
    rounded = chances.astype(jnp.bfloat16)
    grad_values = jnp.einsum(
        "bhqk,bqhd->bkhd", rounded, grad_mixture, preferred_element_type=jnp.float32
    )
    grad_chances = jnp.einsum(
        "bqhd,bkhd->bhqk", grad_mixture, value_part, preferred_element_type=jnp.float32
    )
    grad_scores = (
        chances * (grad_chances - jnp.sum(grad_chances * chances, -1, keepdims=True))
    ).astype(jnp.bfloat16)
    grad_queries = (
        jnp.einsum("bhqk,bkhd->bqhd", grad_scores, key_part, preferred_element_type=jnp.float32)
        * factor
    )
    grad_keys = (
        jnp.einsum("bhqk,bqhd->bkhd", grad_scores, queries, preferred_element_type=jnp.float32)
        * factor
    )
    return (grad_queries, grad_keys, grad_values)


def block_forward(inputs, weights, attend):
    first_gain, first_bias, project, output, second_gain, second_bias, expand, narrow = weights
    normed = layer_norm(
        inputs, first_gain.astype(jnp.float32), first_bias.astype(jnp.float32)
    ).astype(jnp.bfloat16)
    triple = product(normed, project).astype(jnp.bfloat16)
    mixture, attend_stored = attend(triple)
    middle = inputs + product(mixture, output)
    second = layer_norm(
        middle, second_gain.astype(jnp.float32), second_bias.astype(jnp.float32)
    ).astype(jnp.bfloat16)
    lifted = product(second, expand)
    hidden = smooth_gate(lifted).astype(jnp.bfloat16)
    result = middle + product(hidden, narrow)
    stored = (inputs, normed, attend_stored, mixture, middle, second, lifted, hidden)
    return (result, stored)


def block_backward(grad_result, weights, stored, attend_back):
    first_gain, first_bias, project, output, second_gain, second_bias, expand, narrow = weights
    inputs, normed, attend_stored, mixture, middle, second, lifted, hidden = stored
    grad_branch = grad_result.astype(jnp.bfloat16)
    grad_narrow = left_product(hidden, grad_branch)
    grad_hidden = right_product(grad_branch, narrow)
    grad_lifted = jax.vjp(smooth_gate, lifted)[1](grad_hidden)[0].astype(jnp.bfloat16)
    grad_expand = left_product(second, grad_lifted)
    grad_second = right_product(grad_lifted, expand)
    pullback = jax.vjp(
        layer_norm, middle, second_gain.astype(jnp.float32), second_bias.astype(jnp.float32)
    )[1]
    grad_middle, grad_gain_two, grad_bias_two = pullback(grad_second)
    grad_middle = grad_middle + grad_result
    grad_attended = grad_middle.astype(jnp.bfloat16)
    grad_output = left_product(mixture, grad_attended)
    grad_mixture = right_product(grad_attended, output).astype(jnp.bfloat16)
    grad_triple = attend_back(grad_mixture, attend_stored)
    grad_project = left_product(normed, grad_triple)
    grad_normed = right_product(grad_triple, project)
    pullback = jax.vjp(
        layer_norm, inputs, first_gain.astype(jnp.float32), first_bias.astype(jnp.float32)
    )[1]
    grad_inputs, grad_gain_one, grad_bias_one = pullback(grad_normed)
    grad_inputs = grad_inputs + grad_middle
    return (
        grad_inputs,
        (
            grad_gain_one,
            grad_bias_one,
            grad_project,
            grad_output,
            grad_gain_two,
            grad_bias_two,
            grad_expand,
            grad_narrow,
        ),
    )


def body(
    byte_inputs,
    segment_ids,
    cotangent,
    patch_weight,
    coarse_first_gain,
    coarse_first_bias,
    coarse_project,
    coarse_output,
    coarse_second_gain,
    coarse_second_bias,
    coarse_expand,
    coarse_narrow,
    fine_first_gain,
    fine_first_bias,
    fine_project,
    fine_output,
    fine_second_gain,
    fine_second_bias,
    fine_expand,
    fine_narrow,
):
    coarse_full = (
        lax.all_gather(patch_weight, "fsdp", axis=0, tiled=True),
        lax.all_gather(coarse_first_gain, "fsdp", axis=0, tiled=True),
        lax.all_gather(coarse_first_bias, "fsdp", axis=0, tiled=True),
        lax.all_gather(coarse_project, "fsdp", axis=0, tiled=True),
        lax.all_gather(coarse_output, "fsdp", axis=1, tiled=True),
        lax.all_gather(coarse_second_gain, "fsdp", axis=0, tiled=True),
        lax.all_gather(coarse_second_bias, "fsdp", axis=0, tiled=True),
        lax.all_gather(coarse_expand, "fsdp", axis=0, tiled=True),
        lax.all_gather(coarse_narrow, "fsdp", axis=1, tiled=True),
    )
    fine_full = (
        lax.all_gather(fine_first_gain, "fsdp", axis=0, tiled=True),
        lax.all_gather(fine_first_bias, "fsdp", axis=0, tiled=True),
        lax.all_gather(fine_project, "fsdp", axis=0, tiled=True),
        lax.all_gather(fine_output, "fsdp", axis=1, tiled=True),
        lax.all_gather(fine_second_gain, "fsdp", axis=0, tiled=True),
        lax.all_gather(fine_second_bias, "fsdp", axis=0, tiled=True),
        lax.all_gather(fine_expand, "fsdp", axis=0, tiled=True),
        lax.all_gather(fine_narrow, "fsdp", axis=1, tiled=True),
    )
    byte_rows = byte_inputs[0]
    bytes_here = byte_rows.shape[0]
    patches = bytes_here // PATCH
    segment_row = segment_ids[0]
    all_patches = segment_row.shape[0]
    places = jnp.arange(all_patches)
    coarse_allowed = (
        (places[:, None] >= places[None, :]) & (segment_row[:, None] == segment_row[None, :])
    )[None]
    inner = jnp.arange(PATCH)
    fine_allowed = (inner[:, None] >= inner[None, :])[None]

    def coarse_attend(triple):
        head_block = lax.all_to_all(
            triple.reshape(patches, 3, D), "seq", split_axis=2, concat_axis=0, tiled=True
        )
        all_rows = head_block.shape[0]
        columns = head_block.shape[2]
        local_heads = columns // HEAD_DIM
        queries = head_block[:, 0].reshape(1, all_rows, local_heads, HEAD_DIM)
        key_part = head_block[:, 1].reshape(1, all_rows, local_heads, HEAD_DIM)
        value_part = head_block[:, 2].reshape(1, all_rows, local_heads, HEAD_DIM)
        mixture, log_total = attend_forward(queries, key_part, value_part, coarse_allowed)
        merged = mixture.reshape(all_rows, columns).astype(jnp.bfloat16)
        back_rows = lax.all_to_all(merged, "seq", split_axis=0, concat_axis=1, tiled=True)
        return (back_rows, (queries, key_part, value_part, log_total))

    def coarse_back(grad_mixture, stored):
        queries, key_part, value_part, log_total = stored
        head_grad = lax.all_to_all(grad_mixture, "seq", split_axis=1, concat_axis=0, tiled=True)
        all_rows = head_grad.shape[0]
        columns = head_grad.shape[1]
        grad_queries, grad_keys, grad_values = attend_backward(
            queries,
            key_part,
            value_part,
            coarse_allowed,
            log_total,
            head_grad.reshape(1, all_rows, columns // HEAD_DIM, HEAD_DIM),
        )
        stacked = jnp.stack(
            [
                grad_queries.reshape(all_rows, columns),
                grad_keys.reshape(all_rows, columns),
                grad_values.reshape(all_rows, columns),
            ],
            1,
        ).astype(jnp.bfloat16)
        back_rows = lax.all_to_all(stacked, "seq", split_axis=0, concat_axis=2, tiled=True)
        return back_rows.reshape(back_rows.shape[0], 3 * D)

    def fine_attend(triple):
        grouped = triple.reshape(patches, PATCH, 3, D // HEAD_DIM, HEAD_DIM)
        queries = grouped[:, :, 0]
        key_part = grouped[:, :, 1]
        value_part = grouped[:, :, 2]
        mixture, log_total = attend_forward(queries, key_part, value_part, fine_allowed)
        return (
            mixture.reshape(bytes_here, D).astype(jnp.bfloat16),
            (queries, key_part, value_part, log_total),
        )

    def fine_back(grad_mixture, stored):
        queries, key_part, value_part, log_total = stored
        grad_queries, grad_keys, grad_values = attend_backward(
            queries,
            key_part,
            value_part,
            fine_allowed,
            log_total,
            grad_mixture.reshape(patches, PATCH, D // HEAD_DIM, HEAD_DIM),
        )
        stacked = jnp.stack([grad_queries, grad_keys, grad_values], 2).astype(jnp.bfloat16)
        return stacked.reshape(bytes_here, 3 * D)

    grouped_bytes = byte_rows.reshape(patches, PATCH * D)
    embedded = product(grouped_bytes, coarse_full[0])
    coarse_out, coarse_stored = block_forward(embedded, coarse_full[1:], coarse_attend)
    coarse_low = coarse_out.astype(jnp.bfloat16)
    arrived = shifted(coarse_low[-1:], "seq", 1)
    offset = lax.axis_index("seq") * patches
    padded = jnp.concatenate([segment_row[:1] - 1, segment_row])
    before = lax.dynamic_slice_in_dim(padded, offset, patches)
    current = lax.dynamic_slice_in_dim(segment_row, offset, patches)
    joined = (before == current).astype(jnp.float32)[:, None]
    previous = jnp.concatenate([arrived, coarse_low[:-1]]).astype(jnp.float32) * joined
    fine_in = (
        byte_rows.astype(jnp.float32).reshape(patches, PATCH, D) + previous[:, None, :]
    ).reshape(bytes_here, D)
    layer_rows, fine_stored = block_forward(fine_in, fine_full, fine_attend)
    fine_weights_back = (
        lax.all_gather(fine_first_gain, "fsdp", axis=0, tiled=True),
        lax.all_gather(fine_first_bias, "fsdp", axis=0, tiled=True),
        lax.all_gather(fine_project, "fsdp", axis=0, tiled=True),
        lax.all_gather(fine_output, "fsdp", axis=1, tiled=True),
        lax.all_gather(fine_second_gain, "fsdp", axis=0, tiled=True),
        lax.all_gather(fine_second_bias, "fsdp", axis=0, tiled=True),
        lax.all_gather(fine_expand, "fsdp", axis=0, tiled=True),
        lax.all_gather(fine_narrow, "fsdp", axis=1, tiled=True),
    )
    grad_fine_in, fine_grads = block_backward(
        cotangent[0].astype(jnp.float32), fine_weights_back, fine_stored, fine_back
    )
    grad_previous = jnp.sum(grad_fine_in.reshape(patches, PATCH, D), 1) * joined
    arrived_back = shifted(grad_previous[:1], "seq", -1)
    grad_coarse_out = jnp.concatenate([grad_previous[1:], arrived_back])
    coarse_weights_back = (
        lax.all_gather(patch_weight, "fsdp", axis=0, tiled=True),
        lax.all_gather(coarse_first_gain, "fsdp", axis=0, tiled=True),
        lax.all_gather(coarse_first_bias, "fsdp", axis=0, tiled=True),
        lax.all_gather(coarse_project, "fsdp", axis=0, tiled=True),
        lax.all_gather(coarse_output, "fsdp", axis=1, tiled=True),
        lax.all_gather(coarse_second_gain, "fsdp", axis=0, tiled=True),
        lax.all_gather(coarse_second_bias, "fsdp", axis=0, tiled=True),
        lax.all_gather(coarse_expand, "fsdp", axis=0, tiled=True),
        lax.all_gather(coarse_narrow, "fsdp", axis=1, tiled=True),
    )
    grad_embedded, coarse_grads = block_backward(
        grad_coarse_out, coarse_weights_back[1:], coarse_stored, coarse_back
    )
    grad_embed_low = grad_embedded.astype(jnp.bfloat16)
    grad_patch = left_product(grouped_bytes, grad_embed_low)
    grad_grouped = right_product(grad_embed_low, coarse_weights_back[0])
    input_gradient = (grad_fine_in + grad_grouped.reshape(bytes_here, D)).astype(jnp.bfloat16)
    shards = (
        lax.psum_scatter(grad_patch, "fsdp", scatter_dimension=0, tiled=True),
        lax.psum_scatter(coarse_grads[0], "fsdp", scatter_dimension=0, tiled=True),
        lax.psum_scatter(coarse_grads[1], "fsdp", scatter_dimension=0, tiled=True),
        lax.psum_scatter(coarse_grads[2], "fsdp", scatter_dimension=0, tiled=True),
        lax.psum_scatter(coarse_grads[3], "fsdp", scatter_dimension=1, tiled=True),
        lax.psum_scatter(coarse_grads[4], "fsdp", scatter_dimension=0, tiled=True),
        lax.psum_scatter(coarse_grads[5], "fsdp", scatter_dimension=0, tiled=True),
        lax.psum_scatter(coarse_grads[6], "fsdp", scatter_dimension=0, tiled=True),
        lax.psum_scatter(coarse_grads[7], "fsdp", scatter_dimension=1, tiled=True),
        lax.psum_scatter(fine_grads[0], "fsdp", scatter_dimension=0, tiled=True),
        lax.psum_scatter(fine_grads[1], "fsdp", scatter_dimension=0, tiled=True),
        lax.psum_scatter(fine_grads[2], "fsdp", scatter_dimension=0, tiled=True),
        lax.psum_scatter(fine_grads[3], "fsdp", scatter_dimension=1, tiled=True),
        lax.psum_scatter(fine_grads[4], "fsdp", scatter_dimension=0, tiled=True),
        lax.psum_scatter(fine_grads[5], "fsdp", scatter_dimension=0, tiled=True),
        lax.psum_scatter(fine_grads[6], "fsdp", scatter_dimension=0, tiled=True),
        lax.psum_scatter(fine_grads[7], "fsdp", scatter_dimension=1, tiled=True),
    )
    totals = (
        lax.psum(shards[0].astype(jnp.bfloat16), "seq").astype(jnp.float32),
        lax.psum(shards[1].astype(jnp.bfloat16), "seq").astype(jnp.float32),
        lax.psum(shards[2].astype(jnp.bfloat16), "seq").astype(jnp.float32),
        lax.psum(shards[3].astype(jnp.bfloat16), "seq").astype(jnp.float32),
        lax.psum(shards[4].astype(jnp.bfloat16), "seq").astype(jnp.float32),
        lax.psum(shards[5].astype(jnp.bfloat16), "seq").astype(jnp.float32),
        lax.psum(shards[6].astype(jnp.bfloat16), "seq").astype(jnp.float32),
        lax.psum(shards[7].astype(jnp.bfloat16), "seq").astype(jnp.float32),
        lax.psum(shards[8].astype(jnp.bfloat16), "seq").astype(jnp.float32),
        lax.psum(shards[9].astype(jnp.bfloat16), "seq").astype(jnp.float32),
        lax.psum(shards[10].astype(jnp.bfloat16), "seq").astype(jnp.float32),
        lax.psum(shards[11].astype(jnp.bfloat16), "seq").astype(jnp.float32),
        lax.psum(shards[12].astype(jnp.bfloat16), "seq").astype(jnp.float32),
        lax.psum(shards[13].astype(jnp.bfloat16), "seq").astype(jnp.float32),
        lax.psum(shards[14].astype(jnp.bfloat16), "seq").astype(jnp.float32),
        lax.psum(shards[15].astype(jnp.bfloat16), "seq").astype(jnp.float32),
        lax.psum(shards[16].astype(jnp.bfloat16), "seq").astype(jnp.float32),
    )
    layer_output = layer_rows.astype(jnp.bfloat16)[None]
    return (
        layer_output,
        input_gradient[None],
        totals[0],
        totals[1],
        totals[2],
        totals[3],
        totals[4],
        totals[5],
        totals[6],
        totals[7],
        totals[8],
        totals[9],
        totals[10],
        totals[11],
        totals[12],
        totals[13],
        totals[14],
        totals[15],
        totals[16],
    )


MESH = pl.DeviceIdType.MESH
HBM = pltpu.MemorySpace.HBM
VMEM = pltpu.MemorySpace.VMEM


class Place:
    def __init__(self):
        self.core = lax.axis_index("seq")
        self.at = lax.axis_index("fsdp")
        self.z = self.at // 4
        self.plane = self.at % 4
        self.near = 1 + self.core
        self.far = 2 - self.core

    def flip(self, mask):
        return self.at ^ mask

    def across(self, mask):
        return (self.core, self.at ^ mask)

    def partner(self):
        return (1 - self.core, self.at)


def enter(place, masks, partner=True):
    barrier = pltpu.get_barrier_semaphore()
    for mask in masks:
        pl.semaphore_signal(barrier, inc=1, device_id=place.across(mask), device_id_type=MESH)
    if partner:
        pl.semaphore_signal(barrier, inc=1, device_id=place.partner(), device_id_type=MESH)
    pl.semaphore_wait(barrier, len(masks) + (1 if partner else 0))


MASKS = (1, 2, 4, 8, 12)


class Gather:
    EVENTS = 12

    def __init__(self, place, source, buffer, rows, first, column, width, z_first, sends, receives, local):
        self.p, self.source, self.buffer, self.rows, self.first = place, source, buffer, rows, first
        self.z_first, self.sends, self.receives, self.local = z_first, sends, receives, local
        self.half = width // 2
        self.column, self.width = column, width
        self.mine = pl.ds(pl.multiple_of(column + place.core * self.half, 128), self.half)
        self.theirs = pl.ds(pl.multiple_of(column + (1 - place.core) * self.half, 128), self.half)
        self.started = []

    def group(self, plane, columns=None):
        return self.buffer.at[:, plane, self.rows, self.mine if columns is None else columns]

    def block(self, z, plane):
        return self.buffer.at[z, plane, self.rows, self.mine]

    def send(self, event, view, device, source=None):
        copy = pltpu.make_async_remote_copy(
            src_ref=view if source is None else source,
            dst_ref=view,
            send_sem=self.sends.at[event],
            recv_sem=self.receives.at[event],
            device_id=device,
            device_id_type=MESH,
        )
        copy.start()
        self.started.append(copy)

    def arrived(self, event, view):
        pltpu.make_async_remote_copy(
            src_ref=view,
            dst_ref=view,
            send_sem=self.sends.at[event],
            recv_sem=self.receives.at[event],
            device_id=self.p.partner(),
            device_id_type=MESH,
        ).wait_recv()

    def start(self):
        p = self.p
        own = self.source.at[self.rows, pl.ds(pl.multiple_of(self.first + p.core * self.half, 128), self.half)]
        self.copy = pltpu.make_async_copy(own, self.block(p.z, p.plane), self.local)
        self.copy.start()
        if not self.z_first:
            self.send(6, self.block(p.z, p.plane), p.across(p.near), own)
        for j in (1, 2, 3):
            self.send(j - 1, self.block(p.z, p.plane), p.across(4 * j), own)

    def one(self):
        p = self.p
        self.copy.wait()
        if self.z_first:
            for j in (1, 2, 3):
                self.arrived(j - 1, self.block(p.z ^ j, p.plane))
            self.send(6, self.group(p.plane), p.across(p.near))
            self.send(7, self.group(p.plane), p.across(p.far))
            self.send(9, self.group(p.plane), p.partner())
        else:
            self.arrived(6, self.block(p.z, p.plane ^ p.near))
            for j in (1, 2, 3):
                self.send(2 + j, self.block(p.z, p.plane ^ p.near), p.across(4 * j))

    def two(self):
        p = self.p
        if self.z_first:
            self.arrived(6, self.group(p.plane ^ p.near))
        else:
            for j in (1, 2, 3):
                self.arrived(j - 1, self.block(p.z ^ j, p.plane))
            self.send(7, self.group(p.plane), p.across(p.far))
            self.send(9, self.group(p.plane), p.partner())
            for j in (1, 2, 3):
                self.arrived(2 + j, self.block(p.z ^ j, p.plane ^ p.near))
        self.send(8, self.group(p.plane ^ p.near), p.across(p.far))
        self.send(10, self.group(p.plane ^ p.near), p.partner())

    def three(self):
        p = self.p
        self.arrived(7, self.group(p.plane ^ p.far))
        self.send(11, self.group(p.plane ^ p.far), p.partner())
        self.arrived(8, self.group(p.plane ^ 3))
        self.send(12, self.group(p.plane ^ 3), p.partner())

    def four(self):
        p = self.p
        self.arrived(9, self.group(p.plane, self.theirs))
        self.arrived(10, self.group(p.plane ^ p.far, self.theirs))
        self.arrived(11, self.group(p.plane ^ p.near, self.theirs))
        self.arrived(12, self.group(p.plane ^ 3, self.theirs))

    def drain(self):
        for copy in self.started:
            copy.wait_send()


def run_gathers(gathers, ahead, tick):
    n = len(gathers)
    for k in range(min(ahead, n)):
        gathers[k].start()
    for t in range(n + 3):
        if t < n:
            gathers[t].one()
            if t + ahead < n:
                gathers[t + ahead].start()
        if 0 <= t - 1 < n:
            gathers[t - 1].two()
        if 0 <= t - 2 < n:
            gathers[t - 2].three()
        if 0 <= t - 3 < n:
            gathers[t - 3].four()
        tick(t)
    for g in gathers:
        g.drain()


class PatchForward:
    def __init__(self, small, rows, patch, w, segments, outs):
        self.small, self.rows, self.patch, self.w, self.segments = small, rows, patch, w, segments
        self.embedded, self.normed, self.triple, self.chances, self.mixture = outs[:5]
        self.middle, self.second, self.lifted, self.hidden, self.result = outs[5:]

    def weight(self, column, width):
        return self.w[:, :, :, column : column + width].reshape(D, width)

    def embed(self, first):
        def step(z, _):
            columns = pl.ds(pl.multiple_of(z * 2 * D, 128), 2 * D)
            rows = self.rows[:, :, columns].reshape(self.embedded.shape[0], 2 * D)
            term = product(rows, self.patch[z].reshape(2 * D, D))
            self.embedded[...] += term
            return 0

        if first == 0:
            self.embedded[...] = jnp.zeros_like(self.embedded)
        lax.fori_loop(first, first + 2, step, 0)

    def project(self):
        unit, _ = normalize(self.embedded[...])
        self.normed[...] = (unit * self.small[0:1] + self.small[1:2]).astype(jnp.bfloat16)
        self.triple[...] = product(self.normed[...], self.weight(0, 3 * D)).astype(jnp.bfloat16)

    def attend(self, first):
        count = self.triple.shape[0]
        row = lax.broadcasted_iota(jnp.int32, (count, count), 0)
        column = lax.broadcasted_iota(jnp.int32, (count, count), 1)
        allowed = (column <= row) & (self.segments[1][...] == self.segments[0][...])

        def step(pair, _):
            lanes = [pl.ds(pl.multiple_of(i * D + pair * 128, 128), 128) for i in range(3)]
            queries = head_lanes(self.triple[:, lanes[0]])
            keys = self.triple[:, lanes[1]]
            values = head_lanes(self.triple[:, lanes[2]])
            mixed = None
            for head in range(2):
                found = chances_of(queries[head], keys, allowed)
                self.chances[pair * 2 + head] = found
                term = product(found.astype(jnp.bfloat16), values[head])
                mixed = term if mixed is None else mixed + term
            self.mixture[:, lanes[0]] = mixed.astype(jnp.bfloat16)
            return 0

        lax.fori_loop(first, first + 3, step, 0)

    def join(self):
        middle = self.embedded[...] + right_product(self.mixture[...], self.weight(3 * D, D))
        self.middle[...] = middle
        self.result[...] = middle
        unit, _ = normalize(middle)
        self.second[...] = (unit * self.small[2:3] + self.small[3:4]).astype(jnp.bfloat16)

    def lift(self, half):
        here = slice(half * 2 * D, half * 2 * D + 2 * D)
        lifted = product(self.second[...], self.weight(4 * D + half * 2 * D, 2 * D))
        self.lifted[:, here] = lifted
        self.hidden[:, here] = smooth_gate(lifted).astype(jnp.bfloat16)

    def lower(self, half):
        here = slice(half * 2 * D, half * 2 * D + 2 * D)
        self.result[...] += right_product(self.hidden[:, here], self.weight(8 * D + half * 2 * D, 2 * D))


def gather_kernel(plan, ahead, *refs):
    sources, small, rows, segments, rest = refs[:9], refs[9], refs[10], refs[11:13], refs[13:]
    buffers, small_out, all_rows, patch_outs, rest = rest[:3], rest[3], rest[4], rest[5:15], rest[15:]
    sends, receives, local, value, arriving, small_sends, small_receives, row_sems, patch, w, loads = rest
    place = Place()
    enter(place, MASKS)
    value[0] = small[...]
    total = Total(place, (1, 2, 4, 8), value, arriving, small_sends, small_receives, small_out)
    stay = pltpu.make_async_copy(rows, all_rows.at[place.core], row_sems.at[0])
    stay.start()
    cross = pltpu.make_async_remote_copy(
        src_ref=rows, dst_ref=all_rows.at[place.core], send_sem=row_sems.at[1], recv_sem=row_sems.at[2],
        device_id=place.partner(), device_id_type=MESH,
    )
    cross.start()
    gathers = []
    for k, (source, buffer, first, rows_here, start, column, width, z_first) in enumerate(plan):
        gathers.append(
            Gather(place, sources[source], buffers[buffer], pl.ds(first, rows_here), start, column, width, z_first,
                   sends.at[k], receives.at[k], local.at[k])
        )
    forward = PatchForward(small_out, all_rows, patch, w, segments, patch_outs)
    waiting = []
    patches = sum(p[1] == 0 for p in plan)
    held = sum(p[1] < 2 for p in plan)

    def fetched():
        while waiting:
            waiting.pop().wait()

    def rows_there():
        stay.wait()
        cross.wait()

    base = patches + 4
    pieces = {
        base: (rows_there, fetched, functools.partial(forward.embed, 0)),
        base + 1: (functools.partial(forward.embed, 2),),
        base + 2: (fetched, forward.project),
        base + 3: (functools.partial(forward.attend, 0),),
        base + 4: (functools.partial(forward.attend, 3),),
        base + 5: (fetched, forward.join),
        base + 6: (functools.partial(forward.lift, 0),),
        base + 7: (functools.partial(forward.lift, 1),),
        base + 8: (fetched, functools.partial(forward.lower, 0)),
        base + 9: (functools.partial(forward.lower, 1),),
    }

    def tick(t):
        total.advance()
        for piece in pieces.get(t, ()):
            piece()
        k = t - 3
        if 0 <= k < held:
            _, buffer, first, count, _, column, width, _ = plan[k]
            part = (slice(None), slice(None), pl.ds(first, count), pl.ds(column, width))
            copy = pltpu.make_async_copy(buffers[buffer].at[part], (patch, w)[buffer].at[part], loads.at[k])
            copy.start()
            waiting.append(copy)

    run_gathers(gathers, ahead, tick)


def forward_plan(step=1536, patch_rows=96):
    plan = []
    for first in range(0, 384, patch_rows):
        plan.append((0, 0, first, patch_rows, 0, 0, 768))
    for block in (1, 2):
        column = 0
        for i, width in enumerate((2304, 768, 3072, 3072)):
            for start in range(0, width, step):
                plan.append((4 * block - 3 + i, block, 0, 48, start, column + start, min(step, width - start)))
            column += width
    return tuple(p + (i % 5 != 4,) for i, p in enumerate(plan))


PLAN = forward_plan()


def gather_all(sources, small, rows, segments, ahead=3, plan=PLAN):
    n = len(plan)
    bf, f32 = jnp.bfloat16, jnp.float32
    count = 2 * rows.shape[0]
    outs = [((8, D), f32), ((2,) + rows.shape, bf), ((count, D), f32), ((count, D), bf), ((count, 3 * D), bf),
            ((D // HEAD_DIM, count, count), f32), ((count, D), bf), ((count, D), f32), ((count, D), bf), ((count, 4 * D), f32),
            ((count, 4 * D), bf), ((count, D), f32)]
    shapes = ((4, 4, 384, D), (4, 4, 48, 12 * D))
    return pl.pallas_call(
        functools.partial(gather_kernel, plan, ahead),
        out_shape=[jax.ShapeDtypeStruct(shape, bf) for shape in shapes + shapes[1:]]
        + [jax.ShapeDtypeStruct(*out) for out in outs],
        in_specs=[pl.BlockSpec(memory_space=VMEM)] * 10 + [pl.BlockSpec(memory_space=HBM)] + [pl.BlockSpec(memory_space=VMEM)] * 2,
        out_specs=[pl.BlockSpec(memory_space=HBM)] * 3 + [pl.BlockSpec(memory_space=VMEM)] * len(outs),
        scratch_shapes=[
            pltpu.SemaphoreType.DMA((n, 13)),
            pltpu.SemaphoreType.DMA((n, 13)),
            pltpu.SemaphoreType.DMA((n,)),
            pltpu.VMEM((5, 8, 768), jnp.float32),
            pltpu.VMEM((4, 8, 768), jnp.float32),
            pltpu.SemaphoreType.DMA((4,)),
            pltpu.SemaphoreType.DMA((4,)),
            pltpu.SemaphoreType.DMA((3,)),
            pltpu.VMEM(shapes[0], bf),
            pltpu.VMEM(shapes[1], bf),
            pltpu.SemaphoreType.DMA((n,)),
        ],
        compiler_params=pltpu.CompilerParams(collective_id=0, has_side_effects=True, vmem_limit_bytes=64_000_000),
        name="gather_all",
    )(*sources, small, rows, *segments)


class Total:
    def __init__(self, place, masks, value, arriving, sends, receives, result):
        self.p, self.masks, self.value, self.arriving = place, masks, value, arriving
        self.sends, self.receives, self.result = sends, receives, result
        self.step, self.copy = 0, None

    def advance(self):
        if self.step > len(self.masks):
            return
        if self.copy is not None:
            self.copy.wait()
            i = self.step - 1
            self.value[i + 1] = self.value[i] + self.arriving[i]
        if self.step < len(self.masks):
            i = self.step
            mask = self.masks[i]
            self.copy = pltpu.make_async_remote_copy(
                src_ref=self.value.at[i],
                dst_ref=self.arriving.at[i],
                send_sem=self.sends.at[i],
                recv_sem=self.receives.at[i],
                device_id=self.p.across(mask) if mask else self.p.partner(),
                device_id_type=MESH,
            )
            self.copy.start()
        else:
            self.result[...] = self.value[len(self.masks)]
        self.step += 1


def add(left, right):
    return left.astype(jnp.float32) + right.astype(jnp.float32)


class Reduce:
    def __init__(self, place, held, paired, far, near, line, out, rows, column, width, z_last, sends, receives):
        self.p, self.held, self.from_partner, self.from_far = place, held, paired, far
        self.from_near, self.from_line, self.out, self.rows = near, line, out, rows
        self.z_last, self.sends, self.receives = z_last, sends, receives
        self.half = width // 2
        whole = out.shape[1] // 2
        self.own = pl.ds(column // 2, self.half)
        self.mine = pl.ds(pl.multiple_of(column // 2 + place.core * whole, 128), self.half)
        self.theirs = pl.ds(pl.multiple_of(column // 2 + (1 - place.core) * whole, 128), self.half)
        self.started = []

    def send(self, event, source, target, device):
        copy = pltpu.make_async_remote_copy(
            src_ref=source, dst_ref=target, send_sem=self.sends.at[event], recv_sem=self.receives.at[event],
            device_id=device, device_id_type=MESH,
        )
        copy.start()
        self.started.append(copy)

    def arrived(self, event, target):
        pltpu.make_async_remote_copy(
            src_ref=target, dst_ref=target, send_sem=self.sends.at[event], recv_sem=self.receives.at[event],
            device_id=self.p.partner(), device_id_type=MESH,
        ).wait_recv()

    def pair(self, theirs):
        self.send(0, theirs, self.from_partner, self.p.partner())
        self.paired = self.started.pop()

    def fold(self, plane, others):
        def step(z, _):
            self.held[z, plane] = add(self.held[z, plane], others[z]).astype(jnp.bfloat16)
            return 0

        lax.fori_loop(0, 4, step, 0)

    def one(self):
        p = self.p
        if self.from_partner is not None:
            self.arrived(0, self.from_partner)
            self.fold(p.plane ^ p.far, self.from_partner.at[:, p.plane ^ p.far])
        self.send(1, self.held.at[:, p.plane ^ p.far], self.from_far.at[0], p.across(p.far))
        if self.from_partner is not None:
            self.fold(p.plane ^ 3, self.from_partner.at[:, p.plane ^ 3])
        self.send(2, self.held.at[:, p.plane ^ 3], self.from_far.at[1], p.across(p.far))
        if self.from_partner is not None:
            self.fold(p.plane, self.from_partner.at[:, p.plane])
            self.fold(p.plane ^ p.near, self.from_partner.at[:, p.plane ^ p.near])

    def two(self):
        p = self.p
        self.arrived(2, self.from_far.at[1])
        self.fold(p.plane ^ p.near, self.from_far.at[1])
        if self.z_last:
            self.send(3, self.held.at[:, p.plane ^ p.near], self.from_near, p.across(p.near))
        else:
            for j in (1, 2, 3):
                self.send(6 + j, self.held.at[p.z ^ j, p.plane ^ p.near], self.from_line.at[2 + j], p.across(4 * j))
        self.arrived(1, self.from_far.at[0])
        self.fold(p.plane, self.from_far.at[0])
        if not self.z_last:
            for j in (1, 2, 3):
                self.send(3 + j, self.held.at[p.z ^ j, p.plane], self.from_line.at[j - 1], p.across(4 * j))

    def three(self):
        p = self.p
        if self.z_last:
            self.arrived(3, self.from_near)
            self.fold(p.plane, self.from_near)
            for j in (1, 2, 3):
                self.send(3 + j, self.held.at[p.z ^ j, p.plane], self.from_line.at[j - 1], p.across(4 * j))
        else:
            for j in (1, 2, 3):
                self.arrived(6 + j, self.from_line.at[2 + j])
            near = (add(self.held[p.z, p.plane ^ p.near], self.from_line[3]) + add(self.from_line[4], self.from_line[5]))
            self.held[p.z, p.plane ^ p.near] = near.astype(jnp.bfloat16)
            self.send(3, self.held.at[p.z, p.plane ^ p.near], self.from_near.at[0], p.across(p.near))

    def four(self):
        p = self.p
        for j in (1, 2, 3):
            self.arrived(3 + j, self.from_line.at[j - 1])
        total = add(self.held[p.z, p.plane], self.from_line[0]) + add(self.from_line[1], self.from_line[2])
        if not self.z_last:
            self.arrived(3, self.from_near.at[0])
            total = total + self.from_near[0].astype(jnp.float32)
        self.out[self.rows, self.mine] = total
        view = self.out.at[self.rows, self.mine]
        self.send(10, view, view, p.partner())

    def drain(self):
        for copy in self.started:
            copy.wait_send()
        self.started = []

    def five(self):
        self.arrived(10, self.out.at[self.rows, self.theirs])


def backward_plan(step=1536, patch_rows=96):
    plan = []
    for array, width in ((6, 768), (8, 3072), (7, 3072), (5, 2304), (4, 3072), (3, 3072), (2, 768), (1, 2304)):
        for start in range(0, width, step):
            plan.append((array, 0, 48, start, min(step, width - start)))
    for first in range(0, 384, patch_rows):
        plan.append((0, first, patch_rows, 0, 768))
    return tuple(p + (i % 5 != 4,) for i, p in enumerate(plan))


BACK_PLAN = backward_plan()
SLOTS = 8
LAGS = (2, 3, 4, 5)
ARRAYS = 9


def reduce_kernel(plan, patch, lefts, rights, small, outs, small_out, slots, pairs, fars, nears, lines, staging, left_held,
                  right_held, sends, receives, loads, left_sems, right_sems, value, arriving, small_sends, small_receives):
    place = Place()
    enter(place, MASKS)
    n = len(plan)
    value[0] = small[...]
    total = Total(place, (0, 1, 2, 4, 8), value, arriving, small_sends, small_receives, small_out)
    used = [0, 0]
    reduces, copies, staged, steps, order = [], {}, [], [], []
    for k, (array, first, rows, column, width, z_last) in enumerate(plan):
        kind = 0 if array == 0 else 1
        slot = used[kind] % SLOTS
        used[kind] += 1
        half = width // 2
        cut = (lambda ref, half=half: ref if half == ref.shape[-1] else ref.at[..., pl.ds(0, half)])
        r = Reduce(place, cut(slots[kind].at[slot]), cut(pairs.at[used[kind] - 1]) if array > 4 else None, cut(fars[kind].at[used[kind] - 1]),
                   cut(nears[kind].at[used[kind] - 1]), cut(lines[kind].at[used[kind] - 1]), outs[array],
                   pl.ds(first, rows), column, width, z_last, sends.at[k], receives.at[k])
        r.staging = cut(staging.at[(used[kind] - 1) % 2])
        r.paired = None
        reduces.append(r)
        if array > 4:
            steps.append((k, r.theirs))
        if array:
            steps.append((k, r.mine))
            if array not in order:
                order.append(array)

    def left_view(index):
        return left_held.at[index % 2, pl.ds(0, lefts[order[index] - 1].shape[0])]

    def left_copy(index):
        return pltpu.make_async_copy(lefts[order[index] - 1], left_view(index), left_sems.at[index % 2])

    def right_view(index):
        k = steps[index][0]
        return right_held.at[index % 3, pl.ds(0, rights[plan[k][0] - 1].shape[0]), pl.ds(0, reduces[k].half)]

    def right_copy(index):
        k, columns = steps[index]
        return pltpu.make_async_copy(rights[plan[k][0] - 1].at[:, columns], right_view(index), right_sems.at[index % 3])

    done, begun = [0], [0]

    def make(target, k):
        index = done[0]
        if plan[k][0] != order[begun[0] - 1] or begun[0] == 0:
            left_copy(begun[0]).wait()
            begun[0] += 1
            if begun[0] < len(order):
                left_copy(begun[0]).start()
        left, right = left_view(begun[0] - 1), right_view(index)
        right_copy(index).wait()
        rows = D // 2

        def part(i, _):
            columns = pl.ds(pl.multiple_of(i * rows, 128), rows)
            term = left_product(left[:, columns], right[...]).astype(jnp.bfloat16)
            target[pl.ds(i * 2, 2)] = term.reshape((2,) + target.shape[1:])
            return 0

        lax.fori_loop(0, 2, part, 0)
        done[0] += 1
        if index + 3 < len(steps):
            right_copy(index + 3).start()

    left_copy(0).start()
    for index in range(3):
        right_copy(index).start()

    def load(k):
        array = plan[k][0]
        r = reduces[k]
        if k - SLOTS >= 0:
            reduces[k - SLOTS].drain()
        if array == 0:
            copies[k] = pltpu.make_async_copy(patch.at[:, :, r.rows, r.own], r.held, loads.at[k])
            copies[k].start()
            return
        if array > 4:
            if len(staged) > 1:
                staged[-2].paired.wait_send()
            make(r.staging, k)
            r.pair(r.staging)
            staged.append(r)
        make(r.held, k)

    load(0)
    for t in range(n + LAGS[-1]):
        if t + 1 < n:
            load(t + 1)
        if t < n:
            if t in copies:
                copies[t].wait()
            reduces[t].one()
        for lag, name in zip(LAGS, ("two", "three", "four", "five")):
            if 0 <= t - lag < n:
                getattr(reduces[t - lag], name)()
        total.advance()
    for r in reduces:
        r.drain()
    for r in staged[-2:]:
        r.paired.wait_send()


def reduce_all(patch, terms, small, plan=BACK_PLAN):
    n = len(plan)
    bf = jnp.bfloat16
    counts = [sum(p[0] == 0 for p in plan), sum(p[0] > 0 for p in plan), sum(p[0] > 4 for p in plan)]
    shapes = tuple((max(p[2] for p in plan if c(p[0])), max(p[4] for p in plan if c(p[0])) // 2) for c in (lambda a: a == 0, lambda a: a > 0))

    inputs = 2 * ARRAYS

    def kernel(*refs):
        patch, lefts, rights, small = refs[0], refs[1:ARRAYS], refs[ARRAYS : inputs - 1], refs[inputs - 1]
        outs, small_out = refs[inputs : inputs + ARRAYS], refs[inputs + ARRAYS]
        pairs, rest = refs[inputs + ARRAYS + 1], refs[inputs + ARRAYS + 2 :]
        slots, fars, nears, lines = (rest[2 * i : 2 * i + 2] for i in range(4))
        reduce_kernel(plan, patch, lefts, rights, small, outs, small_out, slots, pairs, fars, nears, lines, *rest[8:])

    scratch = [pltpu.VMEM((counts[2], 4, 4) + shapes[1], bf)]
    scratch += [pltpu.VMEM((min(SLOTS, counts[i]), 4, 4) + shapes[i], bf) for i in (0, 1)]
    for lead in ((2, 4), (4,), (6,)):
        scratch += [pltpu.VMEM((counts[i],) + lead + shapes[i], bf) for i in (0, 1)]
    depth = max(left.shape[0] for left, _ in terms)
    scratch += [
        pltpu.VMEM((2, 4, 4) + shapes[1], bf),
        pltpu.VMEM((2, depth, D), bf),
        pltpu.VMEM((3, depth, shapes[1][1]), bf),
        pltpu.SemaphoreType.DMA((n, 11)),
        pltpu.SemaphoreType.DMA((n, 11)),
        pltpu.SemaphoreType.DMA((n,)),
        pltpu.SemaphoreType.DMA((2,)),
        pltpu.SemaphoreType.DMA((3,)),
        pltpu.VMEM((6, 8, 768), jnp.float32),
        pltpu.VMEM((5, 8, 768), jnp.float32),
        pltpu.SemaphoreType.DMA((5,)),
        pltpu.SemaphoreType.DMA((5,)),
    ]
    patch = patch.reshape(4, 4, patch.shape[0] // 16, patch.shape[1])
    outs = [(patch.shape[2], 2 * patch.shape[3])] + [(left.shape[1] // 16, right.shape[1]) for left, right in terms] + [(8, 768)]
    return pl.pallas_call(
        kernel,
        out_shape=[jax.ShapeDtypeStruct(out, jnp.float32) for out in outs],
        in_specs=[pl.BlockSpec(memory_space=HBM)] * (inputs - 1) + [pl.BlockSpec(memory_space=VMEM)],
        out_specs=[pl.BlockSpec(memory_space=VMEM)] * (ARRAYS + 1),
        scratch_shapes=scratch,
        compiler_params=pltpu.CompilerParams(collective_id=1, has_side_effects=True, vmem_limit_bytes=67_000_000),
        name="reduce_all",
    )(patch, *[left for left, _ in terms], *[right for _, right in terms], small)


def fast_body(byte_inputs, segment_ids, cotangent, patch_weight, *weights):
    coarse, fine = weights[:8], weights[8:]
    core, at = lax.axis_index("seq"), lax.axis_index("fsdp")
    vectors = jnp.stack([w[i] for w in (coarse, fine) for i in (0, 1, 4, 5)]).astype(jnp.float32)
    small = lax.dynamic_update_slice(jnp.zeros((8, D), jnp.float32), vectors, (0, at * vectors.shape[1]))
    sources = [patch_weight]
    for w in (coarse, fine):
        sources += [w[2], w[3].T, w[6], w[7].T]
    byte_rows = byte_inputs[0]
    bytes_here = byte_rows.shape[0]
    patches = bytes_here // PATCH
    segment_row = segment_ids[0]
    all_patches = segment_row.shape[0]
    patch_full, coarse_full, fine_full, small, all_rows, *stored, coarse_out = gather_all(
        sources, small, byte_rows.reshape(patches, PATCH * D), (segment_row[None], segment_row[:, None])
    )
    patch_full = patch_full.reshape(-1, D)

    def mine(values):
        width = values.shape[1] // 2
        return lax.dynamic_slice_in_dim(values, core * width, width, 1)

    embedded, coarse_normed, coarse_triple, chances, coarse_mixture, coarse_middle, coarse_second, lifted, coarse_hidden = stored
    grouped_bytes = all_rows.reshape(all_patches, PATCH * D)
    coarse_low = coarse_out.astype(jnp.bfloat16)
    joined = jnp.concatenate([jnp.zeros((1,), bool), segment_row[1:] == segment_row[:-1]]).astype(jnp.float32)[:, None]
    previous = jnp.concatenate([jnp.zeros((1, D), jnp.bfloat16), coarse_low[:-1]]).astype(jnp.float32) * joined
    previous = lax.dynamic_slice_in_dim(previous, core * patches, patches)
    (layer_rows, grad_fine_in, grad_previous, fine_vectors, normed, mixture, second, hidden, grad_middle, grad_lifted,
     grad_triple) = fine_block(byte_rows, previous, cotangent[0], small, fine_full.reshape(D, -1))
    fine_terms = [(normed, grad_triple), (grad_middle, mixture), (second, grad_lifted), (cotangent[0], hidden)]
    grad_previous = lax.all_gather(grad_previous, "seq", axis=0, tiled=True) * joined
    grad_coarse_out = jnp.concatenate([grad_previous[1:], jnp.zeros((1, D), jnp.float32)])
    grad_branch, coarse_grad_lifted, grad_attended, coarse_grad_triple, grad_embed_low, coarse_vectors, input_gradient = coarse_block_back(
        grad_coarse_out, embedded, coarse_middle, lifted, coarse_triple, chances, small, coarse_full.reshape(D, -1), patch_full,
        grad_fine_in,
    )
    grad_patch = left_product(grouped_bytes, mine(grad_embed_low)).astype(jnp.bfloat16)
    coarse_terms = [
        (coarse_normed, coarse_grad_triple), (grad_attended, coarse_mixture), (coarse_second, coarse_grad_lifted),
        (grad_branch, coarse_hidden),
    ]
    once = (core == 0).astype(jnp.float32)
    small = coarse_vectors * once + fine_vectors
    *shards, small = reduce_all(grad_patch, coarse_terms + fine_terms, small)
    small = lax.dynamic_slice_in_dim(small, at * vectors.shape[1], vectors.shape[1], 1)

    def gradients(parts, first):
        return (small[first], small[first + 1], parts[0], parts[1].T, small[first + 2], small[first + 3], parts[2], parts[3].T)

    return (layer_rows[None], input_gradient[None], shards[0]) + gradients(shards[1:5], 0) + gradients(shards[5:], 4)


def normalize(values):
    centred = values - jnp.mean(values, -1, keepdims=True)
    scale = lax.rsqrt(jnp.mean(centred * centred, -1, keepdims=True) + epsilon)
    return centred * scale, scale


def normalize_back(grad, unit, scale, norm_gain):
    scaled = grad * norm_gain
    return scale * (
        scaled - jnp.mean(scaled, -1, keepdims=True) - unit * jnp.mean(scaled * unit, -1, keepdims=True)
    )


def gate_both(values):
    root = math.sqrt(2.0 / math.pi)
    square = values * values
    bend = jnp.tanh(root * values * (1.0 + 0.044715 * square))
    half = 0.5 + 0.5 * bend
    slope = half + 0.5 * values * (1.0 - bend * bend) * (root * (1.0 + 3.0 * 0.044715 * square))
    return values * half, slope


def head_lanes(pair):
    lane = lax.broadcasted_iota(jnp.int32, pair.shape, 1)
    zero = jnp.zeros_like(pair)
    return jnp.where(lane < HEAD_DIM, pair, zero), jnp.where(lane < HEAD_DIM, zero, pair)


def chances_of(queries, keys, allowed):
    scores = right_product(queries, keys) * (1.0 / math.sqrt(HEAD_DIM))
    scores = jnp.where(allowed, scores, -1e30)
    powers = jnp.exp(scores - jnp.max(scores, -1, keepdims=True))
    return powers * (1.0 / jnp.sum(powers, -1, keepdims=True))


TILE = 128
PAIRS = 6


def fine_kernel(byte_ref, previous_ref, cotangent_ref, small_ref, w_ref,
                out_ref, grad_in_ref, patch_grad_ref, vectors_ref,
                normed_ref, mixture_ref, second_ref, hidden_ref, low_ref, lifted_grad_ref, triple_grad_ref,
                triple, chances, result, grad_second):
    rows = byte_ref.shape[0]
    bf = jnp.bfloat16
    first_gain, first_bias, second_gain, second_bias = (small_ref[i : i + 1] for i in (4, 5, 6, 7))
    previous = previous_ref[...]
    inputs = (
        byte_ref[...].astype(jnp.float32).reshape(rows // PATCH, PATCH, D) + previous[:, None, :]
    ).reshape(rows, D)
    unit_one, scale_one = normalize(inputs)
    normed = (unit_one * first_gain + first_bias).astype(bf)
    normed_ref[...] = normed
    triple[...] = product(normed, w_ref[:, : 3 * D]).astype(bf)
    row = lax.broadcasted_iota(jnp.int32, (TILE, TILE), 0)
    column = lax.broadcasted_iota(jnp.int32, (TILE, TILE), 1)
    allowed = (row // PATCH == column // PATCH) & (column <= row)
    tiles = rows // TILE

    def attend(pair, _):
        lanes = [pl.ds(pl.multiple_of(i * D + pair * 128, 128), 128) for i in range(3)]
        for tile in range(tiles):
            here = slice(tile * TILE, tile * TILE + TILE)
            queries = head_lanes(triple[here, lanes[0]])
            keys = triple[here, lanes[1]]
            values = head_lanes(triple[here, lanes[2]])
            mixed = None
            for head in range(2):
                found = chances_of(queries[head], keys, allowed)
                chances[pair * 2 + head, here] = found
                term = product(found.astype(bf), values[head])
                mixed = term if mixed is None else mixed + term
            mixture_ref[here, lanes[0]] = mixed.astype(bf)
        return 0

    lax.fori_loop(0, PAIRS, attend, 0)
    middle = inputs + right_product(mixture_ref[...], w_ref[:, 3 * D : 4 * D])
    unit_two, scale_two = normalize(middle)
    second = (unit_two * second_gain + second_bias).astype(bf)
    second_ref[...] = second
    grad_low = cotangent_ref[...]
    result[...] = middle
    for j in range(4):
        here = slice(j * D, j * D + D)
        expand = w_ref[:, 4 * D + j * D : 5 * D + j * D]
        narrow_t = w_ref[:, 8 * D + j * D : 9 * D + j * D]
        hidden, slope = gate_both(product(second, expand))
        hidden = hidden.astype(bf)
        hidden_ref[:, here] = hidden
        lifted_grad = (product(grad_low, narrow_t) * slope).astype(bf)
        lifted_grad_ref[:, here] = lifted_grad
        result[...] += right_product(hidden, narrow_t)
        term = right_product(lifted_grad, expand)
        if j:
            grad_second[...] += term
        else:
            grad_second[...] = term
    out_ref[...] = result[...].astype(bf)
    grad_two = grad_second[...]
    grad_middle = grad_low.astype(jnp.float32) + normalize_back(grad_two, unit_two, scale_two, second_gain)
    low = grad_middle.astype(bf)
    low_ref[...] = low
    grad_second[...] = grad_middle
    grad_mixture = product(low, w_ref[:, 3 * D : 4 * D]).astype(bf)
    result[...] = grad_mixture.astype(jnp.float32)

    def attend_back(pair, _):
        lanes = [pl.ds(pl.multiple_of(i * D + pair * 128, 128), 128) for i in range(3)]
        factor = 1.0 / math.sqrt(HEAD_DIM)
        for tile in range(tiles):
            here = slice(tile * TILE, tile * TILE + TILE)
            queries = head_lanes(triple[here, lanes[0]])
            keys = head_lanes(triple[here, lanes[1]])
            values = triple[here, lanes[2]]
            mixed = head_lanes(result[here, lanes[0]].astype(bf))
            sums = [None, None, None]
            for head in range(2):
                found = chances[pair * 2 + head, here]
                grad = right_product(mixed[head], values)
                scores = (found * (grad - jnp.sum(grad * found, -1, keepdims=True))).astype(bf)
                terms = (
                    product(scores, keys[head]),
                    left_product(scores, queries[head]),
                    left_product(found.astype(bf), mixed[head]),
                )
                sums = [t if s is None else s + t for s, t in zip(sums, terms)]
            triple_grad_ref[here, lanes[0]] = (sums[0] * factor).astype(bf)
            triple_grad_ref[here, lanes[1]] = (sums[1] * factor).astype(bf)
            triple_grad_ref[here, lanes[2]] = sums[2].astype(bf)
        return 0

    lax.fori_loop(0, PAIRS, attend_back, 0)
    grad_one = right_product(triple_grad_ref[...], w_ref[:, : 3 * D])
    grad_in = grad_second[...] + normalize_back(grad_one, unit_one, scale_one, first_gain)
    grad_in_ref[...] = grad_in
    patch_grad_ref[...] = jnp.sum(grad_in.reshape(rows // PATCH, PATCH, D), 1)
    terms = [jnp.sum(t, 0, keepdims=True) for t in (grad_one * unit_one, grad_one, grad_two * unit_two, grad_two)]

    @pl.when(pl.program_id(0) == 0)
    def _():
        vectors_ref[...] = jnp.zeros_like(vectors_ref)

    for i, term in enumerate(terms):
        vectors_ref[4 + i : 5 + i] += term


def fine_block(byte_rows, previous, cotangent, small, full, rows=256):
    count = byte_rows.shape[0]
    bf, f32 = jnp.bfloat16, jnp.float32

    def spec(height, width):
        return pl.BlockSpec((height, width), lambda i: (i, 0))

    def whole(shape):
        return pl.BlockSpec(shape, lambda i: (0, 0), pipeline_mode=pl.Buffered(1))

    outs = [(rows, D, bf), (rows, D, f32), (rows // PATCH, D, f32), None]
    outs += [(rows, D, bf)] * 3 + [(rows, 4 * D, bf), (rows, D, bf), (rows, 4 * D, bf), (rows, 3 * D, bf)]
    steps = count // rows
    return pl.pallas_call(
        fine_kernel,
        grid=(steps,),
        out_shape=[
            jax.ShapeDtypeStruct((o[0] * steps, o[1]), o[2]) if o else jax.ShapeDtypeStruct((8, D), f32) for o in outs
        ],
        in_specs=[spec(rows, D), spec(rows // PATCH, D), spec(rows, D), whole((8, D)), whole(full.shape)],
        out_specs=[spec(o[0], o[1]) if o else pl.BlockSpec((8, D), lambda i: (0, 0)) for o in outs],
        scratch_shapes=[
            pltpu.VMEM((rows, 3 * D), bf),
            pltpu.VMEM((2 * PAIRS, rows, TILE), f32),
            pltpu.VMEM((rows, D), f32),
            pltpu.VMEM((rows, D), f32),
        ],
        compiler_params=pltpu.CompilerParams(dimension_semantics=("arbitrary",), vmem_limit_bytes=64_000_000),
        name="fine_block",
    )(byte_rows, previous, cotangent, small, full)


def coarse_kernel(grad_ref, embedded_ref, middle_ref, lifted_ref, triple, chances, small_ref, w_hbm, patch_hbm, bytes_hbm,
                  branch_ref, lifted_grad_ref, low_ref, triple_grad_ref, embed_ref, vectors_ref, out_ref,
                  w, patch, byte_grad, spread, mixed_ref, grad_second, sems):
    bf = jnp.bfloat16
    core = lax.axis_index("seq")
    parts = ((8 * D, 4 * D), (4 * D, 4 * D), (3 * D, D), (0, 3 * D))
    copies = [
        pltpu.make_async_copy(w_hbm.at[:, pl.ds(*part)], w.at[:, pl.ds(*part)], sems.at[i]) for i, part in enumerate(parts)
    ]
    copies.append(pltpu.make_async_copy(patch_hbm, patch, sems.at[4]))
    copies.append(pltpu.make_async_copy(bytes_hbm, byte_grad, sems.at[5]))
    for copy in copies:
        copy.start()
    first_gain, second_gain = small_ref[0:1], small_ref[2:3]
    branch = grad_ref[...].astype(bf)
    branch_ref[...] = branch
    unit_two, scale_two = normalize(middle_ref[...])
    copies[0].wait()
    copies[1].wait()
    for j in range(4):
        here = slice(j * D, j * D + D)
        _, slope = gate_both(lifted_ref[:, here])
        lifted_grad = (product(branch, w[:, 8 * D + j * D : 9 * D + j * D]) * slope).astype(bf)
        lifted_grad_ref[:, here] = lifted_grad
        term = right_product(lifted_grad, w[:, 4 * D + j * D : 5 * D + j * D])
        if j:
            grad_second[...] += term
        else:
            grad_second[...] = term
    grad_two = grad_second[...]
    grad_middle = grad_ref[...] + normalize_back(grad_two, unit_two, scale_two, second_gain)
    low = grad_middle.astype(bf)
    low_ref[...] = low
    copies[2].wait()
    mixed_ref[...] = product(low, w[:, 3 * D : 4 * D]).astype(bf)

    def attend_back(pair, _):
        lanes = [pl.ds(pl.multiple_of(i * D + pair * 128, 128), 128) for i in range(3)]
        factor = 1.0 / math.sqrt(HEAD_DIM)
        queries = head_lanes(triple[:, lanes[0]])
        keys = head_lanes(triple[:, lanes[1]])
        values = triple[:, lanes[2]]
        mixed = head_lanes(mixed_ref[:, lanes[0]])
        sums = [None, None, None]
        for head in range(2):
            found = chances[pair * 2 + head]
            grad = right_product(mixed[head], values)
            scores = (found * (grad - jnp.sum(grad * found, -1, keepdims=True))).astype(bf)
            terms = (
                product(scores, keys[head]),
                left_product(scores, queries[head]),
                left_product(found.astype(bf), mixed[head]),
            )
            sums = [t if s is None else s + t for s, t in zip(sums, terms)]
        triple_grad_ref[:, lanes[0]] = (sums[0] * factor).astype(bf)
        triple_grad_ref[:, lanes[1]] = (sums[1] * factor).astype(bf)
        triple_grad_ref[:, lanes[2]] = sums[2].astype(bf)
        return 0

    lax.fori_loop(0, PAIRS, attend_back, 0)
    copies[3].wait()
    grad_one = right_product(triple_grad_ref[...], w[:, : 3 * D])
    unit_one, scale_one = normalize(embedded_ref[...])
    embed_ref[...] = (grad_middle + normalize_back(grad_one, unit_one, scale_one, first_gain)).astype(bf)
    terms = [grad_one * unit_one, grad_one, grad_two * unit_two, grad_two]
    vectors_ref[...] = jnp.concatenate([jnp.sum(t, 0, keepdims=True) for t in terms] + [jnp.zeros((4, D), jnp.float32)], 0)
    patches = byte_grad.shape[0] // PATCH
    rows = embed_ref[pl.ds(pl.multiple_of(core * patches, 128), patches)]
    copies[4].wait()
    copies[5].wait()
    for i in range(PATCH):
        term = right_product(rows, patch[i * D : i * D + D])
        for j in range(D // 128):
            spread[j, pl.ds(i, patches, stride=PATCH)] = term[:, j * 128 : j * 128 + 128]
    for j in range(D // 128):
        here = slice(j * 128, j * 128 + 128)
        out_ref[:, here] = (byte_grad[:, here] + spread[j]).astype(bf)


def coarse_block_back(grad, embedded, middle, lifted, triple, chances, small, full, patch, byte_grad):
    count = grad.shape[0]
    bf, f32 = jnp.bfloat16, jnp.float32
    outs = [((count, D), bf), ((count, 4 * D), bf), ((count, D), bf), ((count, 3 * D), bf), ((count, D), bf), ((8, D), f32),
            (byte_grad.shape, bf)]
    return pl.pallas_call(
        coarse_kernel,
        out_shape=[jax.ShapeDtypeStruct(*out) for out in outs],
        in_specs=[pl.BlockSpec(memory_space=VMEM)] * 7 + [pl.BlockSpec(memory_space=HBM)] * 3,
        out_specs=[pl.BlockSpec(memory_space=VMEM)] * len(outs),
        scratch_shapes=[
            pltpu.VMEM(full.shape, bf),
            pltpu.VMEM(patch.shape, bf),
            pltpu.VMEM(byte_grad.shape, f32),
            pltpu.VMEM((D // 128, byte_grad.shape[0], 128), f32),
            pltpu.VMEM((count, D), bf),
            pltpu.VMEM((count, D), f32),
            pltpu.SemaphoreType.DMA((6,)),
        ],
        compiler_params=pltpu.CompilerParams(vmem_limit_bytes=64_000_000),
        name="coarse_block_back",
    )(grad, embedded, middle, lifted, triple, chances, small, full, patch, byte_grad)


def solution(mesh):
    return jax.shard_map(
        fast_body if (mesh.shape["seq"], mesh.shape["fsdp"]) == (2, 16) else body,
        mesh=mesh,
        in_specs=(
            P("fsdp", "seq", None),
            P("fsdp", None),
            P("fsdp", "seq", None),
            P("fsdp", None),
            P("fsdp"),
            P("fsdp"),
            P("fsdp", None),
            P(None, "fsdp"),
            P("fsdp"),
            P("fsdp"),
            P("fsdp", None),
            P(None, "fsdp"),
            P("fsdp"),
            P("fsdp"),
            P("fsdp", None),
            P(None, "fsdp"),
            P("fsdp"),
            P("fsdp"),
            P("fsdp", None),
            P(None, "fsdp"),
        ),
        out_specs=(
            P("fsdp", "seq", None),
            P("fsdp", "seq", None),
            P("fsdp", None),
            P("fsdp"),
            P("fsdp"),
            P("fsdp", None),
            P(None, "fsdp"),
            P("fsdp"),
            P("fsdp"),
            P("fsdp", None),
            P(None, "fsdp"),
            P("fsdp"),
            P("fsdp"),
            P("fsdp", None),
            P(None, "fsdp"),
            P("fsdp"),
            P("fsdp"),
            P("fsdp", None),
            P(None, "fsdp"),
        ),
        check_vma=False,
    )
```

```python
import functools
import math

import jax
import jax.numpy as jnp
from jax import lax
from jax.experimental import pallas as pl
from jax.experimental.pallas import tpu as pltpu
from jax.sharding import PartitionSpec as P


D = 768
HEAD_DIM = 64
PATCH = 8


epsilon = 1e-05


def shifted(block, axis, distance):
    devices = range(lax.axis_size(axis))
    route = [(i - distance, i) for i in devices if i - distance in devices]
    return lax.ppermute(block, axis, route)


def layer_norm(values, norm_gain, norm_bias):
    center = jnp.mean(values, -1, keepdims=True)
    centred = values - center
    spread = jnp.mean(centred * centred, -1, keepdims=True)
    return centred * lax.rsqrt(spread + epsilon) * norm_gain + norm_bias


def smooth_gate(values):
    return jax.nn.gelu(values, approximate=True)


def product(left_side, right_side):
    return jnp.dot(left_side, right_side, preferred_element_type=jnp.float32)


def left_product(left_side, right_side):
    return lax.dot_general(
        left_side, right_side, (((0,), (0,)), ((), ())), preferred_element_type=jnp.float32
    )


def right_product(left_side, right_side):
    return lax.dot_general(
        left_side, right_side, (((1,), (1,)), ((), ())), preferred_element_type=jnp.float32
    )


def attend_forward(queries, key_part, value_part, allowed):
    factor = 1.0 / math.sqrt(HEAD_DIM)
    scores = (
        jnp.einsum("bqhd,bkhd->bhqk", queries, key_part, preferred_element_type=jnp.float32)
        * factor
    )
    scores = jnp.where(allowed[:, None], scores, -1e30)
    highest = jnp.max(scores, -1, keepdims=True)
    log_total = highest + jnp.log(jnp.sum(jnp.exp(scores - highest), -1, keepdims=True))
    rounded = jnp.exp(scores - log_total).astype(jnp.bfloat16)
    mixture = jnp.einsum("bhqk,bkhd->bqhd", rounded, value_part, preferred_element_type=jnp.float32)
    return (mixture, log_total)


def attend_backward(queries, key_part, value_part, allowed, log_total, grad_mixture):
    factor = 1.0 / math.sqrt(HEAD_DIM)
    scores = (
        jnp.einsum("bqhd,bkhd->bhqk", queries, key_part, preferred_element_type=jnp.float32)
        * factor
    )
    scores = jnp.where(allowed[:, None], scores, -1e30)
    chances = jnp.exp(scores - log_total)
    rounded = chances.astype(jnp.bfloat16)
    grad_values = jnp.einsum(
        "bhqk,bqhd->bkhd", rounded, grad_mixture, preferred_element_type=jnp.float32
    )
    grad_chances = jnp.einsum(
        "bqhd,bkhd->bhqk", grad_mixture, value_part, preferred_element_type=jnp.float32
    )
    grad_scores = (
        chances * (grad_chances - jnp.sum(grad_chances * chances, -1, keepdims=True))
    ).astype(jnp.bfloat16)
    grad_queries = (
        jnp.einsum("bhqk,bkhd->bqhd", grad_scores, key_part, preferred_element_type=jnp.float32)
        * factor
    )
    grad_keys = (
        jnp.einsum("bhqk,bqhd->bkhd", grad_scores, queries, preferred_element_type=jnp.float32)
        * factor
    )
    return (grad_queries, grad_keys, grad_values)


def block_forward(inputs, weights, attend):
    first_gain, first_bias, project, output, second_gain, second_bias, expand, narrow = weights
    normed = layer_norm(
        inputs, first_gain.astype(jnp.float32), first_bias.astype(jnp.float32)
    ).astype(jnp.bfloat16)
    triple = product(normed, project).astype(jnp.bfloat16)
    mixture, attend_stored = attend(triple)
    middle = inputs + product(mixture, output)
    second = layer_norm(
        middle, second_gain.astype(jnp.float32), second_bias.astype(jnp.float32)
    ).astype(jnp.bfloat16)
    lifted = product(second, expand)
    hidden = smooth_gate(lifted).astype(jnp.bfloat16)
    result = middle + product(hidden, narrow)
    stored = (inputs, normed, attend_stored, mixture, middle, second, lifted, hidden)
    return (result, stored)


def block_backward(grad_result, weights, stored, attend_back):
    first_gain, first_bias, project, output, second_gain, second_bias, expand, narrow = weights
    inputs, normed, attend_stored, mixture, middle, second, lifted, hidden = stored
    grad_branch = grad_result.astype(jnp.bfloat16)
    grad_narrow = left_product(hidden, grad_branch)
    grad_hidden = right_product(grad_branch, narrow)
    grad_lifted = jax.vjp(smooth_gate, lifted)[1](grad_hidden)[0].astype(jnp.bfloat16)
    grad_expand = left_product(second, grad_lifted)
    grad_second = right_product(grad_lifted, expand)
    pullback = jax.vjp(
        layer_norm, middle, second_gain.astype(jnp.float32), second_bias.astype(jnp.float32)
    )[1]
    grad_middle, grad_gain_two, grad_bias_two = pullback(grad_second)
    grad_middle = grad_middle + grad_result
    grad_attended = grad_middle.astype(jnp.bfloat16)
    grad_output = left_product(mixture, grad_attended)
    grad_mixture = right_product(grad_attended, output).astype(jnp.bfloat16)
    grad_triple = attend_back(grad_mixture, attend_stored)
    grad_project = left_product(normed, grad_triple)
    grad_normed = right_product(grad_triple, project)
    pullback = jax.vjp(
        layer_norm, inputs, first_gain.astype(jnp.float32), first_bias.astype(jnp.float32)
    )[1]
    grad_inputs, grad_gain_one, grad_bias_one = pullback(grad_normed)
    grad_inputs = grad_inputs + grad_middle
    return (
        grad_inputs,
        (
            grad_gain_one,
            grad_bias_one,
            grad_project,
            grad_output,
            grad_gain_two,
            grad_bias_two,
            grad_expand,
            grad_narrow,
        ),
    )


def body(
    byte_inputs,
    segment_ids,
    cotangent,
    patch_weight,
    coarse_first_gain,
    coarse_first_bias,
    coarse_project,
    coarse_output,
    coarse_second_gain,
    coarse_second_bias,
    coarse_expand,
    coarse_narrow,
    fine_first_gain,
    fine_first_bias,
    fine_project,
    fine_output,
    fine_second_gain,
    fine_second_bias,
    fine_expand,
    fine_narrow,
):
    coarse_full = (
        lax.all_gather(patch_weight, "fsdp", axis=0, tiled=True),
        lax.all_gather(coarse_first_gain, "fsdp", axis=0, tiled=True),
        lax.all_gather(coarse_first_bias, "fsdp", axis=0, tiled=True),
        lax.all_gather(coarse_project, "fsdp", axis=0, tiled=True),
        lax.all_gather(coarse_output, "fsdp", axis=1, tiled=True),
        lax.all_gather(coarse_second_gain, "fsdp", axis=0, tiled=True),
        lax.all_gather(coarse_second_bias, "fsdp", axis=0, tiled=True),
        lax.all_gather(coarse_expand, "fsdp", axis=0, tiled=True),
        lax.all_gather(coarse_narrow, "fsdp", axis=1, tiled=True),
    )
    fine_full = (
        lax.all_gather(fine_first_gain, "fsdp", axis=0, tiled=True),
        lax.all_gather(fine_first_bias, "fsdp", axis=0, tiled=True),
        lax.all_gather(fine_project, "fsdp", axis=0, tiled=True),
        lax.all_gather(fine_output, "fsdp", axis=1, tiled=True),
        lax.all_gather(fine_second_gain, "fsdp", axis=0, tiled=True),
        lax.all_gather(fine_second_bias, "fsdp", axis=0, tiled=True),
        lax.all_gather(fine_expand, "fsdp", axis=0, tiled=True),
        lax.all_gather(fine_narrow, "fsdp", axis=1, tiled=True),
    )
    byte_rows = byte_inputs[0]
    bytes_here = byte_rows.shape[0]
    patches = bytes_here // PATCH
    segment_row = segment_ids[0]
    all_patches = segment_row.shape[0]
    places = jnp.arange(all_patches)
    coarse_allowed = (
        (places[:, None] >= places[None, :]) & (segment_row[:, None] == segment_row[None, :])
    )[None]
    inner = jnp.arange(PATCH)
    fine_allowed = (inner[:, None] >= inner[None, :])[None]

    def coarse_attend(triple):
        head_block = lax.all_to_all(
            triple.reshape(patches, 3, D), "seq", split_axis=2, concat_axis=0, tiled=True
        )
        all_rows = head_block.shape[0]
        columns = head_block.shape[2]
        local_heads = columns // HEAD_DIM
        queries = head_block[:, 0].reshape(1, all_rows, local_heads, HEAD_DIM)
        key_part = head_block[:, 1].reshape(1, all_rows, local_heads, HEAD_DIM)
        value_part = head_block[:, 2].reshape(1, all_rows, local_heads, HEAD_DIM)
        mixture, log_total = attend_forward(queries, key_part, value_part, coarse_allowed)
        merged = mixture.reshape(all_rows, columns).astype(jnp.bfloat16)
        back_rows = lax.all_to_all(merged, "seq", split_axis=0, concat_axis=1, tiled=True)
        return (back_rows, (queries, key_part, value_part, log_total))

    def coarse_back(grad_mixture, stored):
        queries, key_part, value_part, log_total = stored
        head_grad = lax.all_to_all(grad_mixture, "seq", split_axis=1, concat_axis=0, tiled=True)
        all_rows = head_grad.shape[0]
        columns = head_grad.shape[1]
        grad_queries, grad_keys, grad_values = attend_backward(
            queries,
            key_part,
            value_part,
            coarse_allowed,
            log_total,
            head_grad.reshape(1, all_rows, columns // HEAD_DIM, HEAD_DIM),
        )
        stacked = jnp.stack(
            [
                grad_queries.reshape(all_rows, columns),
                grad_keys.reshape(all_rows, columns),
                grad_values.reshape(all_rows, columns),
            ],
            1,
        ).astype(jnp.bfloat16)
        back_rows = lax.all_to_all(stacked, "seq", split_axis=0, concat_axis=2, tiled=True)
        return back_rows.reshape(back_rows.shape[0], 3 * D)

    def fine_attend(triple):
        grouped = triple.reshape(patches, PATCH, 3, D // HEAD_DIM, HEAD_DIM)
        queries = grouped[:, :, 0]
        key_part = grouped[:, :, 1]
        value_part = grouped[:, :, 2]
        mixture, log_total = attend_forward(queries, key_part, value_part, fine_allowed)
        return (
            mixture.reshape(bytes_here, D).astype(jnp.bfloat16),
            (queries, key_part, value_part, log_total),
        )

    def fine_back(grad_mixture, stored):
        queries, key_part, value_part, log_total = stored
        grad_queries, grad_keys, grad_values = attend_backward(
            queries,
            key_part,
            value_part,
            fine_allowed,
            log_total,
            grad_mixture.reshape(patches, PATCH, D // HEAD_DIM, HEAD_DIM),
        )
        stacked = jnp.stack([grad_queries, grad_keys, grad_values], 2).astype(jnp.bfloat16)
        return stacked.reshape(bytes_here, 3 * D)

    grouped_bytes = byte_rows.reshape(patches, PATCH * D)
    embedded = product(grouped_bytes, coarse_full[0])
    coarse_out, coarse_stored = block_forward(embedded, coarse_full[1:], coarse_attend)
    coarse_low = coarse_out.astype(jnp.bfloat16)
    arrived = shifted(coarse_low[-1:], "seq", 1)
    offset = lax.axis_index("seq") * patches
    padded = jnp.concatenate([segment_row[:1] - 1, segment_row])
    before = lax.dynamic_slice_in_dim(padded, offset, patches)
    current = lax.dynamic_slice_in_dim(segment_row, offset, patches)
    joined = (before == current).astype(jnp.float32)[:, None]
    previous = jnp.concatenate([arrived, coarse_low[:-1]]).astype(jnp.float32) * joined
    fine_in = (
        byte_rows.astype(jnp.float32).reshape(patches, PATCH, D) + previous[:, None, :]
    ).reshape(bytes_here, D)
    layer_rows, fine_stored = block_forward(fine_in, fine_full, fine_attend)
    fine_weights_back = (
        lax.all_gather(fine_first_gain, "fsdp", axis=0, tiled=True),
        lax.all_gather(fine_first_bias, "fsdp", axis=0, tiled=True),
        lax.all_gather(fine_project, "fsdp", axis=0, tiled=True),
        lax.all_gather(fine_output, "fsdp", axis=1, tiled=True),
        lax.all_gather(fine_second_gain, "fsdp", axis=0, tiled=True),
        lax.all_gather(fine_second_bias, "fsdp", axis=0, tiled=True),
        lax.all_gather(fine_expand, "fsdp", axis=0, tiled=True),
        lax.all_gather(fine_narrow, "fsdp", axis=1, tiled=True),
    )
    grad_fine_in, fine_grads = block_backward(
        cotangent[0].astype(jnp.float32), fine_weights_back, fine_stored, fine_back
    )
    grad_previous = jnp.sum(grad_fine_in.reshape(patches, PATCH, D), 1) * joined
    arrived_back = shifted(grad_previous[:1], "seq", -1)
    grad_coarse_out = jnp.concatenate([grad_previous[1:], arrived_back])
    coarse_weights_back = (
        lax.all_gather(patch_weight, "fsdp", axis=0, tiled=True),
        lax.all_gather(coarse_first_gain, "fsdp", axis=0, tiled=True),
        lax.all_gather(coarse_first_bias, "fsdp", axis=0, tiled=True),
        lax.all_gather(coarse_project, "fsdp", axis=0, tiled=True),
        lax.all_gather(coarse_output, "fsdp", axis=1, tiled=True),
        lax.all_gather(coarse_second_gain, "fsdp", axis=0, tiled=True),
        lax.all_gather(coarse_second_bias, "fsdp", axis=0, tiled=True),
        lax.all_gather(coarse_expand, "fsdp", axis=0, tiled=True),
        lax.all_gather(coarse_narrow, "fsdp", axis=1, tiled=True),
    )
    grad_embedded, coarse_grads = block_backward(
        grad_coarse_out, coarse_weights_back[1:], coarse_stored, coarse_back
    )
    grad_embed_low = grad_embedded.astype(jnp.bfloat16)
    grad_patch = left_product(grouped_bytes, grad_embed_low)
    grad_grouped = right_product(grad_embed_low, coarse_weights_back[0])
    input_gradient = (grad_fine_in + grad_grouped.reshape(bytes_here, D)).astype(jnp.bfloat16)
    shards = (
        lax.psum_scatter(grad_patch, "fsdp", scatter_dimension=0, tiled=True),
        lax.psum_scatter(coarse_grads[0], "fsdp", scatter_dimension=0, tiled=True),
        lax.psum_scatter(coarse_grads[1], "fsdp", scatter_dimension=0, tiled=True),
        lax.psum_scatter(coarse_grads[2], "fsdp", scatter_dimension=0, tiled=True),
        lax.psum_scatter(coarse_grads[3], "fsdp", scatter_dimension=1, tiled=True),
        lax.psum_scatter(coarse_grads[4], "fsdp", scatter_dimension=0, tiled=True),
        lax.psum_scatter(coarse_grads[5], "fsdp", scatter_dimension=0, tiled=True),
        lax.psum_scatter(coarse_grads[6], "fsdp", scatter_dimension=0, tiled=True),
        lax.psum_scatter(coarse_grads[7], "fsdp", scatter_dimension=1, tiled=True),
        lax.psum_scatter(fine_grads[0], "fsdp", scatter_dimension=0, tiled=True),
        lax.psum_scatter(fine_grads[1], "fsdp", scatter_dimension=0, tiled=True),
        lax.psum_scatter(fine_grads[2], "fsdp", scatter_dimension=0, tiled=True),
        lax.psum_scatter(fine_grads[3], "fsdp", scatter_dimension=1, tiled=True),
        lax.psum_scatter(fine_grads[4], "fsdp", scatter_dimension=0, tiled=True),
        lax.psum_scatter(fine_grads[5], "fsdp", scatter_dimension=0, tiled=True),
        lax.psum_scatter(fine_grads[6], "fsdp", scatter_dimension=0, tiled=True),
        lax.psum_scatter(fine_grads[7], "fsdp", scatter_dimension=1, tiled=True),
    )
    totals = (
        lax.psum(shards[0].astype(jnp.bfloat16), "seq").astype(jnp.float32),
        lax.psum(shards[1].astype(jnp.bfloat16), "seq").astype(jnp.float32),
        lax.psum(shards[2].astype(jnp.bfloat16), "seq").astype(jnp.float32),
        lax.psum(shards[3].astype(jnp.bfloat16), "seq").astype(jnp.float32),
        lax.psum(shards[4].astype(jnp.bfloat16), "seq").astype(jnp.float32),
        lax.psum(shards[5].astype(jnp.bfloat16), "seq").astype(jnp.float32),
        lax.psum(shards[6].astype(jnp.bfloat16), "seq").astype(jnp.float32),
        lax.psum(shards[7].astype(jnp.bfloat16), "seq").astype(jnp.float32),
        lax.psum(shards[8].astype(jnp.bfloat16), "seq").astype(jnp.float32),
        lax.psum(shards[9].astype(jnp.bfloat16), "seq").astype(jnp.float32),
        lax.psum(shards[10].astype(jnp.bfloat16), "seq").astype(jnp.float32),
        lax.psum(shards[11].astype(jnp.bfloat16), "seq").astype(jnp.float32),
        lax.psum(shards[12].astype(jnp.bfloat16), "seq").astype(jnp.float32),
        lax.psum(shards[13].astype(jnp.bfloat16), "seq").astype(jnp.float32),
        lax.psum(shards[14].astype(jnp.bfloat16), "seq").astype(jnp.float32),
        lax.psum(shards[15].astype(jnp.bfloat16), "seq").astype(jnp.float32),
        lax.psum(shards[16].astype(jnp.bfloat16), "seq").astype(jnp.float32),
    )
    layer_output = layer_rows.astype(jnp.bfloat16)[None]
    return (
        layer_output,
        input_gradient[None],
        totals[0],
        totals[1],
        totals[2],
        totals[3],
        totals[4],
        totals[5],
        totals[6],
        totals[7],
        totals[8],
        totals[9],
        totals[10],
        totals[11],
        totals[12],
        totals[13],
        totals[14],
        totals[15],
        totals[16],
    )


MESH = pl.DeviceIdType.MESH
HBM = pltpu.MemorySpace.HBM
VMEM = pltpu.MemorySpace.VMEM


class Place:
    def __init__(self):
        self.core = lax.axis_index("seq")
        self.at = lax.axis_index("fsdp")
        self.z = self.at // 4
        self.plane = self.at % 4
        self.near = 1 + self.core
        self.far = 2 - self.core

    def flip(self, mask):
        return self.at ^ mask

    def across(self, mask):
        return (self.core, self.at ^ mask)

    def partner(self):
        return (1 - self.core, self.at)


def enter(place, masks, partner=True):
    barrier = pltpu.get_barrier_semaphore()
    for mask in masks:
        pl.semaphore_signal(barrier, inc=1, device_id=place.across(mask), device_id_type=MESH)
    if partner:
        pl.semaphore_signal(barrier, inc=1, device_id=place.partner(), device_id_type=MESH)
    pl.semaphore_wait(barrier, len(masks) + (1 if partner else 0))


MASKS = (1, 2, 4, 8, 12)


class Gather:
    EVENTS = 12

    def __init__(self, place, source, buffer, rows, first, column, width, z_first, sends, receives, local):
        self.p, self.source, self.buffer, self.rows, self.first = place, source, buffer, rows, first
        self.z_first, self.sends, self.receives, self.local = z_first, sends, receives, local
        self.half = width // 2
        self.column, self.width = column, width
        self.mine = pl.ds(pl.multiple_of(column + place.core * self.half, 128), self.half)
        self.theirs = pl.ds(pl.multiple_of(column + (1 - place.core) * self.half, 128), self.half)
        self.started = []

    def group(self, plane, columns=None):
        return self.buffer.at[:, plane, self.rows, self.mine if columns is None else columns]

    def block(self, z, plane):
        return self.buffer.at[z, plane, self.rows, self.mine]

    def send(self, event, view, device, source=None):
        copy = pltpu.make_async_remote_copy(
            src_ref=view if source is None else source,
            dst_ref=view,
            send_sem=self.sends.at[event],
            recv_sem=self.receives.at[event],
            device_id=device,
            device_id_type=MESH,
        )
        copy.start()
        self.started.append(copy)

    def arrived(self, event, view):
        pltpu.make_async_remote_copy(
            src_ref=view,
            dst_ref=view,
            send_sem=self.sends.at[event],
            recv_sem=self.receives.at[event],
            device_id=self.p.partner(),
            device_id_type=MESH,
        ).wait_recv()

    def start(self):
        p = self.p
        own = self.source.at[self.rows, pl.ds(pl.multiple_of(self.first + p.core * self.half, 128), self.half)]
        self.copy = pltpu.make_async_copy(own, self.block(p.z, p.plane), self.local)
        self.copy.start()
        if not self.z_first:
            self.send(6, self.block(p.z, p.plane), p.across(p.near), own)
        for j in (1, 2, 3):
            self.send(j - 1, self.block(p.z, p.plane), p.across(4 * j), own)

    def one(self):
        p = self.p
        self.copy.wait()
        if self.z_first:
            for j in (1, 2, 3):
                self.arrived(j - 1, self.block(p.z ^ j, p.plane))
            self.send(6, self.group(p.plane), p.across(p.near))
            self.send(7, self.group(p.plane), p.across(p.far))
            self.send(9, self.group(p.plane), p.partner())
        else:
            self.arrived(6, self.block(p.z, p.plane ^ p.near))
            for j in (1, 2, 3):
                self.send(2 + j, self.block(p.z, p.plane ^ p.near), p.across(4 * j))

    def two(self):
        p = self.p
        if self.z_first:
            self.arrived(6, self.group(p.plane ^ p.near))
        else:
            for j in (1, 2, 3):
                self.arrived(j - 1, self.block(p.z ^ j, p.plane))
            self.send(7, self.group(p.plane), p.across(p.far))
            self.send(9, self.group(p.plane), p.partner())
            for j in (1, 2, 3):
                self.arrived(2 + j, self.block(p.z ^ j, p.plane ^ p.near))
        self.send(8, self.group(p.plane ^ p.near), p.across(p.far))
        self.send(10, self.group(p.plane ^ p.near), p.partner())

    def three(self):
        p = self.p
        self.arrived(7, self.group(p.plane ^ p.far))
        self.send(11, self.group(p.plane ^ p.far), p.partner())
        self.arrived(8, self.group(p.plane ^ 3))
        self.send(12, self.group(p.plane ^ 3), p.partner())

    def four(self):
        p = self.p
        self.arrived(9, self.group(p.plane, self.theirs))
        self.arrived(10, self.group(p.plane ^ p.far, self.theirs))
        self.arrived(11, self.group(p.plane ^ p.near, self.theirs))
        self.arrived(12, self.group(p.plane ^ 3, self.theirs))

    def drain(self):
        for copy in self.started:
            copy.wait_send()


def run_gathers(gathers, ahead, tick):
    n = len(gathers)
    for k in range(min(ahead, n)):
        gathers[k].start()
    for t in range(n + 3):
        if t < n:
            gathers[t].one()
            if t + ahead < n:
                gathers[t + ahead].start()
        if 0 <= t - 1 < n:
            gathers[t - 1].two()
        if 0 <= t - 2 < n:
            gathers[t - 2].three()
        if 0 <= t - 3 < n:
            gathers[t - 3].four()
        tick(t)
    for g in gathers:
        g.drain()


class PatchForward:
    def __init__(self, small, rows, patch, w, segments, outs):
        self.small, self.rows, self.patch, self.w, self.segments = small, rows, patch, w, segments
        self.embedded, self.normed, self.triple, self.chances, self.mixture = outs[:5]
        self.middle, self.second, self.lifted, self.hidden, self.result = outs[5:]

    def weight(self, column, width):
        return self.w[:, :, :, column : column + width].reshape(D, width)

    def embed(self, first):
        def step(z, _):
            columns = pl.ds(pl.multiple_of(z * 2 * D, 128), 2 * D)
            rows = self.rows[:, :, columns].reshape(self.embedded.shape[0], 2 * D)
            term = product(rows, self.patch[z].reshape(2 * D, D))
            self.embedded[...] += term
            return 0

        if first == 0:
            self.embedded[...] = jnp.zeros_like(self.embedded)
        lax.fori_loop(first, first + 2, step, 0)

    def project(self):
        unit, _ = normalize(self.embedded[...])
        self.normed[...] = (unit * self.small[0:1] + self.small[1:2]).astype(jnp.bfloat16)
        self.triple[...] = product(self.normed[...], self.weight(0, 3 * D)).astype(jnp.bfloat16)

    def attend(self, first):
        count = self.triple.shape[0]
        row = lax.broadcasted_iota(jnp.int32, (count, count), 0)
        column = lax.broadcasted_iota(jnp.int32, (count, count), 1)
        allowed = (column <= row) & (self.segments[1][...] == self.segments[0][...])

        def step(pair, _):
            lanes = [pl.ds(pl.multiple_of(i * D + pair * 128, 128), 128) for i in range(3)]
            queries = head_lanes(self.triple[:, lanes[0]])
            keys = self.triple[:, lanes[1]]
            values = head_lanes(self.triple[:, lanes[2]])
            mixed = None
            for head in range(2):
                found = chances_of(queries[head], keys, allowed)
                self.chances[pair * 2 + head] = found
                term = product(found.astype(jnp.bfloat16), values[head])
                mixed = term if mixed is None else mixed + term
            self.mixture[:, lanes[0]] = mixed.astype(jnp.bfloat16)
            return 0

        lax.fori_loop(first, first + 3, step, 0)

    def join(self):
        middle = self.embedded[...] + right_product(self.mixture[...], self.weight(3 * D, D))
        self.middle[...] = middle
        self.result[...] = middle
        unit, _ = normalize(middle)
        self.second[...] = (unit * self.small[2:3] + self.small[3:4]).astype(jnp.bfloat16)

    def lift(self, half):
        here = slice(half * 2 * D, half * 2 * D + 2 * D)
        lifted = product(self.second[...], self.weight(4 * D + half * 2 * D, 2 * D))
        self.lifted[:, here] = lifted
        self.hidden[:, here] = smooth_gate(lifted).astype(jnp.bfloat16)

    def lower(self, half):
        here = slice(half * 2 * D, half * 2 * D + 2 * D)
        self.result[...] += right_product(self.hidden[:, here], self.weight(8 * D + half * 2 * D, 2 * D))


def gather_kernel(plan, ahead, *refs):
    sources, small, rows, segments, rest = refs[:9], refs[9], refs[10], refs[11:13], refs[13:]
    buffers, small_out, all_rows, patch_outs, rest = rest[:3], rest[3], rest[4], rest[5:15], rest[15:]
    sends, receives, local, value, arriving, small_sends, small_receives, row_sems, patch, w, loads = rest
    place = Place()
    enter(place, MASKS)
    value[0] = small[...]
    total = Total(place, (1, 2, 4, 8), value, arriving, small_sends, small_receives, small_out)
    stay = pltpu.make_async_copy(rows, all_rows.at[place.core], row_sems.at[0])
    stay.start()
    cross = pltpu.make_async_remote_copy(
        src_ref=rows, dst_ref=all_rows.at[place.core], send_sem=row_sems.at[1], recv_sem=row_sems.at[2],
        device_id=place.partner(), device_id_type=MESH,
    )
    cross.start()
    gathers = []
    for k, (source, buffer, first, rows_here, start, column, width, z_first) in enumerate(plan):
        gathers.append(
            Gather(place, sources[source], buffers[buffer], pl.ds(first, rows_here), start, column, width, z_first,
                   sends.at[k], receives.at[k], local.at[k])
        )
    forward = PatchForward(small_out, all_rows, patch, w, segments, patch_outs)
    waiting = []
    patches = sum(p[1] == 0 for p in plan)
    held = sum(p[1] < 2 for p in plan)

    def fetched():
        while waiting:
            waiting.pop().wait()

    def rows_there():
        stay.wait()
        cross.wait()

    base = patches + 4
    pieces = {
        base: (rows_there, fetched, functools.partial(forward.embed, 0)),
        base + 1: (functools.partial(forward.embed, 2),),
        base + 2: (fetched, forward.project),
        base + 3: (functools.partial(forward.attend, 0),),
        base + 4: (functools.partial(forward.attend, 3),),
        base + 5: (fetched, forward.join),
        base + 6: (functools.partial(forward.lift, 0),),
        base + 7: (functools.partial(forward.lift, 1),),
        base + 8: (fetched, functools.partial(forward.lower, 0)),
        base + 9: (functools.partial(forward.lower, 1),),
    }

    def tick(t):
        total.advance()
        for piece in pieces.get(t, ()):
            piece()
        k = t - 3
        if 0 <= k < held:
            _, buffer, first, count, _, column, width, _ = plan[k]
            part = (slice(None), slice(None), pl.ds(first, count), pl.ds(column, width))
            copy = pltpu.make_async_copy(buffers[buffer].at[part], (patch, w)[buffer].at[part], loads.at[k])
            copy.start()
            waiting.append(copy)

    run_gathers(gathers, ahead, tick)


def forward_plan(step=1536, patch_rows=96):
    plan = []
    for first in range(0, 384, patch_rows):
        plan.append((0, 0, first, patch_rows, 0, 0, 768))
    for block in (1, 2):
        column = 0
        for i, width in enumerate((2304, 768, 3072, 3072)):
            for start in range(0, width, step):
                plan.append((4 * block - 3 + i, block, 0, 48, start, column + start, min(step, width - start)))
            column += width
    return tuple(p + (i % 5 != 4,) for i, p in enumerate(plan))


PLAN = forward_plan()


def gather_all(sources, small, rows, segments, ahead=3, plan=PLAN):
    n = len(plan)
    bf, f32 = jnp.bfloat16, jnp.float32
    count = 2 * rows.shape[0]
    outs = [((8, D), f32), ((2,) + rows.shape, bf), ((count, D), f32), ((count, D), bf), ((count, 3 * D), bf),
            ((D // HEAD_DIM, count, count), f32), ((count, D), bf), ((count, D), f32), ((count, D), bf), ((count, 4 * D), f32),
            ((count, 4 * D), bf), ((count, D), f32)]
    shapes = ((4, 4, 384, D), (4, 4, 48, 12 * D))
    return pl.pallas_call(
        functools.partial(gather_kernel, plan, ahead),
        out_shape=[jax.ShapeDtypeStruct(shape, bf) for shape in shapes + shapes[1:]]
        + [jax.ShapeDtypeStruct(*out) for out in outs],
        in_specs=[pl.BlockSpec(memory_space=VMEM)] * 10 + [pl.BlockSpec(memory_space=HBM)] + [pl.BlockSpec(memory_space=VMEM)] * 2,
        out_specs=[pl.BlockSpec(memory_space=HBM)] * 3 + [pl.BlockSpec(memory_space=VMEM)] * len(outs),
        scratch_shapes=[
            pltpu.SemaphoreType.DMA((n, 13)),
            pltpu.SemaphoreType.DMA((n, 13)),
            pltpu.SemaphoreType.DMA((n,)),
            pltpu.VMEM((5, 8, 768), jnp.float32),
            pltpu.VMEM((4, 8, 768), jnp.float32),
            pltpu.SemaphoreType.DMA((4,)),
            pltpu.SemaphoreType.DMA((4,)),
            pltpu.SemaphoreType.DMA((3,)),
            pltpu.VMEM(shapes[0], bf),
            pltpu.VMEM(shapes[1], bf),
            pltpu.SemaphoreType.DMA((n,)),
        ],
        compiler_params=pltpu.CompilerParams(collective_id=0, has_side_effects=True, vmem_limit_bytes=64_000_000),
        name="gather_all",
    )(*sources, small, rows, *segments)


class Total:
    def __init__(self, place, masks, value, arriving, sends, receives, result):
        self.p, self.masks, self.value, self.arriving = place, masks, value, arriving
        self.sends, self.receives, self.result = sends, receives, result
        self.step, self.copy = 0, None

    def advance(self):
        if self.step > len(self.masks):
            return
        if self.copy is not None:
            self.copy.wait()
            i = self.step - 1
            self.value[i + 1] = self.value[i] + self.arriving[i]
        if self.step < len(self.masks):
            i = self.step
            mask = self.masks[i]
            self.copy = pltpu.make_async_remote_copy(
                src_ref=self.value.at[i],
                dst_ref=self.arriving.at[i],
                send_sem=self.sends.at[i],
                recv_sem=self.receives.at[i],
                device_id=self.p.across(mask) if mask else self.p.partner(),
                device_id_type=MESH,
            )
            self.copy.start()
        else:
            self.result[...] = self.value[len(self.masks)]
        self.step += 1


def add(left, right):
    return left.astype(jnp.float32) + right.astype(jnp.float32)


class Reduce:
    def __init__(self, place, held, paired, far, near, line, out, rows, column, width, z_last, sends, receives):
        self.p, self.held, self.from_partner, self.from_far = place, held, paired, far
        self.from_near, self.from_line, self.out, self.rows = near, line, out, rows
        self.z_last, self.sends, self.receives = z_last, sends, receives
        self.half = width // 2
        whole = out.shape[1] // 2
        self.own = pl.ds(column // 2, self.half)
        self.mine = pl.ds(pl.multiple_of(column // 2 + place.core * whole, 128), self.half)
        self.theirs = pl.ds(pl.multiple_of(column // 2 + (1 - place.core) * whole, 128), self.half)
        self.started = []

    def send(self, event, source, target, device):
        copy = pltpu.make_async_remote_copy(
            src_ref=source, dst_ref=target, send_sem=self.sends.at[event], recv_sem=self.receives.at[event],
            device_id=device, device_id_type=MESH,
        )
        copy.start()
        self.started.append(copy)

    def arrived(self, event, target):
        pltpu.make_async_remote_copy(
            src_ref=target, dst_ref=target, send_sem=self.sends.at[event], recv_sem=self.receives.at[event],
            device_id=self.p.partner(), device_id_type=MESH,
        ).wait_recv()

    def pair(self, theirs):
        self.send(0, theirs, self.from_partner, self.p.partner())
        self.paired = self.started.pop()

    def fold(self, plane, others):
        def step(z, _):
            self.held[z, plane] = add(self.held[z, plane], others[z]).astype(jnp.bfloat16)
            return 0

        lax.fori_loop(0, 4, step, 0)

    def one(self):
        p = self.p
        if self.from_partner is not None:
            self.arrived(0, self.from_partner)
            self.fold(p.plane ^ p.far, self.from_partner.at[:, p.plane ^ p.far])
        self.send(1, self.held.at[:, p.plane ^ p.far], self.from_far.at[0], p.across(p.far))
        if self.from_partner is not None:
            self.fold(p.plane ^ 3, self.from_partner.at[:, p.plane ^ 3])
        self.send(2, self.held.at[:, p.plane ^ 3], self.from_far.at[1], p.across(p.far))
        if self.from_partner is not None:
            self.fold(p.plane, self.from_partner.at[:, p.plane])
            self.fold(p.plane ^ p.near, self.from_partner.at[:, p.plane ^ p.near])

    def two(self):
        p = self.p
        self.arrived(2, self.from_far.at[1])
        self.fold(p.plane ^ p.near, self.from_far.at[1])
        if self.z_last:
            self.send(3, self.held.at[:, p.plane ^ p.near], self.from_near, p.across(p.near))
        else:
            for j in (1, 2, 3):
                self.send(6 + j, self.held.at[p.z ^ j, p.plane ^ p.near], self.from_line.at[2 + j], p.across(4 * j))
        self.arrived(1, self.from_far.at[0])
        self.fold(p.plane, self.from_far.at[0])
        if not self.z_last:
            for j in (1, 2, 3):
                self.send(3 + j, self.held.at[p.z ^ j, p.plane], self.from_line.at[j - 1], p.across(4 * j))

    def three(self):
        p = self.p
        if self.z_last:
            self.arrived(3, self.from_near)
            self.fold(p.plane, self.from_near)
            for j in (1, 2, 3):
                self.send(3 + j, self.held.at[p.z ^ j, p.plane], self.from_line.at[j - 1], p.across(4 * j))
        else:
            for j in (1, 2, 3):
                self.arrived(6 + j, self.from_line.at[2 + j])
            near = (add(self.held[p.z, p.plane ^ p.near], self.from_line[3]) + add(self.from_line[4], self.from_line[5]))
            self.held[p.z, p.plane ^ p.near] = near.astype(jnp.bfloat16)
            self.send(3, self.held.at[p.z, p.plane ^ p.near], self.from_near.at[0], p.across(p.near))

    def four(self):
        p = self.p
        for j in (1, 2, 3):
            self.arrived(3 + j, self.from_line.at[j - 1])
        total = add(self.held[p.z, p.plane], self.from_line[0]) + add(self.from_line[1], self.from_line[2])
        if not self.z_last:
            self.arrived(3, self.from_near.at[0])
            total = total + self.from_near[0].astype(jnp.float32)
        self.out[self.rows, self.mine] = total
        view = self.out.at[self.rows, self.mine]
        self.send(10, view, view, p.partner())

    def drain(self):
        for copy in self.started:
            copy.wait_send()
        self.started = []

    def five(self):
        self.arrived(10, self.out.at[self.rows, self.theirs])


def backward_plan(step=1536, patch_rows=96):
    plan = []
    for array, width in ((6, 768), (8, 3072), (7, 3072), (5, 2304), (4, 3072), (3, 3072), (2, 768), (1, 2304)):
        for start in range(0, width, step):
            plan.append((array, 0, 48, start, min(step, width - start)))
    for first in range(0, 384, patch_rows):
        plan.append((0, first, patch_rows, 0, 768))
    return tuple(p + (i % 5 != 4,) for i, p in enumerate(plan))


BACK_PLAN = backward_plan()
SLOTS = 8
LAGS = (2, 3, 4, 5)
ARRAYS = 9


def reduce_kernel(plan, patch, lefts, rights, small, outs, small_out, slots, pairs, fars, nears, lines, staging, left_held,
                  right_held, sends, receives, loads, left_sems, right_sems, value, arriving, small_sends, small_receives):
    place = Place()
    enter(place, MASKS)
    n = len(plan)
    value[0] = small[...]
    total = Total(place, (0, 1, 2, 4, 8), value, arriving, small_sends, small_receives, small_out)
    used = [0, 0]
    reduces, copies, staged, steps, order = [], {}, [], [], []
    for k, (array, first, rows, column, width, z_last) in enumerate(plan):
        kind = 0 if array == 0 else 1
        slot = used[kind] % SLOTS
        used[kind] += 1
        half = width // 2
        cut = (lambda ref, half=half: ref if half == ref.shape[-1] else ref.at[..., pl.ds(0, half)])
        r = Reduce(place, cut(slots[kind].at[slot]), cut(pairs.at[used[kind] - 1]) if array > 4 else None, cut(fars[kind].at[used[kind] - 1]),
                   cut(nears[kind].at[used[kind] - 1]), cut(lines[kind].at[used[kind] - 1]), outs[array],
                   pl.ds(first, rows), column, width, z_last, sends.at[k], receives.at[k])
        r.staging = cut(staging.at[(used[kind] - 1) % 2])
        r.paired = None
        reduces.append(r)
        if array > 4:
            steps.append((k, r.theirs))
        if array:
            steps.append((k, r.mine))
            if array not in order:
                order.append(array)

    def left_view(index):
        return left_held.at[index % 2, pl.ds(0, lefts[order[index] - 1].shape[0])]

    def left_copy(index):
        return pltpu.make_async_copy(lefts[order[index] - 1], left_view(index), left_sems.at[index % 2])

    def right_view(index):
        k = steps[index][0]
        return right_held.at[index % 3, pl.ds(0, rights[plan[k][0] - 1].shape[0]), pl.ds(0, reduces[k].half)]

    def right_copy(index):
        k, columns = steps[index]
        return pltpu.make_async_copy(rights[plan[k][0] - 1].at[:, columns], right_view(index), right_sems.at[index % 3])

    done, begun = [0], [0]

    def make(target, k):
        index = done[0]
        if plan[k][0] != order[begun[0] - 1] or begun[0] == 0:
            left_copy(begun[0]).wait()
            begun[0] += 1
            if begun[0] < len(order):
                left_copy(begun[0]).start()
        left, right = left_view(begun[0] - 1), right_view(index)
        right_copy(index).wait()
        rows = D // 2

        def part(i, _):
            columns = pl.ds(pl.multiple_of(i * rows, 128), rows)
            term = left_product(left[:, columns], right[...]).astype(jnp.bfloat16)
            target[pl.ds(i * 2, 2)] = term.reshape((2,) + target.shape[1:])
            return 0

        lax.fori_loop(0, 2, part, 0)
        done[0] += 1
        if index + 3 < len(steps):
            right_copy(index + 3).start()

    left_copy(0).start()
    for index in range(3):
        right_copy(index).start()

    def load(k):
        array = plan[k][0]
        r = reduces[k]
        if k - SLOTS >= 0:
            reduces[k - SLOTS].drain()
        if array == 0:
            copies[k] = pltpu.make_async_copy(patch.at[:, :, r.rows, r.own], r.held, loads.at[k])
            copies[k].start()
            return
        if array > 4:
            if len(staged) > 1:
                staged[-2].paired.wait_send()
            make(r.staging, k)
            r.pair(r.staging)
            staged.append(r)
        make(r.held, k)

    load(0)
    for t in range(n + LAGS[-1]):
        if t < n:
            if t in copies:
                copies[t].wait()
            reduces[t].one()
        if t + 1 < n:
            load(t + 1)
        for lag, name in zip(LAGS, ("two", "three", "four", "five")):
            if 0 <= t - lag < n:
                getattr(reduces[t - lag], name)()
        total.advance()
    for r in reduces:
        r.drain()
    for r in staged[-2:]:
        r.paired.wait_send()


def reduce_all(patch, terms, small, plan=BACK_PLAN):
    n = len(plan)
    bf = jnp.bfloat16
    counts = [sum(p[0] == 0 for p in plan), sum(p[0] > 0 for p in plan), sum(p[0] > 4 for p in plan)]
    shapes = tuple((max(p[2] for p in plan if c(p[0])), max(p[4] for p in plan if c(p[0])) // 2) for c in (lambda a: a == 0, lambda a: a > 0))

    inputs = 2 * ARRAYS

    def kernel(*refs):
        patch, lefts, rights, small = refs[0], refs[1:ARRAYS], refs[ARRAYS : inputs - 1], refs[inputs - 1]
        outs, small_out = refs[inputs : inputs + ARRAYS], refs[inputs + ARRAYS]
        pairs, rest = refs[inputs + ARRAYS + 1], refs[inputs + ARRAYS + 2 :]
        slots, fars, nears, lines = (rest[2 * i : 2 * i + 2] for i in range(4))
        reduce_kernel(plan, patch, lefts, rights, small, outs, small_out, slots, pairs, fars, nears, lines, *rest[8:])

    scratch = [pltpu.VMEM((counts[2], 4, 4) + shapes[1], bf)]
    scratch += [pltpu.VMEM((min(SLOTS, counts[i]), 4, 4) + shapes[i], bf) for i in (0, 1)]
    for lead in ((2, 4), (4,), (6,)):
        scratch += [pltpu.VMEM((counts[i],) + lead + shapes[i], bf) for i in (0, 1)]
    depth = max(left.shape[0] for left, _ in terms)
    scratch += [
        pltpu.VMEM((2, 4, 4) + shapes[1], bf),
        pltpu.VMEM((2, depth, D), bf),
        pltpu.VMEM((3, depth, shapes[1][1]), bf),
        pltpu.SemaphoreType.DMA((n, 11)),
        pltpu.SemaphoreType.DMA((n, 11)),
        pltpu.SemaphoreType.DMA((n,)),
        pltpu.SemaphoreType.DMA((2,)),
        pltpu.SemaphoreType.DMA((3,)),
        pltpu.VMEM((6, 8, 768), jnp.float32),
        pltpu.VMEM((5, 8, 768), jnp.float32),
        pltpu.SemaphoreType.DMA((5,)),
        pltpu.SemaphoreType.DMA((5,)),
    ]
    patch = patch.reshape(4, 4, patch.shape[0] // 16, patch.shape[1])
    outs = [(patch.shape[2], 2 * patch.shape[3])] + [(left.shape[1] // 16, right.shape[1]) for left, right in terms] + [(8, 768)]
    return pl.pallas_call(
        kernel,
        out_shape=[jax.ShapeDtypeStruct(out, jnp.float32) for out in outs],
        in_specs=[pl.BlockSpec(memory_space=HBM)] * (inputs - 1) + [pl.BlockSpec(memory_space=VMEM)],
        out_specs=[pl.BlockSpec(memory_space=VMEM)] * (ARRAYS + 1),
        scratch_shapes=scratch,
        compiler_params=pltpu.CompilerParams(collective_id=1, has_side_effects=True, vmem_limit_bytes=67_000_000),
        name="reduce_all",
    )(patch, *[left for left, _ in terms], *[right for _, right in terms], small)


def fast_body(byte_inputs, segment_ids, cotangent, patch_weight, *weights):
    coarse, fine = weights[:8], weights[8:]
    core, at = lax.axis_index("seq"), lax.axis_index("fsdp")
    vectors = jnp.stack([w[i] for w in (coarse, fine) for i in (0, 1, 4, 5)]).astype(jnp.float32)
    small = lax.dynamic_update_slice(jnp.zeros((8, D), jnp.float32), vectors, (0, at * vectors.shape[1]))
    sources = [patch_weight]
    for w in (coarse, fine):
        sources += [w[2], w[3].T, w[6], w[7].T]
    byte_rows = byte_inputs[0]
    bytes_here = byte_rows.shape[0]
    patches = bytes_here // PATCH
    segment_row = segment_ids[0]
    all_patches = segment_row.shape[0]
    patch_full, coarse_full, fine_full, small, all_rows, *stored, coarse_out = gather_all(
        sources, small, byte_rows.reshape(patches, PATCH * D), (segment_row[None], segment_row[:, None])
    )
    patch_full = patch_full.reshape(-1, D)

    def mine(values):
        width = values.shape[1] // 2
        return lax.dynamic_slice_in_dim(values, core * width, width, 1)

    embedded, coarse_normed, coarse_triple, chances, coarse_mixture, coarse_middle, coarse_second, lifted, coarse_hidden = stored
    grouped_bytes = all_rows.reshape(all_patches, PATCH * D)
    coarse_low = coarse_out.astype(jnp.bfloat16)
    joined = jnp.concatenate([jnp.zeros((1,), bool), segment_row[1:] == segment_row[:-1]]).astype(jnp.float32)[:, None]
    previous = jnp.concatenate([jnp.zeros((1, D), jnp.bfloat16), coarse_low[:-1]]).astype(jnp.float32) * joined
    previous = lax.dynamic_slice_in_dim(previous, core * patches, patches)
    (layer_rows, grad_fine_in, grad_previous, fine_vectors, normed, mixture, second, hidden, grad_middle, grad_lifted,
     grad_triple) = fine_block(byte_rows, previous, cotangent[0], small, fine_full.reshape(D, -1))
    fine_terms = [(normed, grad_triple), (grad_middle, mixture), (second, grad_lifted), (cotangent[0], hidden)]
    grad_previous = lax.all_gather(grad_previous, "seq", axis=0, tiled=True) * joined
    grad_coarse_out = jnp.concatenate([grad_previous[1:], jnp.zeros((1, D), jnp.float32)])
    grad_branch, coarse_grad_lifted, grad_attended, coarse_grad_triple, grad_embed_low, coarse_vectors, input_gradient = coarse_block_back(
        grad_coarse_out, embedded, coarse_middle, lifted, coarse_triple, chances, small, coarse_full.reshape(D, -1), patch_full,
        grad_fine_in,
    )
    grad_patch = left_product(grouped_bytes, mine(grad_embed_low)).astype(jnp.bfloat16)
    coarse_terms = [
        (coarse_normed, coarse_grad_triple), (grad_attended, coarse_mixture), (coarse_second, coarse_grad_lifted),
        (grad_branch, coarse_hidden),
    ]
    once = (core == 0).astype(jnp.float32)
    small = coarse_vectors * once + fine_vectors
    *shards, small = reduce_all(grad_patch, coarse_terms + fine_terms, small)
    small = lax.dynamic_slice_in_dim(small, at * vectors.shape[1], vectors.shape[1], 1)

    def gradients(parts, first):
        return (small[first], small[first + 1], parts[0], parts[1].T, small[first + 2], small[first + 3], parts[2], parts[3].T)

    return (layer_rows[None], input_gradient[None], shards[0]) + gradients(shards[1:5], 0) + gradients(shards[5:], 4)


def normalize(values):
    centred = values - jnp.mean(values, -1, keepdims=True)
    scale = lax.rsqrt(jnp.mean(centred * centred, -1, keepdims=True) + epsilon)
    return centred * scale, scale


def normalize_back(grad, unit, scale, norm_gain):
    scaled = grad * norm_gain
    return scale * (
        scaled - jnp.mean(scaled, -1, keepdims=True) - unit * jnp.mean(scaled * unit, -1, keepdims=True)
    )


def gate_both(values):
    root = math.sqrt(2.0 / math.pi)
    square = values * values
    bend = jnp.tanh(root * values * (1.0 + 0.044715 * square))
    half = 0.5 + 0.5 * bend
    slope = half + 0.5 * values * (1.0 - bend * bend) * (root * (1.0 + 3.0 * 0.044715 * square))
    return values * half, slope


def head_lanes(pair):
    lane = lax.broadcasted_iota(jnp.int32, pair.shape, 1)
    zero = jnp.zeros_like(pair)
    return jnp.where(lane < HEAD_DIM, pair, zero), jnp.where(lane < HEAD_DIM, zero, pair)


def chances_of(queries, keys, allowed):
    scores = right_product(queries, keys) * (1.0 / math.sqrt(HEAD_DIM))
    scores = jnp.where(allowed, scores, -1e30)
    powers = jnp.exp(scores - jnp.max(scores, -1, keepdims=True))
    return powers * (1.0 / jnp.sum(powers, -1, keepdims=True))


TILE = 128
PAIRS = 6


def fine_kernel(byte_ref, previous_ref, cotangent_ref, small_ref, w_ref,
                out_ref, grad_in_ref, patch_grad_ref, vectors_ref,
                normed_ref, mixture_ref, second_ref, hidden_ref, low_ref, lifted_grad_ref, triple_grad_ref,
                triple, chances, result, grad_second):
    rows = byte_ref.shape[0]
    bf = jnp.bfloat16
    first_gain, first_bias, second_gain, second_bias = (small_ref[i : i + 1] for i in (4, 5, 6, 7))
    previous = previous_ref[...]
    inputs = (
        byte_ref[...].astype(jnp.float32).reshape(rows // PATCH, PATCH, D) + previous[:, None, :]
    ).reshape(rows, D)
    unit_one, scale_one = normalize(inputs)
    normed = (unit_one * first_gain + first_bias).astype(bf)
    normed_ref[...] = normed
    triple[...] = product(normed, w_ref[:, : 3 * D]).astype(bf)
    row = lax.broadcasted_iota(jnp.int32, (TILE, TILE), 0)
    column = lax.broadcasted_iota(jnp.int32, (TILE, TILE), 1)
    allowed = (row // PATCH == column // PATCH) & (column <= row)
    tiles = rows // TILE

    def attend(pair, _):
        lanes = [pl.ds(pl.multiple_of(i * D + pair * 128, 128), 128) for i in range(3)]
        for tile in range(tiles):
            here = slice(tile * TILE, tile * TILE + TILE)
            queries = head_lanes(triple[here, lanes[0]])
            keys = triple[here, lanes[1]]
            values = head_lanes(triple[here, lanes[2]])
            mixed = None
            for head in range(2):
                found = chances_of(queries[head], keys, allowed)
                chances[pair * 2 + head, here] = found
                term = product(found.astype(bf), values[head])
                mixed = term if mixed is None else mixed + term
            mixture_ref[here, lanes[0]] = mixed.astype(bf)
        return 0

    lax.fori_loop(0, PAIRS, attend, 0)
    middle = inputs + right_product(mixture_ref[...], w_ref[:, 3 * D : 4 * D])
    unit_two, scale_two = normalize(middle)
    second = (unit_two * second_gain + second_bias).astype(bf)
    second_ref[...] = second
    grad_low = cotangent_ref[...]
    result[...] = middle
    for j in range(4):
        here = slice(j * D, j * D + D)
        expand = w_ref[:, 4 * D + j * D : 5 * D + j * D]
        narrow_t = w_ref[:, 8 * D + j * D : 9 * D + j * D]
        hidden, slope = gate_both(product(second, expand))
        hidden = hidden.astype(bf)
        hidden_ref[:, here] = hidden
        lifted_grad = (product(grad_low, narrow_t) * slope).astype(bf)
        lifted_grad_ref[:, here] = lifted_grad
        result[...] += right_product(hidden, narrow_t)
        term = right_product(lifted_grad, expand)
        if j:
            grad_second[...] += term
        else:
            grad_second[...] = term
    out_ref[...] = result[...].astype(bf)
    grad_two = grad_second[...]
    grad_middle = grad_low.astype(jnp.float32) + normalize_back(grad_two, unit_two, scale_two, second_gain)
    low = grad_middle.astype(bf)
    low_ref[...] = low
    grad_second[...] = grad_middle
    grad_mixture = product(low, w_ref[:, 3 * D : 4 * D]).astype(bf)
    result[...] = grad_mixture.astype(jnp.float32)

    def attend_back(pair, _):
        lanes = [pl.ds(pl.multiple_of(i * D + pair * 128, 128), 128) for i in range(3)]
        factor = 1.0 / math.sqrt(HEAD_DIM)
        for tile in range(tiles):
            here = slice(tile * TILE, tile * TILE + TILE)
            queries = head_lanes(triple[here, lanes[0]])
            keys = head_lanes(triple[here, lanes[1]])
            values = triple[here, lanes[2]]
            mixed = head_lanes(result[here, lanes[0]].astype(bf))
            sums = [None, None, None]
            for head in range(2):
                found = chances[pair * 2 + head, here]
                grad = right_product(mixed[head], values)
                scores = (found * (grad - jnp.sum(grad * found, -1, keepdims=True))).astype(bf)
                terms = (
                    product(scores, keys[head]),
                    left_product(scores, queries[head]),
                    left_product(found.astype(bf), mixed[head]),
                )
                sums = [t if s is None else s + t for s, t in zip(sums, terms)]
            triple_grad_ref[here, lanes[0]] = (sums[0] * factor).astype(bf)
            triple_grad_ref[here, lanes[1]] = (sums[1] * factor).astype(bf)
            triple_grad_ref[here, lanes[2]] = sums[2].astype(bf)
        return 0

    lax.fori_loop(0, PAIRS, attend_back, 0)
    grad_one = right_product(triple_grad_ref[...], w_ref[:, : 3 * D])
    grad_in = grad_second[...] + normalize_back(grad_one, unit_one, scale_one, first_gain)
    grad_in_ref[...] = grad_in
    patch_grad_ref[...] = jnp.sum(grad_in.reshape(rows // PATCH, PATCH, D), 1)
    terms = [jnp.sum(t, 0, keepdims=True) for t in (grad_one * unit_one, grad_one, grad_two * unit_two, grad_two)]

    @pl.when(pl.program_id(0) == 0)
    def _():
        vectors_ref[...] = jnp.zeros_like(vectors_ref)

    for i, term in enumerate(terms):
        vectors_ref[4 + i : 5 + i] += term


def fine_block(byte_rows, previous, cotangent, small, full, rows=256):
    count = byte_rows.shape[0]
    bf, f32 = jnp.bfloat16, jnp.float32

    def spec(height, width):
        return pl.BlockSpec((height, width), lambda i: (i, 0))

    def whole(shape):
        return pl.BlockSpec(shape, lambda i: (0, 0), pipeline_mode=pl.Buffered(1))

    outs = [(rows, D, bf), (rows, D, f32), (rows // PATCH, D, f32), None]
    outs += [(rows, D, bf)] * 3 + [(rows, 4 * D, bf), (rows, D, bf), (rows, 4 * D, bf), (rows, 3 * D, bf)]
    steps = count // rows
    return pl.pallas_call(
        fine_kernel,
        grid=(steps,),
        out_shape=[
            jax.ShapeDtypeStruct((o[0] * steps, o[1]), o[2]) if o else jax.ShapeDtypeStruct((8, D), f32) for o in outs
        ],
        in_specs=[spec(rows, D), spec(rows // PATCH, D), spec(rows, D), whole((8, D)), whole(full.shape)],
        out_specs=[spec(o[0], o[1]) if o else pl.BlockSpec((8, D), lambda i: (0, 0)) for o in outs],
        scratch_shapes=[
            pltpu.VMEM((rows, 3 * D), bf),
            pltpu.VMEM((2 * PAIRS, rows, TILE), f32),
            pltpu.VMEM((rows, D), f32),
            pltpu.VMEM((rows, D), f32),
        ],
        compiler_params=pltpu.CompilerParams(dimension_semantics=("arbitrary",), vmem_limit_bytes=64_000_000),
        name="fine_block",
    )(byte_rows, previous, cotangent, small, full)


def coarse_kernel(grad_ref, embedded_ref, middle_ref, lifted_ref, triple, chances, small_ref, w_hbm, patch_hbm, bytes_hbm,
                  branch_ref, lifted_grad_ref, low_ref, triple_grad_ref, embed_ref, vectors_ref, out_ref,
                  w, patch, byte_grad, spread, mixed_ref, grad_second, sems):
    bf = jnp.bfloat16
    core = lax.axis_index("seq")
    parts = ((8 * D, 4 * D), (4 * D, 4 * D), (3 * D, D), (0, 3 * D))
    copies = [
        pltpu.make_async_copy(w_hbm.at[:, pl.ds(*part)], w.at[:, pl.ds(*part)], sems.at[i]) for i, part in enumerate(parts)
    ]
    copies.append(pltpu.make_async_copy(patch_hbm, patch, sems.at[4]))
    copies.append(pltpu.make_async_copy(bytes_hbm, byte_grad, sems.at[5]))
    for copy in copies:
        copy.start()
    first_gain, second_gain = small_ref[0:1], small_ref[2:3]
    branch = grad_ref[...].astype(bf)
    branch_ref[...] = branch
    unit_two, scale_two = normalize(middle_ref[...])
    copies[0].wait()
    copies[1].wait()
    for j in range(4):
        here = slice(j * D, j * D + D)
        _, slope = gate_both(lifted_ref[:, here])
        lifted_grad = (product(branch, w[:, 8 * D + j * D : 9 * D + j * D]) * slope).astype(bf)
        lifted_grad_ref[:, here] = lifted_grad
        term = right_product(lifted_grad, w[:, 4 * D + j * D : 5 * D + j * D])
        if j:
            grad_second[...] += term
        else:
            grad_second[...] = term
    grad_two = grad_second[...]
    grad_middle = grad_ref[...] + normalize_back(grad_two, unit_two, scale_two, second_gain)
    low = grad_middle.astype(bf)
    low_ref[...] = low
    copies[2].wait()
    mixed_ref[...] = product(low, w[:, 3 * D : 4 * D]).astype(bf)

    def attend_back(pair, _):
        lanes = [pl.ds(pl.multiple_of(i * D + pair * 128, 128), 128) for i in range(3)]
        factor = 1.0 / math.sqrt(HEAD_DIM)
        queries = head_lanes(triple[:, lanes[0]])
        keys = head_lanes(triple[:, lanes[1]])
        values = triple[:, lanes[2]]
        mixed = head_lanes(mixed_ref[:, lanes[0]])
        sums = [None, None, None]
        for head in range(2):
            found = chances[pair * 2 + head]
            grad = right_product(mixed[head], values)
            scores = (found * (grad - jnp.sum(grad * found, -1, keepdims=True))).astype(bf)
            terms = (
                product(scores, keys[head]),
                left_product(scores, queries[head]),
                left_product(found.astype(bf), mixed[head]),
            )
            sums = [t if s is None else s + t for s, t in zip(sums, terms)]
        triple_grad_ref[:, lanes[0]] = (sums[0] * factor).astype(bf)
        triple_grad_ref[:, lanes[1]] = (sums[1] * factor).astype(bf)
        triple_grad_ref[:, lanes[2]] = sums[2].astype(bf)
        return 0

    lax.fori_loop(0, PAIRS, attend_back, 0)
    copies[3].wait()
    grad_one = right_product(triple_grad_ref[...], w[:, : 3 * D])
    unit_one, scale_one = normalize(embedded_ref[...])
    embed_ref[...] = (grad_middle + normalize_back(grad_one, unit_one, scale_one, first_gain)).astype(bf)
    terms = [grad_one * unit_one, grad_one, grad_two * unit_two, grad_two]
    vectors_ref[...] = jnp.concatenate([jnp.sum(t, 0, keepdims=True) for t in terms] + [jnp.zeros((4, D), jnp.float32)], 0)
    patches = byte_grad.shape[0] // PATCH
    rows = embed_ref[pl.ds(pl.multiple_of(core * patches, 128), patches)]
    copies[4].wait()
    copies[5].wait()
    for i in range(PATCH):
        term = right_product(rows, patch[i * D : i * D + D])
        for j in range(D // 128):
            spread[j, pl.ds(i, patches, stride=PATCH)] = term[:, j * 128 : j * 128 + 128]
    for j in range(D // 128):
        here = slice(j * 128, j * 128 + 128)
        out_ref[:, here] = (byte_grad[:, here] + spread[j]).astype(bf)


def coarse_block_back(grad, embedded, middle, lifted, triple, chances, small, full, patch, byte_grad):
    count = grad.shape[0]
    bf, f32 = jnp.bfloat16, jnp.float32
    outs = [((count, D), bf), ((count, 4 * D), bf), ((count, D), bf), ((count, 3 * D), bf), ((count, D), bf), ((8, D), f32),
            (byte_grad.shape, bf)]
    return pl.pallas_call(
        coarse_kernel,
        out_shape=[jax.ShapeDtypeStruct(*out) for out in outs],
        in_specs=[pl.BlockSpec(memory_space=VMEM)] * 7 + [pl.BlockSpec(memory_space=HBM)] * 3,
        out_specs=[pl.BlockSpec(memory_space=VMEM)] * len(outs),
        scratch_shapes=[
            pltpu.VMEM(full.shape, bf),
            pltpu.VMEM(patch.shape, bf),
            pltpu.VMEM(byte_grad.shape, f32),
            pltpu.VMEM((D // 128, byte_grad.shape[0], 128), f32),
            pltpu.VMEM((count, D), bf),
            pltpu.VMEM((count, D), f32),
            pltpu.SemaphoreType.DMA((6,)),
        ],
        compiler_params=pltpu.CompilerParams(vmem_limit_bytes=64_000_000),
        name="coarse_block_back",
    )(grad, embedded, middle, lifted, triple, chances, small, full, patch, byte_grad)


def solution(mesh):
    return jax.shard_map(
        fast_body if (mesh.shape["seq"], mesh.shape["fsdp"]) == (2, 16) else body,
        mesh=mesh,
        in_specs=(
            P("fsdp", "seq", None),
            P("fsdp", None),
            P("fsdp", "seq", None),
            P("fsdp", None),
            P("fsdp"),
            P("fsdp"),
            P("fsdp", None),
            P(None, "fsdp"),
            P("fsdp"),
            P("fsdp"),
            P("fsdp", None),
            P(None, "fsdp"),
            P("fsdp"),
            P("fsdp"),
            P("fsdp", None),
            P(None, "fsdp"),
            P("fsdp"),
            P("fsdp"),
            P("fsdp", None),
            P(None, "fsdp"),
        ),
        out_specs=(
            P("fsdp", "seq", None),
            P("fsdp", "seq", None),
            P("fsdp", None),
            P("fsdp"),
            P("fsdp"),
            P("fsdp", None),
            P(None, "fsdp"),
            P("fsdp"),
            P("fsdp"),
            P("fsdp", None),
            P(None, "fsdp"),
            P("fsdp"),
            P("fsdp"),
            P("fsdp", None),
            P(None, "fsdp"),
            P("fsdp"),
            P("fsdp"),
            P("fsdp", None),
            P(None, "fsdp"),
        ),
        check_vma=False,
    )
```
